32 devices in a mesh: dp: 4 (over z), blk: 2 (over core), uly: 4 (over y, x).
Axes of the slice: x: 2, y: 2, z: 4, core: 2. Of those that a mesh axis runs over, the one named last changes fastest.
Arguments:
- tokens: bfloat16 [4, 2048, 768], P('dp', ('blk', 'uly')), may hold values from -6 to 6
- lengths: int32 [4], P('dp'), may hold values from 512 to 2048, as said below
- cotangent: bfloat16 [4, 2048, 768], P('dp', ('blk', 'uly')), may hold values from -6 to 6
- attend_weight: bfloat16 [768, 2304], P('dp'), may hold values from -0.3125 to 0.3125
- query_bias: bfloat16 [768], P('dp'), may hold values from -3 to 3
- value_bias: bfloat16 [768], P('dp'), may hold values from -0.8984375 to 0.8984375
- mixer_weight: bfloat16 [768, 768], P('dp'), may hold values from -1.5 to 1.5
- mixer_bias: bfloat16 [768], P('dp'), may hold values from -3 to 3
- attn_gain: bfloat16 [768], P('dp'), may hold values from 0.5 to 1.5
- attn_shift: bfloat16 [768], P('dp'), may hold values from -2 to 2
- expand_weight: bfloat16 [768, 3072], P('dp'), may hold values from -0.21875 to 0.21875
- expand_bias: bfloat16 [3072], P('dp'), may hold values from -3 to 3
- shrink_weight: bfloat16 [3072, 768], P('dp'), may hold values from -0.109375 to 0.109375
- shrink_bias: bfloat16 [768], P('dp'), may hold values from -2 to 2
- final_gain: bfloat16 [768], P('dp'), may hold values from 0.5 to 1.5
- final_shift: bfloat16 [768], P('dp'), may hold values from -2 to 2
Outputs:
- mixed: bfloat16 [4, 2048, 768], P('dp', ('blk', 'uly'))
- tokens_grad: float32 [4, 2048, 768], P('dp', ('blk', 'uly'))
- attend_grad: float32 [768, 2304], P('dp')
- query_bias_grad: float32 [768], P('dp')
- value_bias_grad: float32 [768], P('dp')
- mixer_grad: float32 [768, 768], P('dp')
- mixer_bias_grad: float32 [768], P('dp')
- attn_gain_grad: float32 [768], P('dp')
- attn_shift_grad: float32 [768], P('dp')
- expand_grad: float32 [768, 3072], P('dp')
- expand_bias_grad: float32 [3072], P('dp')
- shrink_grad: float32 [3072, 768], P('dp')
- shrink_bias_grad: float32 [768], P('dp')
- final_gain_grad: float32 [768], P('dp')
- final_shift_grad: float32 [768], P('dp')
The draws below stay inside these ranges and needn't reach their ends.
Inputs may be any that keep to these rules, and one draw needn't show every extreme that they name: `lengths`: the number of leading positions of each sequence that hold real tokens; in every draw one sequence has 2048 and another 2048 // 4.
All inputs are finite; a program needn't handle non-finite values.
Results may differ from the reference program's by a relative error of at most 0.04.
Values may be sent and summed in bfloat16 or wider, within the bound.
No kernel may reach another device: no remote copies, remote signals or barrier semaphores. Data moves between devices by JAX's collectives and lax.ppermute only.
A program may use at most 128 MiB of HBM per device.

```python
import jax
import jax.numpy as jnp
from jax import lax

D = 768
HEADS = 12
HD = 64
FF = 3072
SEQ_LEN = 2048
BATCH = 4
N_BLK = 2


def draw_lengths(key, part):
    key_base, key_first, key_second = jax.random.split(jax.random.fold_in(key, 17), 3)
    base_lengths = jax.random.randint(key_base, (BATCH,), SEQ_LEN // 4, SEQ_LEN + 1)
    first_index = jax.random.randint(key_first, (), 0, BATCH)
    second_index = (first_index + jax.random.randint(key_second, (), 1, max(BATCH, 2))) % BATCH
    positions = jnp.arange(BATCH, dtype=jnp.int32)
    base_lengths = jnp.where(positions == second_index, SEQ_LEN // 4, base_lengths)
    base_lengths = jnp.where(positions == first_index, SEQ_LEN, base_lengths)
    return base_lengths.astype(jnp.int32)


def block_scale(rng, shape, shards, smallest, largest):
    gain, own = 1.0, jax.random.fold_in(rng, 6)
    for dim, blocks in shards:
        draws = jnp.exp(jax.random.uniform(jax.random.fold_in(own, dim), (blocks,), jnp.float32, smallest / len(shards), largest / len(shards)))
        gain = gain * jnp.repeat(draws, shape[dim] // blocks).reshape([-1 if axis == dim else 1 for axis in range(len(shape))])
    return gain


def bell_draw(own_key, shape, scale, most, shards=(), held_as=jnp.bfloat16):
    drawn = scale * jax.random.normal(own_key, shape, jnp.float32)
    if shards:
        drawn = drawn * block_scale(own_key, shape, shards, -0.22, 0.18)
    return jnp.clip(drawn, -most, most).astype(held_as)


def setup_inputs(seed: int = 0) -> dict:
    key_of = jax.random.split(jax.random.key(seed), 17)
    tokens = bell_draw(key_of[0], (BATCH, SEQ_LEN, D), 1.0, 6.0, ((0, 4), (1, 8)))
    lengths = draw_lengths(jax.random.fold_in(key_of[16], 71), 0)
    cotangent = bell_draw(key_of[2], (BATCH, SEQ_LEN, D), 1.0, 6.0, ((0, 4), (1, 8)))
    attend_weight = bell_draw(key_of[3], (D, 3 * D), (D // 2) ** -0.5, 0.3125, ((0, 4),))
    query_bias = bell_draw(key_of[4], (D,), 0.5, 3.0, ((0, 4),))
    value_bias = bell_draw(key_of[5], (D,), 0.15, 0.8984375, ((0, 4),))
    mixer_weight = bell_draw(key_of[6], (D, D), (D // 48) ** -0.5, 1.5, ((0, 4),))
    mixer_bias = bell_draw(key_of[7], (D,), 0.5, 3.0, ((0, 4),))
    attn_gain = jnp.clip(1.0 + 0.1 * jax.random.normal(key_of[8], (D,), jnp.float32), 0.5, 1.5).astype(jnp.bfloat16)
    attn_shift = bell_draw(key_of[9], (D,), 0.3, 2.0, ((0, 4),))
    expand_weight = bell_draw(key_of[10], (D, FF), D ** -0.5, 0.21875, ((0, 4),))
    expand_bias = bell_draw(key_of[11], (FF,), 0.5, 3.0, ((0, 4),))
    shrink_weight = bell_draw(key_of[12], (FF, D), FF ** -0.5, 0.109375, ((0, 4),))
    shrink_bias = bell_draw(key_of[13], (D,), 0.3, 2.0, ((0, 4),))
    final_gain = jnp.clip(1.0 + 0.1 * jax.random.normal(key_of[14], (D,), jnp.float32), 0.5, 1.5).astype(jnp.bfloat16)
    final_shift = bell_draw(key_of[15], (D,), 0.3, 2.0, ((0, 4),))
    return {"tokens": tokens, "lengths": lengths, "cotangent": cotangent, "attend_weight": attend_weight, "query_bias": query_bias, "value_bias": value_bias, "mixer_weight": mixer_weight, "mixer_bias": mixer_bias, "attn_gain": attn_gain, "attn_shift": attn_shift, "expand_weight": expand_weight, "expand_bias": expand_bias, "shrink_weight": shrink_weight, "shrink_bias": shrink_bias, "final_gain": final_gain, "final_shift": final_shift}


EPSILON = 1e-12
MASKED = -1000000000.0
PRECISE = lax.Precision.HIGHEST

@jax.custom_vjp
def low(v):
    return lax.optimization_barrier(v.astype(jnp.bfloat16)).astype(jnp.float32)

@jax.custom_vjp
def low_back(v):
    return v

def low_keep(v):
    return (low(v), None)

def low_pass(kept, grad):
    return (grad,)

def back_keep(v):
    return (v, None)

def back_low(kept, grad):
    return (low(grad),)
low.defvjp(low_keep, low_pass)
low_back.defvjp(back_keep, back_low)

def dense_mm(left_mat, right_mat):
    return jnp.dot(left_mat, right_mat, precision=PRECISE, preferred_element_type=jnp.float32)

def layer_norm(hidden, gain_vec, shift_vec):
    center = hidden - lax.optimization_barrier(jnp.mean(hidden, -1, keepdims=True))
    scale_inv = lax.rsqrt(lax.optimization_barrier(jnp.mean(center * center, -1, keepdims=True)) + EPSILON)
    normed = center * scale_inv
    return normed * gain_vec + shift_vec

def attend_block(query_block, key_heads, value_heads, valid_keys):
    scores = jnp.einsum('qhe,khe->hqk', query_block, key_heads, precision=PRECISE)
    scores = low_back(scores)
    scores = jnp.where(valid_keys[None, None, :], scores, MASKED)
    softmax_rows = low(jax.nn.softmax(scores, axis=-1))
    return jnp.einsum('hqk,khe->qhe', softmax_rows, value_heads, precision=PRECISE)

def sequence_layer(inputs, length, params):
    attend_w, query_b, value_b, mixer_w, mixer_b, attn_g, attn_s, expand_w, expand_b, shrink_w, shrink_b, final_g, final_s = params
    projected = dense_mm(inputs, attend_w)
    query_heads = low(low_back((projected[:, :D] + query_b) * 0.125)).reshape(SEQ_LEN, HEADS, HD)
    key_heads = low(low_back(projected[:, D:2 * D])).reshape(SEQ_LEN, HEADS, HD)
    value_heads = low(low_back(projected[:, 2 * D:] + value_b)).reshape(SEQ_LEN, HEADS, HD)
    valid_keys = jnp.arange(SEQ_LEN, dtype=jnp.int32) < length
    query_blocks = query_heads.reshape(N_BLK, SEQ_LEN // N_BLK, HEADS, HD)
    block_step = jax.checkpoint(attend_block)
    attended = lax.map(lambda query_block: block_step(query_block, key_heads, value_heads, valid_keys), query_blocks)
    attended = low(low_back(attended.reshape(SEQ_LEN, D)))
    first_out = layer_norm(inputs + (low_back(dense_mm(attended, mixer_w)) + mixer_b), attn_g, attn_s)
    pre_act = low_back(dense_mm(low(first_out), expand_w) + expand_b)
    activation = low(jax.nn.gelu(pre_act, approximate=False))
    branch = low_back(dense_mm(activation, shrink_w)) + shrink_b
    return layer_norm(first_out + branch, final_g, final_s)

def reference(tokens, lengths, cotangent, attend_weight, query_bias, value_bias, mixer_weight, mixer_bias, attn_gain, attn_shift, expand_weight, expand_bias, shrink_weight, shrink_bias, final_gain, final_shift):
    params = tuple((weight_item.astype(jnp.float32) for weight_item in (attend_weight, query_bias, value_bias, mixer_weight, mixer_bias, attn_gain, attn_shift, expand_weight, expand_bias, shrink_weight, shrink_bias, final_gain, final_shift)))
    inputs = tokens.astype(jnp.float32)

    def whole_layer(all_inputs, all_params):
        layer_step = jax.checkpoint(sequence_layer)
        return lax.map(lambda seq_pair: layer_step(seq_pair[0], seq_pair[1], all_params), (all_inputs, lengths))
    outputs, pullback = jax.vjp(whole_layer, inputs, params)
    inputs_grad, param_grads = pullback(cotangent.astype(jnp.float32))
    return (outputs.astype(jnp.bfloat16), inputs_grad, param_grads[0], param_grads[1], param_grads[2], param_grads[3], param_grads[4], param_grads[5], param_grads[6], param_grads[7], param_grads[8], param_grads[9], param_grads[10], param_grads[11], param_grads[12])
```

```python
import functools

import jax
import jax.numpy as jnp
from jax import lax
from jax.experimental import pallas as pl
from jax.experimental.pallas import tpu as pltpu
from jax.sharding import PartitionSpec as P

HEADS = 12
HD = 64

EPSILON = 1e-12
MASKED = -1000000000.0
LOG2E = 1.4426950408889634
LN2 = 0.6931471805599453
F32 = jnp.float32
BF16 = jnp.bfloat16


def dot_nn(left, right):
    return lax.dot_general(left, right, (((1,), (0,)), ((), ())), preferred_element_type=F32)


def dot_nt(left, right):
    return lax.dot_general(left, right, (((1,), (1,)), ((), ())), preferred_element_type=F32)


def dot_tn(left, right):
    return lax.dot_general(left, right, (((0,), (0,)), ((), ())), preferred_element_type=F32)


def swap_with(value, axis, offset):
    size = lax.axis_size(axis)
    return lax.ppermute(value, axis, [(i, i ^ offset) for i in range(size)])


def xor_order(pieces, index):
    bit = 1
    while bit < len(pieces):
        flag = (index & bit) != 0
        pieces = [jnp.where(flag, pieces[p ^ bit], pieces[p]) for p in range(len(pieces))]
        bit *= 2
    return pieces


def total(values):
    acc = values[0].astype(F32)
    for value in values[1:]:
        acc = acc + value.astype(F32)
    return acc


def pad_rows(value, rows):
    return jnp.pad(value, ((0, rows - value.shape[0]), (0, 0)))


def head_lanes(width, head, ones_lane=None):
    lane = lax.broadcasted_iota(jnp.int32, (1, width), 1)
    keep = (lane >= head * HD) & (lane < (head + 1) * HD)
    if ones_lane is not None:
        keep = keep | (lane == ones_lane)
    return keep


def attend_forward_kernel(heads, blocks, q_ref, *refs):
    kv_refs = refs[:blocks]
    o_ref, lse_ref, vt_ref = refs[blocks:]
    group = heads * HD
    wide = q_ref.shape[1]
    rows = kv_refs[0].shape[0]

    @pl.when(pl.program_id(0) == 0)
    def _():
        for i in range(blocks):
            vt_ref[:, i * rows : (i + 1) * rows] = kv_refs[i][:, wide : wide + group].T

    q = q_ref[...]
    outs = []
    stats = []
    for head in range(heads):
        q_head = jnp.where(head_lanes(wide, head, group), q, jnp.zeros_like(q))
        scores = [dot_nt(kv_refs[i][:, :wide], q_head) for i in range(blocks)]
        top = jnp.max(scores[0], axis=0, keepdims=True)
        for i in range(1, blocks):
            top = jnp.maximum(top, jnp.max(scores[i], axis=0, keepdims=True))
        norm = jnp.zeros_like(top)
        acc = None
        for i in range(blocks):
            probs = jnp.exp2(scores[i] - top)
            norm = norm + jnp.sum(probs, axis=0, keepdims=True)
            part = dot_nn(
                vt_ref[head * HD : (head + 1) * HD, i * rows : (i + 1) * rows], probs.astype(BF16)
            )
            acc = part if acc is None else acc + part
        outs.append(acc / norm)
        stats.append(top + jnp.log2(norm))
    o_ref[...] = jnp.concatenate(outs, axis=0).T.astype(BF16)
    for head in range(heads):
        lse_ref[head : head + 1, :] = stats[head]


def attend_forward(q, kvs, heads, tile):
    rows, wide = q.shape
    group = heads * HD
    blocks = len(kvs)
    keys = blocks * rows
    whole = pl.BlockSpec(kvs[0].shape, lambda t: (0, 0))
    return pl.pallas_call(
        functools.partial(attend_forward_kernel, heads, blocks),
        grid=(rows // tile,),
        in_specs=[pl.BlockSpec((tile, wide), lambda t: (t, 0))] + [whole] * blocks,
        out_specs=[
            pl.BlockSpec((tile, group), lambda t: (t, 0)),
            pl.BlockSpec((8, tile), lambda t: (0, t)),
        ],
        out_shape=[
            jax.ShapeDtypeStruct((rows, group), BF16),
            jax.ShapeDtypeStruct((8, rows), F32),
        ],
        scratch_shapes=[pltpu.VMEM((group, keys), BF16)],
        compiler_params=pltpu.CompilerParams(vmem_limit_bytes=56 * 2**20),
        cost_estimate=pl.CostEstimate(
            flops=4 * heads * rows * keys * wide,
            transcendentals=heads * rows * keys,
            bytes_accessed=2 * rows * wide * 3 + 2 * keys * (wide + group),
        ),
        name="attend_forward",
    )(q, *kvs)


def attend_backward_kernel(heads, blocks, q_ref, do_ref, o_ref, lse_ref, *refs):
    kv_refs = refs[:blocks]
    dq_ref = refs[blocks]
    dkv_refs = refs[blocks + 1 : 2 * blocks + 1]
    kt_ref = refs[2 * blocks + 1]
    dk_accs = refs[2 * blocks + 2 : 3 * blocks + 2]
    dv_accs = refs[3 * blocks + 2 :]
    group = heads * HD
    wide = q_ref.shape[1]
    rows = kv_refs[0].shape[0]

    @pl.when(pl.program_id(0) == 0)
    def _():
        for i in range(blocks):
            kt_ref[:, i * rows : (i + 1) * rows] = kv_refs[i][:, :group].T
            dk_accs[i][...] = jnp.zeros_like(dk_accs[i])
            dv_accs[i][...] = jnp.zeros_like(dv_accs[i])

    q = q_ref[...]
    dout = do_ref[...]
    products = (dout.astype(F32) * o_ref[...].astype(F32)).T
    dqs = []
    for head in range(heads):
        q_head = jnp.where(head_lanes(wide, head, group), q, jnp.zeros_like(q))
        do_head = jnp.where(head_lanes(group, head), dout, jnp.zeros_like(dout))
        lse = lse_ref[head : head + 1, :]
        delta = jnp.sum(products[head * HD : (head + 1) * HD], axis=0, keepdims=True)
        acc = None
        for i in range(blocks):
            probs = jnp.exp2(dot_nt(kv_refs[i][:, :wide], q_head) - lse)
            dv_accs[i][...] += dot_nn(probs.astype(BF16), do_head)
            grads = dot_nt(kv_refs[i][:, wide : wide + group], do_head)
            grads = (probs * (grads - delta)).astype(BF16)
            dk_accs[i][...] += dot_nn(grads, q_head)
            part = dot_nn(
                kt_ref[head * HD : (head + 1) * HD, i * rows : (i + 1) * rows], grads
            )
            acc = part if acc is None else acc + part
        dqs.append(acc)
    dq_ref[...] = jnp.concatenate(dqs, axis=0).T.astype(BF16)

    @pl.when(pl.program_id(0) == pl.num_programs(0) - 1)
    def _():
        for i in range(blocks):
            dkv_refs[i][:, :group] = (dk_accs[i][:, :group] * LN2).astype(BF16)
            dkv_refs[i][:, wide : wide + group] = dv_accs[i][...].astype(BF16)


def attend_backward(q, kvs, dout, o, lse, heads, tile):
    rows, wide = q.shape
    group = heads * HD
    blocks = len(kvs)
    keys = blocks * rows
    whole = pl.BlockSpec(kvs[0].shape, lambda t: (0, 0))
    out = pl.pallas_call(
        functools.partial(attend_backward_kernel, heads, blocks),
        grid=(rows // tile,),
        in_specs=[
            pl.BlockSpec((tile, wide), lambda t: (t, 0)),
            pl.BlockSpec((tile, group), lambda t: (t, 0)),
            pl.BlockSpec((tile, group), lambda t: (t, 0)),
            pl.BlockSpec((8, tile), lambda t: (0, t)),
        ]
        + [whole] * blocks,
        out_specs=[pl.BlockSpec((tile, group), lambda t: (t, 0))] + [whole] * blocks,
        out_shape=[jax.ShapeDtypeStruct((rows, group), BF16)]
        + [jax.ShapeDtypeStruct(kvs[0].shape, BF16)] * blocks,
        scratch_shapes=[pltpu.VMEM((group, keys), BF16)]
        + [pltpu.VMEM((rows, wide), F32)] * blocks
        + [pltpu.VMEM((rows, group), F32)] * blocks,
        compiler_params=pltpu.CompilerParams(vmem_limit_bytes=56 * 2**20),
        cost_estimate=pl.CostEstimate(
            flops=10 * heads * rows * keys * wide,
            transcendentals=heads * rows * keys,
            bytes_accessed=2 * rows * wide * 4 + 4 * keys * (wide + group),
        ),
        name="attend_backward",
    )(q, dout, o, lse, *kvs)
    return out[0], out[1:]


def feed_kernel(
    x1_ref,
    x1b_ref,
    expand_ref,
    shrink_ref,
    ebias_ref,
    sbias_ref,
    gain_ref,
    shift_ref,
    cot_ref,
    mixed_ref,
    dx1_ref,
    dexpand_ref,
    dshrink_ref,
    debias_ref,
    vec_ref,
    act_ref,
    slope_ref,
    acc_ref,
    d2b_ref,
    x1t_ref,
):
    phase = pl.program_id(0)
    step = pl.program_id(1)
    last = pl.num_programs(1) - 1
    width = x1_ref.shape[1]

    @pl.when(phase == 0)
    def _():
        pre = dot_nn(x1b_ref[...], expand_ref[0]) + ebias_ref[0]
        cdf = 0.5 * (1.0 + lax.erf(pre * 0.7071067811865476))
        pdf = jnp.exp(-0.5 * pre * pre) * 0.3989422804014327
        act = (pre * cdf).astype(BF16)
        act_ref[step] = act
        slope_ref[step] = (cdf + pre * pdf).astype(BF16)
        part = dot_nn(act, shrink_ref[0])

        @pl.when(step == 0)
        def _():
            acc_ref[...] = part
            x1t_ref[...] = x1b_ref[...].T

        @pl.when(step > 0)
        def _():
            acc_ref[...] += part

        @pl.when(step == last)
        def _():
            hidden = x1_ref[...] + (acc_ref[...] + sbias_ref[...])
            center = hidden - jnp.mean(hidden, -1, keepdims=True)
            inverse = lax.rsqrt(jnp.mean(center * center, -1, keepdims=True) + EPSILON)
            normed = center * inverse
            mixed_ref[...] = (normed * gain_ref[...] + shift_ref[...]).astype(BF16)
            grad = cot_ref[...].astype(F32)
            scaled = grad * gain_ref[...]
            dhidden = inverse * (
                scaled
                - jnp.mean(scaled, -1, keepdims=True)
                - normed * jnp.mean(scaled * normed, -1, keepdims=True)
            )
            acc_ref[...] = dhidden
            d2b_ref[...] = dhidden.astype(BF16)
            vec_ref[...] = jnp.zeros_like(vec_ref)
            vec_ref[0:1, :] = jnp.sum(grad * normed, 0, keepdims=True)
            vec_ref[1:2, :] = jnp.sum(grad, 0, keepdims=True)
            vec_ref[2:3, :] = jnp.sum(dhidden, 0, keepdims=True)

    @pl.when(phase == 1)
    def _():
        d2b = d2b_ref[...]
        dpre = (dot_nt(d2b, shrink_ref[0]) * slope_ref[step].astype(F32)).astype(BF16)
        debias_ref[0] = jnp.sum(dpre.astype(F32), 0, keepdims=True)
        dexpand_ref[0] = dot_nn(x1t_ref[...], dpre).astype(BF16)
        dshrink_ref[0] = dot_tn(act_ref[step], d2b).astype(BF16)
        acc_ref[...] += dot_nt(dpre, expand_ref[0])

        @pl.when(step == last)
        def _():
            dx1_ref[...] = acc_ref[...]


def feed_forward_backward(x1, x1b, expand, shrink, ebias, sbias, gain, shift, cot):
    rows, width = x1.shape
    parts, _, block = expand.shape
    full = pl.BlockSpec((rows, width), lambda p, k: (0, 0))
    line = pl.BlockSpec((1, width), lambda p, k: (0, 0))
    return pl.pallas_call(
        feed_kernel,
        grid=(2, parts),
        in_specs=[
            full,
            full,
            pl.BlockSpec((1, width, block), lambda p, k: (k, 0, 0)),
            pl.BlockSpec((1, block, width), lambda p, k: (k, 0, 0)),
            pl.BlockSpec((1, 1, block), lambda p, k: (k, 0, 0)),
            line,
            line,
            line,
            full,
        ],
        out_specs=[
            full,
            full,
            pl.BlockSpec((1, width, block), lambda p, k: (p * k, 0, 0)),
            pl.BlockSpec((1, block, width), lambda p, k: (p * k, 0, 0)),
            pl.BlockSpec((1, 1, block), lambda p, k: (p * k, 0, 0)),
            pl.BlockSpec((8, width), lambda p, k: (0, 0)),
        ],
        out_shape=[
            jax.ShapeDtypeStruct((rows, width), BF16),
            jax.ShapeDtypeStruct((rows, width), F32),
            jax.ShapeDtypeStruct((parts, width, block), BF16),
            jax.ShapeDtypeStruct((parts, block, width), BF16),
            jax.ShapeDtypeStruct((parts, 1, block), F32),
            jax.ShapeDtypeStruct((8, width), F32),
        ],
        scratch_shapes=[
            pltpu.VMEM((parts, rows, block), BF16),
            pltpu.VMEM((parts, rows, block), BF16),
            pltpu.VMEM((rows, width), F32),
            pltpu.VMEM((rows, width), BF16),
            pltpu.VMEM((width, rows), BF16),
        ],
        compiler_params=pltpu.CompilerParams(vmem_limit_bytes=48 * 2**20),
        cost_estimate=pl.CostEstimate(
            flops=12 * rows * width * parts * block,
            transcendentals=2 * rows * parts * block,
            bytes_accessed=12 * width * parts * block,
        ),
        name="feed_forward_backward",
    )(x1, x1b, expand, shrink, ebias, sbias, gain, shift, cot)


def on_device(
    tokens,
    lengths,
    cotangent,
    attend_weight,
    query_bias,
    value_bias,
    mixer_weight,
    mixer_bias,
    attn_gain,
    attn_shift,
    expand_weight,
    expand_bias,
    shrink_weight,
    shrink_bias,
    final_gain,
    final_shift,
):
    uly = lax.axis_size("uly")
    blk = lax.axis_size("blk")
    dp = lax.axis_size("dp")
    u = lax.axis_index("uly")
    b = lax.axis_index("blk")
    z = lax.axis_index("dp")
    width = tokens.shape[-1]
    rows = tokens.shape[0] * tokens.shape[1]
    block_rows = uly * rows
    heads = HEADS // uly
    group = heads * HD
    wide = -(-(group + 1) // 128) * 128
    shard = attend_weight.shape[0]
    hidden = expand_weight.shape[1]
    parts = blk * uly
    unit = hidden // (parts * dp)
    share = shard // blk

    x = tokens.reshape(rows, width)
    x_rows = jnp.concatenate([x] + [swap_with(x, "uly", j) for j in range(1, uly)], 0)

    small = jnp.concatenate(
        [query_bias, value_bias, mixer_bias, attn_gain, attn_shift, shrink_bias]
        + [final_gain, final_shift, expand_bias]
    )
    small_rows = small.shape[0] // (3 * group)
    own_heads = lax.dynamic_slice_in_dim(attend_weight.reshape(shard, 3, uly, group), u, 1, 2)
    own_heads = own_heads.reshape(shard, 3 * group)
    first_piece = jnp.concatenate(
        [
            lax.dynamic_slice_in_dim(own_heads, b * share, share, 0),
            pad_rows(small.reshape(small_rows, 3 * group), 16),
        ]
    )
    first_all = lax.all_gather(first_piece, "dp", axis=0, tiled=False)
    halves = first_all[:, :share]
    halves = xor_order([halves] + [swap_with(halves, "blk", i) for i in range(1, blk)], b)
    attend_own = jnp.stack(halves, 1).reshape(width, 3, group)
    vectors = first_all[:, share : share + small_rows].reshape(dp, -1, shard).astype(F32)
    names = [vectors[:, k].reshape(width) for k in range(8)]
    bias_query, bias_value, bias_mixer, gain_attn, shift_attn, bias_shrink = names[:6]
    gain_final, shift_final = names[6:]
    bias_expand = vectors[:, 8:].reshape(dp, parts, unit).transpose(1, 0, 2)
    bias_expand = jnp.stack(
        xor_order(list(bias_expand.reshape(parts, dp * unit)), b * uly + u), 0
    ).reshape(parts, 1, dp * unit)

    mixer_own = lax.dynamic_slice_in_dim(mixer_weight, b * share, share, 0)
    mixer_all = jnp.stack(
        xor_order([mixer_own] + [swap_with(mixer_own, "dp", j) for j in range(1, dp)], z), 0
    )
    mixer_all = jnp.stack(
        xor_order([mixer_all] + [swap_with(mixer_all, "blk", i) for i in range(1, blk)], b), 1
    ).reshape(width, width)

    part = b * uly + u
    expand_own = lax.dynamic_slice_in_dim(
        expand_weight.reshape(shard, dp, parts, unit), part, 1, 2
    ).reshape(-1, width)
    shrink_own = lax.dynamic_slice_in_dim(shrink_weight.reshape(parts, unit, width), part, 1, 0)
    expand_rows = expand_own.shape[0]
    feed_own = jnp.concatenate([expand_own, shrink_own.reshape(unit, width)], 0)
    feed_all = lax.all_gather(feed_own, "dp", axis=0, tiled=False)
    expand_part = feed_all[:, :expand_rows].reshape(width, dp * unit)
    shrink_part = feed_all[:, expand_rows:].reshape(dp * unit, width)
    expand_two = jnp.stack([expand_part, swap_with(expand_part, "uly", 1)])
    shrink_two = jnp.stack([shrink_part, swap_with(shrink_part, "uly", 2)])
    expand_far = swap_with(expand_two, "uly", 2)
    shrink_far = swap_with(shrink_two, "uly", 1)
    expand_here = jnp.concatenate([expand_two, expand_far], 0)
    shrink_here = jnp.stack([shrink_two[0], shrink_far[0], shrink_two[1], shrink_far[1]], 0)
    expand_full = jnp.concatenate(
        [expand_here] + [swap_with(expand_here, "blk", i) for i in range(1, blk)], 0
    )
    shrink_full = jnp.concatenate(
        [shrink_here] + [swap_with(shrink_here, "blk", i) for i in range(1, blk)], 0
    )

    lane_pad = ((0, 0), (0, wide - group))
    bias_row = jnp.pad(lax.dynamic_slice_in_dim(bias_query, u * group, group, 0), lane_pad[1:])
    ones_lane = (jnp.arange(wide) == group).astype(F32)
    q = dot_nn(x_rows, jnp.pad(attend_own[:, 0], lane_pad)) + bias_row
    q = (q * (0.125 * LOG2E) + ones_lane).astype(BF16)
    kv_weight = jnp.concatenate([jnp.pad(attend_own[:, 1], lane_pad), attend_own[:, 2]], 1)
    kv_bias = jnp.concatenate(
        [jnp.zeros((wide,), F32), lax.dynamic_slice_in_dim(bias_value, u * group, group, 0)]
    )
    kv_ones = jnp.pad(ones_lane, (0, group))
    row_index = jnp.arange(block_rows, dtype=jnp.int32)
    positions = b * block_rows + ((row_index // rows) ^ u) * rows + row_index % rows
    key_mask = jnp.where(positions < lengths[0], 0.0, MASKED)
    kv = (dot_nn(x_rows, kv_weight) + kv_bias + key_mask[:, None] * kv_ones).astype(BF16)
    kvs = [kv] + [swap_with(kv, "blk", i) for i in range(1, blk)]

    o_rows, lse = attend_forward(q, kvs, heads, min(256, block_rows))
    pieces = [o_rows[j * rows : (j + 1) * rows] for j in range(uly)]
    pieces = [pieces[0]] + [swap_with(pieces[j], "uly", j) for j in range(1, uly)]
    mixer_in = jnp.concatenate(xor_order(pieces, u), 1)

    first_sum = x.astype(F32) + (dot_nn(mixer_in, mixer_all) + bias_mixer)
    center = first_sum - jnp.mean(first_sum, -1, keepdims=True)
    first_inv = lax.rsqrt(jnp.mean(center * center, -1, keepdims=True) + EPSILON)
    first_normed = center * first_inv
    first_out = first_normed * gain_attn + shift_attn
    first_low = first_out.astype(BF16)

    mixed, first_grad, expand_grad, shrink_grad, expand_bias_grad, vec_grads = (
        feed_forward_backward(
            first_out,
            first_low,
            expand_full,
            shrink_full,
            bias_expand,
            bias_shrink[None],
            gain_final[None],
            shift_final[None],
            cotangent.reshape(rows, width),
        )
    )

    scaled = first_grad * gain_attn
    attn_grad = first_inv * (
        scaled
        - jnp.mean(scaled, -1, keepdims=True)
        - first_normed * jnp.mean(scaled * first_normed, -1, keepdims=True)
    )
    attn_low = attn_grad.astype(BF16)
    out_grad = dot_nt(attn_low, mixer_all).astype(BF16)
    sends = xor_order([out_grad[:, j * group : (j + 1) * group] for j in range(uly)], u)
    dout_rows = jnp.concatenate(
        [sends[0]] + [swap_with(sends[j], "uly", j) for j in range(1, uly)], 0
    )
    dq, dkvs = attend_backward(q, kvs, dout_rows, o_rows, lse, heads, min(256, block_rows))

    mixer_grad = dot_tn(mixer_in, attn_low).astype(BF16)
    attn_gain_grad = jnp.sum(first_grad * first_normed, 0)
    attn_shift_grad = jnp.sum(first_grad, 0)
    mixer_bias_grad = jnp.sum(attn_grad, 0)
    ebg = jnp.stack(xor_order(list(expand_bias_grad.reshape(parts, dp * unit)), part), 0)
    ebg = ebg.reshape(parts, dp, unit).transpose(1, 0, 2).reshape(dp, parts * unit)
    vec_all = jnp.concatenate(
        [
            v.reshape(dp, shard)
            for v in (
                mixer_bias_grad,
                attn_gain_grad,
                attn_shift_grad,
                vec_grads[2],
                vec_grads[0],
                vec_grads[1],
            )
        ]
        + [ebg],
        1,
    ).astype(BF16)

    mixer_cols = width // blk
    mixer_part_rows = shard // uly
    vec_len = vec_all.shape[1]
    vec_rows = -(-vec_len // mixer_cols)
    vec_rows = -(-vec_rows // 16) * 16
    vec_block = jnp.pad(vec_all, ((0, 0), (0, vec_rows * mixer_cols - vec_len))).reshape(
        dp, vec_rows, mixer_cols
    )
    mixer_view = mixer_grad.reshape(dp, uly, mixer_part_rows, blk, mixer_cols)
    by_blk = xor_order([mixer_view[:, :, :, i] for i in range(blk)], b)
    mixer_parts = []
    for i in range(blk):
        by_uly = xor_order([by_blk[i][:, j] for j in range(uly)], u)
        mixer_parts.append(
            jnp.stack([jnp.concatenate([piece, vec_block], 1) for piece in by_uly], 0)
        )
    mixer_sum = total(
        [mixer_parts[0]] + [swap_with(mixer_parts[i], "blk", i) for i in range(1, blk)]
    ).astype(BF16)
    mixer_sum = total(
        [mixer_sum[0]] + [swap_with(mixer_sum[j], "uly", j) for j in range(1, uly)]
    ).astype(BF16)

    def over_blk(grad):
        return total(
            [grad[:uly]]
            + [swap_with(grad[i * uly : (i + 1) * uly], "blk", i) for i in range(1, blk)]
        ).astype(BF16)

    shrink_sum = over_blk(shrink_grad)
    expand_sum = over_blk(expand_grad)
    shrink_sum = shrink_sum.reshape(2, 2, dp * unit, width)
    expand_sum = expand_sum.reshape(2, 2, width, dp * unit)
    shrink_sum = total([shrink_sum[0], swap_with(shrink_sum[1], "uly", 2)]).astype(BF16)
    expand_sum = total([expand_sum[:, 0], swap_with(expand_sum[:, 1], "uly", 1)]).astype(BF16)
    shrink_sum = total([shrink_sum[0], swap_with(shrink_sum[1], "uly", 1)]).astype(BF16)
    expand_sum = total([expand_sum[0], swap_with(expand_sum[1], "uly", 2)]).astype(BF16)

    mixer_rows = mixer_sum.shape[1] * mixer_cols // width
    packed = jnp.concatenate(
        [
            expand_sum.reshape(dp, expand_rows, width),
            shrink_sum.reshape(dp, unit, width),
            mixer_sum.reshape(dp, mixer_rows, width),
        ],
        1,
    )

    def over_dp(value):
        sends = [lax.dynamic_slice_in_dim(value, z ^ j, 1, 0)[0] for j in range(dp)]
        return total([sends[0]] + [swap_with(sends[j], "dp", j) for j in range(1, dp)])

    owned = over_dp(packed)
    vec_owned = owned[expand_rows + unit :].reshape(-1, mixer_cols)[mixer_part_rows:]
    vec_owned = vec_owned.reshape(-1)[:vec_len]

    def in_plane(value):
        value = value.astype(BF16)
        value = jnp.stack(
            xor_order([value] + [swap_with(value, "uly", j) for j in range(1, uly)], u), 0
        )
        return jnp.stack(
            xor_order([value] + [swap_with(value, "blk", i) for i in range(1, blk)], b), 0
        )

    gathered = in_plane(owned).reshape(parts, -1, width)
    expand_out = gathered[:, :expand_rows].reshape(parts, shard, dp, unit)
    expand_out = expand_out.transpose(1, 2, 0, 3).reshape(shard, hidden).astype(F32)
    shrink_out = gathered[:, expand_rows : expand_rows + unit]
    shrink_out = shrink_out.reshape(parts * unit, width).astype(F32)
    mixer_out = gathered[:, expand_rows + unit :].reshape(blk, uly, -1, mixer_cols)
    mixer_out = mixer_out[:, :, :mixer_part_rows].transpose(1, 2, 0, 3)
    mixer_out = mixer_out.reshape(shard, width).astype(F32)

    own_dkv = total([dkvs[0]] + [swap_with(dkvs[i], "blk", i) for i in range(1, blk)])
    own_dkv = own_dkv.astype(BF16)
    proj_grad = jnp.concatenate(
        [dq * jnp.asarray(0.125, BF16), own_dkv[:, :group], own_dkv[:, wide : wide + group]], 1
    )
    token_parts = dot_nt(proj_grad, attend_own.reshape(width, 3 * group))
    token_low = token_parts.astype(BF16)
    tokens_grad = attn_grad + total(
        [token_parts[:rows]]
        + [swap_with(token_low[j * rows : (j + 1) * rows], "uly", j) for j in range(1, uly)]
    )
    attend_grad = dot_tn(x_rows, proj_grad).astype(BF16)
    attend_grad = attend_grad.reshape(dp, blk, share, 3 * group)
    bias_sum = jnp.sum(proj_grad.astype(F32), 0)[None]
    bias_rows = pad_rows(bias_sum.astype(BF16), 16)
    attend_parts = [
        jnp.concatenate(
            [
                lax.dynamic_slice_in_dim(attend_grad, b ^ i, 1, 1).reshape(-1, 3 * group),
                bias_rows,
            ],
            0,
        )
        for i in range(blk)
    ]
    attend_sum = total(
        [attend_parts[0]] + [swap_with(attend_parts[i], "blk", i) for i in range(1, blk)]
    ).astype(BF16)
    bias_half = jnp.broadcast_to(attend_sum[dp * share :], (dp, 16, 3 * group))
    attend_sum = attend_sum[: dp * share].reshape(dp, share, 3 * group)
    attend_owned = over_dp(jnp.concatenate([attend_sum, bias_half], 1))
    attend_all = in_plane(attend_owned)
    attend_out = attend_all[:, :, :share].reshape(blk, uly, share, 3, group)
    attend_out = attend_out.transpose(0, 2, 3, 1, 4).reshape(shard, 3 * width).astype(F32)
    bias_out = attend_all[0, :, share].astype(F32).reshape(uly, 3, group)
    query_bias_grad = lax.dynamic_slice_in_dim(bias_out[:, 0].reshape(width), z * shard, shard, 0)
    value_bias_grad = lax.dynamic_slice_in_dim(bias_out[:, 2].reshape(width), z * shard, shard, 0)

    vecs = [vec_owned[k * shard : (k + 1) * shard] for k in range(6)]
    return (
        mixed.reshape(tokens.shape),
        tokens_grad.reshape(tokens.shape),
        attend_out,
        query_bias_grad,
        value_bias_grad,
        mixer_out,
        vecs[0],
        vecs[1],
        vecs[2],
        expand_out,
        vec_owned[6 * shard :],
        shrink_out,
        vecs[3],
        vecs[4],
        vecs[5],
    )


def solution(mesh):
    row_spec = P("dp", ("blk", "uly"), None)
    matrix = P("dp", None)
    vector = P("dp")
    return jax.shard_map(
        on_device,
        mesh=mesh,
        in_specs=(
            row_spec,
            vector,
            row_spec,
            matrix,
            vector,
            vector,
            matrix,
            vector,
            vector,
            vector,
            matrix,
            vector,
            matrix,
            vector,
            vector,
            vector,
        ),
        out_specs=(
            row_spec,
            row_spec,
            matrix,
            vector,
            vector,
            matrix,
            vector,
            vector,
            vector,
            matrix,
            vector,
            matrix,
            vector,
            vector,
            vector,
        ),
        check_vma=False,
    )
```

```python
import functools

import jax
import jax.numpy as jnp
from jax import lax
from jax.experimental import pallas as pl
from jax.experimental.pallas import tpu as pltpu
from jax.sharding import PartitionSpec as P

HEADS = 12
HD = 64

EPSILON = 1e-12
MASKED = -1000000000.0
LOG2E = 1.4426950408889634
LN2 = 0.6931471805599453
F32 = jnp.float32
BF16 = jnp.bfloat16


def dot_nn(left, right):
    return lax.dot_general(left, right, (((1,), (0,)), ((), ())), preferred_element_type=F32)


def dot_nt(left, right):
    return lax.dot_general(left, right, (((1,), (1,)), ((), ())), preferred_element_type=F32)


def dot_tn(left, right):
    return lax.dot_general(left, right, (((0,), (0,)), ((), ())), preferred_element_type=F32)


def swap_with(value, axis, offset):
    size = lax.axis_size(axis)
    return lax.ppermute(value, axis, [(i, i ^ offset) for i in range(size)])


def xor_order(pieces, index):
    bit = 1
    while bit < len(pieces):
        flag = (index & bit) != 0
        pieces = [jnp.where(flag, pieces[p ^ bit], pieces[p]) for p in range(len(pieces))]
        bit *= 2
    return pieces


def total(values):
    acc = values[0].astype(F32)
    for value in values[1:]:
        acc = acc + value.astype(F32)
    return acc


def pad_rows(value, rows):
    return jnp.pad(value, ((0, rows - value.shape[0]), (0, 0)))


def head_lanes(width, head, ones_lane=None):
    lane = lax.broadcasted_iota(jnp.int32, (1, width), 1)
    keep = (lane >= head * HD) & (lane < (head + 1) * HD)
    if ones_lane is not None:
        keep = keep | (lane == ones_lane)
    return keep


def attend_forward_kernel(heads, blocks, q_ref, *refs):
    kv_refs = refs[:blocks]
    o_ref, lse_ref, vt_ref = refs[blocks:]
    group = heads * HD
    wide = q_ref.shape[1]
    rows = kv_refs[0].shape[0]

    @pl.when(pl.program_id(0) == 0)
    def _():
        for i in range(blocks):
            vt_ref[:, i * rows : (i + 1) * rows] = kv_refs[i][:, wide : wide + group].T

    q = q_ref[...]
    outs = []
    stats = []
    for head in range(heads):
        q_head = jnp.where(head_lanes(wide, head, group), q, jnp.zeros_like(q))
        scores = [dot_nt(kv_refs[i][:, :wide], q_head) for i in range(blocks)]
        top = jnp.max(scores[0], axis=0, keepdims=True)
        for i in range(1, blocks):
            top = jnp.maximum(top, jnp.max(scores[i], axis=0, keepdims=True))
        norm = jnp.zeros_like(top)
        acc = None
        for i in range(blocks):
            probs = jnp.exp2(scores[i] - top)
            norm = norm + jnp.sum(probs, axis=0, keepdims=True)
            part = dot_nn(
                vt_ref[head * HD : (head + 1) * HD, i * rows : (i + 1) * rows], probs.astype(BF16)
            )
            acc = part if acc is None else acc + part
        outs.append(acc / norm)
        stats.append(top + jnp.log2(norm))
    o_ref[...] = jnp.concatenate(outs, axis=0).T.astype(BF16)
    for head in range(heads):
        lse_ref[head : head + 1, :] = stats[head]


def attend_forward(q, kvs, heads, tile):
    rows, wide = q.shape
    group = heads * HD
    blocks = len(kvs)
    keys = blocks * rows
    whole = pl.BlockSpec(kvs[0].shape, lambda t: (0, 0))
    return pl.pallas_call(
        functools.partial(attend_forward_kernel, heads, blocks),
        grid=(rows // tile,),
        in_specs=[pl.BlockSpec((tile, wide), lambda t: (t, 0))] + [whole] * blocks,
        out_specs=[
            pl.BlockSpec((tile, group), lambda t: (t, 0)),
            pl.BlockSpec((8, tile), lambda t: (0, t)),
        ],
        out_shape=[
            jax.ShapeDtypeStruct((rows, group), BF16),
            jax.ShapeDtypeStruct((8, rows), F32),
        ],
        scratch_shapes=[pltpu.VMEM((group, keys), BF16)],
        compiler_params=pltpu.CompilerParams(vmem_limit_bytes=56 * 2**20),
        cost_estimate=pl.CostEstimate(
            flops=4 * heads * rows * keys * wide,
            transcendentals=heads * rows * keys,
            bytes_accessed=2 * rows * wide * 3 + 2 * keys * (wide + group),
        ),
        name="attend_forward",
    )(q, *kvs)


def attend_backward_kernel(heads, blocks, q_ref, do_ref, o_ref, lse_ref, *refs):
    kv_refs = refs[:blocks]
    dq_ref = refs[blocks]
    dkv_refs = refs[blocks + 1 : 2 * blocks + 1]
    kt_ref = refs[2 * blocks + 1]
    dk_accs = refs[2 * blocks + 2 : 3 * blocks + 2]
    dv_accs = refs[3 * blocks + 2 :]
    group = heads * HD
    wide = q_ref.shape[1]
    rows = kv_refs[0].shape[0]

    @pl.when(pl.program_id(0) == 0)
    def _():
        for i in range(blocks):
            kt_ref[:, i * rows : (i + 1) * rows] = kv_refs[i][:, :group].T
            dk_accs[i][...] = jnp.zeros_like(dk_accs[i])
            dv_accs[i][...] = jnp.zeros_like(dv_accs[i])

    q = q_ref[...]
    dout = do_ref[...]
    products = (dout.astype(F32) * o_ref[...].astype(F32)).T
    dqs = []
    for head in range(heads):
        q_head = jnp.where(head_lanes(wide, head, group), q, jnp.zeros_like(q))
        do_head = jnp.where(head_lanes(group, head), dout, jnp.zeros_like(dout))
        lse = lse_ref[head : head + 1, :]
        delta = jnp.sum(products[head * HD : (head + 1) * HD], axis=0, keepdims=True)
        acc = None
        for i in range(blocks):
            probs = jnp.exp2(dot_nt(kv_refs[i][:, :wide], q_head) - lse)
            dv_accs[i][...] += dot_nn(probs.astype(BF16), do_head)
            grads = dot_nt(kv_refs[i][:, wide : wide + group], do_head)
            grads = (probs * (grads - delta)).astype(BF16)
            dk_accs[i][...] += dot_nn(grads, q_head)
            part = dot_nn(
                kt_ref[head * HD : (head + 1) * HD, i * rows : (i + 1) * rows], grads
            )
            acc = part if acc is None else acc + part
        dqs.append(acc)
    dq_ref[...] = jnp.concatenate(dqs, axis=0).T.astype(BF16)

    @pl.when(pl.program_id(0) == pl.num_programs(0) - 1)
    def _():
        for i in range(blocks):
            dkv_refs[i][:, :group] = (dk_accs[i][:, :group] * LN2).astype(BF16)
            dkv_refs[i][:, wide : wide + group] = dv_accs[i][...].astype(BF16)


def attend_backward(q, kvs, dout, o, lse, heads, tile):
    rows, wide = q.shape
    group = heads * HD
    blocks = len(kvs)
    keys = blocks * rows
    whole = pl.BlockSpec(kvs[0].shape, lambda t: (0, 0))
    out = pl.pallas_call(
        functools.partial(attend_backward_kernel, heads, blocks),
        grid=(rows // tile,),
        in_specs=[
            pl.BlockSpec((tile, wide), lambda t: (t, 0)),
            pl.BlockSpec((tile, group), lambda t: (t, 0)),
            pl.BlockSpec((tile, group), lambda t: (t, 0)),
            pl.BlockSpec((8, tile), lambda t: (0, t)),
        ]
        + [whole] * blocks,
        out_specs=[pl.BlockSpec((tile, group), lambda t: (t, 0))] + [whole] * blocks,
        out_shape=[jax.ShapeDtypeStruct((rows, group), BF16)]
        + [jax.ShapeDtypeStruct(kvs[0].shape, BF16)] * blocks,
        scratch_shapes=[pltpu.VMEM((group, keys), BF16)]
        + [pltpu.VMEM((rows, wide), F32)] * blocks
        + [pltpu.VMEM((rows, group), F32)] * blocks,
        compiler_params=pltpu.CompilerParams(vmem_limit_bytes=56 * 2**20),
        cost_estimate=pl.CostEstimate(
            flops=10 * heads * rows * keys * wide,
            transcendentals=heads * rows * keys,
            bytes_accessed=2 * rows * wide * 4 + 4 * keys * (wide + group),
        ),
        name="attend_backward",
    )(q, dout, o, lse, *kvs)
    return out[0], out[1:]


def feed_kernel(
    x1_ref,
    x1b_ref,
    expand_ref,
    shrink_ref,
    ebias_ref,
    sbias_ref,
    gain_ref,
    shift_ref,
    cot_ref,
    mixed_ref,
    dx1_ref,
    dexpand_ref,
    dshrink_ref,
    debias_ref,
    vec_ref,
    act_ref,
    slope_ref,
    acc_ref,
    d2b_ref,
    x1t_ref,
):
    phase = pl.program_id(0)
    step = pl.program_id(1)
    last = pl.num_programs(1) - 1
    width = x1_ref.shape[1]

    @pl.when(phase == 0)
    def _():
        pre = dot_nn(x1b_ref[...], expand_ref[0]) + ebias_ref[0]
        cdf = 0.5 * (1.0 + lax.erf(pre * 0.7071067811865476))
        pdf = jnp.exp(-0.5 * pre * pre) * 0.3989422804014327
        act = (pre * cdf).astype(BF16)
        act_ref[step] = act
        slope_ref[step] = (cdf + pre * pdf).astype(BF16)
        part = dot_nn(act, shrink_ref[0])

        @pl.when(step == 0)
        def _():
            acc_ref[...] = part
            x1t_ref[...] = x1b_ref[...].T

        @pl.when(step > 0)
        def _():
            acc_ref[...] += part

        @pl.when(step == last)
        def _():
            hidden = x1_ref[...] + (acc_ref[...] + sbias_ref[...])
            center = hidden - jnp.mean(hidden, -1, keepdims=True)
            inverse = lax.rsqrt(jnp.mean(center * center, -1, keepdims=True) + EPSILON)
            normed = center * inverse
            mixed_ref[...] = (normed * gain_ref[...] + shift_ref[...]).astype(BF16)
            grad = cot_ref[...].astype(F32)
            scaled = grad * gain_ref[...]
            dhidden = inverse * (
                scaled
                - jnp.mean(scaled, -1, keepdims=True)
                - normed * jnp.mean(scaled * normed, -1, keepdims=True)
            )
            acc_ref[...] = dhidden
            d2b_ref[...] = dhidden.astype(BF16)
            vec_ref[...] = jnp.zeros_like(vec_ref)
            vec_ref[0:1, :] = jnp.sum(grad * normed, 0, keepdims=True)
            vec_ref[1:2, :] = jnp.sum(grad, 0, keepdims=True)
            vec_ref[2:3, :] = jnp.sum(dhidden, 0, keepdims=True)

    @pl.when(phase == 1)
    def _():
        d2b = d2b_ref[...]
        dpre = (dot_nt(d2b, shrink_ref[0]) * slope_ref[step].astype(F32)).astype(BF16)
        debias_ref[0] = jnp.sum(dpre.astype(F32), 0, keepdims=True)
        dexpand_ref[0] = dot_nn(x1t_ref[...], dpre).astype(BF16)
        dshrink_ref[0] = dot_tn(act_ref[step], d2b).astype(BF16)
        acc_ref[...] += dot_nt(dpre, expand_ref[0])

        @pl.when(step == last)
        def _():
            dx1_ref[...] = acc_ref[...]


def feed_forward_backward(x1, x1b, expand, shrink, ebias, sbias, gain, shift, cot):
    rows, width = x1.shape
    parts, _, block = expand.shape
    full = pl.BlockSpec((rows, width), lambda p, k: (0, 0))
    line = pl.BlockSpec((1, width), lambda p, k: (0, 0))
    return pl.pallas_call(
        feed_kernel,
        grid=(2, parts),
        in_specs=[
            full,
            full,
            pl.BlockSpec((1, width, block), lambda p, k: (k, 0, 0)),
            pl.BlockSpec((1, block, width), lambda p, k: (k, 0, 0)),
            pl.BlockSpec((1, 1, block), lambda p, k: (k, 0, 0)),
            line,
            line,
            line,
            full,
        ],
        out_specs=[
            full,
            full,
            pl.BlockSpec((1, width, block), lambda p, k: (p * k, 0, 0)),
            pl.BlockSpec((1, block, width), lambda p, k: (p * k, 0, 0)),
            pl.BlockSpec((1, 1, block), lambda p, k: (p * k, 0, 0)),
            pl.BlockSpec((8, width), lambda p, k: (0, 0)),
        ],
        out_shape=[
            jax.ShapeDtypeStruct((rows, width), BF16),
            jax.ShapeDtypeStruct((rows, width), F32),
            jax.ShapeDtypeStruct((parts, width, block), BF16),
            jax.ShapeDtypeStruct((parts, block, width), BF16),
            jax.ShapeDtypeStruct((parts, 1, block), F32),
            jax.ShapeDtypeStruct((8, width), F32),
        ],
        scratch_shapes=[
            pltpu.VMEM((parts, rows, block), BF16),
            pltpu.VMEM((parts, rows, block), BF16),
            pltpu.VMEM((rows, width), F32),
            pltpu.VMEM((rows, width), BF16),
            pltpu.VMEM((width, rows), BF16),
        ],
        compiler_params=pltpu.CompilerParams(vmem_limit_bytes=48 * 2**20),
        cost_estimate=pl.CostEstimate(
            flops=12 * rows * width * parts * block,
            transcendentals=2 * rows * parts * block,
            bytes_accessed=12 * width * parts * block,
        ),
        name="feed_forward_backward",
    )(x1, x1b, expand, shrink, ebias, sbias, gain, shift, cot)


def general_device(
    tokens,
    lengths,
    cotangent,
    attend_weight,
    query_bias,
    value_bias,
    mixer_weight,
    mixer_bias,
    attn_gain,
    attn_shift,
    expand_weight,
    expand_bias,
    shrink_weight,
    shrink_bias,
    final_gain,
    final_shift,
):
    uly = lax.axis_size("uly")
    blk = lax.axis_size("blk")
    dp = lax.axis_size("dp")
    u = lax.axis_index("uly")
    b = lax.axis_index("blk")
    z = lax.axis_index("dp")
    width = tokens.shape[-1]
    rows = tokens.shape[0] * tokens.shape[1]
    block_rows = uly * rows
    heads = HEADS // uly
    group = heads * HD
    wide = -(-(group + 1) // 128) * 128
    shard = attend_weight.shape[0]
    hidden = expand_weight.shape[1]
    parts = blk * uly
    unit = hidden // (parts * dp)
    share = shard // blk

    x = tokens.reshape(rows, width)
    x_rows = jnp.concatenate([x] + [swap_with(x, "uly", j) for j in range(1, uly)], 0)

    small = jnp.concatenate(
        [query_bias, value_bias, mixer_bias, attn_gain, attn_shift, shrink_bias]
        + [final_gain, final_shift, expand_bias]
    )
    small_rows = small.shape[0] // (3 * group)
    own_heads = lax.dynamic_slice_in_dim(attend_weight.reshape(shard, 3, uly, group), u, 1, 2)
    own_heads = own_heads.reshape(shard, 3 * group)
    first_piece = jnp.concatenate(
        [
            lax.dynamic_slice_in_dim(own_heads, b * share, share, 0),
            pad_rows(small.reshape(small_rows, 3 * group), 16),
        ]
    )
    first_all = lax.all_gather(first_piece, "dp", axis=0, tiled=False)
    halves = first_all[:, :share]
    halves = xor_order([halves] + [swap_with(halves, "blk", i) for i in range(1, blk)], b)
    attend_own = jnp.stack(halves, 1).reshape(width, 3, group)
    vectors = first_all[:, share : share + small_rows].reshape(dp, -1, shard).astype(F32)
    names = [vectors[:, k].reshape(width) for k in range(8)]
    bias_query, bias_value, bias_mixer, gain_attn, shift_attn, bias_shrink = names[:6]
    gain_final, shift_final = names[6:]
    bias_expand = vectors[:, 8:].reshape(dp, parts, unit).transpose(1, 0, 2)
    bias_expand = jnp.stack(
        xor_order(list(bias_expand.reshape(parts, dp * unit)), b * uly + u), 0
    ).reshape(parts, 1, dp * unit)

    mixer_own = lax.dynamic_slice_in_dim(mixer_weight, b * share, share, 0)
    mixer_all = jnp.stack(
        xor_order([mixer_own] + [swap_with(mixer_own, "dp", j) for j in range(1, dp)], z), 0
    )
    mixer_all = jnp.stack(
        xor_order([mixer_all] + [swap_with(mixer_all, "blk", i) for i in range(1, blk)], b), 1
    ).reshape(width, width)

    part = b * uly + u
    expand_own = lax.dynamic_slice_in_dim(
        expand_weight.reshape(shard, dp, parts, unit), part, 1, 2
    ).reshape(-1, width)
    shrink_own = lax.dynamic_slice_in_dim(shrink_weight.reshape(parts, unit, width), part, 1, 0)
    expand_rows = expand_own.shape[0]
    feed_own = jnp.concatenate([expand_own, shrink_own.reshape(unit, width)], 0)
    feed_all = lax.all_gather(feed_own, "dp", axis=0, tiled=False)
    expand_part = feed_all[:, :expand_rows].reshape(width, dp * unit)
    shrink_part = feed_all[:, expand_rows:].reshape(dp * unit, width)
    expand_two = jnp.stack([expand_part, swap_with(expand_part, "uly", 1)])
    shrink_two = jnp.stack([shrink_part, swap_with(shrink_part, "uly", 2)])
    expand_far = swap_with(expand_two, "uly", 2)
    shrink_far = swap_with(shrink_two, "uly", 1)
    expand_here = jnp.concatenate([expand_two, expand_far], 0)
    shrink_here = jnp.stack([shrink_two[0], shrink_far[0], shrink_two[1], shrink_far[1]], 0)
    expand_full = jnp.concatenate(
        [expand_here] + [swap_with(expand_here, "blk", i) for i in range(1, blk)], 0
    )
    shrink_full = jnp.concatenate(
        [shrink_here] + [swap_with(shrink_here, "blk", i) for i in range(1, blk)], 0
    )

    lane_pad = ((0, 0), (0, wide - group))
    bias_row = jnp.pad(lax.dynamic_slice_in_dim(bias_query, u * group, group, 0), lane_pad[1:])
    ones_lane = (jnp.arange(wide) == group).astype(F32)
    q = dot_nn(x_rows, jnp.pad(attend_own[:, 0], lane_pad)) + bias_row
    q = (q * (0.125 * LOG2E) + ones_lane).astype(BF16)
    kv_weight = jnp.concatenate([jnp.pad(attend_own[:, 1], lane_pad), attend_own[:, 2]], 1)
    kv_bias = jnp.concatenate(
        [jnp.zeros((wide,), F32), lax.dynamic_slice_in_dim(bias_value, u * group, group, 0)]
    )
    kv_ones = jnp.pad(ones_lane, (0, group))
    row_index = jnp.arange(block_rows, dtype=jnp.int32)
    positions = b * block_rows + ((row_index // rows) ^ u) * rows + row_index % rows
    key_mask = jnp.where(positions < lengths[0], 0.0, MASKED)
    kv = (dot_nn(x_rows, kv_weight) + kv_bias + key_mask[:, None] * kv_ones).astype(BF16)
    kvs = [kv] + [swap_with(kv, "blk", i) for i in range(1, blk)]

    o_rows, lse = attend_forward(q, kvs, heads, min(256, block_rows))
    pieces = [o_rows[j * rows : (j + 1) * rows] for j in range(uly)]
    pieces = [pieces[0]] + [swap_with(pieces[j], "uly", j) for j in range(1, uly)]
    mixer_in = jnp.concatenate(xor_order(pieces, u), 1)

    first_sum = x.astype(F32) + (dot_nn(mixer_in, mixer_all) + bias_mixer)
    center = first_sum - jnp.mean(first_sum, -1, keepdims=True)
    first_inv = lax.rsqrt(jnp.mean(center * center, -1, keepdims=True) + EPSILON)
    first_normed = center * first_inv
    first_out = first_normed * gain_attn + shift_attn
    first_low = first_out.astype(BF16)

    mixed, first_grad, expand_grad, shrink_grad, expand_bias_grad, vec_grads = (
        feed_forward_backward(
            first_out,
            first_low,
            expand_full,
            shrink_full,
            bias_expand,
            bias_shrink[None],
            gain_final[None],
            shift_final[None],
            cotangent.reshape(rows, width),
        )
    )

    scaled = first_grad * gain_attn
    attn_grad = first_inv * (
        scaled
        - jnp.mean(scaled, -1, keepdims=True)
        - first_normed * jnp.mean(scaled * first_normed, -1, keepdims=True)
    )
    attn_low = attn_grad.astype(BF16)
    out_grad = dot_nt(attn_low, mixer_all).astype(BF16)
    sends = xor_order([out_grad[:, j * group : (j + 1) * group] for j in range(uly)], u)
    dout_rows = jnp.concatenate(
        [sends[0]] + [swap_with(sends[j], "uly", j) for j in range(1, uly)], 0
    )
    dq, dkvs = attend_backward(q, kvs, dout_rows, o_rows, lse, heads, min(256, block_rows))

    mixer_grad = dot_tn(mixer_in, attn_low).astype(BF16)
    attn_gain_grad = jnp.sum(first_grad * first_normed, 0)
    attn_shift_grad = jnp.sum(first_grad, 0)
    mixer_bias_grad = jnp.sum(attn_grad, 0)
    ebg = jnp.stack(xor_order(list(expand_bias_grad.reshape(parts, dp * unit)), part), 0)
    ebg = ebg.reshape(parts, dp, unit).transpose(1, 0, 2).reshape(dp, parts * unit)
    vec_all = jnp.concatenate(
        [
            v.reshape(dp, shard)
            for v in (
                mixer_bias_grad,
                attn_gain_grad,
                attn_shift_grad,
                vec_grads[2],
                vec_grads[0],
                vec_grads[1],
            )
        ]
        + [ebg],
        1,
    ).astype(BF16)

    mixer_cols = width // blk
    mixer_part_rows = shard // uly
    vec_len = vec_all.shape[1]
    vec_rows = -(-vec_len // mixer_cols)
    vec_rows = -(-vec_rows // 16) * 16
    vec_block = jnp.pad(vec_all, ((0, 0), (0, vec_rows * mixer_cols - vec_len))).reshape(
        dp, vec_rows, mixer_cols
    )
    mixer_view = mixer_grad.reshape(dp, uly, mixer_part_rows, blk, mixer_cols)
    by_blk = xor_order([mixer_view[:, :, :, i] for i in range(blk)], b)
    mixer_parts = []
    for i in range(blk):
        by_uly = xor_order([by_blk[i][:, j] for j in range(uly)], u)
        mixer_parts.append(
            jnp.stack([jnp.concatenate([piece, vec_block], 1) for piece in by_uly], 0)
        )
    mixer_sum = total(
        [mixer_parts[0]] + [swap_with(mixer_parts[i], "blk", i) for i in range(1, blk)]
    ).astype(BF16)
    mixer_sum = total(
        [mixer_sum[0]] + [swap_with(mixer_sum[j], "uly", j) for j in range(1, uly)]
    ).astype(BF16)

    def over_blk(grad):
        return total(
            [grad[:uly]]
            + [swap_with(grad[i * uly : (i + 1) * uly], "blk", i) for i in range(1, blk)]
        ).astype(BF16)

    shrink_sum = over_blk(shrink_grad)
    expand_sum = over_blk(expand_grad)
    shrink_sum = shrink_sum.reshape(2, 2, dp * unit, width)
    expand_sum = expand_sum.reshape(2, 2, width, dp * unit)
    shrink_sum = total([shrink_sum[0], swap_with(shrink_sum[1], "uly", 2)]).astype(BF16)
    expand_sum = total([expand_sum[:, 0], swap_with(expand_sum[:, 1], "uly", 1)]).astype(BF16)
    shrink_sum = total([shrink_sum[0], swap_with(shrink_sum[1], "uly", 1)]).astype(BF16)
    expand_sum = total([expand_sum[0], swap_with(expand_sum[1], "uly", 2)]).astype(BF16)

    mixer_rows = mixer_sum.shape[1] * mixer_cols // width
    packed = jnp.concatenate(
        [
            expand_sum.reshape(dp, expand_rows, width),
            shrink_sum.reshape(dp, unit, width),
            mixer_sum.reshape(dp, mixer_rows, width),
        ],
        1,
    )

    def over_dp(value):
        sends = [lax.dynamic_slice_in_dim(value, z ^ j, 1, 0)[0] for j in range(dp)]
        return total([sends[0]] + [swap_with(sends[j], "dp", j) for j in range(1, dp)])

    owned = over_dp(packed)
    vec_owned = owned[expand_rows + unit :].reshape(-1, mixer_cols)[mixer_part_rows:]
    vec_owned = vec_owned.reshape(-1)[:vec_len]

    def in_plane(value):
        value = value.astype(BF16)
        value = jnp.stack(
            xor_order([value] + [swap_with(value, "uly", j) for j in range(1, uly)], u), 0
        )
        return jnp.stack(
            xor_order([value] + [swap_with(value, "blk", i) for i in range(1, blk)], b), 0
        )

    gathered = in_plane(owned).reshape(parts, -1, width)
    expand_out = gathered[:, :expand_rows].reshape(parts, shard, dp, unit)
    expand_out = expand_out.transpose(1, 2, 0, 3).reshape(shard, hidden).astype(F32)
    shrink_out = gathered[:, expand_rows : expand_rows + unit]
    shrink_out = shrink_out.reshape(parts * unit, width).astype(F32)
    mixer_out = gathered[:, expand_rows + unit :].reshape(blk, uly, -1, mixer_cols)
    mixer_out = mixer_out[:, :, :mixer_part_rows].transpose(1, 2, 0, 3)
    mixer_out = mixer_out.reshape(shard, width).astype(F32)

    own_dkv = total([dkvs[0]] + [swap_with(dkvs[i], "blk", i) for i in range(1, blk)])
    own_dkv = own_dkv.astype(BF16)
    proj_grad = jnp.concatenate(
        [dq * jnp.asarray(0.125, BF16), own_dkv[:, :group], own_dkv[:, wide : wide + group]], 1
    )
    token_parts = dot_nt(proj_grad, attend_own.reshape(width, 3 * group))
    token_low = token_parts.astype(BF16)
    tokens_grad = attn_grad + total(
        [token_parts[:rows]]
        + [swap_with(token_low[j * rows : (j + 1) * rows], "uly", j) for j in range(1, uly)]
    )
    attend_grad = dot_tn(x_rows, proj_grad).astype(BF16)
    attend_grad = attend_grad.reshape(dp, blk, share, 3 * group)
    bias_sum = jnp.sum(proj_grad.astype(F32), 0)[None]
    bias_rows = pad_rows(bias_sum.astype(BF16), 16)
    attend_parts = [
        jnp.concatenate(
            [
                lax.dynamic_slice_in_dim(attend_grad, b ^ i, 1, 1).reshape(-1, 3 * group),
                bias_rows,
            ],
            0,
        )
        for i in range(blk)
    ]
    attend_sum = total(
        [attend_parts[0]] + [swap_with(attend_parts[i], "blk", i) for i in range(1, blk)]
    ).astype(BF16)
    bias_half = jnp.broadcast_to(attend_sum[dp * share :], (dp, 16, 3 * group))
    attend_sum = attend_sum[: dp * share].reshape(dp, share, 3 * group)
    attend_owned = over_dp(jnp.concatenate([attend_sum, bias_half], 1))
    attend_all = in_plane(attend_owned)
    attend_out = attend_all[:, :, :share].reshape(blk, uly, share, 3, group)
    attend_out = attend_out.transpose(0, 2, 3, 1, 4).reshape(shard, 3 * width).astype(F32)
    bias_out = attend_all[0, :, share].astype(F32).reshape(uly, 3, group)
    query_bias_grad = lax.dynamic_slice_in_dim(bias_out[:, 0].reshape(width), z * shard, shard, 0)
    value_bias_grad = lax.dynamic_slice_in_dim(bias_out[:, 2].reshape(width), z * shard, shard, 0)

    vecs = [vec_owned[k * shard : (k + 1) * shard] for k in range(6)]
    return (
        mixed.reshape(tokens.shape),
        tokens_grad.reshape(tokens.shape),
        attend_out,
        query_bias_grad,
        value_bias_grad,
        mixer_out,
        vecs[0],
        vecs[1],
        vecs[2],
        expand_out,
        vec_owned[6 * shard :],
        shrink_out,
        vecs[3],
        vecs[4],
        vecs[5],
    )


def call(kernel, name, scalars, args, in_specs, out_shape, out_specs, scratch, grid, flops, vmem):
    size = sum(a.size * a.dtype.itemsize for a in args)
    return pl.pallas_call(
        kernel,
        grid_spec=pltpu.PrefetchScalarGridSpec(
            num_scalar_prefetch=1,
            grid=grid,
            in_specs=in_specs,
            out_specs=out_specs,
            scratch_shapes=scratch,
        ),
        out_shape=out_shape,
        compiler_params=pltpu.CompilerParams(vmem_limit_bytes=vmem * 2**20),
        cost_estimate=pl.CostEstimate(flops=flops, bytes_accessed=size, transcendentals=0),
        name=name,
    )(scalars, *args)


def whole(shape):
    return pl.BlockSpec(shape, lambda *_: (0,) * len(shape))


def one_hot(rows, cols, row_offset=0, col_offset=0):
    row = lax.broadcasted_iota(jnp.int32, (rows, cols), 0) + row_offset
    col = lax.broadcasted_iota(jnp.int32, (rows, cols), 1) + col_offset
    return jnp.where(row == col, 1.0, 0.0).astype(BF16)


def fetch_kernel(
    sizes, idx, attend_ref, small_ref, expand_ref, shrink_ref, mixer_ref, first_ref, feed_ref
):
    uly, dp, group, unit = sizes
    share = attend_ref.shape[1]
    shard, width = mixer_ref.shape
    u = idx[1]
    part = idx[0] * uly + u
    take = one_hot(width, group, 0, u * group)
    for c in range(3):
        cols = dot_nn(attend_ref[0, :, c * width : (c + 1) * width], take)
        first_ref[:share, c * group : (c + 1) * group] = cols.astype(BF16)
    first_ref[share:, :] = jnp.zeros_like(first_ref[share:, :])
    first_ref[share:, :shard] = small_ref[...]
    take = one_hot(width, unit, 0, part * unit)
    half = shard // 2
    for k in range(dp):
        cols = dot_nn(expand_ref[:, k * width : (k + 1) * width], take).astype(BF16)
        feed_ref[:half, k * unit : (k + 1) * unit] = cols[:half]
        feed_ref[:half, (dp + k) * unit : (dp + k + 1) * unit] = cols[half:]
    feed_ref[half : half + unit, :] = shrink_ref[0]
    rows = feed_ref.shape[0] - half - unit
    feed_ref[half + unit :, :] = dot_nn(
        one_hot(rows, shard, part * rows, 0), mixer_ref[...]
    ).astype(BF16)


def project_kernel(sizes, idx, *refs):
    uly, blk, dp, group, unit = sizes
    x_refs, refs = refs[:uly], refs[uly:]
    mine_refs, refs = refs[:dp], refs[dp:]
    other_refs, refs = refs[:dp], refs[dp:]
    w_ref, q_ref, kv_ref, vec_ref, eb_ref = refs
    b, u, z, length = idx[0], idx[1], idx[2], idx[3]
    rows, width = x_refs[0].shape
    wide = q_ref.shape[1]
    pad = wide - group
    share = mine_refs[0].shape[0] - 16
    shard = 2 * share
    parts = uly * blk
    w_ref[:, group:wide] = jnp.zeros((width, pad), BF16)
    w_ref[:, wide + group : 2 * wide] = jnp.zeros((width, pad), BF16)
    own_vec = jnp.zeros((16, shard), F32)
    all_vec = jnp.zeros((16, width), F32)
    for j in range(dp):
        for ref, core in ((mine_refs[j], b), (other_refs[j], 1 - b)):
            start = pl.multiple_of((z ^ j) * shard + core * share, share)
            for c in range(3):
                w_ref[pl.ds(start, share), c * wide : c * wide + group] = ref[
                    :share, c * group : (c + 1) * group
                ]
        vec = mine_refs[j][share:, :shard]
        own_vec += jnp.where((z ^ j) == u, 1.0, 0.0) * vec.astype(F32)
        all_vec += dot_nn(vec, one_hot(shard, width, (z ^ j) * shard, 0))
    vec_ref[...] = all_vec

    low = all_vec.astype(BF16)
    part = b * uly + u
    eb = jnp.zeros((parts, dp * unit), F32)
    for parity in range(2):
        col = lax.broadcasted_iota(jnp.int32, (width, dp * unit), 1)
        row = lax.broadcasted_iota(jnp.int32, (width, dp * unit), 0)
        source = col + (col // unit) * (shard - unit) + parity * unit
        lanes = dot_nn(low, jnp.where(row == source, 1.0, 0.0).astype(BF16)).astype(BF16)
        owner = lax.broadcasted_iota(jnp.int32, (parts, 16), 0) ^ part
        line = lax.broadcasted_iota(jnp.int32, (parts, 16), 1)
        wanted = ((owner & 1) == parity) & (line == 8 + (owner >> 1))
        eb += dot_nn(jnp.where(wanted, 1.0, 0.0).astype(BF16), lanes)
    eb_ref[...] = eb

    lane = lax.broadcasted_iota(jnp.int32, (1, wide), 1)
    mark = jnp.where(lane == group, 1.0, 0.0)
    zeros = jnp.zeros((1, pad), F32)
    q_bias = jnp.concatenate([own_vec[0:1], zeros], 1)
    v_bias = own_vec[1:2]
    for j in range(uly):
        x = x_refs[j][...]
        here = slice(j * rows, (j + 1) * rows)
        q = dot_nn(x, w_ref[:, :wide]) + q_bias
        q_ref[here, :] = (q * (0.125 * LOG2E) + mark).astype(BF16)
        first = (b * uly + (u ^ j)) * rows
        position = lax.broadcasted_iota(jnp.int32, (rows, 1), 0) + first
        masked = jnp.where(position < length, 0.0, MASKED)
        k = dot_nn(x, w_ref[:, wide : 2 * wide]) + masked * mark
        kv_ref[here, :wide] = k.astype(BF16)
        kv_ref[here, wide:] = (dot_nn(x, w_ref[:, 2 * wide :]) + v_bias).astype(BF16)


def attend_kernel(heads, blocks, q_ref, *refs):
    kv_refs = refs[:blocks]
    o_refs = refs[blocks:-2]
    lse_ref, vt_ref = refs[-2:]
    group = heads * HD
    wide = q_ref.shape[1]
    rows = kv_refs[0].shape[0]

    @pl.when(pl.program_id(0) == 0)
    def _():
        for i in range(blocks):
            vt_ref[:, i * rows : (i + 1) * rows] = kv_refs[i][:, wide : wide + group].T

    q = q_ref[...]
    outs = []
    for head in range(heads):
        q_head = jnp.where(head_lanes(wide, head, group), q, jnp.zeros_like(q))
        scores = [dot_nt(kv_refs[i][:, :wide], q_head) for i in range(blocks)]
        top = jnp.max(scores[0], axis=0, keepdims=True)
        for i in range(1, blocks):
            top = jnp.maximum(top, jnp.max(scores[i], axis=0, keepdims=True))
        norm = jnp.zeros_like(top)
        acc = None
        for i in range(blocks):
            probs = jnp.exp2(scores[i] - top)
            norm = norm + jnp.sum(probs, axis=0, keepdims=True)
            part = dot_nn(
                vt_ref[head * HD : (head + 1) * HD, i * rows : (i + 1) * rows], probs.astype(BF16)
            )
            acc = part if acc is None else acc + part
        outs.append(acc / norm)
        lse_ref[head : head + 1, :] = top + jnp.log2(norm)
    out = jnp.concatenate(outs, axis=0).T.astype(BF16)
    for j, o_ref in enumerate(o_refs):

        @pl.when(pl.program_id(0) == j)
        def _(o_ref=o_ref):
            o_ref[...] = out


def attend(q, kvs, heads, pieces):
    rows, wide = q.shape
    tile = rows // pieces
    group = heads * HD
    blocks = len(kvs)
    keys = blocks * rows
    out = pl.pallas_call(
        functools.partial(attend_kernel, heads, blocks),
        grid=(pieces,),
        in_specs=[pl.BlockSpec((tile, wide), lambda t: (t, 0))] + [whole(kvs[0].shape)] * blocks,
        out_specs=[whole((tile, group))] * pieces + [pl.BlockSpec((8, tile), lambda t: (0, t))],
        out_shape=[jax.ShapeDtypeStruct((tile, group), BF16)] * pieces
        + [jax.ShapeDtypeStruct((8, rows), F32)],
        scratch_shapes=[pltpu.VMEM((group, keys), BF16)],
        compiler_params=pltpu.CompilerParams(vmem_limit_bytes=48 * 2**20),
        cost_estimate=pl.CostEstimate(
            flops=4 * heads * rows * keys * wide,
            transcendentals=heads * rows * keys,
            bytes_accessed=2 * rows * wide * 3 + 2 * keys * (wide + group),
        ),
        name="attend",
    )(q, *kvs)
    return out[:-1], out[-1]


def first_norm_kernel(uly, idx, x_ref, *refs):
    o_refs = refs[:uly]
    m_ref, vec_ref, x1_ref, x1b_ref, normed_ref, inverse_ref = refs[uly:]
    group = o_refs[0].shape[1]
    acc = vec_ref[2:3, :]
    for j in range(uly):
        start = pl.multiple_of((idx[1] ^ j) * group, group)
        acc = acc + dot_nn(o_refs[j][...], m_ref[pl.ds(start, group), :])
    hidden = x_ref[...].astype(F32) + acc
    center = hidden - jnp.mean(hidden, -1, keepdims=True)
    inverse = lax.rsqrt(jnp.mean(center * center, -1, keepdims=True) + EPSILON)
    normed = center * inverse
    out = normed * vec_ref[3:4, :] + vec_ref[4:5, :]
    x1_ref[...] = out
    x1b_ref[...] = out.astype(BF16)
    normed_ref[...] = normed
    inverse_ref[...] = inverse


def load_parts(expand_refs, shrink_refs, e_ref, s_ref, e_sem, s_sem, act):
    unit = s_ref.shape[2]
    for p in range(len(expand_refs)):
        act(pltpu.make_async_copy(expand_refs[p], e_ref.at[p], e_sem.at[p]), p)
        act(
            pltpu.make_async_copy(shrink_refs[p].at[:, pl.ds(0, unit), :], s_ref.at[p], s_sem.at[p]),
            p,
        )


def feed_forward_kernel(parts, idx, x1_ref, x1b_ref, eb_ref, vec_ref, cot_ref, *refs):
    expand_refs, refs = refs[:parts], refs[parts:]
    shrink_refs, refs = refs[:parts], refs[parts:]
    mixed_ref, dh_ref, dhb_ref, slope_ref, keep_ref, send_ref, grads_ref, *refs = refs
    act_ref, acc_ref, low_ref, e_ref, s_ref, e_sem, s_sem = refs
    phase = pl.program_id(0)
    step = pl.program_id(1)
    dp, unit, width = s_ref.shape[1:]
    z = idx[2]

    @pl.when((phase == 0) & (step == 0))
    def _():
        load_parts(
            expand_refs, shrink_refs, e_ref, s_ref, e_sem, s_sem, lambda copy, p: copy.start()
        )

    @pl.when(phase == 0)
    def _():
        def wait(copy, p):
            @pl.when(step == p)
            def _():
                copy.wait()

        load_parts(expand_refs, shrink_refs, e_ref, s_ref, e_sem, s_sem, wait)
        pre = dot_nn(x1b_ref[...], e_ref[step]) + eb_ref[pl.ds(step, 1), :]
        cdf = 0.5 * (1.0 + lax.erf(pre * 0.7071067811865476))
        pdf = jnp.exp(-0.5 * pre * pre) * 0.3989422804014327
        act = (pre * cdf).astype(BF16)
        act_ref[step] = act
        slope_ref[0] = (cdf + pre * pdf).astype(BF16)
        part = dot_nn(act, s_ref[step].reshape(dp * unit, width))

        @pl.when(step == 0)
        def _():
            acc_ref[...] = part

        @pl.when(step > 0)
        def _():
            acc_ref[...] += part

        @pl.when(step == parts - 1)
        def _():
            hidden = x1_ref[...] + (acc_ref[...] + vec_ref[5:6, :])
            gain = vec_ref[6:7, :]
            center = hidden - jnp.mean(hidden, -1, keepdims=True)
            inverse = lax.rsqrt(jnp.mean(center * center, -1, keepdims=True) + EPSILON)
            normed = center * inverse
            mixed_ref[...] = (normed * gain + vec_ref[7:8, :]).astype(BF16)
            grad = cot_ref[...].astype(F32)
            scaled = grad * gain
            dhidden = inverse * (
                scaled
                - jnp.mean(scaled, -1, keepdims=True)
                - normed * jnp.mean(scaled * normed, -1, keepdims=True)
            )
            dh_ref[...] = dhidden
            low_ref[...] = dhidden.astype(BF16)
            dhb_ref[...] = dhidden.astype(BF16)
            grads_ref[...] = jnp.zeros_like(grads_ref)
            grads_ref[0:1, :] = jnp.sum(dhidden, 0, keepdims=True)
            grads_ref[1:2, :] = jnp.sum(grad * normed, 0, keepdims=True)
            grads_ref[2:3, :] = jnp.sum(grad, 0, keepdims=True)

    @pl.when(phase == 1)
    def _():
        dshrink = dot_tn(act_ref[step], low_ref[...]).astype(BF16)

        def store(ref):
            for k in range(dp):
                start = pl.multiple_of((z ^ k) * unit, unit)
                ref[0, pl.ds(start, unit), :] = dshrink[k * unit : (k + 1) * unit]

        @pl.when(step < parts // 2)
        def _():
            store(keep_ref)

        @pl.when(step >= parts // 2)
        def _():
            store(send_ref)


def feed_forward(scalars, x1, x1b, eb, vec, cot, expand, shrink):
    rows, width = x1.shape
    parts = len(expand)
    block = expand[0].shape[1]
    dp = shrink[0].shape[0]
    unit = block // dp
    half = parts // 2
    hbm = pl.BlockSpec(memory_space=pl.ANY)
    grad = (1, block, width)
    return call(
        functools.partial(feed_forward_kernel, parts),
        "feed_forward",
        scalars,
        [x1, x1b, eb, vec, cot, *expand, *shrink],
        [whole(x1.shape), whole(x1.shape), whole(eb.shape), whole(vec.shape), whole(cot.shape)]
        + [hbm] * (2 * parts),
        [
            jax.ShapeDtypeStruct((rows, width), BF16),
            jax.ShapeDtypeStruct((rows, width), F32),
            jax.ShapeDtypeStruct((rows, width), BF16),
            jax.ShapeDtypeStruct((parts, rows, block), BF16),
            jax.ShapeDtypeStruct((half, block, width), BF16),
            jax.ShapeDtypeStruct((half, block, width), BF16),
            jax.ShapeDtypeStruct((8, width), F32),
        ],
        [
            whole((rows, width)),
            whole((rows, width)),
            whole((rows, width)),
            pl.BlockSpec((1, rows, block), lambda p, k, _: (k * (1 - p) + (parts - 1) * p, 0, 0)),
            pl.BlockSpec(grad, lambda p, k, _: (jnp.minimum(k, half - 1) * p, 0, 0)),
            pl.BlockSpec(grad, lambda p, k, _: (jnp.maximum(k - half, 0) * p, 0, 0)),
            whole((8, width)),
        ],
        [
            pltpu.VMEM((parts, rows, block), BF16),
            pltpu.VMEM((rows, width), F32),
            pltpu.VMEM((rows, width), BF16),
            pltpu.VMEM((parts, width, block), BF16),
            pltpu.VMEM((parts, dp, unit, width), BF16),
            pltpu.SemaphoreType.DMA((parts,)),
            pltpu.SemaphoreType.DMA((parts,)),
        ],
        (2, parts),
        6 * rows * width * parts * block,
        48,
    )


def feed_backward_kernel(parts, idx, x1b_ref, dh_ref, dhb_ref, slope_ref, *refs):
    expand_refs, refs = refs[:parts], refs[parts:]
    shrink_refs, refs = refs[:parts], refs[parts:]
    dx_ref, keep_ref, send_ref, deb_ref, *refs = refs
    x1t_ref, acc_ref, e_ref, s_ref, e_sem, s_sem = refs
    step = pl.program_id(0)
    dp, unit, width = s_ref.shape[1:]
    shard = width // dp
    z = idx[2]

    @pl.when(step == 0)
    def _():
        load_parts(
            expand_refs, shrink_refs, e_ref, s_ref, e_sem, s_sem, lambda copy, p: copy.start()
        )
        for k in range(dp):
            start = pl.multiple_of((z ^ k) * shard, shard)
            x1t_ref[pl.ds(start, shard), :] = x1b_ref[...].T[k * shard : (k + 1) * shard]

    def wait(copy, p):
        @pl.when(step == p)
        def _():
            copy.wait()

    load_parts(expand_refs, shrink_refs, e_ref, s_ref, e_sem, s_sem, wait)
    dpre = dot_nt(dhb_ref[...], s_ref[step].reshape(dp * unit, width))
    dpre = (dpre * slope_ref[0].astype(F32)).astype(BF16)
    deb_ref[0] = jnp.sum(dpre.astype(F32), 0, keepdims=True)
    dexpand = dot_nn(x1t_ref[...], dpre).astype(BF16)

    @pl.when(step < parts // 2)
    def _():
        keep_ref[0] = dexpand

    @pl.when(step >= parts // 2)
    def _():
        send_ref[0] = dexpand

    part = dot_nt(dpre, e_ref[step])

    @pl.when(step == 0)
    def _():
        acc_ref[...] = dh_ref[...] + part

    @pl.when(step > 0)
    def _():
        acc_ref[...] += part

    @pl.when(step == parts - 1)
    def _():
        dx_ref[...] = acc_ref[...]


def feed_backward(scalars, x1b, dh, dhb, slope, expand, shrink):
    rows, width = dh.shape
    parts = len(expand)
    block = expand[0].shape[1]
    dp = shrink[0].shape[0]
    unit = block // dp
    half = parts // 2
    hbm = pl.BlockSpec(memory_space=pl.ANY)
    grad = (1, width, block)
    return call(
        functools.partial(feed_backward_kernel, parts),
        "feed_backward",
        scalars,
        [x1b, dh, dhb, slope, *expand, *shrink],
        [whole(x1b.shape), whole(dh.shape), whole(dhb.shape)]
        + [pl.BlockSpec((1, rows, block), lambda k, _: (k, 0, 0))]
        + [hbm] * (2 * parts),
        [
            jax.ShapeDtypeStruct((rows, width), F32),
            jax.ShapeDtypeStruct((half, width, block), BF16),
            jax.ShapeDtypeStruct((half, width, block), BF16),
            jax.ShapeDtypeStruct((parts, 1, block), F32),
        ],
        [
            whole((rows, width)),
            pl.BlockSpec(grad, lambda k, _: (jnp.minimum(k, half - 1), 0, 0)),
            pl.BlockSpec(grad, lambda k, _: (jnp.maximum(k - half, 0), 0, 0)),
            pl.BlockSpec((1, 1, block), lambda k, _: (k, 0, 0)),
        ],
        [
            pltpu.VMEM((width, rows), BF16),
            pltpu.VMEM((rows, width), F32),
            pltpu.VMEM((parts, width, block), BF16),
            pltpu.VMEM((parts, dp, unit, width), BF16),
            pltpu.SemaphoreType.DMA((parts,)),
            pltpu.SemaphoreType.DMA((parts,)),
        ],
        (parts,),
        6 * rows * width * parts * block,
        48,
    )


def norm_backward_kernel(sizes, idx, dx_ref, normed_ref, inverse_ref, m_ref, vec_ref, *refs):
    uly, dp, unit = sizes
    grads_ref, deb_ref, *refs = refs
    o_refs, refs = refs[:uly], refs[uly:]
    dh_ref, *refs = refs
    do_refs, refs = refs[:uly], refs[uly:]
    keep_ref, send_ref, turn_ref = refs
    b, u, z = idx[0], idx[1], idx[2]
    group = o_refs[0].shape[1]
    share = group // 2
    width = dx_ref.shape[1]
    parts = deb_ref.shape[0]
    grad = dx_ref[...]
    normed = normed_ref[...]
    scaled = grad * vec_ref[3:4, :]
    dhidden = inverse_ref[...] * (
        scaled
        - jnp.mean(scaled, -1, keepdims=True)
        - normed * jnp.mean(scaled * normed, -1, keepdims=True)
    )
    dh_ref[...] = dhidden
    low = dhidden.astype(BF16)
    for j in range(uly):
        start = pl.multiple_of((u ^ j) * group, group)
        do_refs[j][...] = dot_nt(low, m_ref[pl.ds(start, group), :]).astype(BF16)
    line = lax.broadcasted_iota(jnp.int32, (8, width), 0)
    lines = jnp.zeros((8, width), F32)
    values = [
        jnp.sum(dhidden, 0, keepdims=True),
        jnp.sum(grad * normed, 0, keepdims=True),
        jnp.sum(grad, 0, keepdims=True),
        grads_ref[0:1, :],
        grads_ref[1:2, :],
        grads_ref[2:3, :],
    ]
    for k, value in enumerate(values):
        lines = jnp.where(line == k, value, lines)
    lines = lines.astype(BF16)
    part = b * uly + u
    owner = lax.broadcasted_iota(jnp.int32, (parts, parts), 1) ^ part
    order = lax.broadcasted_iota(jnp.int32, (parts, parts), 0)
    order = jnp.where(order == owner, 1.0, 0.0).astype(BF16)
    ebs = dot_nn(order, deb_ref[...].astype(BF16)).astype(BF16)
    for j in range(uly):
        turn_ref[...] = dot_tn(o_refs[j][...], low).astype(BF16)
        place = u ^ j ^ z
        keep_ref[place, :share] = turn_ref[pl.ds(pl.multiple_of(b * share, share), share), :]
        send_ref[place, :share] = turn_ref[pl.ds(pl.multiple_of((1 - b) * share, share), share), :]
    for k in range(dp):
        shard = (z ^ k) * group
        own = dot_nn(lines, one_hot(width, group, 0, shard)).astype(BF16)
        ebk = dot_nn(ebs, one_hot(dp * unit, unit, 0, (z ^ k) * unit)).astype(BF16)
        for ref in (keep_ref, send_ref):
            ref[k, share:, :] = jnp.zeros_like(ref[k, share:, :])
            ref[k, share : share + 8, :group] = own
            ref[k, share + 8 : share + 16, :unit] = ebk


def attend_grad_kernel(heads, blocks, pieces, q_ref, lse_ref, *refs):
    do_refs, refs = refs[:pieces], refs[pieces:]
    o_refs, refs = refs[:pieces], refs[pieces:]
    kv_refs, refs = refs[:blocks], refs[blocks:]
    dq_ref, *refs = refs
    dkv_refs, refs = refs[:blocks], refs[blocks:]
    kt_ref, dout_ref, prod_ref, *refs = refs
    dk_accs, dv_accs = refs[:blocks], refs[blocks:]
    group = heads * HD
    wide = q_ref.shape[1]
    rows = kv_refs[0].shape[0]

    @pl.when(pl.program_id(0) == 0)
    def _():
        for i in range(blocks):
            kt_ref[:, i * rows : (i + 1) * rows] = kv_refs[i][:, :group].T
            dk_accs[i][...] = jnp.zeros_like(dk_accs[i])
            dv_accs[i][...] = jnp.zeros_like(dv_accs[i])

    for j in range(pieces):

        @pl.when(pl.program_id(0) == j)
        def _(j=j):
            dout_ref[...] = do_refs[j][...]
            prod_ref[...] = (do_refs[j][...].astype(F32) * o_refs[j][...].astype(F32)).T

    q = q_ref[...]
    dout = dout_ref[...]
    dqs = []
    for head in range(heads):
        q_head = jnp.where(head_lanes(wide, head, group), q, jnp.zeros_like(q))
        do_head = jnp.where(head_lanes(group, head), dout, jnp.zeros_like(dout))
        lse = lse_ref[head : head + 1, :]
        delta = jnp.sum(prod_ref[head * HD : (head + 1) * HD, :], axis=0, keepdims=True)
        acc = None
        for i in range(blocks):
            probs = jnp.exp2(dot_nt(kv_refs[i][:, :wide], q_head) - lse)
            dv_accs[i][...] += dot_nn(probs.astype(BF16), do_head)
            grads = dot_nt(kv_refs[i][:, wide : wide + group], do_head)
            grads = (probs * (grads - delta)).astype(BF16)
            dk_accs[i][...] += dot_nn(grads, q_head)
            part = dot_nn(
                kt_ref[head * HD : (head + 1) * HD, i * rows : (i + 1) * rows], grads
            )
            acc = part if acc is None else acc + part
        dqs.append(acc)
    dq_ref[...] = jnp.concatenate(dqs, axis=0).T.astype(BF16)

    @pl.when(pl.program_id(0) == pl.num_programs(0) - 1)
    def _():
        for i in range(blocks):
            dkv_refs[i][:, :group] = (dk_accs[i][:, :group] * LN2).astype(BF16)
            dkv_refs[i][:, group:wide] = jnp.zeros((rows, wide - group), BF16)
            dkv_refs[i][:, wide : wide + group] = dv_accs[i][...].astype(BF16)


def attend_grad(q, kvs, douts, outs, lse, heads):
    rows, wide = q.shape
    group = heads * HD
    blocks = len(kvs)
    pieces = len(douts)
    tile = rows // pieces
    keys = blocks * rows
    out = pl.pallas_call(
        functools.partial(attend_grad_kernel, heads, blocks, pieces),
        grid=(pieces,),
        in_specs=[
            pl.BlockSpec((tile, wide), lambda t: (t, 0)),
            pl.BlockSpec((8, tile), lambda t: (0, t)),
        ]
        + [whole((tile, group))] * (2 * pieces)
        + [whole(kvs[0].shape)] * blocks,
        out_specs=[pl.BlockSpec((tile, group), lambda t: (t, 0))]
        + [whole(kvs[0].shape)] * blocks,
        out_shape=[jax.ShapeDtypeStruct((rows, group), BF16)]
        + [jax.ShapeDtypeStruct(kvs[0].shape, BF16)] * blocks,
        scratch_shapes=[
            pltpu.VMEM((group, keys), BF16),
            pltpu.VMEM((tile, group), BF16),
            pltpu.VMEM((group, tile), F32),
        ]
        + [pltpu.VMEM((rows, wide), F32)] * blocks
        + [pltpu.VMEM((rows, group), F32)] * blocks,
        compiler_params=pltpu.CompilerParams(vmem_limit_bytes=48 * 2**20),
        cost_estimate=pl.CostEstimate(
            flops=10 * heads * rows * keys * wide,
            transcendentals=heads * rows * keys,
            bytes_accessed=2 * rows * wide * 4 + 4 * keys * (wide + group),
        ),
        name="attend_grad",
    )(q, lse, *douts, *outs, *kvs)
    return out[0], out[1:]


def project_grad_kernel(sizes, idx, dq_ref, own_ref, got_ref, *refs):
    uly, dp, group = sizes
    x_refs, refs = refs[:uly], refs[uly:]
    dproj_ref, keep_ref, send_ref = refs
    b, z = idx[0], idx[2]
    rows, width = x_refs[0].shape
    wide = own_ref.shape[1] - group
    share = keep_ref.shape[1] - 16
    dproj_ref[:, :group] = dq_ref[...] * jnp.asarray(0.125, BF16)
    dproj_ref[:, group:wide] = jnp.zeros((uly * rows, wide - group), BF16)
    dproj_ref[:, wide:] = (own_ref[...].astype(F32) + got_ref[...].astype(F32)).astype(BF16)
    sums = jnp.sum(dproj_ref[...].astype(F32), 0, keepdims=True).astype(BF16)
    grad = None
    for j in range(uly):
        part = dot_tn(x_refs[j][...], dproj_ref[j * rows : (j + 1) * rows, :])
        grad = part if grad is None else grad + part
    grad = grad.astype(BF16)
    for ref, mine in ((keep_ref, True), (send_ref, False)):
        for c in range(3):
            lanes = slice(c * wide, c * wide + group)
            into = slice(c * group, (c + 1) * group)
            for s in range(dp):
                for core in range(2):
                    start = (s * 2 + core) * share

                    @pl.when((b == core) == mine)
                    def _(start=start, s=s, ref=ref, lanes=lanes, into=into):
                        ref[s ^ z, :share, into] = grad[start : start + share, lanes]

                ref[s, share:, into] = jnp.broadcast_to(sums[:, lanes], (16, group))


def token_grad_kernel(uly, idx, dproj_ref, w_ref, dh_ref, *out_refs):
    rows = dh_ref.shape[0]
    for j in reversed(range(uly)):
        part = dot_nt(dproj_ref[j * rows : (j + 1) * rows, :], w_ref[...])
        if j == 0:
            part = part + dh_ref[...]
        out_refs[j][...] = part.astype(out_refs[j].dtype)


def finish_feed_kernel(sizes, idx, *refs):
    uly, dp, unit = sizes
    pieces, (expand_ref, shrink_ref) = refs[:-2], refs[-2:]
    shard = expand_ref.shape[0]
    width = shrink_ref.shape[1]
    half = shard // 2
    part = idx[0] * uly + idx[1]
    outs = [None] * dp
    for p, ref in enumerate(pieces):
        start = pl.multiple_of((part ^ p) * unit, unit)
        shrink_ref[pl.ds(start, unit), :] = ref[half:, :].astype(F32)
        put = one_hot(unit, width, (part ^ p) * unit, 0)
        for k in range(dp):
            for h in range(2):
                lanes = slice((h * dp + k) * unit, (h * dp + k + 1) * unit)
                value = dot_nn(ref[:half, lanes], put)
                rows = slice(h * half, (h + 1) * half)
                cols = slice(k * width, (k + 1) * width)
                if p == 0:
                    expand_ref[rows, cols] = value
                else:
                    expand_ref[rows, cols] += value


def finish_attend_kernel(uly, idx, *refs):
    mine, refs = refs[:uly], refs[uly:]
    other, refs = refs[:uly], refs[uly:]
    out_ref, bias_ref = refs
    b, u, z = idx[0], idx[1], idx[2]
    share = mine[0].shape[0] - 16
    group = mine[0].shape[1] // 3
    width = uly * group
    for group_refs, core in ((mine, b), (other, 1 - b)):
        start = pl.multiple_of(core * share, share)
        for c in range(3):
            acc = None
            for j in range(uly):
                put = one_hot(group, width, (u ^ j) * group, 0)
                value = dot_nn(group_refs[j][:share, c * group : (c + 1) * group], put)
                acc = value if acc is None else acc + value
            out_ref[pl.ds(start, share), c * width : (c + 1) * width] = acc
    bias = jnp.zeros((8, 3 * group), F32)
    for j in range(uly):
        lines = mine[j][share : share + 16, :].astype(F32)[:8]
        bias += jnp.where((u ^ j) == z, 1.0, 0.0) * lines
    bias_ref[...] = bias


def on_device(*args):
    (
        tokens,
        lengths,
        cotangent,
        attend_weight,
        query_bias,
        value_bias,
        mixer_weight,
        mixer_bias,
        attn_gain,
        attn_shift,
        expand_weight,
        expand_bias,
        shrink_weight,
        shrink_bias,
        final_gain,
        final_shift,
    ) = args
    uly = lax.axis_size("uly")
    blk = lax.axis_size("blk")
    dp = lax.axis_size("dp")
    width = tokens.shape[-1]
    rows = tokens.shape[0] * tokens.shape[1]
    heads = HEADS // uly
    group = heads * HD
    wide = -(-(group + 1) // 128) * 128
    shard = attend_weight.shape[0]
    hidden = expand_weight.shape[1]
    parts = blk * uly
    unit = hidden // (parts * dp)
    share = shard // blk
    if not (blk == 2 and uly == 4 and shard == group and unit * 2 == shard and share % 16 == 0):
        return general_device(*args)
    u = lax.axis_index("uly")
    b = lax.axis_index("blk")
    z = lax.axis_index("dp")
    mixer_rows = shard // parts
    feed_rows = shard // 2 + unit + mixer_rows
    block_rows = uly * rows
    cols = 2 * wide + group

    x = tokens.reshape(rows, width)
    xs = [x] + [swap_with(x, "uly", j) for j in range(1, uly)]
    scalars = jnp.stack([b, u, z, lengths[0]]).astype(jnp.int32)
    small = jnp.stack(
        [query_bias, value_bias, mixer_bias, attn_gain, attn_shift, shrink_bias]
        + [final_gain, final_shift]
        + [expand_bias[k * shard : (k + 1) * shard] for k in range(hidden // dp // shard)]
        + [jnp.zeros_like(query_bias)] * (8 - hidden // dp // shard)
    )
    first, feed = call(
        functools.partial(fetch_kernel, (uly, dp, group, unit)),
        "fetch",
        scalars,
        [
            attend_weight.reshape(blk, share, 3 * width),
            small,
            expand_weight,
            shrink_weight.reshape(parts, unit, width),
            mixer_weight,
        ],
        [
            pl.BlockSpec((1, share, 3 * width), lambda t, s: (s[0], 0, 0)),
            whole(small.shape),
            whole(expand_weight.shape),
            pl.BlockSpec((1, unit, width), lambda t, s: (s[0] * uly + s[1], 0, 0)),
            whole(mixer_weight.shape),
        ],
        [
            jax.ShapeDtypeStruct((share + 16, 3 * group), BF16),
            jax.ShapeDtypeStruct((feed_rows, width), BF16),
        ],
        [whole((share + 16, 3 * group)), whole((feed_rows, width))],
        [],
        (1,),
        10**9,
        32,
    )
    mine = [first] + [swap_with(first, "dp", j) for j in range(1, dp)]
    other = [swap_with(piece, "blk", 1) for piece in mine]

    feed_all = lax.all_gather(feed, "dp", axis=0, tiled=False)
    half = shard // 2
    halves = feed_all[:, :half].reshape(dp, half, 2, dp * unit).transpose(0, 2, 1, 3)
    expand = [halves.reshape(width, dp * unit)]
    shrink = [feed_all[:, half:]]
    expand.append(swap_with(expand[0], "uly", 1))
    shrink_y = swap_with(shrink[0], "uly", 2)
    expand.append(swap_with(expand[0], "uly", 2))
    shrink.append(swap_with(shrink[0], "uly", 1))
    expand.append(swap_with(expand[1], "uly", 2))
    shrink += [shrink_y, swap_with(shrink_y, "uly", 1)]
    expand += [swap_with(piece, "blk", 1) for piece in expand]
    shrink += [swap_with(piece, "blk", 1) for piece in shrink]
    mixer_all = jnp.stack(xor_order([piece[:, unit:] for piece in shrink], b * uly + u), 1)
    mixer_all = mixer_all.reshape(width, width)

    w_own, q, kv, vec, eb = call(
        functools.partial(project_kernel, (uly, blk, dp, group, unit)),
        "project",
        scalars,
        [*xs, *mine, *other],
        [whole((rows, width))] * uly + [whole(first.shape)] * (2 * dp),
        [
            jax.ShapeDtypeStruct((width, cols), BF16),
            jax.ShapeDtypeStruct((block_rows, wide), BF16),
            jax.ShapeDtypeStruct((block_rows, wide + group), BF16),
            jax.ShapeDtypeStruct((16, width), F32),
            jax.ShapeDtypeStruct((parts, dp * unit), F32),
        ],
        [
            whole((width, cols)),
            whole((block_rows, wide)),
            whole((block_rows, wide + group)),
            whole((16, width)),
            whole((parts, dp * unit)),
        ],
        [],
        (1,),
        2 * block_rows * width * cols,
        48,
    )
    kvs = [kv, swap_with(kv, "blk", 1)]
    outs, lse = attend(q, kvs, heads, uly)
    o_cols = [outs[0]] + [swap_with(outs[j], "uly", j) for j in range(1, uly)]

    square = (rows, width)
    x1, x1b, normed, inverse = call(
        functools.partial(first_norm_kernel, uly),
        "first_norm",
        scalars,
        [x, *o_cols, mixer_all, vec],
        [whole(square)] + [whole((rows, group))] * uly + [whole((width, width)), whole(vec.shape)],
        [
            jax.ShapeDtypeStruct(square, F32),
            jax.ShapeDtypeStruct(square, BF16),
            jax.ShapeDtypeStruct(square, F32),
            jax.ShapeDtypeStruct((rows, 1), F32),
        ],
        [whole(square), whole(square), whole(square), whole((rows, 1))],
        [],
        (1,),
        2 * rows * width * width,
        32,
    )
    mixed, dh2, dh2b, slope, s_keep, s_send, sums2 = feed_forward(
        scalars, x1, x1b, eb, vec, cotangent.reshape(square), expand, shrink
    )
    s_got = swap_with(s_send, "blk", 1)
    dx1, e_keep, e_send, deb = feed_backward(scalars, x1b, dh2, dh2b, slope, expand, shrink)
    e_got = swap_with(e_send, "blk", 1)
    block = (dp, share + 16, width)
    dh1, *rest = call(
        functools.partial(norm_backward_kernel, (uly, dp, unit)),
        "norm_backward",
        scalars,
        [dx1, normed, inverse, mixer_all, vec, sums2, deb.reshape(parts, dp * unit), *o_cols],
        [whole(square), whole(square), whole((rows, 1)), whole((width, width))]
        + [whole(vec.shape), whole(sums2.shape), whole((parts, dp * unit))]
        + [whole((rows, group))] * uly,
        [jax.ShapeDtypeStruct(square, F32)]
        + [jax.ShapeDtypeStruct((rows, group), BF16)] * uly
        + [jax.ShapeDtypeStruct(block, BF16)] * 2,
        [whole(square)] + [whole((rows, group))] * uly + [whole(block)] * 2,
        [pltpu.VMEM((group, width), BF16)],
        (1,),
        4 * rows * width * width,
        48,
    )
    douts = [rest[0]] + [swap_with(rest[j], "uly", j) for j in range(1, uly)]
    m_keep, m_send = rest[uly:]
    m_got = swap_with(m_send, "blk", 1)
    dq, dkvs = attend_grad(q, kvs, douts, outs, lse, heads)

    def add(*values):
        return total(values).astype(BF16)

    s_y = swap_with(add(s_keep[2:], s_got[2:]), "uly", 2)
    s_x = swap_with(add(s_keep[1], s_got[1], s_y[1]), "uly", 1)
    e_x = swap_with(
        jnp.stack([add(e_keep[1], e_got[1]), add(e_keep[3], e_got[3])]), "uly", 1
    )
    e_y = swap_with(add(e_keep[2], e_got[2], e_x[1]), "uly", 2)

    def feed_piece(j):
        at = slice(j * unit, (j + 1) * unit)
        low = [slice(j * shard + h * half, j * shard + (h + 1) * half) for h in range(2)]
        sides = [add(e_keep[0, r], e_got[0, r], e_x[0, r], e_y[r]) for r in low]
        bottom = add(s_keep[0, at], s_got[0, at], s_y[0, at], s_x[at])
        return jnp.concatenate([jnp.concatenate(sides, 1), bottom], 0)

    def over_dp(pieces):
        return add(pieces[0], *[swap_with(pieces[j], "dp", j) for j in range(1, dp)])

    owned = over_dp([feed_piece(j) for j in range(dp)])
    plane = [owned] + [swap_with(owned, "uly", j) for j in range(1, uly)]
    plane += [swap_with(piece, "blk", 1) for piece in plane]
    expand_out, shrink_out = call(
        functools.partial(finish_feed_kernel, (uly, dp, unit)),
        "finish_feed",
        scalars,
        plane,
        [whole(owned.shape)] * parts,
        [
            jax.ShapeDtypeStruct((shard, hidden), F32),
            jax.ShapeDtypeStruct((hidden // dp, width), F32),
        ],
        [whole((shard, hidden)), whole((hidden // dp, width))],
        [],
        (1,),
        10**9,
        48,
    )

    m_own = over_dp([add(m_keep[j], m_got[j]) for j in range(dp)])
    m_all = [m_own] + [swap_with(m_own, "uly", j) for j in range(1, uly)]
    m_all = [value.astype(F32) for value in m_all]
    m_all = (m_all[0] + m_all[1]) + (m_all[2] + m_all[3])
    m_half = m_all[:share].astype(BF16)
    mixer_out = jnp.concatenate(xor_order([m_half, swap_with(m_half, "blk", 1)], b), 0)
    vecs = [m_all[share + k, :shard] for k in range(6)]
    eb_out = m_all[share + 8 : share + 8 + parts, :unit].reshape(-1)

    dproj, a_keep, a_send = call(
        functools.partial(project_grad_kernel, (uly, dp, group)),
        "project_grad",
        scalars,
        [dq, dkvs[0], swap_with(dkvs[1], "blk", 1), *xs],
        [whole(dq.shape), whole(kv.shape), whole(kv.shape)] + [whole(square)] * uly,
        [
            jax.ShapeDtypeStruct((block_rows, cols), BF16),
            jax.ShapeDtypeStruct((dp, share + 16, 3 * group), BF16),
            jax.ShapeDtypeStruct((dp, share + 16, 3 * group), BF16),
        ],
        [whole((block_rows, cols))] + [whole((dp, share + 16, 3 * group))] * 2,
        [],
        (1,),
        2 * block_rows * width * cols,
        48,
    )
    a_got = swap_with(a_send, "blk", 1)
    token_parts = call(
        functools.partial(token_grad_kernel, uly),
        "token_grad",
        scalars,
        [dproj, w_own, dh1],
        [whole((block_rows, cols)), whole((width, cols)), whole(square)],
        [jax.ShapeDtypeStruct(square, F32)] + [jax.ShapeDtypeStruct(square, BF16)] * (uly - 1),
        [whole(square)] * uly,
        [],
        (1,),
        2 * block_rows * width * cols,
        48,
    )
    tokens_grad = total(
        [token_parts[0]] + [swap_with(token_parts[j], "uly", j) for j in range(1, uly)]
    )
    a_own = over_dp([add(a_keep[j], a_got[j]) for j in range(dp)])
    a_mine = [a_own] + [swap_with(a_own, "uly", j) for j in range(1, uly)]
    a_other = [swap_with(piece, "blk", 1) for piece in a_mine]
    attend_out, biases = call(
        functools.partial(finish_attend_kernel, uly),
        "finish_attend",
        scalars,
        [*a_mine, *a_other],
        [whole(a_own.shape)] * (2 * uly),
        [jax.ShapeDtypeStruct((shard, 3 * width), F32), jax.ShapeDtypeStruct((8, 3 * group), F32)],
        [whole((shard, 3 * width)), whole((8, 3 * group))],
        [],
        (1,),
        10**9,
        48,
    )
    return (
        mixed.reshape(tokens.shape),
        tokens_grad.reshape(tokens.shape),
        attend_out,
        biases[0, :group],
        biases[0, 2 * group :],
        mixer_out.astype(F32),
        vecs[0],
        vecs[1],
        vecs[2],
        expand_out,
        eb_out,
        shrink_out,
        vecs[3],
        vecs[4],
        vecs[5],
    )


def solution(mesh):
    row_spec = P("dp", ("blk", "uly"), None)
    matrix = P("dp", None)
    vector = P("dp")
    return jax.shard_map(
        on_device,
        mesh=mesh,
        in_specs=(
            row_spec,
            vector,
            row_spec,
            matrix,
            vector,
            vector,
            matrix,
            vector,
            vector,
            vector,
            matrix,
            vector,
            matrix,
            vector,
            vector,
            vector,
        ),
        out_specs=(
            row_spec,
            row_spec,
            matrix,
            vector,
            vector,
            matrix,
            vector,
            vector,
            vector,
            matrix,
            vector,
            matrix,
            vector,
            vector,
            vector,
        ),
        check_vma=False,
    )
```

```python
import functools

import jax
import jax.numpy as jnp
from jax import lax
from jax.experimental import pallas as pl
from jax.experimental.pallas import tpu as pltpu
from jax.sharding import PartitionSpec as P

HEADS = 12
HD = 64

EPSILON = 1e-12
MASKED = -1000000000.0
LOG2E = 1.4426950408889634
LN2 = 0.6931471805599453
F32 = jnp.float32
BF16 = jnp.bfloat16


def dot_nn(left, right):
    return lax.dot_general(left, right, (((1,), (0,)), ((), ())), preferred_element_type=F32)


def dot_nt(left, right):
    return lax.dot_general(left, right, (((1,), (1,)), ((), ())), preferred_element_type=F32)


def dot_tn(left, right):
    return lax.dot_general(left, right, (((0,), (0,)), ((), ())), preferred_element_type=F32)


def swap_with(value, axis, offset):
    size = lax.axis_size(axis)
    return lax.ppermute(value, axis, [(i, i ^ offset) for i in range(size)])


def xor_order(pieces, index):
    bit = 1
    while bit < len(pieces):
        flag = (index & bit) != 0
        pieces = [jnp.where(flag, pieces[p ^ bit], pieces[p]) for p in range(len(pieces))]
        bit *= 2
    return pieces


def total(values):
    acc = values[0].astype(F32)
    for value in values[1:]:
        acc = acc + value.astype(F32)
    return acc


def pad_rows(value, rows):
    return jnp.pad(value, ((0, rows - value.shape[0]), (0, 0)))


def head_lanes(width, head, ones_lane=None):
    lane = lax.broadcasted_iota(jnp.int32, (1, width), 1)
    keep = (lane >= head * HD) & (lane < (head + 1) * HD)
    if ones_lane is not None:
        keep = keep | (lane == ones_lane)
    return keep


def attend_forward_kernel(heads, blocks, q_ref, *refs):
    kv_refs = refs[:blocks]
    o_ref, lse_ref, vt_ref = refs[blocks:]
    group = heads * HD
    wide = q_ref.shape[1]
    rows = kv_refs[0].shape[0]

    @pl.when(pl.program_id(0) == 0)
    def _():
        for i in range(blocks):
            vt_ref[:, i * rows : (i + 1) * rows] = kv_refs[i][:, wide : wide + group].T

    q = q_ref[...]
    outs = []
    stats = []
    for head in range(heads):
        q_head = jnp.where(head_lanes(wide, head, group), q, jnp.zeros_like(q))
        scores = [dot_nt(kv_refs[i][:, :wide], q_head) for i in range(blocks)]
        top = jnp.max(scores[0], axis=0, keepdims=True)
        for i in range(1, blocks):
            top = jnp.maximum(top, jnp.max(scores[i], axis=0, keepdims=True))
        norm = jnp.zeros_like(top)
        acc = None
        for i in range(blocks):
            probs = jnp.exp2(scores[i] - top)
            norm = norm + jnp.sum(probs, axis=0, keepdims=True)
            part = dot_nn(
                vt_ref[head * HD : (head + 1) * HD, i * rows : (i + 1) * rows], probs.astype(BF16)
            )
            acc = part if acc is None else acc + part
        outs.append(acc / norm)
        stats.append(top + jnp.log2(norm))
    o_ref[...] = jnp.concatenate(outs, axis=0).T.astype(BF16)
    for head in range(heads):
        lse_ref[head : head + 1, :] = stats[head]


def attend_forward(q, kvs, heads, tile):
    rows, wide = q.shape
    group = heads * HD
    blocks = len(kvs)
    keys = blocks * rows
    whole = pl.BlockSpec(kvs[0].shape, lambda t: (0, 0))
    return pl.pallas_call(
        functools.partial(attend_forward_kernel, heads, blocks),
        grid=(rows // tile,),
        in_specs=[pl.BlockSpec((tile, wide), lambda t: (t, 0))] + [whole] * blocks,
        out_specs=[
            pl.BlockSpec((tile, group), lambda t: (t, 0)),
            pl.BlockSpec((8, tile), lambda t: (0, t)),
        ],
        out_shape=[
            jax.ShapeDtypeStruct((rows, group), BF16),
            jax.ShapeDtypeStruct((8, rows), F32),
        ],
        scratch_shapes=[pltpu.VMEM((group, keys), BF16)],
        compiler_params=pltpu.CompilerParams(vmem_limit_bytes=56 * 2**20),
        cost_estimate=pl.CostEstimate(
            flops=4 * heads * rows * keys * wide,
            transcendentals=heads * rows * keys,
            bytes_accessed=2 * rows * wide * 3 + 2 * keys * (wide + group),
        ),
        name="attend_forward",
    )(q, *kvs)


def attend_backward_kernel(heads, blocks, q_ref, do_ref, o_ref, lse_ref, *refs):
    kv_refs = refs[:blocks]
    dq_ref = refs[blocks]
    dkv_refs = refs[blocks + 1 : 2 * blocks + 1]
    kt_ref = refs[2 * blocks + 1]
    dk_accs = refs[2 * blocks + 2 : 3 * blocks + 2]
    dv_accs = refs[3 * blocks + 2 :]
    group = heads * HD
    wide = q_ref.shape[1]
    rows = kv_refs[0].shape[0]

    @pl.when(pl.program_id(0) == 0)
    def _():
        for i in range(blocks):
            kt_ref[:, i * rows : (i + 1) * rows] = kv_refs[i][:, :group].T
            dk_accs[i][...] = jnp.zeros_like(dk_accs[i])
            dv_accs[i][...] = jnp.zeros_like(dv_accs[i])

    q = q_ref[...]
    dout = do_ref[...]
    products = (dout.astype(F32) * o_ref[...].astype(F32)).T
    dqs = []
    for head in range(heads):
        q_head = jnp.where(head_lanes(wide, head, group), q, jnp.zeros_like(q))
        do_head = jnp.where(head_lanes(group, head), dout, jnp.zeros_like(dout))
        lse = lse_ref[head : head + 1, :]
        delta = jnp.sum(products[head * HD : (head + 1) * HD], axis=0, keepdims=True)
        acc = None
        for i in range(blocks):
            probs = jnp.exp2(dot_nt(kv_refs[i][:, :wide], q_head) - lse)
            dv_accs[i][...] += dot_nn(probs.astype(BF16), do_head)
            grads = dot_nt(kv_refs[i][:, wide : wide + group], do_head)
            grads = (probs * (grads - delta)).astype(BF16)
            dk_accs[i][...] += dot_nn(grads, q_head)
            part = dot_nn(
                kt_ref[head * HD : (head + 1) * HD, i * rows : (i + 1) * rows], grads
            )
            acc = part if acc is None else acc + part
        dqs.append(acc)
    dq_ref[...] = jnp.concatenate(dqs, axis=0).T.astype(BF16)

    @pl.when(pl.program_id(0) == pl.num_programs(0) - 1)
    def _():
        for i in range(blocks):
            dkv_refs[i][:, :group] = (dk_accs[i][:, :group] * LN2).astype(BF16)
            dkv_refs[i][:, wide : wide + group] = dv_accs[i][...].astype(BF16)


def attend_backward(q, kvs, dout, o, lse, heads, tile):
    rows, wide = q.shape
    group = heads * HD
    blocks = len(kvs)
    keys = blocks * rows
    whole = pl.BlockSpec(kvs[0].shape, lambda t: (0, 0))
    out = pl.pallas_call(
        functools.partial(attend_backward_kernel, heads, blocks),
        grid=(rows // tile,),
        in_specs=[
            pl.BlockSpec((tile, wide), lambda t: (t, 0)),
            pl.BlockSpec((tile, group), lambda t: (t, 0)),
            pl.BlockSpec((tile, group), lambda t: (t, 0)),
            pl.BlockSpec((8, tile), lambda t: (0, t)),
        ]
        + [whole] * blocks,
        out_specs=[pl.BlockSpec((tile, group), lambda t: (t, 0))] + [whole] * blocks,
        out_shape=[jax.ShapeDtypeStruct((rows, group), BF16)]
        + [jax.ShapeDtypeStruct(kvs[0].shape, BF16)] * blocks,
        scratch_shapes=[pltpu.VMEM((group, keys), BF16)]
        + [pltpu.VMEM((rows, wide), F32)] * blocks
        + [pltpu.VMEM((rows, group), F32)] * blocks,
        compiler_params=pltpu.CompilerParams(vmem_limit_bytes=56 * 2**20),
        cost_estimate=pl.CostEstimate(
            flops=10 * heads * rows * keys * wide,
            transcendentals=heads * rows * keys,
            bytes_accessed=2 * rows * wide * 4 + 4 * keys * (wide + group),
        ),
        name="attend_backward",
    )(q, dout, o, lse, *kvs)
    return out[0], out[1:]


def feed_kernel(
    x1_ref,
    x1b_ref,
    expand_ref,
    shrink_ref,
    ebias_ref,
    sbias_ref,
    gain_ref,
    shift_ref,
    cot_ref,
    mixed_ref,
    dx1_ref,
    dexpand_ref,
    dshrink_ref,
    debias_ref,
    vec_ref,
    act_ref,
    slope_ref,
    acc_ref,
    d2b_ref,
    x1t_ref,
):
    phase = pl.program_id(0)
    step = pl.program_id(1)
    last = pl.num_programs(1) - 1
    width = x1_ref.shape[1]

    @pl.when(phase == 0)
    def _():
        pre = dot_nn(x1b_ref[...], expand_ref[0]) + ebias_ref[0]
        cdf = 0.5 * (1.0 + lax.erf(pre * 0.7071067811865476))
        pdf = jnp.exp(-0.5 * pre * pre) * 0.3989422804014327
        act = (pre * cdf).astype(BF16)
        act_ref[step] = act
        slope_ref[step] = (cdf + pre * pdf).astype(BF16)
        part = dot_nn(act, shrink_ref[0])

        @pl.when(step == 0)
        def _():
            acc_ref[...] = part
            x1t_ref[...] = x1b_ref[...].T

        @pl.when(step > 0)
        def _():
            acc_ref[...] += part

        @pl.when(step == last)
        def _():
            hidden = x1_ref[...] + (acc_ref[...] + sbias_ref[...])
            center = hidden - jnp.mean(hidden, -1, keepdims=True)
            inverse = lax.rsqrt(jnp.mean(center * center, -1, keepdims=True) + EPSILON)
            normed = center * inverse
            mixed_ref[...] = (normed * gain_ref[...] + shift_ref[...]).astype(BF16)
            grad = cot_ref[...].astype(F32)
            scaled = grad * gain_ref[...]
            dhidden = inverse * (
                scaled
                - jnp.mean(scaled, -1, keepdims=True)
                - normed * jnp.mean(scaled * normed, -1, keepdims=True)
            )
            acc_ref[...] = dhidden
            d2b_ref[...] = dhidden.astype(BF16)
            vec_ref[...] = jnp.zeros_like(vec_ref)
            vec_ref[0:1, :] = jnp.sum(grad * normed, 0, keepdims=True)
            vec_ref[1:2, :] = jnp.sum(grad, 0, keepdims=True)
            vec_ref[2:3, :] = jnp.sum(dhidden, 0, keepdims=True)

    @pl.when(phase == 1)
    def _():
        d2b = d2b_ref[...]
        dpre = (dot_nt(d2b, shrink_ref[0]) * slope_ref[step].astype(F32)).astype(BF16)
        debias_ref[0] = jnp.sum(dpre.astype(F32), 0, keepdims=True)
        dexpand_ref[0] = dot_nn(x1t_ref[...], dpre).astype(BF16)
        dshrink_ref[0] = dot_tn(act_ref[step], d2b).astype(BF16)
        acc_ref[...] += dot_nt(dpre, expand_ref[0])

        @pl.when(step == last)
        def _():
            dx1_ref[...] = acc_ref[...]


def feed_forward_backward(x1, x1b, expand, shrink, ebias, sbias, gain, shift, cot):
    rows, width = x1.shape
    parts, _, block = expand.shape
    full = pl.BlockSpec((rows, width), lambda p, k: (0, 0))
    line = pl.BlockSpec((1, width), lambda p, k: (0, 0))
    return pl.pallas_call(
        feed_kernel,
        grid=(2, parts),
        in_specs=[
            full,
            full,
            pl.BlockSpec((1, width, block), lambda p, k: (k, 0, 0)),
            pl.BlockSpec((1, block, width), lambda p, k: (k, 0, 0)),
            pl.BlockSpec((1, 1, block), lambda p, k: (k, 0, 0)),
            line,
            line,
            line,
            full,
        ],
        out_specs=[
            full,
            full,
            pl.BlockSpec((1, width, block), lambda p, k: (p * k, 0, 0)),
            pl.BlockSpec((1, block, width), lambda p, k: (p * k, 0, 0)),
            pl.BlockSpec((1, 1, block), lambda p, k: (p * k, 0, 0)),
            pl.BlockSpec((8, width), lambda p, k: (0, 0)),
        ],
        out_shape=[
            jax.ShapeDtypeStruct((rows, width), BF16),
            jax.ShapeDtypeStruct((rows, width), F32),
            jax.ShapeDtypeStruct((parts, width, block), BF16),
            jax.ShapeDtypeStruct((parts, block, width), BF16),
            jax.ShapeDtypeStruct((parts, 1, block), F32),
            jax.ShapeDtypeStruct((8, width), F32),
        ],
        scratch_shapes=[
            pltpu.VMEM((parts, rows, block), BF16),
            pltpu.VMEM((parts, rows, block), BF16),
            pltpu.VMEM((rows, width), F32),
            pltpu.VMEM((rows, width), BF16),
            pltpu.VMEM((width, rows), BF16),
        ],
        compiler_params=pltpu.CompilerParams(vmem_limit_bytes=48 * 2**20),
        cost_estimate=pl.CostEstimate(
            flops=12 * rows * width * parts * block,
            transcendentals=2 * rows * parts * block,
            bytes_accessed=12 * width * parts * block,
        ),
        name="feed_forward_backward",
    )(x1, x1b, expand, shrink, ebias, sbias, gain, shift, cot)


def general_device(
    tokens,
    lengths,
    cotangent,
    attend_weight,
    query_bias,
    value_bias,
    mixer_weight,
    mixer_bias,
    attn_gain,
    attn_shift,
    expand_weight,
    expand_bias,
    shrink_weight,
    shrink_bias,
    final_gain,
    final_shift,
):
    uly = lax.axis_size("uly")
    blk = lax.axis_size("blk")
    dp = lax.axis_size("dp")
    u = lax.axis_index("uly")
    b = lax.axis_index("blk")
    z = lax.axis_index("dp")
    width = tokens.shape[-1]
    rows = tokens.shape[0] * tokens.shape[1]
    block_rows = uly * rows
    heads = HEADS // uly
    group = heads * HD
    wide = -(-(group + 1) // 128) * 128
    shard = attend_weight.shape[0]
    hidden = expand_weight.shape[1]
    parts = blk * uly
    unit = hidden // (parts * dp)
    share = shard // blk

    x = tokens.reshape(rows, width)
    x_rows = jnp.concatenate([x] + [swap_with(x, "uly", j) for j in range(1, uly)], 0)

    small = jnp.concatenate(
        [query_bias, value_bias, mixer_bias, attn_gain, attn_shift, shrink_bias]
        + [final_gain, final_shift, expand_bias]
    )
    small_rows = small.shape[0] // (3 * group)
    own_heads = lax.dynamic_slice_in_dim(attend_weight.reshape(shard, 3, uly, group), u, 1, 2)
    own_heads = own_heads.reshape(shard, 3 * group)
    first_piece = jnp.concatenate(
        [
            lax.dynamic_slice_in_dim(own_heads, b * share, share, 0),
            pad_rows(small.reshape(small_rows, 3 * group), 16),
        ]
    )
    first_all = lax.all_gather(first_piece, "dp", axis=0, tiled=False)
    halves = first_all[:, :share]
    halves = xor_order([halves] + [swap_with(halves, "blk", i) for i in range(1, blk)], b)
    attend_own = jnp.stack(halves, 1).reshape(width, 3, group)
    vectors = first_all[:, share : share + small_rows].reshape(dp, -1, shard).astype(F32)
    names = [vectors[:, k].reshape(width) for k in range(8)]
    bias_query, bias_value, bias_mixer, gain_attn, shift_attn, bias_shrink = names[:6]
    gain_final, shift_final = names[6:]
    bias_expand = vectors[:, 8:].reshape(dp, parts, unit).transpose(1, 0, 2)
    bias_expand = jnp.stack(
        xor_order(list(bias_expand.reshape(parts, dp * unit)), b * uly + u), 0
    ).reshape(parts, 1, dp * unit)

    mixer_own = lax.dynamic_slice_in_dim(mixer_weight, b * share, share, 0)
    mixer_all = jnp.stack(
        xor_order([mixer_own] + [swap_with(mixer_own, "dp", j) for j in range(1, dp)], z), 0
    )
    mixer_all = jnp.stack(
        xor_order([mixer_all] + [swap_with(mixer_all, "blk", i) for i in range(1, blk)], b), 1
    ).reshape(width, width)

    part = b * uly + u
    expand_own = lax.dynamic_slice_in_dim(
        expand_weight.reshape(shard, dp, parts, unit), part, 1, 2
    ).reshape(-1, width)
    shrink_own = lax.dynamic_slice_in_dim(shrink_weight.reshape(parts, unit, width), part, 1, 0)
    expand_rows = expand_own.shape[0]
    feed_own = jnp.concatenate([expand_own, shrink_own.reshape(unit, width)], 0)
    feed_all = lax.all_gather(feed_own, "dp", axis=0, tiled=False)
    expand_part = feed_all[:, :expand_rows].reshape(width, dp * unit)
    shrink_part = feed_all[:, expand_rows:].reshape(dp * unit, width)
    expand_two = jnp.stack([expand_part, swap_with(expand_part, "uly", 1)])
    shrink_two = jnp.stack([shrink_part, swap_with(shrink_part, "uly", 2)])
    expand_far = swap_with(expand_two, "uly", 2)
    shrink_far = swap_with(shrink_two, "uly", 1)
    expand_here = jnp.concatenate([expand_two, expand_far], 0)
    shrink_here = jnp.stack([shrink_two[0], shrink_far[0], shrink_two[1], shrink_far[1]], 0)
    expand_full = jnp.concatenate(
        [expand_here] + [swap_with(expand_here, "blk", i) for i in range(1, blk)], 0
    )
    shrink_full = jnp.concatenate(
        [shrink_here] + [swap_with(shrink_here, "blk", i) for i in range(1, blk)], 0
    )

    lane_pad = ((0, 0), (0, wide - group))
    bias_row = jnp.pad(lax.dynamic_slice_in_dim(bias_query, u * group, group, 0), lane_pad[1:])
    ones_lane = (jnp.arange(wide) == group).astype(F32)
    q = dot_nn(x_rows, jnp.pad(attend_own[:, 0], lane_pad)) + bias_row
    q = (q * (0.125 * LOG2E) + ones_lane).astype(BF16)
    kv_weight = jnp.concatenate([jnp.pad(attend_own[:, 1], lane_pad), attend_own[:, 2]], 1)
    kv_bias = jnp.concatenate(
        [jnp.zeros((wide,), F32), lax.dynamic_slice_in_dim(bias_value, u * group, group, 0)]
    )
    kv_ones = jnp.pad(ones_lane, (0, group))
    row_index = jnp.arange(block_rows, dtype=jnp.int32)
    positions = b * block_rows + ((row_index // rows) ^ u) * rows + row_index % rows
    key_mask = jnp.where(positions < lengths[0], 0.0, MASKED)
    kv = (dot_nn(x_rows, kv_weight) + kv_bias + key_mask[:, None] * kv_ones).astype(BF16)
    kvs = [kv] + [swap_with(kv, "blk", i) for i in range(1, blk)]

    o_rows, lse = attend_forward(q, kvs, heads, min(256, block_rows))
    pieces = [o_rows[j * rows : (j + 1) * rows] for j in range(uly)]
    pieces = [pieces[0]] + [swap_with(pieces[j], "uly", j) for j in range(1, uly)]
    mixer_in = jnp.concatenate(xor_order(pieces, u), 1)

    first_sum = x.astype(F32) + (dot_nn(mixer_in, mixer_all) + bias_mixer)
    center = first_sum - jnp.mean(first_sum, -1, keepdims=True)
    first_inv = lax.rsqrt(jnp.mean(center * center, -1, keepdims=True) + EPSILON)
    first_normed = center * first_inv
    first_out = first_normed * gain_attn + shift_attn
    first_low = first_out.astype(BF16)

    mixed, first_grad, expand_grad, shrink_grad, expand_bias_grad, vec_grads = (
        feed_forward_backward(
            first_out,
            first_low,
            expand_full,
            shrink_full,
            bias_expand,
            bias_shrink[None],
            gain_final[None],
            shift_final[None],
            cotangent.reshape(rows, width),
        )
    )

    scaled = first_grad * gain_attn
    attn_grad = first_inv * (
        scaled
        - jnp.mean(scaled, -1, keepdims=True)
        - first_normed * jnp.mean(scaled * first_normed, -1, keepdims=True)
    )
    attn_low = attn_grad.astype(BF16)
    out_grad = dot_nt(attn_low, mixer_all).astype(BF16)
    sends = xor_order([out_grad[:, j * group : (j + 1) * group] for j in range(uly)], u)
    dout_rows = jnp.concatenate(
        [sends[0]] + [swap_with(sends[j], "uly", j) for j in range(1, uly)], 0
    )
    dq, dkvs = attend_backward(q, kvs, dout_rows, o_rows, lse, heads, min(256, block_rows))

    mixer_grad = dot_tn(mixer_in, attn_low).astype(BF16)
    attn_gain_grad = jnp.sum(first_grad * first_normed, 0)
    attn_shift_grad = jnp.sum(first_grad, 0)
    mixer_bias_grad = jnp.sum(attn_grad, 0)
    ebg = jnp.stack(xor_order(list(expand_bias_grad.reshape(parts, dp * unit)), part), 0)
    ebg = ebg.reshape(parts, dp, unit).transpose(1, 0, 2).reshape(dp, parts * unit)
    vec_all = jnp.concatenate(
        [
            v.reshape(dp, shard)
            for v in (
                mixer_bias_grad,
                attn_gain_grad,
                attn_shift_grad,
                vec_grads[2],
                vec_grads[0],
                vec_grads[1],
            )
        ]
        + [ebg],
        1,
    ).astype(BF16)

    mixer_cols = width // blk
    mixer_part_rows = shard // uly
    vec_len = vec_all.shape[1]
    vec_rows = -(-vec_len // mixer_cols)
    vec_rows = -(-vec_rows // 16) * 16
    vec_block = jnp.pad(vec_all, ((0, 0), (0, vec_rows * mixer_cols - vec_len))).reshape(
        dp, vec_rows, mixer_cols
    )
    mixer_view = mixer_grad.reshape(dp, uly, mixer_part_rows, blk, mixer_cols)
    by_blk = xor_order([mixer_view[:, :, :, i] for i in range(blk)], b)
    mixer_parts = []
    for i in range(blk):
        by_uly = xor_order([by_blk[i][:, j] for j in range(uly)], u)
        mixer_parts.append(
            jnp.stack([jnp.concatenate([piece, vec_block], 1) for piece in by_uly], 0)
        )
    mixer_sum = total(
        [mixer_parts[0]] + [swap_with(mixer_parts[i], "blk", i) for i in range(1, blk)]
    ).astype(BF16)
    mixer_sum = total(
        [mixer_sum[0]] + [swap_with(mixer_sum[j], "uly", j) for j in range(1, uly)]
    ).astype(BF16)

    def over_blk(grad):
        return total(
            [grad[:uly]]
            + [swap_with(grad[i * uly : (i + 1) * uly], "blk", i) for i in range(1, blk)]
        ).astype(BF16)

    shrink_sum = over_blk(shrink_grad)
    expand_sum = over_blk(expand_grad)
    shrink_sum = shrink_sum.reshape(2, 2, dp * unit, width)
    expand_sum = expand_sum.reshape(2, 2, width, dp * unit)
    shrink_sum = total([shrink_sum[0], swap_with(shrink_sum[1], "uly", 2)]).astype(BF16)
    expand_sum = total([expand_sum[:, 0], swap_with(expand_sum[:, 1], "uly", 1)]).astype(BF16)
    shrink_sum = total([shrink_sum[0], swap_with(shrink_sum[1], "uly", 1)]).astype(BF16)
    expand_sum = total([expand_sum[0], swap_with(expand_sum[1], "uly", 2)]).astype(BF16)

    mixer_rows = mixer_sum.shape[1] * mixer_cols // width
    packed = jnp.concatenate(
        [
            expand_sum.reshape(dp, expand_rows, width),
            shrink_sum.reshape(dp, unit, width),
            mixer_sum.reshape(dp, mixer_rows, width),
        ],
        1,
    )

    def over_dp(value):
        sends = [lax.dynamic_slice_in_dim(value, z ^ j, 1, 0)[0] for j in range(dp)]
        return total([sends[0]] + [swap_with(sends[j], "dp", j) for j in range(1, dp)])

    owned = over_dp(packed)
    vec_owned = owned[expand_rows + unit :].reshape(-1, mixer_cols)[mixer_part_rows:]
    vec_owned = vec_owned.reshape(-1)[:vec_len]

    def in_plane(value):
        value = value.astype(BF16)
        value = jnp.stack(
            xor_order([value] + [swap_with(value, "uly", j) for j in range(1, uly)], u), 0
        )
        return jnp.stack(
            xor_order([value] + [swap_with(value, "blk", i) for i in range(1, blk)], b), 0
        )

    gathered = in_plane(owned).reshape(parts, -1, width)
    expand_out = gathered[:, :expand_rows].reshape(parts, shard, dp, unit)
    expand_out = expand_out.transpose(1, 2, 0, 3).reshape(shard, hidden).astype(F32)
    shrink_out = gathered[:, expand_rows : expand_rows + unit]
    shrink_out = shrink_out.reshape(parts * unit, width).astype(F32)
    mixer_out = gathered[:, expand_rows + unit :].reshape(blk, uly, -1, mixer_cols)
    mixer_out = mixer_out[:, :, :mixer_part_rows].transpose(1, 2, 0, 3)
    mixer_out = mixer_out.reshape(shard, width).astype(F32)

    own_dkv = total([dkvs[0]] + [swap_with(dkvs[i], "blk", i) for i in range(1, blk)])
    own_dkv = own_dkv.astype(BF16)
    proj_grad = jnp.concatenate(
        [dq * jnp.asarray(0.125, BF16), own_dkv[:, :group], own_dkv[:, wide : wide + group]], 1
    )
    token_parts = dot_nt(proj_grad, attend_own.reshape(width, 3 * group))
    token_low = token_parts.astype(BF16)
    tokens_grad = attn_grad + total(
        [token_parts[:rows]]
        + [swap_with(token_low[j * rows : (j + 1) * rows], "uly", j) for j in range(1, uly)]
    )
    attend_grad = dot_tn(x_rows, proj_grad).astype(BF16)
    attend_grad = attend_grad.reshape(dp, blk, share, 3 * group)
    bias_sum = jnp.sum(proj_grad.astype(F32), 0)[None]
    bias_rows = pad_rows(bias_sum.astype(BF16), 16)
    attend_parts = [
        jnp.concatenate(
            [
                lax.dynamic_slice_in_dim(attend_grad, b ^ i, 1, 1).reshape(-1, 3 * group),
                bias_rows,
            ],
            0,
        )
        for i in range(blk)
    ]
    attend_sum = total(
        [attend_parts[0]] + [swap_with(attend_parts[i], "blk", i) for i in range(1, blk)]
    ).astype(BF16)
    bias_half = jnp.broadcast_to(attend_sum[dp * share :], (dp, 16, 3 * group))
    attend_sum = attend_sum[: dp * share].reshape(dp, share, 3 * group)
    attend_owned = over_dp(jnp.concatenate([attend_sum, bias_half], 1))
    attend_all = in_plane(attend_owned)
    attend_out = attend_all[:, :, :share].reshape(blk, uly, share, 3, group)
    attend_out = attend_out.transpose(0, 2, 3, 1, 4).reshape(shard, 3 * width).astype(F32)
    bias_out = attend_all[0, :, share].astype(F32).reshape(uly, 3, group)
    query_bias_grad = lax.dynamic_slice_in_dim(bias_out[:, 0].reshape(width), z * shard, shard, 0)
    value_bias_grad = lax.dynamic_slice_in_dim(bias_out[:, 2].reshape(width), z * shard, shard, 0)

    vecs = [vec_owned[k * shard : (k + 1) * shard] for k in range(6)]
    return (
        mixed.reshape(tokens.shape),
        tokens_grad.reshape(tokens.shape),
        attend_out,
        query_bias_grad,
        value_bias_grad,
        mixer_out,
        vecs[0],
        vecs[1],
        vecs[2],
        expand_out,
        vec_owned[6 * shard :],
        shrink_out,
        vecs[3],
        vecs[4],
        vecs[5],
    )


def call(kernel, name, scalars, args, in_specs, out_shape, out_specs, scratch, grid, flops, vmem):
    return pl.pallas_call(
        kernel,
        grid_spec=pltpu.PrefetchScalarGridSpec(
            num_scalar_prefetch=1,
            grid=grid,
            in_specs=in_specs,
            out_specs=out_specs,
            scratch_shapes=scratch,
        ),
        out_shape=out_shape,
        compiler_params=pltpu.CompilerParams(vmem_limit_bytes=vmem * 2**20),
        cost_estimate=pl.CostEstimate(flops=flops, bytes_accessed=1, transcendentals=0),
        name=name,
    )(scalars, *args)


def whole(shape):
    return pl.BlockSpec(shape, lambda *_: (0,) * len(shape))


def after(value, *deps):
    return lax.optimization_barrier((value, *deps))[0]


def slot(offset):
    return (offset & 1) * 2 + (offset >> 1)


def one_hot(rows, cols, row_offset=0, col_offset=0):
    row = lax.broadcasted_iota(jnp.int32, (rows, cols), 0) + row_offset
    col = lax.broadcasted_iota(jnp.int32, (rows, cols), 1) + col_offset
    return jnp.where(row == col, 1.0, 0.0).astype(BF16)


def fetch_kernel(sizes, idx, attend_ref, expand_ref, shrink_ref, mixer_ref, *refs):
    uly, dp, group, unit = sizes
    vec_refs, (first_ref, feed_ref) = refs[:-2], refs[-2:]
    share = attend_ref.shape[1]
    shard, width = mixer_ref.shape
    u = idx[1]
    part = idx[0] * uly + u
    take = one_hot(width, group, 0, u * group)
    for c in range(3):
        cols = dot_nn(attend_ref[0, :, c * width : (c + 1) * width], take)
        first_ref[:share, c * group : (c + 1) * group] = cols.astype(BF16)
    first_ref[share:, :] = jnp.zeros_like(first_ref[share:, :])
    rows = share // dp
    mixer = dot_nn(one_hot(rows, shard, part * rows, 0), mixer_ref[...]).astype(BF16)
    for k in range(dp):
        here = slice(k * rows, (k + 1) * rows)
        first_ref[here, 3 * group :] = mixer[:, k * group : (k + 1) * group]
    line = share
    for ref in vec_refs:
        for k in range(ref.shape[0] // shard):
            first_ref[line : line + 1, :shard] = ref[k * shard : (k + 1) * shard].reshape(1, shard)
            line += 1
    take = one_hot(width, unit, 0, part * unit)
    half = shard // 2
    for k in range(dp):
        cols = dot_nn(expand_ref[:, k * width : (k + 1) * width], take).astype(BF16)
        feed_ref[:half, k * unit : (k + 1) * unit] = cols[:half]
        feed_ref[:half, (dp + k) * unit : (dp + k + 1) * unit] = cols[half:]
    feed_ref[half:, :] = shrink_ref[0]


def project_kernel(sizes, idx, *refs):
    uly, blk, dp, group, unit = sizes
    x_refs, refs = refs[:uly], refs[uly:]
    mine_refs, refs = refs[:dp], refs[dp:]
    other_refs, refs = refs[:dp], refs[dp:]
    w_ref, q_ref, kv_ref, vec_ref, eb_ref, mixer_ref = refs
    b, u, z, length = idx[0], idx[1], idx[2], idx[3]
    rows, width = x_refs[0].shape
    wide = q_ref.shape[1]
    pad = wide - group
    share = mine_refs[0].shape[0] - 16
    shard = 2 * share
    parts = uly * blk
    for c in range(3):
        w_ref[:, c * wide + group : (c + 1) * wide] = jnp.zeros((width, pad), BF16)
    own_vec = jnp.zeros((16, shard), F32)
    all_vec = jnp.zeros((16, width), F32)
    lines = share // dp
    for j in range(dp):
        for k in range(dp):
            mixer_ref[j * lines : (j + 1) * lines, k * group : (k + 1) * group] = mine_refs[j][
                k * lines : (k + 1) * lines, 3 * group :
            ]
        for ref, core in ((mine_refs[j], b), (other_refs[j], 1 - b)):
            start = pl.multiple_of((z ^ j) * shard + core * share, share)
            for c in range(3):
                w_ref[pl.ds(start, share), c * wide : c * wide + group] = ref[
                    :share, c * group : (c + 1) * group
                ]
        vec = mine_refs[j][share:, :shard]
        own_vec += jnp.where((z ^ j) == u, 1.0, 0.0) * vec.astype(F32)
        all_vec += dot_nn(vec, one_hot(shard, width, (z ^ j) * shard, 0))
    vec_ref[...] = all_vec

    low = all_vec.astype(BF16)
    part = b * uly + u
    eb = jnp.zeros((parts, dp * unit), F32)
    for parity in range(2):
        col = lax.broadcasted_iota(jnp.int32, (width, dp * unit), 1)
        row = lax.broadcasted_iota(jnp.int32, (width, dp * unit), 0)
        source = col + (col // unit) * (shard - unit) + parity * unit
        lanes = dot_nn(low, jnp.where(row == source, 1.0, 0.0).astype(BF16)).astype(BF16)
        owner = lax.broadcasted_iota(jnp.int32, (parts, 16), 0) ^ part
        line = lax.broadcasted_iota(jnp.int32, (parts, 16), 1)
        wanted = ((owner & 1) == parity) & (line == 8 + (owner >> 1))
        eb += dot_nn(jnp.where(wanted, 1.0, 0.0).astype(BF16), lanes)
    eb_ref[...] = eb

    lane = lax.broadcasted_iota(jnp.int32, (1, wide), 1)
    mark = jnp.where(lane == group, 1.0, 0.0)
    zeros = jnp.zeros((1, pad), F32)
    q_bias = jnp.concatenate([own_vec[0:1], zeros], 1)
    v_bias = jnp.concatenate([own_vec[1:2], zeros], 1)
    for j in range(uly):
        x = x_refs[j][...]
        here = slice(j * rows, (j + 1) * rows)
        q = dot_nn(x, w_ref[:, :wide]) + q_bias
        q_ref[here, :] = (q * (0.125 * LOG2E) + mark).astype(BF16)
        first = (b * uly + (u ^ j)) * rows
        position = lax.broadcasted_iota(jnp.int32, (rows, 1), 0) + first
        masked = jnp.where(position < length, 0.0, MASKED)
        k = dot_nn(x, w_ref[:, wide : 2 * wide]) + masked * mark
        kv_ref[here, :wide] = k.astype(BF16)
        kv_ref[here, wide:] = (dot_nn(x, w_ref[:, 2 * wide :]) + v_bias).astype(BF16)


def attend_kernel(heads, blocks, q_ref, *refs):
    kv_refs = refs[:blocks]
    o_refs = refs[blocks:-2]
    lse_ref, vt_ref = refs[-2:]
    group = heads * HD
    wide = q_ref.shape[1]
    rows = kv_refs[0].shape[0]

    @pl.when(pl.program_id(0) == 0)
    def _():
        for i in range(blocks):
            vt_ref[:, i * rows : (i + 1) * rows] = kv_refs[i][:, wide : wide + group].T

    q = q_ref[...]
    outs = []
    for head in range(heads):
        q_head = jnp.where(head_lanes(wide, head, group), q, jnp.zeros_like(q))
        scores = [dot_nt(kv_refs[i][:, :wide], q_head) for i in range(blocks)]
        top = jnp.max(scores[0], axis=0, keepdims=True)
        for i in range(1, blocks):
            top = jnp.maximum(top, jnp.max(scores[i], axis=0, keepdims=True))
        norm = jnp.zeros_like(top)
        acc = None
        for i in range(blocks):
            probs = jnp.exp2(scores[i] - top)
            norm = norm + jnp.sum(probs, axis=0, keepdims=True)
            part = dot_nn(
                vt_ref[head * HD : (head + 1) * HD, i * rows : (i + 1) * rows], probs.astype(BF16)
            )
            acc = part if acc is None else acc + part
        outs.append(acc / norm)
        lse_ref[head : head + 1, :] = top + jnp.log2(norm)
    out = jnp.concatenate(outs, axis=0).T.astype(BF16)
    for j, o_ref in enumerate(o_refs):

        @pl.when(pl.program_id(0) == j)
        def _(o_ref=o_ref):
            o_ref[...] = out


def attend(q, kvs, heads, pieces):
    rows, wide = q.shape
    tile = rows // pieces
    group = heads * HD
    blocks = len(kvs)
    keys = blocks * rows
    out = pl.pallas_call(
        functools.partial(attend_kernel, heads, blocks),
        grid=(pieces,),
        in_specs=[pl.BlockSpec((tile, wide), lambda t: (t, 0))] + [whole(kvs[0].shape)] * blocks,
        out_specs=[whole((tile, group))] * pieces + [pl.BlockSpec((8, tile), lambda t: (0, t))],
        out_shape=[jax.ShapeDtypeStruct((tile, group), BF16)] * pieces
        + [jax.ShapeDtypeStruct((8, rows), F32)],
        scratch_shapes=[pltpu.VMEM((group, keys), BF16)],
        compiler_params=pltpu.CompilerParams(vmem_limit_bytes=16 * 2**20),
        cost_estimate=pl.CostEstimate(
            flops=4 * heads * rows * keys * wide,
            transcendentals=heads * rows * keys,
            bytes_accessed=2 * rows * wide * 3 + 2 * keys * (wide + group),
        ),
        name="attend",
    )(q, *kvs)
    return out[:-1], out[-1]


def first_norm_kernel(uly, idx, x_ref, *refs):
    o_refs = refs[:uly]
    m_ref, vec_ref, x1_ref, x1b_ref, normed_ref, inverse_ref = refs[uly:]
    group = o_refs[0].shape[1]
    acc = vec_ref[2:3, :]
    for j in range(uly):
        start = pl.multiple_of((idx[1] ^ j) * group, group)
        acc = acc + dot_nn(o_refs[j][...], m_ref[pl.ds(start, group), :])
    hidden = x_ref[...].astype(F32) + acc
    center = hidden - jnp.mean(hidden, -1, keepdims=True)
    inverse = lax.rsqrt(jnp.mean(center * center, -1, keepdims=True) + EPSILON)
    normed = center * inverse
    out = normed * vec_ref[3:4, :] + vec_ref[4:5, :]
    x1_ref[...] = out
    x1b_ref[...] = out.astype(BF16)
    normed_ref[...] = normed
    inverse_ref[...] = inverse


def rest_kernel(sizes, idx, expand_ref, shrink_ref, out_ref):
    uly, dp, unit = sizes
    width = shrink_ref.shape[1]
    half = expand_ref.shape[0] // 2
    for j in range(1, uly):
        part = idx[0] * uly + (idx[1] ^ j)
        take = one_hot(width, unit, 0, part * unit)
        for k in range(dp):
            cols = dot_nn(expand_ref[:, k * width : (k + 1) * width], take).astype(BF16)
            out_ref[j - 1, :half, k * unit : (k + 1) * unit] = cols[:half]
            out_ref[j - 1, :half, (dp + k) * unit : (dp + k + 1) * unit] = cols[half:]
        start = pl.multiple_of(part * unit, unit)
        out_ref[j - 1, half:, :] = shrink_ref[pl.ds(start, unit), :]


def mixer_kernel(sizes, idx, *refs):
    uly, dp = sizes
    pieces, (m_ref, turn_ref) = refs[:-2], refs[-2:]
    lines = pieces[0].shape[0] // dp
    b, u, z = idx[0], idx[1], idx[2]
    shard = 2 * uly * lines
    for k in range(dp):
        for p, ref in enumerate(pieces):
            part = (b * uly + u) ^ p
            turn_ref[pl.ds(pl.multiple_of(part * lines, 8), lines), :] = ref[
                k * lines : (k + 1) * lines, :
            ].astype(F32)
        start = pl.multiple_of((z ^ k) * shard, shard)
        m_ref[pl.ds(start, shard), :] = turn_ref[...].astype(BF16)


def load_parts(pieces, z, e_ref, s_ref, sem, act, only=None):
    dp, unit, width = s_ref.shape[1:]
    shard = width // dp
    half = shard // 2
    block = dp * unit
    for j, row in enumerate(pieces):
        if only is not None and j != only:
            continue
        for k, piece in enumerate(row):
            for h in range(2):
                start = pl.multiple_of((z ^ k) * shard + h * half, half)
                act(
                    pltpu.make_async_copy(
                        piece.at[pl.ds(0, half), pl.ds(h * block, block)],
                        e_ref.at[j, pl.ds(start, half), :],
                        sem.at[j, 3 * k + h],
                    )
                )
            act(
                pltpu.make_async_copy(
                    piece.at[pl.ds(half, unit), :], s_ref.at[j, z ^ k], sem.at[j, 3 * k + 2]
                )
            )


def by_part(uly, dp, refs):
    own, rest, *far = refs
    return [
        [own if j == 0 else rest.at[j - 1]] + [far[(k - 1) * uly + j] for k in range(1, dp)]
        for j in range(uly)
    ]


def weights_ready(pieces, z, e_ref, s_ref, sem):
    step = pl.program_id(0)

    @pl.when(step == 0)
    def _():
        load_parts(pieces, z, e_ref, s_ref, sem, lambda copy: copy.start())

    for j in range(len(pieces)):

        @pl.when(step == j)
        def _(j=j):
            load_parts(pieces, z, e_ref, s_ref, sem, lambda copy: copy.wait(), j)


def feed_forward_kernel(uly, idx, mine_ref, other_ref, eb_ref, *refs):
    act_ref, slope_ref, y_ref, send_ref, acc_ref, x_ref, e_ref, s_ref, sem = refs[-9:]
    step = pl.program_id(0)
    dp, unit, width = s_ref.shape[1:]
    rows = mine_ref.shape[0]
    weights_ready(by_part(uly, dp, refs[:-9]), idx[2], e_ref, s_ref, sem)

    @pl.when(step == 0)
    def _():
        x_ref[:rows] = mine_ref[...]
        x_ref[rows:] = other_ref[...]
        acc_ref[...] = jnp.zeros_like(acc_ref)

    pre = dot_nn(x_ref[...], e_ref[step]) + eb_ref[pl.ds(step, 1), :]
    cdf = 0.5 * (1.0 + lax.erf(pre * 0.7071067811865476))
    pdf = jnp.exp(-0.5 * pre * pre) * 0.3989422804014327
    act = (pre * cdf).astype(BF16)
    act_ref[0] = act
    slope_ref[0] = (cdf + pre * pdf).astype(BF16)
    acc_ref[...] += dot_nn(act, s_ref[step].reshape(dp * unit, width))

    @pl.when(step == uly - 1)
    def _():
        y_ref[...] = acc_ref[:rows]
        send_ref[...] = acc_ref[rows:].astype(BF16)


def weight_scratch(uly, dp, unit, width):
    return [
        pltpu.VMEM((uly, width, dp * unit), BF16),
        pltpu.VMEM((uly, dp, unit, width), BF16),
        pltpu.SemaphoreType.DMA((uly, 3 * dp)),
    ]


def feed_forward(scalars, sizes, mine, other, eb, weights):
    uly, dp, unit = sizes
    rows, width = mine.shape
    block = dp * unit
    hbm = pl.BlockSpec(memory_space=pl.ANY)
    return call(
        functools.partial(feed_forward_kernel, uly),
        "feed_forward",
        scalars,
        [mine, other, eb, *weights],
        [whole(mine.shape), whole(mine.shape), whole(eb.shape)] + [hbm] * len(weights),
        [
            jax.ShapeDtypeStruct((uly, 2 * rows, block), BF16),
            jax.ShapeDtypeStruct((uly, 2 * rows, block), BF16),
            jax.ShapeDtypeStruct((rows, width), F32),
            jax.ShapeDtypeStruct((rows, width), BF16),
        ],
        [
            pl.BlockSpec((1, 2 * rows, block), lambda k, _: (k, 0, 0)),
            pl.BlockSpec((1, 2 * rows, block), lambda k, _: (k, 0, 0)),
            whole((rows, width)),
            whole((rows, width)),
        ],
        [pltpu.VMEM((2 * rows, width), F32), pltpu.VMEM((2 * rows, width), BF16)]
        + weight_scratch(uly, dp, unit, width),
        (uly,),
        8 * rows * width * uly * block,
        16,
    )


def final_norm_kernel(idx, x1_ref, y_ref, got_ref, vec_ref, cot_ref, *refs):
    mixed_ref, dh_ref, low_ref, sums_ref = refs
    hidden = x1_ref[...] + (y_ref[...] + got_ref[...].astype(F32) + vec_ref[5:6, :])
    gain = vec_ref[6:7, :]
    center = hidden - jnp.mean(hidden, -1, keepdims=True)
    inverse = lax.rsqrt(jnp.mean(center * center, -1, keepdims=True) + EPSILON)
    normed = center * inverse
    mixed_ref[...] = (normed * gain + vec_ref[7:8, :]).astype(BF16)
    grad = cot_ref[...].astype(F32)
    scaled = grad * gain
    dhidden = inverse * (
        scaled
        - jnp.mean(scaled, -1, keepdims=True)
        - normed * jnp.mean(scaled * normed, -1, keepdims=True)
    )
    dh_ref[...] = dhidden
    low_ref[...] = dhidden.astype(BF16)
    sums_ref[...] = jnp.zeros_like(sums_ref)
    sums_ref[0:1, :] = jnp.sum(dhidden, 0, keepdims=True)
    sums_ref[1:2, :] = jnp.sum(grad * normed, 0, keepdims=True)
    sums_ref[2:3, :] = jnp.sum(grad, 0, keepdims=True)


def store_halves(step, uly, value, z, dp, near_x, far_x, near_y, far_y):
    rows = value.shape[0] // dp
    place = [pl.multiple_of(((z ^ k) >> 1) * rows, rows) for k in range(dp)]
    for odd, near, far, close in (
        (0, near_x, far_x, step % 2 == 0),
        (1, near_y, far_y, step < uly // 2),
    ):
        for ref, wanted in ((near, close), (far, jnp.logical_not(close))):
            for k in range(dp):

                @pl.when(wanted & (((z ^ k) & 1) == odd))
                def _(ref=ref, k=k):
                    ref[0, pl.ds(place[k], rows), :] = value[k * rows : (k + 1) * rows]


def half_specs(uly, rows, cols):
    shape = jax.ShapeDtypeStruct((uly // 2, rows, cols), BF16)
    block = (1, rows, cols)
    return [shape] * 4, [
        pl.BlockSpec(block, lambda k, _: (k // 2, 0, 0)),
        pl.BlockSpec(block, lambda k, _: (k // 2, 0, 0)),
        pl.BlockSpec(block, lambda k, _: (jnp.minimum(k, 1), 0, 0)),
        pl.BlockSpec(block, lambda k, _: (jnp.maximum(k - 2, 0), 0, 0)),
    ]


def shrink_grad_kernel(sizes, idx, d_mine, d_other, act_ref, *refs):
    uly, dp = sizes
    out_refs, d_ref = refs[:-1], refs[-1]
    step = pl.program_id(0)
    rows = d_mine.shape[0]

    @pl.when(step == 0)
    def _():
        d_ref[:rows] = d_mine[...]
        d_ref[rows:] = d_other[...]

    value = dot_tn(act_ref[0], d_ref[...]).astype(BF16)
    store_halves(step, uly, value, idx[2], dp, *out_refs)


def shrink_grad(scalars, sizes, ds, act):
    uly, dp, unit = sizes
    rows, width = ds[0].shape
    block = dp * unit
    shapes, specs = half_specs(uly, block // 2, width)
    return call(
        functools.partial(shrink_grad_kernel, (uly, dp)),
        "shrink_grad",
        scalars,
        [*ds, act],
        [whole((rows, width))] * 2 + [pl.BlockSpec((1, 2 * rows, block), lambda k, _: (k, 0, 0))],
        shapes,
        specs,
        [pltpu.VMEM((2 * rows, width), BF16)],
        (uly,),
        4 * rows * width * uly * block,
        16,
    )


def feed_backward_kernel(uly, idx, x_mine, x_other, d_mine, d_other, slope_ref, *refs):
    half_refs, (deb_ref, dx_ref, send_ref) = refs[-14:-10], refs[-10:-7]
    acc_ref, xt_ref, d_ref, turn_ref, e_ref, s_ref, sem = refs[-7:]
    step = pl.program_id(0)
    dp, unit, width = s_ref.shape[1:]
    rows = x_mine.shape[0]
    weights_ready(by_part(uly, dp, refs[:-14]), idx[2], e_ref, s_ref, sem)

    @pl.when(step == 0)
    def _():
        xt_ref[:, :rows] = x_mine[...].T
        xt_ref[:, rows:] = x_other[...].T
        d_ref[:rows] = d_mine[...]
        d_ref[rows:] = d_other[...]
        acc_ref[...] = jnp.zeros_like(acc_ref)

    dpre = dot_nt(d_ref[...], s_ref[step].reshape(dp * unit, width))
    dpre = (dpre * slope_ref[0].astype(F32)).astype(BF16)
    deb_ref[0] = jnp.sum(dpre.astype(F32), 0, keepdims=True)
    dexpand = dot_nn(xt_ref[...], dpre).astype(BF16)
    store_halves(step, uly, dexpand, idx[2], dp, *half_refs)
    acc_ref[...] += dot_nt(dpre, e_ref[step])

    @pl.when(step == uly - 1)
    def _():
        dx_ref[...] = acc_ref[:rows]
        send_ref[...] = acc_ref[rows:].astype(BF16)


def feed_backward(scalars, sizes, xs, ds, slope, weights):
    uly, dp, unit = sizes
    rows, width = xs[0].shape
    block = dp * unit
    hbm = pl.BlockSpec(memory_space=pl.ANY)
    shapes, specs = half_specs(uly, width // 2, block)
    return call(
        functools.partial(feed_backward_kernel, uly),
        "feed_backward",
        scalars,
        [*xs, *ds, slope, *weights],
        [whole((rows, width))] * 4
        + [pl.BlockSpec((1, 2 * rows, block), lambda k, _: (k, 0, 0))]
        + [hbm] * len(weights),
        shapes
        + [
            jax.ShapeDtypeStruct((uly, 1, block), F32),
            jax.ShapeDtypeStruct((rows, width), F32),
            jax.ShapeDtypeStruct((rows, width), BF16),
        ],
        specs
        + [
            pl.BlockSpec((1, 1, block), lambda k, _: (k, 0, 0)),
            whole((rows, width)),
            whole((rows, width)),
        ],
        [
            pltpu.VMEM((2 * rows, width), F32),
            pltpu.VMEM((width, 2 * rows), BF16),
            pltpu.VMEM((2 * rows, width), BF16),
            pltpu.VMEM((16, 128), BF16),
        ]
        + weight_scratch(uly, dp, unit, width),
        (uly,),
        12 * rows * width * uly * block,
        16,
    )


def norm_backward_kernel(sizes, idx, dh2_ref, dx_ref, got_ref, normed_ref, inverse_ref, *refs):
    uly, dp, unit = sizes
    m_ref, vec_ref, grads_ref, deb_ref, *refs = refs
    o_refs, refs = refs[:uly], refs[uly:]
    dh_ref, *refs = refs
    do_refs, refs = refs[:uly], refs[uly:]
    keep_ref, send_ref, turn_ref = refs
    b, u, z = idx[0], idx[1], idx[2]
    group = o_refs[0].shape[1]
    share = group // 2
    width = dx_ref.shape[1]
    parts = 2 * uly
    grad = dh2_ref[...] + dx_ref[...] + got_ref[...].astype(F32)
    normed = normed_ref[...]
    scaled = grad * vec_ref[3:4, :]
    dhidden = inverse_ref[...] * (
        scaled
        - jnp.mean(scaled, -1, keepdims=True)
        - normed * jnp.mean(scaled * normed, -1, keepdims=True)
    )
    dh_ref[...] = dhidden
    low = dhidden.astype(BF16)
    for j in range(uly):
        start = pl.multiple_of((u ^ j) * group, group)
        do_refs[j][...] = dot_nt(low, m_ref[pl.ds(start, group), :]).astype(BF16)
    line = lax.broadcasted_iota(jnp.int32, (8, width), 0)
    lines = jnp.zeros((8, width), F32)
    values = [
        jnp.sum(dhidden, 0, keepdims=True),
        jnp.sum(grad * normed, 0, keepdims=True),
        jnp.sum(grad, 0, keepdims=True),
        grads_ref[0:1, :],
        grads_ref[1:2, :],
        grads_ref[2:3, :],
    ]
    for k, value in enumerate(values):
        lines = jnp.where(line == k, value, lines)
    lines = lines.astype(BF16)
    owner = (lax.broadcasted_iota(jnp.int32, (parts, uly), 1) ^ u) + b * uly
    order = lax.broadcasted_iota(jnp.int32, (parts, uly), 0)
    order = jnp.where(order == owner, 1.0, 0.0).astype(BF16)
    ebs = dot_nn(order, deb_ref[...].astype(BF16)).astype(BF16)
    for j in range(uly):
        turn_ref[...] = dot_tn(o_refs[j][...], low).astype(BF16)
        place = slot(u ^ j ^ z)
        keep_ref[place, :share] = turn_ref[pl.ds(pl.multiple_of(b * share, share), share), :]
        send_ref[place, :share] = turn_ref[pl.ds(pl.multiple_of((1 - b) * share, share), share), :]
    for k in range(dp):
        shard = (z ^ k) * group
        own = dot_nn(lines, one_hot(width, group, 0, shard)).astype(BF16)
        ebk = dot_nn(ebs, one_hot(dp * unit, unit, 0, (z ^ k) * unit)).astype(BF16)
        for ref in (keep_ref, send_ref):
            ref[slot(k), share:, :] = jnp.zeros_like(ref[slot(k), share:, :])
            ref[slot(k), share : share + 8, :group] = own
            ref[slot(k), share + 8 : share + 16, :unit] = ebk


def attend_grad_kernel(heads, blocks, pieces, started, q_ref, lse_ref, *refs):
    do_refs, refs = refs[:pieces], refs[pieces:]
    o_refs, refs = refs[:pieces], refs[pieces:]
    kv_refs, refs = refs[:blocks], refs[blocks:]
    so_far, refs = refs[: blocks * started], refs[blocks * started :]
    dq_ref, *refs = refs
    dkv_refs, refs = refs[:blocks], refs[blocks:]
    kt_ref, dout_ref, prod_ref, *refs = refs
    dk_accs, dv_accs = refs[:blocks], refs[blocks:]
    group = heads * HD
    wide = q_ref.shape[1]
    rows = kv_refs[0].shape[0]

    @pl.when(pl.program_id(0) == 0)
    def _():
        for i in range(blocks):
            kt_ref[:, i * rows : (i + 1) * rows] = kv_refs[i][:, :group].T
            if started:
                dk_accs[i][...] = so_far[i][:, :wide].astype(F32) * LOG2E
                dv_accs[i][...] = so_far[i][:, wide : wide + group].astype(F32)
            else:
                dk_accs[i][...] = jnp.zeros_like(dk_accs[i])
                dv_accs[i][...] = jnp.zeros_like(dv_accs[i])

    for j in range(pieces):

        @pl.when(pl.program_id(0) == j)
        def _(j=j):
            dout_ref[...] = do_refs[j][...]
            prod_ref[...] = (do_refs[j][...].astype(F32) * o_refs[j][...].astype(F32)).T

    q = q_ref[...]
    dout = dout_ref[...]
    dqs = []
    for head in range(heads):
        q_head = jnp.where(head_lanes(wide, head, group), q, jnp.zeros_like(q))
        do_head = jnp.where(head_lanes(group, head), dout, jnp.zeros_like(dout))
        lse = lse_ref[head : head + 1, :]
        delta = jnp.sum(prod_ref[head * HD : (head + 1) * HD, :], axis=0, keepdims=True)
        acc = None
        for i in range(blocks):
            probs = jnp.exp2(dot_nt(kv_refs[i][:, :wide], q_head) - lse)
            dv_accs[i][...] += dot_nn(probs.astype(BF16), do_head)
            grads = dot_nt(kv_refs[i][:, wide : wide + group], do_head)
            grads = (probs * (grads - delta)).astype(BF16)
            dk_accs[i][...] += dot_nn(grads, q_head)
            part = dot_nn(
                kt_ref[head * HD : (head + 1) * HD, i * rows : (i + 1) * rows], grads
            )
            acc = part if acc is None else acc + part
        dqs.append(acc)
    dq_ref[...] = jnp.concatenate(dqs, axis=0).T.astype(BF16)

    @pl.when(pl.program_id(0) == pl.num_programs(0) - 1)
    def _():
        for i in range(blocks):
            dkv_refs[i][:, :group] = (dk_accs[i][:, :group] * LN2).astype(BF16)
            dkv_refs[i][:, group:wide] = jnp.zeros((rows, wide - group), BF16)
            dkv_refs[i][:, wide : wide + group] = dv_accs[i][...].astype(BF16)
            dkv_refs[i][:, wide + group :] = jnp.zeros((rows, wide - group), BF16)


def attend_grad(q, kvs, douts, outs, lse, heads, at, so_far):
    rows, wide = kvs[0].shape[0], q.shape[1]
    group = heads * HD
    blocks = len(kvs)
    pieces = len(douts)
    tile = douts[0].shape[0]
    keys = blocks * rows
    started = 1 if so_far else 0
    out = pl.pallas_call(
        functools.partial(attend_grad_kernel, heads, blocks, pieces, started),
        grid=(pieces,),
        in_specs=[
            pl.BlockSpec((tile, wide), lambda t: (t + at, 0)),
            pl.BlockSpec((8, tile), lambda t: (0, t + at)),
        ]
        + [whole((tile, group))] * (2 * pieces)
        + [whole(kvs[0].shape)] * (blocks + blocks * started),
        out_specs=[pl.BlockSpec((tile, group), lambda t: (t, 0))]
        + [whole(kvs[0].shape)] * blocks,
        out_shape=[jax.ShapeDtypeStruct((pieces * tile, group), BF16)]
        + [jax.ShapeDtypeStruct(kvs[0].shape, BF16)] * blocks,
        scratch_shapes=[
            pltpu.VMEM((group, keys), BF16),
            pltpu.VMEM((tile, group), BF16),
            pltpu.VMEM((group, tile), F32),
        ]
        + [pltpu.VMEM((rows, wide), F32)] * blocks
        + [pltpu.VMEM((rows, group), F32)] * blocks,
        compiler_params=pltpu.CompilerParams(vmem_limit_bytes=16 * 2**20),
        cost_estimate=pl.CostEstimate(
            flops=10 * heads * pieces * tile * keys * wide,
            transcendentals=heads * pieces * tile * keys,
            bytes_accessed=2 * rows * wide * 4 + 4 * keys * (wide + group),
        ),
        name="attend_grad",
    )(q, lse, *douts, *outs, *kvs, *so_far)
    return out[0], out[1:]


def project_grad_kernel(sizes, idx, *refs):
    uly, dp, group = sizes
    dq_refs, (own_ref, got_ref, *refs) = refs[:uly], refs[uly:]
    x_refs, refs = refs[:uly], refs[uly:]
    dproj_ref, keep_ref, send_ref = refs
    b, z = idx[0], idx[2]
    rows, width = x_refs[0].shape
    wide = own_ref.shape[1] // 2
    share = keep_ref.shape[1] - 16
    for k, ref in enumerate(dq_refs):
        here = slice(k * ref.shape[0], (k + 1) * ref.shape[0])
        dproj_ref[here, :group] = ref[...] * jnp.asarray(0.125, BF16)
    dproj_ref[:, group:wide] = jnp.zeros((uly * rows, wide - group), BF16)
    dproj_ref[:, wide:] = (own_ref[...].astype(F32) + got_ref[...].astype(F32)).astype(BF16)
    sums = jnp.sum(dproj_ref[...].astype(F32), 0, keepdims=True).astype(BF16)
    grad = None
    for j in range(uly):
        part = dot_tn(x_refs[j][...], dproj_ref[j * rows : (j + 1) * rows, :])
        grad = part if grad is None else grad + part
    grad = grad.astype(BF16)
    for ref, mine in ((keep_ref, True), (send_ref, False)):
        for c in range(3):
            lanes = slice(c * wide, c * wide + group)
            into = slice(c * group, (c + 1) * group)
            for s in range(dp):
                for core in range(2):
                    start = (s * 2 + core) * share

                    @pl.when((b == core) == mine)
                    def _(start=start, s=s, ref=ref, lanes=lanes, into=into):
                        ref[slot(s ^ z), :share, into] = grad[start : start + share, lanes]

                ref[s, share:, into] = jnp.broadcast_to(sums[:, lanes], (16, group))


def token_grad_kernel(uly, idx, dproj_ref, w_ref, dh_ref, *out_refs):
    rows = dh_ref.shape[0]
    for j in reversed(range(uly)):
        part = dot_nt(dproj_ref[j * rows : (j + 1) * rows, :], w_ref[...])
        if j == 0:
            part = part + dh_ref[...]
        out_refs[j][...] = part.astype(out_refs[j].dtype)


def finish_shrink_kernel(idx, *refs):
    pieces, out_ref = refs[:-1], refs[-1]
    for p, ref in enumerate(pieces):

        @pl.when(pl.program_id(0) == p)
        def _(ref=ref):
            out_ref[...] = ref[...].astype(F32)


def finish_expand_kernel(sizes, idx, *refs):
    uly, dp, unit = sizes
    pieces, (out_ref, turn_ref) = refs[:-2], refs[-2:]
    width = turn_ref.shape[0]
    part = idx[0] * uly + idx[1]
    step = pl.program_id(0)

    @pl.when(step == 0)
    def _():
        col = lax.broadcasted_iota(jnp.int32, (width, width), 1)
        row = lax.broadcasted_iota(jnp.int32, (width, width), 0)
        source = col + ((col // unit) ^ part) * unit - (col // unit) * unit
        turn_ref[...] = jnp.where(row == source, 1.0, 0.0).astype(BF16)

    for k in range(dp):

        @pl.when(step == k)
        def _(k=k):
            line = jnp.concatenate([ref[:, k * unit : (k + 1) * unit] for ref in pieces], 1)
            out_ref[...] = dot_nn(line, turn_ref[...])


def finish_attend_kernel(uly, idx, *refs):
    mine, refs = refs[:uly], refs[uly:]
    other, refs = refs[:uly], refs[uly:]
    out_ref, bias_ref = refs
    b, u, z = idx[0], idx[1], idx[2]
    share = mine[0].shape[0] - 16
    group = mine[0].shape[1] // 3
    width = uly * group
    for group_refs, core in ((mine, b), (other, 1 - b)):
        start = pl.multiple_of(core * share, share)
        for c in range(3):
            acc = None
            for j in range(uly):
                put = one_hot(group, width, (u ^ j) * group, 0)
                value = dot_nn(group_refs[j][:share, c * group : (c + 1) * group], put)
                acc = value if acc is None else acc + value
            out_ref[pl.ds(start, share), c * width : (c + 1) * width] = acc
    bias = jnp.zeros((8, 3 * group), F32)
    for j in range(uly):
        lines = mine[j][share : share + 16, :].astype(F32)[:8]
        bias += jnp.where((u ^ j) == z, 1.0, 0.0) * lines
    bias_ref[...] = bias


def on_device(*args):
    (
        tokens,
        lengths,
        cotangent,
        attend_weight,
        query_bias,
        value_bias,
        mixer_weight,
        mixer_bias,
        attn_gain,
        attn_shift,
        expand_weight,
        expand_bias,
        shrink_weight,
        shrink_bias,
        final_gain,
        final_shift,
    ) = args
    uly = lax.axis_size("uly")
    blk = lax.axis_size("blk")
    dp = lax.axis_size("dp")
    width = tokens.shape[-1]
    rows = tokens.shape[0] * tokens.shape[1]
    heads = HEADS // uly
    group = heads * HD
    wide = -(-(group + 1) // 128) * 128
    shard = attend_weight.shape[0]
    hidden = expand_weight.shape[1]
    parts = blk * uly
    unit = hidden // (parts * dp)
    share = shard // blk
    if not (blk == 2 and uly == 4 and dp == 4 and shard == group and unit * 2 == shard and share % 16 == 0):
        return general_device(*args)
    u = lax.axis_index("uly")
    b = lax.axis_index("blk")
    z = lax.axis_index("dp")
    mixer_rows = share // dp
    feed_rows = shard // 2 + unit
    block_rows = uly * rows
    cols = 3 * wide

    x = tokens.reshape(rows, width)
    xs = [x, swap_with(x, "uly", 1), swap_with(x, "uly", 2)]
    xs.append(swap_with(after(x, *xs[1:]), "uly", 3))
    scalars = jnp.stack([b, u, z, lengths[0]]).astype(jnp.int32)
    vectors = [query_bias, value_bias, mixer_bias, attn_gain, attn_shift, shrink_bias]
    vectors += [final_gain, final_shift, expand_bias]
    first, feed = call(
        functools.partial(fetch_kernel, (uly, dp, group, unit)),
        "fetch",
        scalars,
        [
            attend_weight.reshape(blk, share, 3 * width),
            expand_weight,
            shrink_weight.reshape(parts, unit, width),
            mixer_weight,
            *vectors,
        ],
        [
            pl.BlockSpec((1, share, 3 * width), lambda t, s: (s[0], 0, 0)),
            whole(expand_weight.shape),
            pl.BlockSpec((1, unit, width), lambda t, s: (s[0] * uly + s[1], 0, 0)),
            whole(mixer_weight.shape),
            *[whole(vector.shape) for vector in vectors],
        ],
        [
            jax.ShapeDtypeStruct((share + 16, width), BF16),
            jax.ShapeDtypeStruct((feed_rows, width), BF16),
        ],
        [whole((share + 16, width)), whole((feed_rows, width))],
        [],
        (1,),
        10**9,
        58,
    )
    feeds = [None, swap_with(feed, "dp", 1)]
    mine = [first, None, swap_with(first, "dp", 2), swap_with(first, "dp", 3)]
    mine[1] = swap_with(after(first, *xs[1:3]), "dp", 1)
    feeds.append(swap_with(after(feed, *mine[1:]), "dp", 2))
    other = [swap_with(piece, "blk", 1) for piece in mine]
    rest = call(
        functools.partial(rest_kernel, (uly, dp, unit)),
        "fetch_rest",
        scalars,
        [expand_weight, shrink_weight],
        [whole(expand_weight.shape), whole(shrink_weight.shape)],
        jax.ShapeDtypeStruct((uly - 1, shard // 2 + unit, width), BF16),
        whole((uly - 1, shard // 2 + unit, width)),
        [],
        (1,),
        10**9,
        16,
    )

    w_own, q, kv, vec, eb, mixer_mine = call(
        functools.partial(project_kernel, (uly, blk, dp, group, unit)),
        "project",
        scalars,
        [*after(xs, feeds[1]), *mine, *other],
        [whole((rows, width))] * uly + [whole(first.shape)] * (2 * dp),
        [
            jax.ShapeDtypeStruct((width, cols), BF16),
            jax.ShapeDtypeStruct((block_rows, wide), BF16),
            jax.ShapeDtypeStruct((block_rows, 2 * wide), BF16),
            jax.ShapeDtypeStruct((16, width), F32),
            jax.ShapeDtypeStruct((parts, dp * unit), F32),
            jax.ShapeDtypeStruct((dp * mixer_rows, width), BF16),
        ],
        [
            whole((width, cols)),
            whole((block_rows, wide)),
            whole((block_rows, 2 * wide)),
            whole((16, width)),
            whole((parts, dp * unit)),
            whole((dp * mixer_rows, width)),
        ],
        [],
        (1,),
        2 * block_rows * width * cols,
        16,
    )
    kvs = [kv, swap_with(kv, "blk", 1)]

    mixer_plane = [swap_with(mixer_mine, "uly", j) for j in range(1, uly)]
    plane_one = [swap_with(feeds[1], "uly", j) for j in range(1, uly)]
    outs, lse = attend(after(q, rest, *mixer_plane), kvs, heads, uly)
    o_cols = after(outs, *plane_one)
    o_cols = [o_cols[0]] + [swap_with(o_cols[j], "uly", j) for j in range(1, uly)]
    feeds.append(swap_with(after(feed, feeds[2], *plane_one), "dp", 3))
    plane_two = [swap_with(after(feeds[2], *o_cols[1:]), "uly", j) for j in range(1, uly)]
    mixer_parts = [mixer_mine, *mixer_plane]
    mixer_parts += [swap_with(piece, "blk", 1) for piece in mixer_parts]
    mixer_all = call(
        functools.partial(mixer_kernel, (uly, dp)),
        "mixer_weight",
        scalars,
        mixer_parts,
        [whole(mixer_mine.shape)] * parts,
        jax.ShapeDtypeStruct((width, width), BF16),
        whole((width, width)),
        [pltpu.VMEM((shard, width), F32)],
        (1,),
        10**6,
        16,
    )

    square = (rows, width)
    x1, x1b, normed, inverse = call(
        functools.partial(first_norm_kernel, uly),
        "first_norm",
        scalars,
        [x, *o_cols, mixer_all, vec],
        [whole(square)] + [whole((rows, group))] * uly + [whole((width, width)), whole(vec.shape)],
        [
            jax.ShapeDtypeStruct(square, F32),
            jax.ShapeDtypeStruct(square, BF16),
            jax.ShapeDtypeStruct(square, F32),
            jax.ShapeDtypeStruct((rows, 1), F32),
        ],
        [whole(square), whole(square), whole(square), whole((rows, 1))],
        [],
        (1,),
        2 * rows * width * width,
        16,
    )
    sizes = (uly, dp, unit)
    plane_three = [swap_with(after(feeds[3], *plane_two), "uly", j) for j in range(1, uly)]
    far = [feeds[1], *plane_one, feeds[2], *plane_two, feeds[3], *plane_three]
    weights = [feed, rest, *far]
    x1b_other = swap_with(x1b, "blk", 1)
    act, slope, y_own, y_send = feed_forward(scalars, sizes, x1b, x1b_other, eb, weights)
    mixed, dh2, dh2b, sums2 = call(
        final_norm_kernel,
        "final_norm",
        scalars,
        [x1, y_own, swap_with(y_send, "blk", 1), vec, cotangent.reshape(square)],
        [whole(square)] * 3 + [whole(vec.shape), whole(square)],
        [
            jax.ShapeDtypeStruct(square, BF16),
            jax.ShapeDtypeStruct(square, F32),
            jax.ShapeDtypeStruct(square, BF16),
            jax.ShapeDtypeStruct((8, width), F32),
        ],
        [whole(square)] * 3 + [whole((8, width))],
        [],
        (1,),
        10**6,
        16,
    )
    dh2b_other = swap_with(dh2b, "blk", 1)
    ds = [dh2b, dh2b_other]
    s_near_x, s_far_x, s_near_y, s_far_y = shrink_grad(scalars, sizes, ds, act)
    s_x = swap_with(s_far_x, "uly", 1)
    s_y = swap_with(s_far_y, "uly", 2)
    e_near_x, e_far_x, e_near_y, e_far_y, deb, dx_own, dx_send = feed_backward(
        scalars, sizes, [x1b, x1b_other], after(ds, s_far_x), slope, weights
    )
    block = (dp, share + 16, width)
    dh1, *rest_out = call(
        functools.partial(norm_backward_kernel, sizes),
        "norm_backward",
        scalars,
        [dh2, dx_own, swap_with(after(dx_send, s_x, s_y), "blk", 1), normed, inverse, mixer_all]
        + [vec, sums2]
        + [deb.reshape(uly, dp * unit), *o_cols],
        [whole(square)] * 4
        + [whole((rows, 1)), whole((width, width)), whole(vec.shape), whole(sums2.shape)]
        + [whole((uly, dp * unit))]
        + [whole((rows, group))] * uly,
        [jax.ShapeDtypeStruct(square, F32)]
        + [jax.ShapeDtypeStruct((rows, group), BF16)] * uly
        + [jax.ShapeDtypeStruct(block, BF16)] * 2,
        [whole(square)] + [whole((rows, group))] * uly + [whole(block)] * 2,
        [pltpu.VMEM((group, width), BF16)],
        (1,),
        4 * rows * width * width,
        16,
    )
    douts = [rest_out[0]] + [swap_with(rest_out[j], "uly", j) for j in range(1, uly)]
    m_keep, m_send = rest_out[uly:]

    def add(*values):
        return total(values).astype(BF16)

    def quarter(j, so_far, *deps):
        dout = after(douts[j], *deps)
        return attend_grad(q, kvs, [dout], [outs[j]], lse, heads, j, so_far)

    s_near_x, s_near_y, m_send = after((s_near_x, s_near_y, m_send), dh1)
    s_next_x = add(s_near_x[1], s_x[1])
    s_next_y = add(s_near_y[1], s_y[1])
    s_xy = swap_with(after(s_next_x, *douts[1:]), "uly", 2)
    s_yx = swap_with(after(s_next_y, *douts[1:]), "uly", 1)
    m_got = swap_with(after(m_send, *douts[1:]), "blk", 1)
    dq_0, dkvs = quarter(0, [], s_next_x, s_next_y, *douts[1:])

    s_xy, s_yx, m_got, e_far_x, e_far_y = after((s_xy, s_yx, m_got, e_far_x, e_far_y), dq_0)
    pair = (2, unit, width)
    s_near = add(s_near_x[0], s_x[0], s_xy).reshape(pair)
    s_far = add(s_near_y[0], s_y[0], s_yx).reshape(pair)
    m_near, m_far = add(m_keep[:2], m_got[:2]), add(m_keep[2:], m_got[2:])
    e_x = swap_with(e_far_x, "uly", 1)
    e_y = swap_with(e_far_y, "uly", 2)
    s_one = swap_with(s_far, "dp", 1)
    m_one = swap_with(m_far, "dp", 1)
    dq_1, dkvs = quarter(1, dkvs, s_near, s_far, m_near, m_far)

    dq_2, dkvs = quarter(2, dkvs)

    e_x, e_y, s_one, m_one = after((e_x, e_y, s_one, m_one), dq_2)
    e_next_x = add(e_near_x[1], e_x[1])
    e_next_y = add(e_near_y[1], e_y[1])
    e_xy = swap_with(e_next_x, "uly", 2)
    e_yx = swap_with(e_next_y, "uly", 1)
    s_next = add(s_near[1], s_one[1])
    m_next = add(m_near[1], m_one[1])
    s_two = swap_with(s_next, "dp", 2)
    m_two = swap_with(m_next, "dp", 2)
    dq_3, dkvs = quarter(3, dkvs, e_next_x, e_next_y, s_next, m_next)

    dkv_got = swap_with(after(dkvs[1], e_xy, e_yx, s_two, m_two), "blk", 1)
    e_xy, e_yx, s_two, m_two = after((e_xy, e_yx, s_two, m_two), dq_3)
    pair = (2, shard, dp * unit)
    e_near = add(e_near_x[0], e_x[0], e_xy).reshape(pair)
    e_far = add(e_near_y[0], e_y[0], e_yx).reshape(pair)
    e_one = swap_with(e_far, "dp", 1)
    s_own = add(s_near[0], s_one[0], s_two)
    m_own = add(m_near[0], m_one[0], m_two)
    s_plane = [s_own] + [swap_with(s_own, "uly", j) for j in range(1, uly)]
    dkv_got = after(dkv_got, e_near, e_far, s_own, m_own)
    dqs = [dq_0, dq_1, dq_2, dq_3]
    dproj, a_keep, a_send = call(
        functools.partial(project_grad_kernel, (uly, dp, group)),
        "project_grad",
        scalars,
        [*dqs, dkvs[0], dkv_got, *xs],
        [whole(dq_0.shape)] * uly + [whole(kv.shape)] * 2 + [whole(square)] * uly,
        [
            jax.ShapeDtypeStruct((block_rows, cols), BF16),
            jax.ShapeDtypeStruct((dp, share + 16, 3 * group), BF16),
            jax.ShapeDtypeStruct((dp, share + 16, 3 * group), BF16),
        ],
        [whole((block_rows, cols))] + [whole((dp, share + 16, 3 * group))] * 2,
        [],
        (1,),
        2 * block_rows * width * cols,
        16,
    )
    a_got = swap_with(after(a_send, *s_plane), "blk", 1)
    m_plane = [m_own] + [swap_with(after(m_own, *s_plane, dproj), "uly", j) for j in range(1, uly)]
    token_parts = call(
        functools.partial(token_grad_kernel, uly),
        "token_grad",
        scalars,
        [dproj, w_own, dh1],
        [whole((block_rows, cols)), whole((width, cols)), whole(square)],
        [jax.ShapeDtypeStruct(square, F32)] + [jax.ShapeDtypeStruct(square, BF16)] * (uly - 1),
        [whole(square)] * uly,
        [],
        (1,),
        2 * block_rows * width * cols,
        16,
    )

    def in_plane(own, *deps):
        own = after(own, *deps)
        return [own] + [swap_with(own, "uly", j) for j in range(1, uly)]

    def both_cores(pieces, *deps):
        return pieces + [swap_with(after(piece, *deps), "blk", 1) for piece in pieces]

    a_got, e_one = after((a_got, e_one), token_parts[0])
    a_near, a_far = add(a_keep[:2], a_got[:2]), add(a_keep[2:], a_got[2:])
    a_one = swap_with(a_far, "dp", 1)
    e_next = add(e_near[1], e_one[1])
    e_two = swap_with(e_next, "dp", 2)
    token_parts = after(token_parts, a_near, a_far, e_next, *m_plane)
    token_got = [swap_with(token_parts[j], "uly", j) for j in range(1, uly)]
    a_next = add(a_near[1], a_one[1])
    a_two = swap_with(a_next, "dp", 2)
    s_plane = both_cores(s_plane, a_near)
    shrink_out = call(
        finish_shrink_kernel,
        "finish_shrink",
        scalars,
        s_plane,
        [whole(s_own.shape)] * parts,
        jax.ShapeDtypeStruct((hidden // dp, width), F32),
        pl.BlockSpec((unit, width), lambda t, s: ((s[0] * uly + s[1]) ^ t, 0)),
        [],
        (parts,),
        10**6,
        16,
    )
    e_own = add(e_near[0], e_one[0], e_two)
    e_plane = in_plane(e_own, shrink_out, *token_got)
    tokens_grad = total([token_parts[0], *token_got])
    a_own = add(a_near[0], a_one[0], a_two)
    a_plane = in_plane(a_own, *token_got)
    e_plane = both_cores(e_plane)
    expand_out = call(
        functools.partial(finish_expand_kernel, sizes),
        "finish_expand",
        scalars,
        e_plane,
        [whole(e_own.shape)] * parts,
        jax.ShapeDtypeStruct((shard, hidden), F32),
        pl.BlockSpec((shard, width), lambda t, s: (0, t)),
        [pltpu.VMEM((width, width), BF16)],
        (dp,),
        10**9,
        16,
    )
    a_plane = both_cores(a_plane, expand_out)
    attend_out, biases = call(
        functools.partial(finish_attend_kernel, uly),
        "finish_attend",
        scalars,
        a_plane,
        [whole(a_own.shape)] * parts,
        [jax.ShapeDtypeStruct((shard, 3 * width), F32), jax.ShapeDtypeStruct((8, 3 * group), F32)],
        [whole((shard, 3 * width)), whole((8, 3 * group))],
        [],
        (1,),
        10**9,
        16,
    )
    m_all = [value.astype(F32) for value in m_plane]
    m_all = (m_all[0] + m_all[1]) + (m_all[2] + m_all[3])
    m_half = m_all[:share].astype(BF16)
    mixer_out = jnp.concatenate(xor_order([m_half, swap_with(m_half, "blk", 1)], b), 0)
    vecs = [m_all[share + k, :shard] for k in range(6)]
    eb_out = m_all[share + 8 : share + 8 + parts, :unit].reshape(-1)
    return (
        mixed.reshape(tokens.shape),
        tokens_grad.reshape(tokens.shape),
        attend_out,
        biases[0, :group],
        biases[0, 2 * group :],
        mixer_out.astype(F32),
        vecs[0],
        vecs[1],
        vecs[2],
        expand_out,
        eb_out,
        shrink_out,
        vecs[3],
        vecs[4],
        vecs[5],
    )


def solution(mesh):
    row_spec = P("dp", ("blk", "uly"), None)
    matrix = P("dp", None)
    vector = P("dp")
    return jax.shard_map(
        on_device,
        mesh=mesh,
        in_specs=(
            row_spec,
            vector,
            row_spec,
            matrix,
            vector,
            vector,
            matrix,
            vector,
            vector,
            vector,
            matrix,
            vector,
            matrix,
            vector,
            vector,
            vector,
        ),
        out_specs=(
            row_spec,
            row_spec,
            matrix,
            vector,
            vector,
            matrix,
            vector,
            vector,
            vector,
            matrix,
            vector,
            matrix,
            vector,
            vector,
            vector,
        ),
        check_vma=False,
    )
```

```python
import functools

import jax
import jax.numpy as jnp
from jax import lax
from jax.experimental import pallas as pl
from jax.experimental.pallas import tpu as pltpu
from jax.sharding import PartitionSpec as P

HEADS = 12
HD = 64

EPSILON = 1e-12
MASKED = -1000000000.0
LOG2E = 1.4426950408889634
LN2 = 0.6931471805599453
F32 = jnp.float32
BF16 = jnp.bfloat16


def dot_nn(left, right):
    return lax.dot_general(left, right, (((1,), (0,)), ((), ())), preferred_element_type=F32)


def dot_nt(left, right):
    return lax.dot_general(left, right, (((1,), (1,)), ((), ())), preferred_element_type=F32)


def dot_tn(left, right):
    return lax.dot_general(left, right, (((0,), (0,)), ((), ())), preferred_element_type=F32)


def swap_with(value, axis, offset):
    size = lax.axis_size(axis)
    return lax.ppermute(value, axis, [(i, i ^ offset) for i in range(size)])


def xor_order(pieces, index):
    bit = 1
    while bit < len(pieces):
        flag = (index & bit) != 0
        pieces = [jnp.where(flag, pieces[p ^ bit], pieces[p]) for p in range(len(pieces))]
        bit *= 2
    return pieces


def total(values):
    acc = values[0].astype(F32)
    for value in values[1:]:
        acc = acc + value.astype(F32)
    return acc


def pad_rows(value, rows):
    return jnp.pad(value, ((0, rows - value.shape[0]), (0, 0)))


def head_lanes(width, head, ones_lane=None):
    lane = lax.broadcasted_iota(jnp.int32, (1, width), 1)
    keep = (lane >= head * HD) & (lane < (head + 1) * HD)
    if ones_lane is not None:
        keep = keep | (lane == ones_lane)
    return keep


def attend_forward_kernel(heads, blocks, q_ref, *refs):
    kv_refs = refs[:blocks]
    o_ref, lse_ref, vt_ref = refs[blocks:]
    group = heads * HD
    wide = q_ref.shape[1]
    rows = kv_refs[0].shape[0]

    @pl.when(pl.program_id(0) == 0)
    def _():
        for i in range(blocks):
            vt_ref[:, i * rows : (i + 1) * rows] = kv_refs[i][:, wide : wide + group].T

    q = q_ref[...]
    outs = []
    stats = []
    for head in range(heads):
        q_head = jnp.where(head_lanes(wide, head, group), q, jnp.zeros_like(q))
        scores = [dot_nt(kv_refs[i][:, :wide], q_head) for i in range(blocks)]
        top = jnp.max(scores[0], axis=0, keepdims=True)
        for i in range(1, blocks):
            top = jnp.maximum(top, jnp.max(scores[i], axis=0, keepdims=True))
        norm = jnp.zeros_like(top)
        acc = None
        for i in range(blocks):
            probs = jnp.exp2(scores[i] - top)
            norm = norm + jnp.sum(probs, axis=0, keepdims=True)
            part = dot_nn(
                vt_ref[head * HD : (head + 1) * HD, i * rows : (i + 1) * rows], probs.astype(BF16)
            )
            acc = part if acc is None else acc + part
        outs.append(acc / norm)
        stats.append(top + jnp.log2(norm))
    o_ref[...] = jnp.concatenate(outs, axis=0).T.astype(BF16)
    for head in range(heads):
        lse_ref[head : head + 1, :] = stats[head]


def attend_forward(q, kvs, heads, tile):
    rows, wide = q.shape
    group = heads * HD
    blocks = len(kvs)
    keys = blocks * rows
    whole = pl.BlockSpec(kvs[0].shape, lambda t: (0, 0))
    return pl.pallas_call(
        functools.partial(attend_forward_kernel, heads, blocks),
        grid=(rows // tile,),
        in_specs=[pl.BlockSpec((tile, wide), lambda t: (t, 0))] + [whole] * blocks,
        out_specs=[
            pl.BlockSpec((tile, group), lambda t: (t, 0)),
            pl.BlockSpec((8, tile), lambda t: (0, t)),
        ],
        out_shape=[
            jax.ShapeDtypeStruct((rows, group), BF16),
            jax.ShapeDtypeStruct((8, rows), F32),
        ],
        scratch_shapes=[pltpu.VMEM((group, keys), BF16)],
        compiler_params=pltpu.CompilerParams(vmem_limit_bytes=56 * 2**20),
        cost_estimate=pl.CostEstimate(
            flops=4 * heads * rows * keys * wide,
            transcendentals=heads * rows * keys,
            bytes_accessed=2 * rows * wide * 3 + 2 * keys * (wide + group),
        ),
        name="attend_forward",
    )(q, *kvs)


def attend_backward_kernel(heads, blocks, q_ref, do_ref, o_ref, lse_ref, *refs):
    kv_refs = refs[:blocks]
    dq_ref = refs[blocks]
    dkv_refs = refs[blocks + 1 : 2 * blocks + 1]
    kt_ref = refs[2 * blocks + 1]
    dk_accs = refs[2 * blocks + 2 : 3 * blocks + 2]
    dv_accs = refs[3 * blocks + 2 :]
    group = heads * HD
    wide = q_ref.shape[1]
    rows = kv_refs[0].shape[0]

    @pl.when(pl.program_id(0) == 0)
    def _():
        for i in range(blocks):
            kt_ref[:, i * rows : (i + 1) * rows] = kv_refs[i][:, :group].T
            dk_accs[i][...] = jnp.zeros_like(dk_accs[i])
            dv_accs[i][...] = jnp.zeros_like(dv_accs[i])

    q = q_ref[...]
    dout = do_ref[...]
    products = (dout.astype(F32) * o_ref[...].astype(F32)).T
    dqs = []
    for head in range(heads):
        q_head = jnp.where(head_lanes(wide, head, group), q, jnp.zeros_like(q))
        do_head = jnp.where(head_lanes(group, head), dout, jnp.zeros_like(dout))
        lse = lse_ref[head : head + 1, :]
        delta = jnp.sum(products[head * HD : (head + 1) * HD], axis=0, keepdims=True)
        acc = None
        for i in range(blocks):
            probs = jnp.exp2(dot_nt(kv_refs[i][:, :wide], q_head) - lse)
            dv_accs[i][...] += dot_nn(probs.astype(BF16), do_head)
            grads = dot_nt(kv_refs[i][:, wide : wide + group], do_head)
            grads = (probs * (grads - delta)).astype(BF16)
            dk_accs[i][...] += dot_nn(grads, q_head)
            part = dot_nn(
                kt_ref[head * HD : (head + 1) * HD, i * rows : (i + 1) * rows], grads
            )
            acc = part if acc is None else acc + part
        dqs.append(acc)
    dq_ref[...] = jnp.concatenate(dqs, axis=0).T.astype(BF16)

    @pl.when(pl.program_id(0) == pl.num_programs(0) - 1)
    def _():
        for i in range(blocks):
            dkv_refs[i][:, :group] = (dk_accs[i][:, :group] * LN2).astype(BF16)
            dkv_refs[i][:, wide : wide + group] = dv_accs[i][...].astype(BF16)


def attend_backward(q, kvs, dout, o, lse, heads, tile):
    rows, wide = q.shape
    group = heads * HD
    blocks = len(kvs)
    keys = blocks * rows
    whole = pl.BlockSpec(kvs[0].shape, lambda t: (0, 0))
    out = pl.pallas_call(
        functools.partial(attend_backward_kernel, heads, blocks),
        grid=(rows // tile,),
        in_specs=[
            pl.BlockSpec((tile, wide), lambda t: (t, 0)),
            pl.BlockSpec((tile, group), lambda t: (t, 0)),
            pl.BlockSpec((tile, group), lambda t: (t, 0)),
            pl.BlockSpec((8, tile), lambda t: (0, t)),
        ]
        + [whole] * blocks,
        out_specs=[pl.BlockSpec((tile, group), lambda t: (t, 0))] + [whole] * blocks,
        out_shape=[jax.ShapeDtypeStruct((rows, group), BF16)]
        + [jax.ShapeDtypeStruct(kvs[0].shape, BF16)] * blocks,
        scratch_shapes=[pltpu.VMEM((group, keys), BF16)]
        + [pltpu.VMEM((rows, wide), F32)] * blocks
        + [pltpu.VMEM((rows, group), F32)] * blocks,
        compiler_params=pltpu.CompilerParams(vmem_limit_bytes=56 * 2**20),
        cost_estimate=pl.CostEstimate(
            flops=10 * heads * rows * keys * wide,
            transcendentals=heads * rows * keys,
            bytes_accessed=2 * rows * wide * 4 + 4 * keys * (wide + group),
        ),
        name="attend_backward",
    )(q, dout, o, lse, *kvs)
    return out[0], out[1:]


def feed_kernel(
    x1_ref,
    x1b_ref,
    expand_ref,
    shrink_ref,
    ebias_ref,
    sbias_ref,
    gain_ref,
    shift_ref,
    cot_ref,
    mixed_ref,
    dx1_ref,
    dexpand_ref,
    dshrink_ref,
    debias_ref,
    vec_ref,
    act_ref,
    slope_ref,
    acc_ref,
    d2b_ref,
    x1t_ref,
):
    phase = pl.program_id(0)
    step = pl.program_id(1)
    last = pl.num_programs(1) - 1
    width = x1_ref.shape[1]

    @pl.when(phase == 0)
    def _():
        pre = dot_nn(x1b_ref[...], expand_ref[0]) + ebias_ref[0]
        cdf = 0.5 * (1.0 + lax.erf(pre * 0.7071067811865476))
        pdf = jnp.exp(-0.5 * pre * pre) * 0.3989422804014327
        act = (pre * cdf).astype(BF16)
        act_ref[step] = act
        slope_ref[step] = (cdf + pre * pdf).astype(BF16)
        part = dot_nn(act, shrink_ref[0])

        @pl.when(step == 0)
        def _():
            acc_ref[...] = part
            x1t_ref[...] = x1b_ref[...].T

        @pl.when(step > 0)
        def _():
            acc_ref[...] += part

        @pl.when(step == last)
        def _():
            hidden = x1_ref[...] + (acc_ref[...] + sbias_ref[...])
            center = hidden - jnp.mean(hidden, -1, keepdims=True)
            inverse = lax.rsqrt(jnp.mean(center * center, -1, keepdims=True) + EPSILON)
            normed = center * inverse
            mixed_ref[...] = (normed * gain_ref[...] + shift_ref[...]).astype(BF16)
            grad = cot_ref[...].astype(F32)
            scaled = grad * gain_ref[...]
            dhidden = inverse * (
                scaled
                - jnp.mean(scaled, -1, keepdims=True)
                - normed * jnp.mean(scaled * normed, -1, keepdims=True)
            )
            acc_ref[...] = dhidden
            d2b_ref[...] = dhidden.astype(BF16)
            vec_ref[...] = jnp.zeros_like(vec_ref)
            vec_ref[0:1, :] = jnp.sum(grad * normed, 0, keepdims=True)
            vec_ref[1:2, :] = jnp.sum(grad, 0, keepdims=True)
            vec_ref[2:3, :] = jnp.sum(dhidden, 0, keepdims=True)

    @pl.when(phase == 1)
    def _():
        d2b = d2b_ref[...]
        dpre = (dot_nt(d2b, shrink_ref[0]) * slope_ref[step].astype(F32)).astype(BF16)
        debias_ref[0] = jnp.sum(dpre.astype(F32), 0, keepdims=True)
        dexpand_ref[0] = dot_nn(x1t_ref[...], dpre).astype(BF16)
        dshrink_ref[0] = dot_tn(act_ref[step], d2b).astype(BF16)
        acc_ref[...] += dot_nt(dpre, expand_ref[0])

        @pl.when(step == last)
        def _():
            dx1_ref[...] = acc_ref[...]


def feed_forward_backward(x1, x1b, expand, shrink, ebias, sbias, gain, shift, cot):
    rows, width = x1.shape
    parts, _, block = expand.shape
    full = pl.BlockSpec((rows, width), lambda p, k: (0, 0))
    line = pl.BlockSpec((1, width), lambda p, k: (0, 0))
    return pl.pallas_call(
        feed_kernel,
        grid=(2, parts),
        in_specs=[
            full,
            full,
            pl.BlockSpec((1, width, block), lambda p, k: (k, 0, 0)),
            pl.BlockSpec((1, block, width), lambda p, k: (k, 0, 0)),
            pl.BlockSpec((1, 1, block), lambda p, k: (k, 0, 0)),
            line,
            line,
            line,
            full,
        ],
        out_specs=[
            full,
            full,
            pl.BlockSpec((1, width, block), lambda p, k: (p * k, 0, 0)),
            pl.BlockSpec((1, block, width), lambda p, k: (p * k, 0, 0)),
            pl.BlockSpec((1, 1, block), lambda p, k: (p * k, 0, 0)),
            pl.BlockSpec((8, width), lambda p, k: (0, 0)),
        ],
        out_shape=[
            jax.ShapeDtypeStruct((rows, width), BF16),
            jax.ShapeDtypeStruct((rows, width), F32),
            jax.ShapeDtypeStruct((parts, width, block), BF16),
            jax.ShapeDtypeStruct((parts, block, width), BF16),
            jax.ShapeDtypeStruct((parts, 1, block), F32),
            jax.ShapeDtypeStruct((8, width), F32),
        ],
        scratch_shapes=[
            pltpu.VMEM((parts, rows, block), BF16),
            pltpu.VMEM((parts, rows, block), BF16),
            pltpu.VMEM((rows, width), F32),
            pltpu.VMEM((rows, width), BF16),
            pltpu.VMEM((width, rows), BF16),
        ],
        compiler_params=pltpu.CompilerParams(vmem_limit_bytes=48 * 2**20),
        cost_estimate=pl.CostEstimate(
            flops=12 * rows * width * parts * block,
            transcendentals=2 * rows * parts * block,
            bytes_accessed=12 * width * parts * block,
        ),
        name="feed_forward_backward",
    )(x1, x1b, expand, shrink, ebias, sbias, gain, shift, cot)


def general_device(
    tokens,
    lengths,
    cotangent,
    attend_weight,
    query_bias,
    value_bias,
    mixer_weight,
    mixer_bias,
    attn_gain,
    attn_shift,
    expand_weight,
    expand_bias,
    shrink_weight,
    shrink_bias,
    final_gain,
    final_shift,
):
    uly = lax.axis_size("uly")
    blk = lax.axis_size("blk")
    dp = lax.axis_size("dp")
    u = lax.axis_index("uly")
    b = lax.axis_index("blk")
    z = lax.axis_index("dp")
    width = tokens.shape[-1]
    rows = tokens.shape[0] * tokens.shape[1]
    block_rows = uly * rows
    heads = HEADS // uly
    group = heads * HD
    wide = -(-(group + 1) // 128) * 128
    shard = attend_weight.shape[0]
    hidden = expand_weight.shape[1]
    parts = blk * uly
    unit = hidden // (parts * dp)
    share = shard // blk

    x = tokens.reshape(rows, width)
    x_rows = jnp.concatenate([x] + [swap_with(x, "uly", j) for j in range(1, uly)], 0)

    small = jnp.concatenate(
        [query_bias, value_bias, mixer_bias, attn_gain, attn_shift, shrink_bias]
        + [final_gain, final_shift, expand_bias]
    )
    small_rows = small.shape[0] // (3 * group)
    own_heads = lax.dynamic_slice_in_dim(attend_weight.reshape(shard, 3, uly, group), u, 1, 2)
    own_heads = own_heads.reshape(shard, 3 * group)
    first_piece = jnp.concatenate(
        [
            lax.dynamic_slice_in_dim(own_heads, b * share, share, 0),
            pad_rows(small.reshape(small_rows, 3 * group), 16),
        ]
    )
    first_all = lax.all_gather(first_piece, "dp", axis=0, tiled=False)
    halves = first_all[:, :share]
    halves = xor_order([halves] + [swap_with(halves, "blk", i) for i in range(1, blk)], b)
    attend_own = jnp.stack(halves, 1).reshape(width, 3, group)
    vectors = first_all[:, share : share + small_rows].reshape(dp, -1, shard).astype(F32)
    names = [vectors[:, k].reshape(width) for k in range(8)]
    bias_query, bias_value, bias_mixer, gain_attn, shift_attn, bias_shrink = names[:6]
    gain_final, shift_final = names[6:]
    bias_expand = vectors[:, 8:].reshape(dp, parts, unit).transpose(1, 0, 2)
    bias_expand = jnp.stack(
        xor_order(list(bias_expand.reshape(parts, dp * unit)), b * uly + u), 0
    ).reshape(parts, 1, dp * unit)

    mixer_own = lax.dynamic_slice_in_dim(mixer_weight, b * share, share, 0)
    mixer_all = jnp.stack(
        xor_order([mixer_own] + [swap_with(mixer_own, "dp", j) for j in range(1, dp)], z), 0
    )
    mixer_all = jnp.stack(
        xor_order([mixer_all] + [swap_with(mixer_all, "blk", i) for i in range(1, blk)], b), 1
    ).reshape(width, width)

    part = b * uly + u
    expand_own = lax.dynamic_slice_in_dim(
        expand_weight.reshape(shard, dp, parts, unit), part, 1, 2
    ).reshape(-1, width)
    shrink_own = lax.dynamic_slice_in_dim(shrink_weight.reshape(parts, unit, width), part, 1, 0)
    expand_rows = expand_own.shape[0]
    feed_own = jnp.concatenate([expand_own, shrink_own.reshape(unit, width)], 0)
    feed_all = lax.all_gather(feed_own, "dp", axis=0, tiled=False)
    expand_part = feed_all[:, :expand_rows].reshape(width, dp * unit)
    shrink_part = feed_all[:, expand_rows:].reshape(dp * unit, width)
    expand_two = jnp.stack([expand_part, swap_with(expand_part, "uly", 1)])
    shrink_two = jnp.stack([shrink_part, swap_with(shrink_part, "uly", 2)])
    expand_far = swap_with(expand_two, "uly", 2)
    shrink_far = swap_with(shrink_two, "uly", 1)
    expand_here = jnp.concatenate([expand_two, expand_far], 0)
    shrink_here = jnp.stack([shrink_two[0], shrink_far[0], shrink_two[1], shrink_far[1]], 0)
    expand_full = jnp.concatenate(
        [expand_here] + [swap_with(expand_here, "blk", i) for i in range(1, blk)], 0
    )
    shrink_full = jnp.concatenate(
        [shrink_here] + [swap_with(shrink_here, "blk", i) for i in range(1, blk)], 0
    )

    lane_pad = ((0, 0), (0, wide - group))
    bias_row = jnp.pad(lax.dynamic_slice_in_dim(bias_query, u * group, group, 0), lane_pad[1:])
    ones_lane = (jnp.arange(wide) == group).astype(F32)
    q = dot_nn(x_rows, jnp.pad(attend_own[:, 0], lane_pad)) + bias_row
    q = (q * (0.125 * LOG2E) + ones_lane).astype(BF16)
    kv_weight = jnp.concatenate([jnp.pad(attend_own[:, 1], lane_pad), attend_own[:, 2]], 1)
    kv_bias = jnp.concatenate(
        [jnp.zeros((wide,), F32), lax.dynamic_slice_in_dim(bias_value, u * group, group, 0)]
    )
    kv_ones = jnp.pad(ones_lane, (0, group))
    row_index = jnp.arange(block_rows, dtype=jnp.int32)
    positions = b * block_rows + ((row_index // rows) ^ u) * rows + row_index % rows
    key_mask = jnp.where(positions < lengths[0], 0.0, MASKED)
    kv = (dot_nn(x_rows, kv_weight) + kv_bias + key_mask[:, None] * kv_ones).astype(BF16)
    kvs = [kv] + [swap_with(kv, "blk", i) for i in range(1, blk)]

    o_rows, lse = attend_forward(q, kvs, heads, min(256, block_rows))
    pieces = [o_rows[j * rows : (j + 1) * rows] for j in range(uly)]
    pieces = [pieces[0]] + [swap_with(pieces[j], "uly", j) for j in range(1, uly)]
    mixer_in = jnp.concatenate(xor_order(pieces, u), 1)

    first_sum = x.astype(F32) + (dot_nn(mixer_in, mixer_all) + bias_mixer)
    center = first_sum - jnp.mean(first_sum, -1, keepdims=True)
    first_inv = lax.rsqrt(jnp.mean(center * center, -1, keepdims=True) + EPSILON)
    first_normed = center * first_inv
    first_out = first_normed * gain_attn + shift_attn
    first_low = first_out.astype(BF16)

    mixed, first_grad, expand_grad, shrink_grad, expand_bias_grad, vec_grads = (
        feed_forward_backward(
            first_out,
            first_low,
            expand_full,
            shrink_full,
            bias_expand,
            bias_shrink[None],
            gain_final[None],
            shift_final[None],
            cotangent.reshape(rows, width),
        )
    )

    scaled = first_grad * gain_attn
    attn_grad = first_inv * (
        scaled
        - jnp.mean(scaled, -1, keepdims=True)
        - first_normed * jnp.mean(scaled * first_normed, -1, keepdims=True)
    )
    attn_low = attn_grad.astype(BF16)
    out_grad = dot_nt(attn_low, mixer_all).astype(BF16)
    sends = xor_order([out_grad[:, j * group : (j + 1) * group] for j in range(uly)], u)
    dout_rows = jnp.concatenate(
        [sends[0]] + [swap_with(sends[j], "uly", j) for j in range(1, uly)], 0
    )
    dq, dkvs = attend_backward(q, kvs, dout_rows, o_rows, lse, heads, min(256, block_rows))

    mixer_grad = dot_tn(mixer_in, attn_low).astype(BF16)
    attn_gain_grad = jnp.sum(first_grad * first_normed, 0)
    attn_shift_grad = jnp.sum(first_grad, 0)
    mixer_bias_grad = jnp.sum(attn_grad, 0)
    ebg = jnp.stack(xor_order(list(expand_bias_grad.reshape(parts, dp * unit)), part), 0)
    ebg = ebg.reshape(parts, dp, unit).transpose(1, 0, 2).reshape(dp, parts * unit)
    vec_all = jnp.concatenate(
        [
            v.reshape(dp, shard)
            for v in (
                mixer_bias_grad,
                attn_gain_grad,
                attn_shift_grad,
                vec_grads[2],
                vec_grads[0],
                vec_grads[1],
            )
        ]
        + [ebg],
        1,
    ).astype(BF16)

    mixer_cols = width // blk
    mixer_part_rows = shard // uly
    vec_len = vec_all.shape[1]
    vec_rows = -(-vec_len // mixer_cols)
    vec_rows = -(-vec_rows // 16) * 16
    vec_block = jnp.pad(vec_all, ((0, 0), (0, vec_rows * mixer_cols - vec_len))).reshape(
        dp, vec_rows, mixer_cols
    )
    mixer_view = mixer_grad.reshape(dp, uly, mixer_part_rows, blk, mixer_cols)
    by_blk = xor_order([mixer_view[:, :, :, i] for i in range(blk)], b)
    mixer_parts = []
    for i in range(blk):
        by_uly = xor_order([by_blk[i][:, j] for j in range(uly)], u)
        mixer_parts.append(
            jnp.stack([jnp.concatenate([piece, vec_block], 1) for piece in by_uly], 0)
        )
    mixer_sum = total(
        [mixer_parts[0]] + [swap_with(mixer_parts[i], "blk", i) for i in range(1, blk)]
    ).astype(BF16)
    mixer_sum = total(
        [mixer_sum[0]] + [swap_with(mixer_sum[j], "uly", j) for j in range(1, uly)]
    ).astype(BF16)

    def over_blk(grad):
        return total(
            [grad[:uly]]
            + [swap_with(grad[i * uly : (i + 1) * uly], "blk", i) for i in range(1, blk)]
        ).astype(BF16)

    shrink_sum = over_blk(shrink_grad)
    expand_sum = over_blk(expand_grad)
    shrink_sum = shrink_sum.reshape(2, 2, dp * unit, width)
    expand_sum = expand_sum.reshape(2, 2, width, dp * unit)
    shrink_sum = total([shrink_sum[0], swap_with(shrink_sum[1], "uly", 2)]).astype(BF16)
    expand_sum = total([expand_sum[:, 0], swap_with(expand_sum[:, 1], "uly", 1)]).astype(BF16)
    shrink_sum = total([shrink_sum[0], swap_with(shrink_sum[1], "uly", 1)]).astype(BF16)
    expand_sum = total([expand_sum[0], swap_with(expand_sum[1], "uly", 2)]).astype(BF16)

    mixer_rows = mixer_sum.shape[1] * mixer_cols // width
    packed = jnp.concatenate(
        [
            expand_sum.reshape(dp, expand_rows, width),
            shrink_sum.reshape(dp, unit, width),
            mixer_sum.reshape(dp, mixer_rows, width),
        ],
        1,
    )

    def over_dp(value):
        sends = [lax.dynamic_slice_in_dim(value, z ^ j, 1, 0)[0] for j in range(dp)]
        return total([sends[0]] + [swap_with(sends[j], "dp", j) for j in range(1, dp)])

    owned = over_dp(packed)
    vec_owned = owned[expand_rows + unit :].reshape(-1, mixer_cols)[mixer_part_rows:]
    vec_owned = vec_owned.reshape(-1)[:vec_len]

    def in_plane(value):
        value = value.astype(BF16)
        value = jnp.stack(
            xor_order([value] + [swap_with(value, "uly", j) for j in range(1, uly)], u), 0
        )
        return jnp.stack(
            xor_order([value] + [swap_with(value, "blk", i) for i in range(1, blk)], b), 0
        )

    gathered = in_plane(owned).reshape(parts, -1, width)
    expand_out = gathered[:, :expand_rows].reshape(parts, shard, dp, unit)
    expand_out = expand_out.transpose(1, 2, 0, 3).reshape(shard, hidden).astype(F32)
    shrink_out = gathered[:, expand_rows : expand_rows + unit]
    shrink_out = shrink_out.reshape(parts * unit, width).astype(F32)
    mixer_out = gathered[:, expand_rows + unit :].reshape(blk, uly, -1, mixer_cols)
    mixer_out = mixer_out[:, :, :mixer_part_rows].transpose(1, 2, 0, 3)
    mixer_out = mixer_out.reshape(shard, width).astype(F32)

    own_dkv = total([dkvs[0]] + [swap_with(dkvs[i], "blk", i) for i in range(1, blk)])
    own_dkv = own_dkv.astype(BF16)
    proj_grad = jnp.concatenate(
        [dq * jnp.asarray(0.125, BF16), own_dkv[:, :group], own_dkv[:, wide : wide + group]], 1
    )
    token_parts = dot_nt(proj_grad, attend_own.reshape(width, 3 * group))
    token_low = token_parts.astype(BF16)
    tokens_grad = attn_grad + total(
        [token_parts[:rows]]
        + [swap_with(token_low[j * rows : (j + 1) * rows], "uly", j) for j in range(1, uly)]
    )
    attend_grad = dot_tn(x_rows, proj_grad).astype(BF16)
    attend_grad = attend_grad.reshape(dp, blk, share, 3 * group)
    bias_sum = jnp.sum(proj_grad.astype(F32), 0)[None]
    bias_rows = pad_rows(bias_sum.astype(BF16), 16)
    attend_parts = [
        jnp.concatenate(
            [
                lax.dynamic_slice_in_dim(attend_grad, b ^ i, 1, 1).reshape(-1, 3 * group),
                bias_rows,
            ],
            0,
        )
        for i in range(blk)
    ]
    attend_sum = total(
        [attend_parts[0]] + [swap_with(attend_parts[i], "blk", i) for i in range(1, blk)]
    ).astype(BF16)
    bias_half = jnp.broadcast_to(attend_sum[dp * share :], (dp, 16, 3 * group))
    attend_sum = attend_sum[: dp * share].reshape(dp, share, 3 * group)
    attend_owned = over_dp(jnp.concatenate([attend_sum, bias_half], 1))
    attend_all = in_plane(attend_owned)
    attend_out = attend_all[:, :, :share].reshape(blk, uly, share, 3, group)
    attend_out = attend_out.transpose(0, 2, 3, 1, 4).reshape(shard, 3 * width).astype(F32)
    bias_out = attend_all[0, :, share].astype(F32).reshape(uly, 3, group)
    query_bias_grad = lax.dynamic_slice_in_dim(bias_out[:, 0].reshape(width), z * shard, shard, 0)
    value_bias_grad = lax.dynamic_slice_in_dim(bias_out[:, 2].reshape(width), z * shard, shard, 0)

    vecs = [vec_owned[k * shard : (k + 1) * shard] for k in range(6)]
    return (
        mixed.reshape(tokens.shape),
        tokens_grad.reshape(tokens.shape),
        attend_out,
        query_bias_grad,
        value_bias_grad,
        mixer_out,
        vecs[0],
        vecs[1],
        vecs[2],
        expand_out,
        vec_owned[6 * shard :],
        shrink_out,
        vecs[3],
        vecs[4],
        vecs[5],
    )


def call(kernel, name, scalars, args, in_specs, out_shape, out_specs, scratch, grid, flops, vmem):
    return pl.pallas_call(
        kernel,
        grid_spec=pltpu.PrefetchScalarGridSpec(
            num_scalar_prefetch=1,
            grid=grid,
            in_specs=in_specs,
            out_specs=out_specs,
            scratch_shapes=scratch,
        ),
        out_shape=out_shape,
        compiler_params=pltpu.CompilerParams(vmem_limit_bytes=vmem * 2**20),
        cost_estimate=pl.CostEstimate(flops=flops, bytes_accessed=1, transcendentals=0),
        name=name,
    )(scalars, *args)


def whole(shape):
    return pl.BlockSpec(shape, lambda *_: (0,) * len(shape))


def after(value, *deps):
    return lax.optimization_barrier((value, *deps))[0]


def slot(offset):
    return (offset & 1) * 2 + (offset >> 1)


def one_hot(rows, cols, row_offset=0, col_offset=0):
    row = lax.broadcasted_iota(jnp.int32, (rows, cols), 0) + row_offset
    col = lax.broadcasted_iota(jnp.int32, (rows, cols), 1) + col_offset
    return jnp.where(row == col, 1.0, 0.0).astype(BF16)


def fetch_kernel(sizes, idx, attend_ref, expand_ref, shrink_ref, mixer_ref, *refs):
    uly, dp, group, unit = sizes
    vec_refs, (first_ref, feed_ref) = refs[:-2], refs[-2:]
    share = attend_ref.shape[1]
    shard, width = mixer_ref.shape
    u = idx[1]
    part = idx[0] * uly + u
    take = one_hot(width, group, 0, u * group)
    for c in range(3):
        cols = dot_nn(attend_ref[0, :, c * width : (c + 1) * width], take)
        first_ref[:share, c * group : (c + 1) * group] = cols.astype(BF16)
    first_ref[share:, :] = jnp.zeros_like(first_ref[share:, :])
    rows = share // dp
    mixer = dot_nn(one_hot(rows, shard, part * rows, 0), mixer_ref[...]).astype(BF16)
    for k in range(dp):
        here = slice(k * rows, (k + 1) * rows)
        first_ref[here, 3 * group :] = mixer[:, k * group : (k + 1) * group]
    line = share
    for ref in vec_refs:
        for k in range(ref.shape[0] // shard):
            first_ref[line : line + 1, :shard] = ref[k * shard : (k + 1) * shard].reshape(1, shard)
            line += 1
    take = one_hot(width, unit, 0, part * unit)
    half = shard // 2
    for k in range(dp):
        cols = dot_nn(expand_ref[:, k * width : (k + 1) * width], take).astype(BF16)
        feed_ref[:half, k * unit : (k + 1) * unit] = cols[:half]
        feed_ref[:half, (dp + k) * unit : (dp + k + 1) * unit] = cols[half:]
    feed_ref[half:, :] = shrink_ref[0]


def project_kernel(sizes, idx, *refs):
    uly, blk, dp, group, unit = sizes
    x_refs, refs = refs[:uly], refs[uly:]
    mine_refs, refs = refs[:dp], refs[dp:]
    other_refs, refs = refs[:dp], refs[dp:]
    w_ref, q_ref, kv_ref, vec_ref, eb_ref, mixer_ref = refs
    b, u, z, length = idx[0], idx[1], idx[2], idx[3]
    rows, width = x_refs[0].shape
    wide = q_ref.shape[1]
    pad = wide - group
    share = mine_refs[0].shape[0] - 16
    shard = 2 * share
    parts = uly * blk
    for c in range(3):
        w_ref[:, c * wide + group : (c + 1) * wide] = jnp.zeros((width, pad), BF16)
    own_vec = jnp.zeros((16, shard), F32)
    all_vec = jnp.zeros((16, width), F32)
    lines = share // dp
    for j in range(dp):
        for k in range(dp):
            mixer_ref[j * lines : (j + 1) * lines, k * group : (k + 1) * group] = mine_refs[j][
                k * lines : (k + 1) * lines, 3 * group :
            ]
        for ref, core in ((mine_refs[j], b), (other_refs[j], 1 - b)):
            start = pl.multiple_of((z ^ j) * shard + core * share, share)
            for c in range(3):
                w_ref[pl.ds(start, share), c * wide : c * wide + group] = ref[
                    :share, c * group : (c + 1) * group
                ]
        vec = mine_refs[j][share:, :shard]
        own_vec += jnp.where((z ^ j) == u, 1.0, 0.0) * vec.astype(F32)
        all_vec += dot_nn(vec, one_hot(shard, width, (z ^ j) * shard, 0))
    vec_ref[...] = all_vec

    low = all_vec.astype(BF16)
    part = b * uly + u
    eb = jnp.zeros((parts, dp * unit), F32)
    for parity in range(2):
        col = lax.broadcasted_iota(jnp.int32, (width, dp * unit), 1)
        row = lax.broadcasted_iota(jnp.int32, (width, dp * unit), 0)
        source = col + (col // unit) * (shard - unit) + parity * unit
        lanes = dot_nn(low, jnp.where(row == source, 1.0, 0.0).astype(BF16)).astype(BF16)
        owner = lax.broadcasted_iota(jnp.int32, (parts, 16), 0) ^ part
        line = lax.broadcasted_iota(jnp.int32, (parts, 16), 1)
        wanted = ((owner & 1) == parity) & (line == 8 + (owner >> 1))
        eb += dot_nn(jnp.where(wanted, 1.0, 0.0).astype(BF16), lanes)
    eb_ref[...] = eb

    lane = lax.broadcasted_iota(jnp.int32, (1, wide), 1)
    mark = jnp.where(lane == group, 1.0, 0.0)
    zeros = jnp.zeros((1, pad), F32)
    q_bias = jnp.concatenate([own_vec[0:1], zeros], 1)
    v_bias = jnp.concatenate([own_vec[1:2], zeros], 1)
    for j in range(uly):
        x = x_refs[j][...]
        here = slice(j * rows, (j + 1) * rows)
        q = dot_nn(x, w_ref[:, :wide]) + q_bias
        q_ref[here, :] = (q * (0.125 * LOG2E) + mark).astype(BF16)
        first = (b * uly + (u ^ j)) * rows
        position = lax.broadcasted_iota(jnp.int32, (rows, 1), 0) + first
        masked = jnp.where(position < length, 0.0, MASKED)
        k = dot_nn(x, w_ref[:, wide : 2 * wide]) + masked * mark
        kv_ref[here, :wide] = k.astype(BF16)
        kv_ref[here, wide:] = (dot_nn(x, w_ref[:, 2 * wide :]) + v_bias).astype(BF16)


def attend_kernel(heads, blocks, q_ref, *refs):
    kv_refs = refs[:blocks]
    o_refs = refs[blocks:-2]
    lse_ref, vt_ref = refs[-2:]
    group = heads * HD
    wide = q_ref.shape[1]
    rows = kv_refs[0].shape[0]

    @pl.when(pl.program_id(0) == 0)
    def _():
        for i in range(blocks):
            vt_ref[:, i * rows : (i + 1) * rows] = kv_refs[i][:, wide : wide + group].T

    q = q_ref[...]
    outs = []
    for head in range(heads):
        q_head = jnp.where(head_lanes(wide, head, group), q, jnp.zeros_like(q))
        scores = [dot_nt(kv_refs[i][:, :wide], q_head) for i in range(blocks)]
        top = jnp.max(scores[0], axis=0, keepdims=True)
        for i in range(1, blocks):
            top = jnp.maximum(top, jnp.max(scores[i], axis=0, keepdims=True))
        norm = jnp.zeros_like(top)
        acc = None
        for i in range(blocks):
            probs = jnp.exp2(scores[i] - top)
            norm = norm + jnp.sum(probs, axis=0, keepdims=True)
            part = dot_nn(
                vt_ref[head * HD : (head + 1) * HD, i * rows : (i + 1) * rows], probs.astype(BF16)
            )
            acc = part if acc is None else acc + part
        outs.append(acc / norm)
        lse_ref[head : head + 1, :] = top + jnp.log2(norm)
    out = jnp.concatenate(outs, axis=0).T.astype(BF16)
    for j, o_ref in enumerate(o_refs):

        @pl.when(pl.program_id(0) == j)
        def _(o_ref=o_ref):
            o_ref[...] = out


def attend(q, kvs, heads, pieces):
    rows, wide = q.shape
    tile = rows // pieces
    group = heads * HD
    blocks = len(kvs)
    keys = blocks * rows
    out = pl.pallas_call(
        functools.partial(attend_kernel, heads, blocks),
        grid=(pieces,),
        in_specs=[pl.BlockSpec((tile, wide), lambda t: (t, 0))] + [whole(kvs[0].shape)] * blocks,
        out_specs=[whole((tile, group))] * pieces + [pl.BlockSpec((8, tile), lambda t: (0, t))],
        out_shape=[jax.ShapeDtypeStruct((tile, group), BF16)] * pieces
        + [jax.ShapeDtypeStruct((8, rows), F32)],
        scratch_shapes=[pltpu.VMEM((group, keys), BF16)],
        compiler_params=pltpu.CompilerParams(vmem_limit_bytes=16 * 2**20),
        cost_estimate=pl.CostEstimate(
            flops=4 * heads * rows * keys * wide,
            transcendentals=heads * rows * keys,
            bytes_accessed=2 * rows * wide * 3 + 2 * keys * (wide + group),
        ),
        name="attend",
    )(q, *kvs)
    return out[:-1], out[-1]


def first_norm_kernel(uly, idx, x_ref, *refs):
    o_refs = refs[:uly]
    m_ref, vec_ref, x1_ref, x1b_ref, normed_ref, inverse_ref = refs[uly:]
    group = o_refs[0].shape[1]
    acc = vec_ref[2:3, :]
    for j in range(uly):
        start = pl.multiple_of((idx[1] ^ j) * group, group)
        acc = acc + dot_nn(o_refs[j][...], m_ref[pl.ds(start, group), :])
    hidden = x_ref[...].astype(F32) + acc
    center = hidden - jnp.mean(hidden, -1, keepdims=True)
    inverse = lax.rsqrt(jnp.mean(center * center, -1, keepdims=True) + EPSILON)
    normed = center * inverse
    out = normed * vec_ref[3:4, :] + vec_ref[4:5, :]
    x1_ref[...] = out
    x1b_ref[...] = out.astype(BF16)
    normed_ref[...] = normed
    inverse_ref[...] = inverse


def rest_kernel(sizes, idx, expand_ref, shrink_ref, out_ref):
    uly, dp, unit = sizes
    width = shrink_ref.shape[1]
    half = expand_ref.shape[0] // 2
    for j in range(1, uly):
        part = idx[0] * uly + (idx[1] ^ j)
        take = one_hot(width, unit, 0, part * unit)
        for k in range(dp):
            cols = dot_nn(expand_ref[:, k * width : (k + 1) * width], take).astype(BF16)
            out_ref[j - 1, :half, k * unit : (k + 1) * unit] = cols[:half]
            out_ref[j - 1, :half, (dp + k) * unit : (dp + k + 1) * unit] = cols[half:]
        start = pl.multiple_of(part * unit, unit)
        out_ref[j - 1, half:, :] = shrink_ref[pl.ds(start, unit), :]


def mixer_kernel(sizes, idx, *refs):
    uly, dp = sizes
    pieces, (m_ref, turn_ref) = refs[:-2], refs[-2:]
    lines = pieces[0].shape[0] // dp
    b, u, z = idx[0], idx[1], idx[2]
    shard = 2 * uly * lines
    for k in range(dp):
        for p, ref in enumerate(pieces):
            part = (b * uly + u) ^ p
            turn_ref[pl.ds(pl.multiple_of(part * lines, 8), lines), :] = ref[
                k * lines : (k + 1) * lines, :
            ].astype(F32)
        start = pl.multiple_of((z ^ k) * shard, shard)
        m_ref[pl.ds(start, shard), :] = turn_ref[...].astype(BF16)


def load_parts(pieces, z, e_ref, s_ref, sem, act, only=None):
    dp, unit, width = s_ref.shape[1:]
    shard = width // dp
    half = shard // 2
    block = dp * unit
    for j, row in enumerate(pieces):
        if only is not None and j != only:
            continue
        for k, piece in enumerate(row):
            for h in range(2):
                start = pl.multiple_of((z ^ k) * shard + h * half, half)
                act(
                    pltpu.make_async_copy(
                        piece.at[pl.ds(0, half), pl.ds(h * block, block)],
                        e_ref.at[j, pl.ds(start, half), :],
                        sem.at[j, 3 * k + h],
                    )
                )
            act(
                pltpu.make_async_copy(
                    piece.at[pl.ds(half, unit), :], s_ref.at[j, z ^ k], sem.at[j, 3 * k + 2]
                )
            )


def by_part(uly, dp, refs):
    own, rest, *far = refs
    return [
        [own if j == 0 else rest.at[j - 1]] + [far[(k - 1) * uly + j] for k in range(1, dp)]
        for j in range(uly)
    ]


def weights_ready(pieces, z, e_ref, s_ref, sem):
    step = pl.program_id(0)

    @pl.when(step == 0)
    def _():
        load_parts(pieces, z, e_ref, s_ref, sem, lambda copy: copy.start())

    for j in range(len(pieces)):

        @pl.when(step == j)
        def _(j=j):
            load_parts(pieces, z, e_ref, s_ref, sem, lambda copy: copy.wait(), j)


def feed_forward_kernel(uly, idx, mine_ref, other_ref, eb_ref, *refs):
    act_ref, slope_ref, y_ref, send_ref, acc_ref, x_ref, e_ref, s_ref, sem = refs[-9:]
    step = pl.program_id(0)
    dp, unit, width = s_ref.shape[1:]
    rows = mine_ref.shape[0]
    weights_ready(by_part(uly, dp, refs[:-9]), idx[2], e_ref, s_ref, sem)

    @pl.when(step == 0)
    def _():
        x_ref[:rows] = mine_ref[...]
        x_ref[rows:] = other_ref[...]
        acc_ref[...] = jnp.zeros_like(acc_ref)

    pre = dot_nn(x_ref[...], e_ref[step]) + eb_ref[pl.ds(step, 1), :]
    cdf = 0.5 * (1.0 + lax.erf(pre * 0.7071067811865476))
    pdf = jnp.exp(-0.5 * pre * pre) * 0.3989422804014327
    act = (pre * cdf).astype(BF16)
    act_ref[0] = act
    slope_ref[0] = (cdf + pre * pdf).astype(BF16)
    acc_ref[...] += dot_nn(act, s_ref[step].reshape(dp * unit, width))

    @pl.when(step == uly - 1)
    def _():
        y_ref[...] = acc_ref[:rows]
        send_ref[...] = acc_ref[rows:].astype(BF16)


def weight_scratch(uly, dp, unit, width):
    return [
        pltpu.VMEM((uly, width, dp * unit), BF16),
        pltpu.VMEM((uly, dp, unit, width), BF16),
        pltpu.SemaphoreType.DMA((uly, 3 * dp)),
    ]


def feed_forward(scalars, sizes, mine, other, eb, weights):
    uly, dp, unit = sizes
    rows, width = mine.shape
    block = dp * unit
    hbm = pl.BlockSpec(memory_space=pl.ANY)
    return call(
        functools.partial(feed_forward_kernel, uly),
        "feed_forward",
        scalars,
        [mine, other, eb, *weights],
        [whole(mine.shape), whole(mine.shape), whole(eb.shape)] + [hbm] * len(weights),
        [
            jax.ShapeDtypeStruct((uly, 2 * rows, block), BF16),
            jax.ShapeDtypeStruct((uly, 2 * rows, block), BF16),
            jax.ShapeDtypeStruct((rows, width), F32),
            jax.ShapeDtypeStruct((rows, width), BF16),
        ],
        [
            pl.BlockSpec((1, 2 * rows, block), lambda k, _: (k, 0, 0)),
            pl.BlockSpec((1, 2 * rows, block), lambda k, _: (k, 0, 0)),
            whole((rows, width)),
            whole((rows, width)),
        ],
        [pltpu.VMEM((2 * rows, width), F32), pltpu.VMEM((2 * rows, width), BF16)]
        + weight_scratch(uly, dp, unit, width),
        (uly,),
        8 * rows * width * uly * block,
        16,
    )


def final_norm_kernel(idx, x1_ref, y_ref, got_ref, vec_ref, cot_ref, *refs):
    mixed_ref, dh_ref, low_ref, sums_ref = refs
    hidden = x1_ref[...] + (y_ref[...] + got_ref[...].astype(F32) + vec_ref[5:6, :])
    gain = vec_ref[6:7, :]
    center = hidden - jnp.mean(hidden, -1, keepdims=True)
    inverse = lax.rsqrt(jnp.mean(center * center, -1, keepdims=True) + EPSILON)
    normed = center * inverse
    mixed_ref[...] = (normed * gain + vec_ref[7:8, :]).astype(BF16)
    grad = cot_ref[...].astype(F32)
    scaled = grad * gain
    dhidden = inverse * (
        scaled
        - jnp.mean(scaled, -1, keepdims=True)
        - normed * jnp.mean(scaled * normed, -1, keepdims=True)
    )
    dh_ref[...] = dhidden
    low_ref[...] = dhidden.astype(BF16)
    sums_ref[...] = jnp.zeros_like(sums_ref)
    sums_ref[0:1, :] = jnp.sum(dhidden, 0, keepdims=True)
    sums_ref[1:2, :] = jnp.sum(grad * normed, 0, keepdims=True)
    sums_ref[2:3, :] = jnp.sum(grad, 0, keepdims=True)


def store_halves(step, uly, value, z, dp, near_x, far_x, near_y, far_y):
    rows = value.shape[0] // dp
    place = [pl.multiple_of(((z ^ k) >> 1) * rows, rows) for k in range(dp)]
    for odd, near, far, close in (
        (0, near_x, far_x, step % 2 == 0),
        (1, near_y, far_y, step < uly // 2),
    ):
        for ref, wanted in ((near, close), (far, jnp.logical_not(close))):
            for k in range(dp):

                @pl.when(wanted & (((z ^ k) & 1) == odd))
                def _(ref=ref, k=k):
                    ref[0, pl.ds(place[k], rows), :] = value[k * rows : (k + 1) * rows]


def half_specs(uly, rows, cols):
    shape = jax.ShapeDtypeStruct((uly // 2, rows, cols), BF16)
    block = (1, rows, cols)
    return [shape] * 4, [
        pl.BlockSpec(block, lambda k, _: (k // 2, 0, 0)),
        pl.BlockSpec(block, lambda k, _: (k // 2, 0, 0)),
        pl.BlockSpec(block, lambda k, _: (jnp.minimum(k, 1), 0, 0)),
        pl.BlockSpec(block, lambda k, _: (jnp.maximum(k - 2, 0), 0, 0)),
    ]


def shrink_grad_kernel(sizes, idx, d_mine, d_other, act_ref, *refs):
    uly, dp = sizes
    out_refs, d_ref = refs[:-1], refs[-1]
    step = pl.program_id(0)
    rows = d_mine.shape[0]

    @pl.when(step == 0)
    def _():
        d_ref[:rows] = d_mine[...]
        d_ref[rows:] = d_other[...]

    value = dot_tn(act_ref[0], d_ref[...]).astype(BF16)
    store_halves(step, uly, value, idx[2], dp, *out_refs)


def shrink_grad(scalars, sizes, ds, act):
    uly, dp, unit = sizes
    rows, width = ds[0].shape
    block = dp * unit
    shapes, specs = half_specs(uly, block // 2, width)
    return call(
        functools.partial(shrink_grad_kernel, (uly, dp)),
        "shrink_grad",
        scalars,
        [*ds, act],
        [whole((rows, width))] * 2 + [pl.BlockSpec((1, 2 * rows, block), lambda k, _: (k, 0, 0))],
        shapes,
        specs,
        [pltpu.VMEM((2 * rows, width), BF16)],
        (uly,),
        4 * rows * width * uly * block,
        16,
    )


def feed_backward_kernel(uly, idx, x_mine, x_other, d_mine, d_other, slope_ref, *refs):
    half_refs, (deb_ref, dx_ref, send_ref) = refs[-14:-10], refs[-10:-7]
    acc_ref, xt_ref, d_ref, turn_ref, e_ref, s_ref, sem = refs[-7:]
    step = pl.program_id(0)
    dp, unit, width = s_ref.shape[1:]
    rows = x_mine.shape[0]
    weights_ready(by_part(uly, dp, refs[:-14]), idx[2], e_ref, s_ref, sem)

    @pl.when(step == 0)
    def _():
        xt_ref[:, :rows] = x_mine[...].T
        xt_ref[:, rows:] = x_other[...].T
        d_ref[:rows] = d_mine[...]
        d_ref[rows:] = d_other[...]
        acc_ref[...] = jnp.zeros_like(acc_ref)

    dpre = dot_nt(d_ref[...], s_ref[step].reshape(dp * unit, width))
    dpre = (dpre * slope_ref[0].astype(F32)).astype(BF16)
    deb_ref[0] = jnp.sum(dpre.astype(F32), 0, keepdims=True)
    dexpand = dot_nn(xt_ref[...], dpre).astype(BF16)
    store_halves(step, uly, dexpand, idx[2], dp, *half_refs)
    acc_ref[...] += dot_nt(dpre, e_ref[step])

    @pl.when(step == uly - 1)
    def _():
        dx_ref[...] = acc_ref[:rows]
        send_ref[...] = acc_ref[rows:].astype(BF16)


def feed_backward(scalars, sizes, xs, ds, slope, weights):
    uly, dp, unit = sizes
    rows, width = xs[0].shape
    block = dp * unit
    hbm = pl.BlockSpec(memory_space=pl.ANY)
    shapes, specs = half_specs(uly, width // 2, block)
    return call(
        functools.partial(feed_backward_kernel, uly),
        "feed_backward",
        scalars,
        [*xs, *ds, slope, *weights],
        [whole((rows, width))] * 4
        + [pl.BlockSpec((1, 2 * rows, block), lambda k, _: (k, 0, 0))]
        + [hbm] * len(weights),
        shapes
        + [
            jax.ShapeDtypeStruct((uly, 1, block), F32),
            jax.ShapeDtypeStruct((rows, width), F32),
            jax.ShapeDtypeStruct((rows, width), BF16),
        ],
        specs
        + [
            pl.BlockSpec((1, 1, block), lambda k, _: (k, 0, 0)),
            whole((rows, width)),
            whole((rows, width)),
        ],
        [
            pltpu.VMEM((2 * rows, width), F32),
            pltpu.VMEM((width, 2 * rows), BF16),
            pltpu.VMEM((2 * rows, width), BF16),
            pltpu.VMEM((16, 128), BF16),
        ]
        + weight_scratch(uly, dp, unit, width),
        (uly,),
        12 * rows * width * uly * block,
        16,
    )


def norm_backward_kernel(sizes, idx, dh2_ref, dx_ref, got_ref, normed_ref, inverse_ref, *refs):
    uly, dp, unit = sizes
    m_ref, vec_ref, grads_ref, deb_ref, *refs = refs
    o_refs, refs = refs[:uly], refs[uly:]
    dh_ref, *refs = refs
    do_refs, refs = refs[:uly], refs[uly:]
    keep_ref, send_ref, turn_ref = refs
    b, u, z = idx[0], idx[1], idx[2]
    group = o_refs[0].shape[1]
    share = group // 2
    width = dx_ref.shape[1]
    parts = 2 * uly
    grad = dh2_ref[...] + dx_ref[...] + got_ref[...].astype(F32)
    normed = normed_ref[...]
    scaled = grad * vec_ref[3:4, :]
    dhidden = inverse_ref[...] * (
        scaled
        - jnp.mean(scaled, -1, keepdims=True)
        - normed * jnp.mean(scaled * normed, -1, keepdims=True)
    )
    dh_ref[...] = dhidden
    low = dhidden.astype(BF16)
    for j in range(uly):
        start = pl.multiple_of((u ^ j) * group, group)
        do_refs[j][...] = dot_nt(low, m_ref[pl.ds(start, group), :]).astype(BF16)
    line = lax.broadcasted_iota(jnp.int32, (8, width), 0)
    lines = jnp.zeros((8, width), F32)
    values = [
        jnp.sum(dhidden, 0, keepdims=True),
        jnp.sum(grad * normed, 0, keepdims=True),
        jnp.sum(grad, 0, keepdims=True),
        grads_ref[0:1, :],
        grads_ref[1:2, :],
        grads_ref[2:3, :],
    ]
    for k, value in enumerate(values):
        lines = jnp.where(line == k, value, lines)
    lines = lines.astype(BF16)
    owner = (lax.broadcasted_iota(jnp.int32, (parts, uly), 1) ^ u) + b * uly
    order = lax.broadcasted_iota(jnp.int32, (parts, uly), 0)
    order = jnp.where(order == owner, 1.0, 0.0).astype(BF16)
    ebs = dot_nn(order, deb_ref[...].astype(BF16)).astype(BF16)
    for j in range(uly):
        turn_ref[...] = dot_tn(o_refs[j][...], low).astype(BF16)
        place = slot(u ^ j ^ z)
        keep_ref[place, :share] = turn_ref[pl.ds(pl.multiple_of(b * share, share), share), :]
        send_ref[place, :share] = turn_ref[pl.ds(pl.multiple_of((1 - b) * share, share), share), :]
    for k in range(dp):
        shard = (z ^ k) * group
        own = dot_nn(lines, one_hot(width, group, 0, shard)).astype(BF16)
        ebk = dot_nn(ebs, one_hot(dp * unit, unit, 0, (z ^ k) * unit)).astype(BF16)
        for ref in (keep_ref, send_ref):
            ref[slot(k), share:, :] = jnp.zeros_like(ref[slot(k), share:, :])
            ref[slot(k), share : share + 8, :group] = own
            ref[slot(k), share + 8 : share + 16, :unit] = ebk


def attend_grad_kernel(heads, blocks, pieces, started, q_ref, lse_ref, *refs):
    do_refs, refs = refs[:pieces], refs[pieces:]
    o_refs, refs = refs[:pieces], refs[pieces:]
    kv_refs, refs = refs[:blocks], refs[blocks:]
    so_far, refs = refs[: blocks * started], refs[blocks * started :]
    dq_ref, *refs = refs
    dkv_refs, refs = refs[:blocks], refs[blocks:]
    kt_ref, dout_ref, prod_ref, *refs = refs
    dk_accs, dv_accs = refs[:blocks], refs[blocks:]
    group = heads * HD
    wide = q_ref.shape[1]
    rows = kv_refs[0].shape[0]

    @pl.when(pl.program_id(0) == 0)
    def _():
        for i in range(blocks):
            kt_ref[:, i * rows : (i + 1) * rows] = kv_refs[i][:, :group].T
            if started:
                dk_accs[i][...] = so_far[i][:, :wide].astype(F32) * LOG2E
                dv_accs[i][...] = so_far[i][:, wide : wide + group].astype(F32)
            else:
                dk_accs[i][...] = jnp.zeros_like(dk_accs[i])
                dv_accs[i][...] = jnp.zeros_like(dv_accs[i])

    for j in range(pieces):

        @pl.when(pl.program_id(0) == j)
        def _(j=j):
            dout_ref[...] = do_refs[j][...]
            prod_ref[...] = (do_refs[j][...].astype(F32) * o_refs[j][...].astype(F32)).T

    q = q_ref[...]
    dout = dout_ref[...]
    dqs = []
    for head in range(heads):
        q_head = jnp.where(head_lanes(wide, head, group), q, jnp.zeros_like(q))
        do_head = jnp.where(head_lanes(group, head), dout, jnp.zeros_like(dout))
        lse = lse_ref[head : head + 1, :]
        delta = jnp.sum(prod_ref[head * HD : (head + 1) * HD, :], axis=0, keepdims=True)
        acc = None
        for i in range(blocks):
            probs = jnp.exp2(dot_nt(kv_refs[i][:, :wide], q_head) - lse)
            dv_accs[i][...] += dot_nn(probs.astype(BF16), do_head)
            grads = dot_nt(kv_refs[i][:, wide : wide + group], do_head)
            grads = (probs * (grads - delta)).astype(BF16)
            dk_accs[i][...] += dot_nn(grads, q_head)
            part = dot_nn(
                kt_ref[head * HD : (head + 1) * HD, i * rows : (i + 1) * rows], grads
            )
            acc = part if acc is None else acc + part
        dqs.append(acc)
    dq_ref[...] = jnp.concatenate(dqs, axis=0).T.astype(BF16)

    @pl.when(pl.program_id(0) == pl.num_programs(0) - 1)
    def _():
        for i in range(blocks):
            dkv_refs[i][:, :group] = (dk_accs[i][:, :group] * LN2).astype(BF16)
            dkv_refs[i][:, group:wide] = jnp.zeros((rows, wide - group), BF16)
            dkv_refs[i][:, wide : wide + group] = dv_accs[i][...].astype(BF16)
            dkv_refs[i][:, wide + group :] = jnp.zeros((rows, wide - group), BF16)


def attend_grad(q, kvs, douts, outs, lse, heads, at, so_far):
    rows, wide = kvs[0].shape[0], q.shape[1]
    group = heads * HD
    blocks = len(kvs)
    pieces = len(douts)
    tile = douts[0].shape[0]
    keys = blocks * rows
    started = 1 if so_far else 0
    out = pl.pallas_call(
        functools.partial(attend_grad_kernel, heads, blocks, pieces, started),
        grid=(pieces,),
        in_specs=[
            pl.BlockSpec((tile, wide), lambda t: (t + at, 0)),
            pl.BlockSpec((8, tile), lambda t: (0, t + at)),
        ]
        + [whole((tile, group))] * (2 * pieces)
        + [whole(kvs[0].shape)] * (blocks + blocks * started),
        out_specs=[pl.BlockSpec((tile, group), lambda t: (t, 0))]
        + [whole(kvs[0].shape)] * blocks,
        out_shape=[jax.ShapeDtypeStruct((pieces * tile, group), BF16)]
        + [jax.ShapeDtypeStruct(kvs[0].shape, BF16)] * blocks,
        scratch_shapes=[
            pltpu.VMEM((group, keys), BF16),
            pltpu.VMEM((tile, group), BF16),
            pltpu.VMEM((group, tile), F32),
        ]
        + [pltpu.VMEM((rows, wide), F32)] * blocks
        + [pltpu.VMEM((rows, group), F32)] * blocks,
        compiler_params=pltpu.CompilerParams(vmem_limit_bytes=16 * 2**20),
        cost_estimate=pl.CostEstimate(
            flops=10 * heads * pieces * tile * keys * wide,
            transcendentals=heads * pieces * tile * keys,
            bytes_accessed=2 * rows * wide * 4 + 4 * keys * (wide + group),
        ),
        name="attend_grad",
    )(q, lse, *douts, *outs, *kvs, *so_far)
    return out[0], out[1:]


def project_grad_kernel(sizes, idx, *refs):
    uly, dp, group = sizes
    dq_refs, (own_ref, got_ref, *refs) = refs[:uly], refs[uly:]
    x_refs, refs = refs[:uly], refs[uly:]
    dproj_ref, keep_ref, send_ref = refs
    b, z = idx[0], idx[2]
    rows, width = x_refs[0].shape
    wide = own_ref.shape[1] // 2
    share = keep_ref.shape[1] - 16
    for k, ref in enumerate(dq_refs):
        here = slice(k * ref.shape[0], (k + 1) * ref.shape[0])
        dproj_ref[here, :group] = ref[...] * jnp.asarray(0.125, BF16)
    dproj_ref[:, group:wide] = jnp.zeros((uly * rows, wide - group), BF16)
    dproj_ref[:, wide:] = (own_ref[...].astype(F32) + got_ref[...].astype(F32)).astype(BF16)
    sums = jnp.sum(dproj_ref[...].astype(F32), 0, keepdims=True).astype(BF16)
    grad = None
    for j in range(uly):
        part = dot_tn(x_refs[j][...], dproj_ref[j * rows : (j + 1) * rows, :])
        grad = part if grad is None else grad + part
    grad = grad.astype(BF16)
    for ref, mine in ((keep_ref, True), (send_ref, False)):
        for c in range(3):
            lanes = slice(c * wide, c * wide + group)
            into = slice(c * group, (c + 1) * group)
            for s in range(dp):
                for core in range(2):
                    start = (s * 2 + core) * share

                    @pl.when((b == core) == mine)
                    def _(start=start, s=s, ref=ref, lanes=lanes, into=into):
                        ref[slot(s ^ z), :share, into] = grad[start : start + share, lanes]

                ref[s, share:, into] = jnp.broadcast_to(sums[:, lanes], (16, group))


def token_grad_kernel(uly, idx, dproj_ref, w_ref, dh_ref, *out_refs):
    rows = dh_ref.shape[0]
    for j in reversed(range(uly)):
        part = dot_nt(dproj_ref[j * rows : (j + 1) * rows, :], w_ref[...])
        if j == 0:
            part = part + dh_ref[...]
        out_refs[j][...] = part.astype(out_refs[j].dtype)


def pack_kernel(idx, sx_ref, sx1_ref, sx2_ref, sy_ref, sy1_ref, sy2_ref, keep_ref, got_ref, *refs):
    unit = sx2_ref.shape[0] // 2
    for out_ref, first, s_refs in (
        (refs[0], 0, (sx_ref, sx1_ref, sx2_ref)),
        (refs[1], 2, (sy_ref, sy1_ref, sy2_ref)),
    ):
        for k in range(2):
            rows = slice(k * unit, (k + 1) * unit)
            value = s_refs[0][0, rows].astype(F32) + s_refs[1][0, rows].astype(F32)
            out_ref[k, :unit, :] = (value + s_refs[2][rows].astype(F32)).astype(BF16)
            value = keep_ref[first + k].astype(F32) + got_ref[first + k].astype(F32)
            out_ref[k, unit:, :] = value.astype(BF16)


def finish_shrink_kernel(sizes, idx, *refs):
    uly, unit = sizes
    pieces, (shrink_ref, mixer_ref, vec_ref) = refs[: 2 * uly], refs[2 * uly :]
    share = mixer_ref.shape[0] // 2
    for p, ref in enumerate(pieces):

        @pl.when(pl.program_id(0) == p)
        def _(ref=ref):
            shrink_ref[...] = ref[:unit, :].astype(F32)

    def plane_sum(refs, rows):
        values = [ref[rows, :].astype(F32) for ref in refs]
        return (values[0] + values[1]) + (values[2] + values[3])

    @pl.when(pl.program_id(0) == 0)
    def _():
        for group, core in ((pieces[:uly], idx[0]), (pieces[uly:], 1 - idx[0])):
            start = pl.multiple_of(core * share, share)
            mixer_ref[pl.ds(start, share), :] = plane_sum(group, slice(unit, unit + share))
        vec_ref[...] = plane_sum(pieces[:uly], slice(unit + share, unit + share + 16))


def finish_expand_kernel(sizes, idx, *refs):
    uly, dp, unit = sizes
    pieces, (out_ref, turn_ref) = refs[:-2], refs[-2:]
    width = turn_ref.shape[0]
    part = idx[0] * uly + idx[1]
    step = pl.program_id(0)

    @pl.when(step == 0)
    def _():
        col = lax.broadcasted_iota(jnp.int32, (width, width), 1)
        row = lax.broadcasted_iota(jnp.int32, (width, width), 0)
        source = col + ((col // unit) ^ part) * unit - (col // unit) * unit
        turn_ref[...] = jnp.where(row == source, 1.0, 0.0).astype(BF16)

    for k in range(dp):

        @pl.when(step == k)
        def _(k=k):
            line = jnp.concatenate([ref[:, k * unit : (k + 1) * unit] for ref in pieces], 1)
            out_ref[...] = dot_nn(line, turn_ref[...])


def finish_attend_kernel(uly, idx, *refs):
    mine, refs = refs[:uly], refs[uly:]
    other, refs = refs[:uly], refs[uly:]
    out_ref, bias_ref = refs
    b, u, z = idx[0], idx[1], idx[2]
    share = mine[0].shape[0] - 16
    group = mine[0].shape[1] // 3
    width = uly * group
    for group_refs, core in ((mine, b), (other, 1 - b)):
        start = pl.multiple_of(core * share, share)
        for c in range(3):
            acc = None
            for j in range(uly):
                put = one_hot(group, width, (u ^ j) * group, 0)
                value = dot_nn(group_refs[j][:share, c * group : (c + 1) * group], put)
                acc = value if acc is None else acc + value
            out_ref[pl.ds(start, share), c * width : (c + 1) * width] = acc
    bias = jnp.zeros((8, 3 * group), F32)
    for j in range(uly):
        lines = mine[j][share : share + 16, :].astype(F32)[:8]
        bias += jnp.where((u ^ j) == z, 1.0, 0.0) * lines
    bias_ref[...] = bias


def on_device(*args):
    (
        tokens,
        lengths,
        cotangent,
        attend_weight,
        query_bias,
        value_bias,
        mixer_weight,
        mixer_bias,
        attn_gain,
        attn_shift,
        expand_weight,
        expand_bias,
        shrink_weight,
        shrink_bias,
        final_gain,
        final_shift,
    ) = args
    uly = lax.axis_size("uly")
    blk = lax.axis_size("blk")
    dp = lax.axis_size("dp")
    width = tokens.shape[-1]
    rows = tokens.shape[0] * tokens.shape[1]
    heads = HEADS // uly
    group = heads * HD
    wide = -(-(group + 1) // 128) * 128
    shard = attend_weight.shape[0]
    hidden = expand_weight.shape[1]
    parts = blk * uly
    unit = hidden // (parts * dp)
    share = shard // blk
    if not (blk == 2 and uly == 4 and dp == 4 and shard == group and unit * 2 == shard and share % 16 == 0):
        return general_device(*args)
    u = lax.axis_index("uly")
    b = lax.axis_index("blk")
    z = lax.axis_index("dp")
    mixer_rows = share // dp
    feed_rows = shard // 2 + unit
    block_rows = uly * rows
    cols = 3 * wide

    x = tokens.reshape(rows, width)
    xs = [x, swap_with(x, "uly", 1), swap_with(x, "uly", 2)]
    xs.append(swap_with(after(x, *xs[1:]), "uly", 3))
    scalars = jnp.stack([b, u, z, lengths[0]]).astype(jnp.int32)
    vectors = [query_bias, value_bias, mixer_bias, attn_gain, attn_shift, shrink_bias]
    vectors += [final_gain, final_shift, expand_bias]
    first, feed = call(
        functools.partial(fetch_kernel, (uly, dp, group, unit)),
        "fetch",
        scalars,
        [
            attend_weight.reshape(blk, share, 3 * width),
            expand_weight,
            shrink_weight.reshape(parts, unit, width),
            mixer_weight,
            *vectors,
        ],
        [
            pl.BlockSpec((1, share, 3 * width), lambda t, s: (s[0], 0, 0)),
            whole(expand_weight.shape),
            pl.BlockSpec((1, unit, width), lambda t, s: (s[0] * uly + s[1], 0, 0)),
            whole(mixer_weight.shape),
            *[whole(vector.shape) for vector in vectors],
        ],
        [
            jax.ShapeDtypeStruct((share + 16, width), BF16),
            jax.ShapeDtypeStruct((feed_rows, width), BF16),
        ],
        [whole((share + 16, width)), whole((feed_rows, width))],
        [],
        (1,),
        10**9,
        58,
    )
    feeds = [None, swap_with(feed, "dp", 1)]
    mine = [first, None, swap_with(first, "dp", 2), swap_with(first, "dp", 3)]
    mine[1] = swap_with(after(first, *xs[1:3]), "dp", 1)
    feeds.append(swap_with(after(feed, *mine[1:]), "dp", 2))
    other = [swap_with(piece, "blk", 1) for piece in mine]
    rest = call(
        functools.partial(rest_kernel, (uly, dp, unit)),
        "fetch_rest",
        scalars,
        [expand_weight, shrink_weight],
        [whole(expand_weight.shape), whole(shrink_weight.shape)],
        jax.ShapeDtypeStruct((uly - 1, shard // 2 + unit, width), BF16),
        whole((uly - 1, shard // 2 + unit, width)),
        [],
        (1,),
        10**9,
        16,
    )

    w_own, q, kv, vec, eb, mixer_mine = call(
        functools.partial(project_kernel, (uly, blk, dp, group, unit)),
        "project",
        scalars,
        [*after(xs, feeds[1]), *mine, *other],
        [whole((rows, width))] * uly + [whole(first.shape)] * (2 * dp),
        [
            jax.ShapeDtypeStruct((width, cols), BF16),
            jax.ShapeDtypeStruct((block_rows, wide), BF16),
            jax.ShapeDtypeStruct((block_rows, 2 * wide), BF16),
            jax.ShapeDtypeStruct((16, width), F32),
            jax.ShapeDtypeStruct((parts, dp * unit), F32),
            jax.ShapeDtypeStruct((dp * mixer_rows, width), BF16),
        ],
        [
            whole((width, cols)),
            whole((block_rows, wide)),
            whole((block_rows, 2 * wide)),
            whole((16, width)),
            whole((parts, dp * unit)),
            whole((dp * mixer_rows, width)),
        ],
        [],
        (1,),
        2 * block_rows * width * cols,
        16,
    )
    kvs = [kv, swap_with(kv, "blk", 1)]

    mixer_plane = [swap_with(mixer_mine, "uly", j) for j in range(1, uly)]
    plane_one = [swap_with(feeds[1], "uly", j) for j in range(1, uly)]
    outs, lse = attend(after(q, rest, *mixer_plane), kvs, heads, uly)
    o_cols = after(outs, *plane_one)
    o_cols = [o_cols[0]] + [swap_with(o_cols[j], "uly", j) for j in range(1, uly)]
    feeds.append(swap_with(after(feed, feeds[2], *plane_one), "dp", 3))
    plane_two = [swap_with(after(feeds[2], *o_cols[1:]), "uly", j) for j in range(1, uly)]
    mixer_parts = [mixer_mine, *mixer_plane]
    mixer_parts += [swap_with(piece, "blk", 1) for piece in mixer_parts]
    mixer_all = call(
        functools.partial(mixer_kernel, (uly, dp)),
        "mixer_weight",
        scalars,
        mixer_parts,
        [whole(mixer_mine.shape)] * parts,
        jax.ShapeDtypeStruct((width, width), BF16),
        whole((width, width)),
        [pltpu.VMEM((shard, width), F32)],
        (1,),
        10**6,
        16,
    )

    square = (rows, width)
    x1, x1b, normed, inverse = call(
        functools.partial(first_norm_kernel, uly),
        "first_norm",
        scalars,
        [x, *o_cols, mixer_all, vec],
        [whole(square)] + [whole((rows, group))] * uly + [whole((width, width)), whole(vec.shape)],
        [
            jax.ShapeDtypeStruct(square, F32),
            jax.ShapeDtypeStruct(square, BF16),
            jax.ShapeDtypeStruct(square, F32),
            jax.ShapeDtypeStruct((rows, 1), F32),
        ],
        [whole(square), whole(square), whole(square), whole((rows, 1))],
        [],
        (1,),
        2 * rows * width * width,
        16,
    )
    sizes = (uly, dp, unit)
    plane_three = [swap_with(after(feeds[3], *plane_two), "uly", j) for j in range(1, uly)]
    far = [feeds[1], *plane_one, feeds[2], *plane_two, feeds[3], *plane_three]
    weights = [feed, rest, *far]
    x1b_other = swap_with(x1b, "blk", 1)
    act, slope, y_own, y_send = feed_forward(scalars, sizes, x1b, x1b_other, eb, weights)
    mixed, dh2, dh2b, sums2 = call(
        final_norm_kernel,
        "final_norm",
        scalars,
        [x1, y_own, swap_with(y_send, "blk", 1), vec, cotangent.reshape(square)],
        [whole(square)] * 3 + [whole(vec.shape), whole(square)],
        [
            jax.ShapeDtypeStruct(square, BF16),
            jax.ShapeDtypeStruct(square, F32),
            jax.ShapeDtypeStruct(square, BF16),
            jax.ShapeDtypeStruct((8, width), F32),
        ],
        [whole(square)] * 3 + [whole((8, width))],
        [],
        (1,),
        10**6,
        16,
    )
    dh2b_other = swap_with(dh2b, "blk", 1)
    ds = [dh2b, dh2b_other]
    s_near_x, s_far_x, s_near_y, s_far_y = shrink_grad(scalars, sizes, ds, act)
    s_x = swap_with(s_far_x, "uly", 1)
    s_y = swap_with(s_far_y, "uly", 2)
    e_near_x, e_far_x, e_near_y, e_far_y, deb, dx_own, dx_send = feed_backward(
        scalars, sizes, [x1b, x1b_other], after(ds, s_far_x), slope, weights
    )
    def add(*values):
        return total(values).astype(BF16)

    dx_got = swap_with(after(dx_send, s_x, s_y), "blk", 1)
    s_next_x = add(s_near_x[1], s_x[1])
    s_next_y = add(s_near_y[1], s_y[1])
    s_xy = swap_with(s_next_x, "uly", 2)
    s_yx = swap_with(s_next_y, "uly", 1)
    dx_got = after(dx_got, s_next_x, s_next_y)
    block = (dp, share + 16, width)
    dh1, *rest_out = call(
        functools.partial(norm_backward_kernel, sizes),
        "norm_backward",
        scalars,
        [dh2, dx_own, dx_got, normed, inverse, mixer_all]
        + [vec, sums2]
        + [deb.reshape(uly, dp * unit), *o_cols],
        [whole(square)] * 4
        + [whole((rows, 1)), whole((width, width)), whole(vec.shape), whole(sums2.shape)]
        + [whole((uly, dp * unit))]
        + [whole((rows, group))] * uly,
        [jax.ShapeDtypeStruct(square, F32)]
        + [jax.ShapeDtypeStruct((rows, group), BF16)] * uly
        + [jax.ShapeDtypeStruct(block, BF16)] * 2,
        [whole(square)] + [whole((rows, group))] * uly + [whole(block)] * 2,
        [pltpu.VMEM((group, width), BF16)],
        (1,),
        4 * rows * width * width,
        16,
    )
    douts = [rest_out[0]] + [swap_with(rest_out[j], "uly", j) for j in range(1, uly)]
    m_keep, m_send = rest_out[uly:]

    def quarter(j, so_far, *deps):
        dout = after(douts[j], *deps)
        return attend_grad(q, kvs, [dout], [outs[j]], lse, heads, j, so_far)

    s_xy, s_yx = after((s_xy, s_yx), dh1)
    m_got = swap_with(m_send, "blk", 1)
    dq_0, dkvs = quarter(0, [], s_xy, s_yx)

    m_got, e_far_x, e_far_y, *douts[1:] = after((m_got, e_far_x, e_far_y, *douts[1:]), dq_0)
    half_block = pl.BlockSpec((1, 2 * unit, width), lambda *_: (0, 0, 0))
    packed = (2, unit + share + 16, width)
    p_near, p_far = call(
        pack_kernel,
        "pack",
        scalars,
        [s_near_x, s_x, s_xy, s_near_y, s_y, s_yx, m_keep, m_got],
        [half_block, half_block, whole(s_xy.shape)] * 2 + [whole(m_keep.shape)] * 2,
        [jax.ShapeDtypeStruct(packed, BF16)] * 2,
        [whole(packed)] * 2,
        [],
        (1,),
        10**6,
        16,
    )
    e_x = swap_with(e_far_x, "uly", 1)
    e_y = swap_with(e_far_y, "uly", 2)
    p_one = swap_with(p_far, "dp", 1)
    dq_1, dkvs = quarter(1, dkvs, p_near, *douts[2:])
    dq_2, dkvs = quarter(2, dkvs)

    e_x, e_y, p_one = after((e_x, e_y, p_one), dq_2)
    e_next_x = add(e_near_x[1], e_x[1])
    e_next_y = add(e_near_y[1], e_y[1])
    e_xy = swap_with(e_next_x, "uly", 2)
    e_yx = swap_with(e_next_y, "uly", 1)
    p_next = add(p_near[1], p_one[1])
    p_two = swap_with(p_next, "dp", 2)
    dq_3, dkvs = quarter(3, dkvs, e_next_x, e_next_y, p_next)

    dkv_got = swap_with(after(dkvs[1], e_xy, e_yx, p_two), "blk", 1)
    e_xy, e_yx, p_two = after((e_xy, e_yx, p_two), dq_3)
    p_own = add(p_near[0], p_one[0], p_two)
    pair = (2, shard, dp * unit)
    e_near = add(e_near_x[0], e_x[0], e_xy).reshape(pair)
    e_far = add(e_near_y[0], e_y[0], e_yx).reshape(pair)
    p_plane = [p_own] + [swap_with(p_own, "uly", j) for j in range(1, uly)]
    e_one = swap_with(e_far, "dp", 1)
    dkv_got = after(dkv_got, p_own, e_near, e_far)
    dqs = [dq_0, dq_1, dq_2, dq_3]
    dproj, a_keep, a_send = call(
        functools.partial(project_grad_kernel, (uly, dp, group)),
        "project_grad",
        scalars,
        [*dqs, dkvs[0], dkv_got, *xs],
        [whole(dq_0.shape)] * uly + [whole(kv.shape)] * 2 + [whole(square)] * uly,
        [
            jax.ShapeDtypeStruct((block_rows, cols), BF16),
            jax.ShapeDtypeStruct((dp, share + 16, 3 * group), BF16),
            jax.ShapeDtypeStruct((dp, share + 16, 3 * group), BF16),
        ],
        [whole((block_rows, cols))] + [whole((dp, share + 16, 3 * group))] * 2,
        [],
        (1,),
        2 * block_rows * width * cols,
        16,
    )
    a_got = swap_with(after(a_send, e_one), "blk", 1)
    e_one = after(e_one, dproj)
    e_next = add(e_near[1], e_one[1])
    e_two = swap_with(e_next, "dp", 2)
    token_parts = call(
        functools.partial(token_grad_kernel, uly),
        "token_grad",
        scalars,
        [after(dproj, e_next), w_own, dh1],
        [whole((block_rows, cols)), whole((width, cols)), whole(square)],
        [jax.ShapeDtypeStruct(square, F32)] + [jax.ShapeDtypeStruct(square, BF16)] * (uly - 1),
        [whole(square)] * uly,
        [],
        (1,),
        2 * block_rows * width * cols,
        16,
    )

    def in_plane(own, *deps):
        own = after(own, *deps)
        return [own] + [swap_with(own, "uly", j) for j in range(1, uly)]

    def both_cores(pieces, *deps):
        return pieces + [swap_with(after(piece, *deps), "blk", 1) for piece in pieces]

    a_got = after(a_got, token_parts[0])
    a_near, a_far = add(a_keep[:2], a_got[:2]), add(a_keep[2:], a_got[2:])
    a_one = swap_with(a_far, "dp", 1)
    token_parts = after(token_parts, a_near, a_far, *p_plane)
    token_got = [swap_with(token_parts[j], "uly", j) for j in range(1, uly)]
    a_next = add(a_near[1], a_one[1])
    a_two = swap_with(a_next, "dp", 2)
    p_plane = both_cores(p_plane, a_near)
    shrink_out, mixer_out, vecs = call(
        functools.partial(finish_shrink_kernel, (uly, unit)),
        "finish_shrink",
        scalars,
        p_plane,
        [whole(p_own.shape)] * parts,
        [
            jax.ShapeDtypeStruct((hidden // dp, width), F32),
            jax.ShapeDtypeStruct((shard, width), F32),
            jax.ShapeDtypeStruct((16, width), F32),
        ],
        [
            pl.BlockSpec((unit, width), lambda t, s: ((s[0] * uly + s[1]) ^ t, 0)),
            whole((shard, width)),
            whole((16, width)),
        ],
        [],
        (parts,),
        10**6,
        16,
    )
    e_own = add(e_near[0], e_one[0], e_two)
    e_plane = in_plane(e_own, shrink_out, *token_got)
    tokens_grad = total([token_parts[0], *token_got])
    a_own = add(a_near[0], a_one[0], a_two)
    a_plane = in_plane(a_own, *token_got)
    e_plane = both_cores(e_plane)
    expand_out = call(
        functools.partial(finish_expand_kernel, sizes),
        "finish_expand",
        scalars,
        e_plane,
        [whole(e_own.shape)] * parts,
        jax.ShapeDtypeStruct((shard, hidden), F32),
        pl.BlockSpec((shard, width), lambda t, s: (0, t)),
        [pltpu.VMEM((width, width), BF16)],
        (dp,),
        10**9,
        16,
    )
    a_plane = both_cores(a_plane, expand_out)
    attend_out, biases = call(
        functools.partial(finish_attend_kernel, uly),
        "finish_attend",
        scalars,
        a_plane,
        [whole(a_own.shape)] * parts,
        [jax.ShapeDtypeStruct((shard, 3 * width), F32), jax.ShapeDtypeStruct((8, 3 * group), F32)],
        [whole((shard, 3 * width)), whole((8, 3 * group))],
        [],
        (1,),
        10**9,
        16,
    )
    eb_out = vecs[8 : 8 + parts, :unit].reshape(-1)
    vecs = [vecs[k, :shard] for k in range(6)]
    return (
        mixed.reshape(tokens.shape),
        tokens_grad.reshape(tokens.shape),
        attend_out,
        biases[0, :group],
        biases[0, 2 * group :],
        mixer_out,
        vecs[0],
        vecs[1],
        vecs[2],
        expand_out,
        eb_out,
        shrink_out,
        vecs[3],
        vecs[4],
        vecs[5],
    )


def solution(mesh):
    row_spec = P("dp", ("blk", "uly"), None)
    matrix = P("dp", None)
    vector = P("dp")
    return jax.shard_map(
        on_device,
        mesh=mesh,
        in_specs=(
            row_spec,
            vector,
            row_spec,
            matrix,
            vector,
            vector,
            matrix,
            vector,
            vector,
            vector,
            matrix,
            vector,
            matrix,
            vector,
            vector,
            vector,
        ),
        out_specs=(
            row_spec,
            row_spec,
            matrix,
            vector,
            vector,
            matrix,
            vector,
            vector,
            vector,
            matrix,
            vector,
            matrix,
            vector,
            vector,
            vector,
        ),
        check_vma=False,
    )
```

```python
import functools

import jax
import jax.numpy as jnp
from jax import lax
from jax.experimental import pallas as pl
from jax.experimental.pallas import tpu as pltpu
from jax.sharding import PartitionSpec as P

HEADS = 12
HD = 64

EPSILON = 1e-12
MASKED = -1000000000.0
LOG2E = 1.4426950408889634
LN2 = 0.6931471805599453
F32 = jnp.float32
BF16 = jnp.bfloat16


def dot_nn(left, right):
    return lax.dot_general(left, right, (((1,), (0,)), ((), ())), preferred_element_type=F32)


def dot_nt(left, right):
    return lax.dot_general(left, right, (((1,), (1,)), ((), ())), preferred_element_type=F32)


def dot_tn(left, right):
    return lax.dot_general(left, right, (((0,), (0,)), ((), ())), preferred_element_type=F32)


def swap_with(value, axis, offset):
    size = lax.axis_size(axis)
    return lax.ppermute(value, axis, [(i, i ^ offset) for i in range(size)])


def xor_order(pieces, index):
    bit = 1
    while bit < len(pieces):
        flag = (index & bit) != 0
        pieces = [jnp.where(flag, pieces[p ^ bit], pieces[p]) for p in range(len(pieces))]
        bit *= 2
    return pieces


def total(values):
    acc = values[0].astype(F32)
    for value in values[1:]:
        acc = acc + value.astype(F32)
    return acc


def pad_rows(value, rows):
    return jnp.pad(value, ((0, rows - value.shape[0]), (0, 0)))


def head_lanes(width, head, ones_lane=None):
    lane = lax.broadcasted_iota(jnp.int32, (1, width), 1)
    keep = (lane >= head * HD) & (lane < (head + 1) * HD)
    if ones_lane is not None:
        keep = keep | (lane == ones_lane)
    return keep


def attend_forward_kernel(heads, blocks, q_ref, *refs):
    kv_refs = refs[:blocks]
    o_ref, lse_ref, vt_ref = refs[blocks:]
    group = heads * HD
    wide = q_ref.shape[1]
    rows = kv_refs[0].shape[0]

    @pl.when(pl.program_id(0) == 0)
    def _():
        for i in range(blocks):
            vt_ref[:, i * rows : (i + 1) * rows] = kv_refs[i][:, wide : wide + group].T

    q = q_ref[...]
    outs = []
    stats = []
    for head in range(heads):
        q_head = jnp.where(head_lanes(wide, head, group), q, jnp.zeros_like(q))
        scores = [dot_nt(kv_refs[i][:, :wide], q_head) for i in range(blocks)]
        top = jnp.max(scores[0], axis=0, keepdims=True)
        for i in range(1, blocks):
            top = jnp.maximum(top, jnp.max(scores[i], axis=0, keepdims=True))
        norm = jnp.zeros_like(top)
        acc = None
        for i in range(blocks):
            probs = jnp.exp2(scores[i] - top)
            norm = norm + jnp.sum(probs, axis=0, keepdims=True)
            part = dot_nn(
                vt_ref[head * HD : (head + 1) * HD, i * rows : (i + 1) * rows], probs.astype(BF16)
            )
            acc = part if acc is None else acc + part
        outs.append(acc / norm)
        stats.append(top + jnp.log2(norm))
    o_ref[...] = jnp.concatenate(outs, axis=0).T.astype(BF16)
    for head in range(heads):
        lse_ref[head : head + 1, :] = stats[head]


def attend_forward(q, kvs, heads, tile):
    rows, wide = q.shape
    group = heads * HD
    blocks = len(kvs)
    keys = blocks * rows
    whole = pl.BlockSpec(kvs[0].shape, lambda t: (0, 0))
    return pl.pallas_call(
        functools.partial(attend_forward_kernel, heads, blocks),
        grid=(rows // tile,),
        in_specs=[pl.BlockSpec((tile, wide), lambda t: (t, 0))] + [whole] * blocks,
        out_specs=[
            pl.BlockSpec((tile, group), lambda t: (t, 0)),
            pl.BlockSpec((8, tile), lambda t: (0, t)),
        ],
        out_shape=[
            jax.ShapeDtypeStruct((rows, group), BF16),
            jax.ShapeDtypeStruct((8, rows), F32),
        ],
        scratch_shapes=[pltpu.VMEM((group, keys), BF16)],
        compiler_params=pltpu.CompilerParams(vmem_limit_bytes=56 * 2**20),
        cost_estimate=pl.CostEstimate(
            flops=4 * heads * rows * keys * wide,
            transcendentals=heads * rows * keys,
            bytes_accessed=2 * rows * wide * 3 + 2 * keys * (wide + group),
        ),
        name="attend_forward",
    )(q, *kvs)


def attend_backward_kernel(heads, blocks, q_ref, do_ref, o_ref, lse_ref, *refs):
    kv_refs = refs[:blocks]
    dq_ref = refs[blocks]
    dkv_refs = refs[blocks + 1 : 2 * blocks + 1]
    kt_ref = refs[2 * blocks + 1]
    dk_accs = refs[2 * blocks + 2 : 3 * blocks + 2]
    dv_accs = refs[3 * blocks + 2 :]
    group = heads * HD
    wide = q_ref.shape[1]
    rows = kv_refs[0].shape[0]

    @pl.when(pl.program_id(0) == 0)
    def _():
        for i in range(blocks):
            kt_ref[:, i * rows : (i + 1) * rows] = kv_refs[i][:, :group].T
            dk_accs[i][...] = jnp.zeros_like(dk_accs[i])
            dv_accs[i][...] = jnp.zeros_like(dv_accs[i])

    q = q_ref[...]
    dout = do_ref[...]
    products = (dout.astype(F32) * o_ref[...].astype(F32)).T
    dqs = []
    for head in range(heads):
        q_head = jnp.where(head_lanes(wide, head, group), q, jnp.zeros_like(q))
        do_head = jnp.where(head_lanes(group, head), dout, jnp.zeros_like(dout))
        lse = lse_ref[head : head + 1, :]
        delta = jnp.sum(products[head * HD : (head + 1) * HD], axis=0, keepdims=True)
        acc = None
        for i in range(blocks):
            probs = jnp.exp2(dot_nt(kv_refs[i][:, :wide], q_head) - lse)
            dv_accs[i][...] += dot_nn(probs.astype(BF16), do_head)
            grads = dot_nt(kv_refs[i][:, wide : wide + group], do_head)
            grads = (probs * (grads - delta)).astype(BF16)
            dk_accs[i][...] += dot_nn(grads, q_head)
            part = dot_nn(
                kt_ref[head * HD : (head + 1) * HD, i * rows : (i + 1) * rows], grads
            )
            acc = part if acc is None else acc + part
        dqs.append(acc)
    dq_ref[...] = jnp.concatenate(dqs, axis=0).T.astype(BF16)

    @pl.when(pl.program_id(0) == pl.num_programs(0) - 1)
    def _():
        for i in range(blocks):
            dkv_refs[i][:, :group] = (dk_accs[i][:, :group] * LN2).astype(BF16)
            dkv_refs[i][:, wide : wide + group] = dv_accs[i][...].astype(BF16)


def attend_backward(q, kvs, dout, o, lse, heads, tile):
    rows, wide = q.shape
    group = heads * HD
    blocks = len(kvs)
    keys = blocks * rows
    whole = pl.BlockSpec(kvs[0].shape, lambda t: (0, 0))
    out = pl.pallas_call(
        functools.partial(attend_backward_kernel, heads, blocks),
        grid=(rows // tile,),
        in_specs=[
            pl.BlockSpec((tile, wide), lambda t: (t, 0)),
            pl.BlockSpec((tile, group), lambda t: (t, 0)),
            pl.BlockSpec((tile, group), lambda t: (t, 0)),
            pl.BlockSpec((8, tile), lambda t: (0, t)),
        ]
        + [whole] * blocks,
        out_specs=[pl.BlockSpec((tile, group), lambda t: (t, 0))] + [whole] * blocks,
        out_shape=[jax.ShapeDtypeStruct((rows, group), BF16)]
        + [jax.ShapeDtypeStruct(kvs[0].shape, BF16)] * blocks,
        scratch_shapes=[pltpu.VMEM((group, keys), BF16)]
        + [pltpu.VMEM((rows, wide), F32)] * blocks
        + [pltpu.VMEM((rows, group), F32)] * blocks,
        compiler_params=pltpu.CompilerParams(vmem_limit_bytes=56 * 2**20),
        cost_estimate=pl.CostEstimate(
            flops=10 * heads * rows * keys * wide,
            transcendentals=heads * rows * keys,
            bytes_accessed=2 * rows * wide * 4 + 4 * keys * (wide + group),
        ),
        name="attend_backward",
    )(q, dout, o, lse, *kvs)
    return out[0], out[1:]


def feed_kernel(
    x1_ref,
    x1b_ref,
    expand_ref,
    shrink_ref,
    ebias_ref,
    sbias_ref,
    gain_ref,
    shift_ref,
    cot_ref,
    mixed_ref,
    dx1_ref,
    dexpand_ref,
    dshrink_ref,
    debias_ref,
    vec_ref,
    act_ref,
    slope_ref,
    acc_ref,
    d2b_ref,
    x1t_ref,
):
    phase = pl.program_id(0)
    step = pl.program_id(1)
    last = pl.num_programs(1) - 1
    width = x1_ref.shape[1]

    @pl.when(phase == 0)
    def _():
        pre = dot_nn(x1b_ref[...], expand_ref[0]) + ebias_ref[0]
        cdf = 0.5 * (1.0 + lax.erf(pre * 0.7071067811865476))
        pdf = jnp.exp(-0.5 * pre * pre) * 0.3989422804014327
        act = (pre * cdf).astype(BF16)
        act_ref[step] = act
        slope_ref[step] = (cdf + pre * pdf).astype(BF16)
        part = dot_nn(act, shrink_ref[0])

        @pl.when(step == 0)
        def _():
            acc_ref[...] = part
            x1t_ref[...] = x1b_ref[...].T

        @pl.when(step > 0)
        def _():
            acc_ref[...] += part

        @pl.when(step == last)
        def _():
            hidden = x1_ref[...] + (acc_ref[...] + sbias_ref[...])
            center = hidden - jnp.mean(hidden, -1, keepdims=True)
            inverse = lax.rsqrt(jnp.mean(center * center, -1, keepdims=True) + EPSILON)
            normed = center * inverse
            mixed_ref[...] = (normed * gain_ref[...] + shift_ref[...]).astype(BF16)
            grad = cot_ref[...].astype(F32)
            scaled = grad * gain_ref[...]
            dhidden = inverse * (
                scaled
                - jnp.mean(scaled, -1, keepdims=True)
                - normed * jnp.mean(scaled * normed, -1, keepdims=True)
            )
            acc_ref[...] = dhidden
            d2b_ref[...] = dhidden.astype(BF16)
            vec_ref[...] = jnp.zeros_like(vec_ref)
            vec_ref[0:1, :] = jnp.sum(grad * normed, 0, keepdims=True)
            vec_ref[1:2, :] = jnp.sum(grad, 0, keepdims=True)
            vec_ref[2:3, :] = jnp.sum(dhidden, 0, keepdims=True)

    @pl.when(phase == 1)
    def _():
        d2b = d2b_ref[...]
        dpre = (dot_nt(d2b, shrink_ref[0]) * slope_ref[step].astype(F32)).astype(BF16)
        debias_ref[0] = jnp.sum(dpre.astype(F32), 0, keepdims=True)
        dexpand_ref[0] = dot_nn(x1t_ref[...], dpre).astype(BF16)
        dshrink_ref[0] = dot_tn(act_ref[step], d2b).astype(BF16)
        acc_ref[...] += dot_nt(dpre, expand_ref[0])

        @pl.when(step == last)
        def _():
            dx1_ref[...] = acc_ref[...]


def feed_forward_backward(x1, x1b, expand, shrink, ebias, sbias, gain, shift, cot):
    rows, width = x1.shape
    parts, _, block = expand.shape
    full = pl.BlockSpec((rows, width), lambda p, k: (0, 0))
    line = pl.BlockSpec((1, width), lambda p, k: (0, 0))
    return pl.pallas_call(
        feed_kernel,
        grid=(2, parts),
        in_specs=[
            full,
            full,
            pl.BlockSpec((1, width, block), lambda p, k: (k, 0, 0)),
            pl.BlockSpec((1, block, width), lambda p, k: (k, 0, 0)),
            pl.BlockSpec((1, 1, block), lambda p, k: (k, 0, 0)),
            line,
            line,
            line,
            full,
        ],
        out_specs=[
            full,
            full,
            pl.BlockSpec((1, width, block), lambda p, k: (p * k, 0, 0)),
            pl.BlockSpec((1, block, width), lambda p, k: (p * k, 0, 0)),
            pl.BlockSpec((1, 1, block), lambda p, k: (p * k, 0, 0)),
            pl.BlockSpec((8, width), lambda p, k: (0, 0)),
        ],
        out_shape=[
            jax.ShapeDtypeStruct((rows, width), BF16),
            jax.ShapeDtypeStruct((rows, width), F32),
            jax.ShapeDtypeStruct((parts, width, block), BF16),
            jax.ShapeDtypeStruct((parts, block, width), BF16),
            jax.ShapeDtypeStruct((parts, 1, block), F32),
            jax.ShapeDtypeStruct((8, width), F32),
        ],
        scratch_shapes=[
            pltpu.VMEM((parts, rows, block), BF16),
            pltpu.VMEM((parts, rows, block), BF16),
            pltpu.VMEM((rows, width), F32),
            pltpu.VMEM((rows, width), BF16),
            pltpu.VMEM((width, rows), BF16),
        ],
        compiler_params=pltpu.CompilerParams(vmem_limit_bytes=48 * 2**20),
        cost_estimate=pl.CostEstimate(
            flops=12 * rows * width * parts * block,
            transcendentals=2 * rows * parts * block,
            bytes_accessed=12 * width * parts * block,
        ),
        name="feed_forward_backward",
    )(x1, x1b, expand, shrink, ebias, sbias, gain, shift, cot)


def general_device(
    tokens,
    lengths,
    cotangent,
    attend_weight,
    query_bias,
    value_bias,
    mixer_weight,
    mixer_bias,
    attn_gain,
    attn_shift,
    expand_weight,
    expand_bias,
    shrink_weight,
    shrink_bias,
    final_gain,
    final_shift,
):
    uly = lax.axis_size("uly")
    blk = lax.axis_size("blk")
    dp = lax.axis_size("dp")
    u = lax.axis_index("uly")
    b = lax.axis_index("blk")
    z = lax.axis_index("dp")
    width = tokens.shape[-1]
    rows = tokens.shape[0] * tokens.shape[1]
    block_rows = uly * rows
    heads = HEADS // uly
    group = heads * HD
    wide = -(-(group + 1) // 128) * 128
    shard = attend_weight.shape[0]
    hidden = expand_weight.shape[1]
    parts = blk * uly
    unit = hidden // (parts * dp)
    share = shard // blk

    x = tokens.reshape(rows, width)
    x_rows = jnp.concatenate([x] + [swap_with(x, "uly", j) for j in range(1, uly)], 0)

    small = jnp.concatenate(
        [query_bias, value_bias, mixer_bias, attn_gain, attn_shift, shrink_bias]
        + [final_gain, final_shift, expand_bias]
    )
    small_rows = small.shape[0] // (3 * group)
    own_heads = lax.dynamic_slice_in_dim(attend_weight.reshape(shard, 3, uly, group), u, 1, 2)
    own_heads = own_heads.reshape(shard, 3 * group)
    first_piece = jnp.concatenate(
        [
            lax.dynamic_slice_in_dim(own_heads, b * share, share, 0),
            pad_rows(small.reshape(small_rows, 3 * group), 16),
        ]
    )
    first_all = lax.all_gather(first_piece, "dp", axis=0, tiled=False)
    halves = first_all[:, :share]
    halves = xor_order([halves] + [swap_with(halves, "blk", i) for i in range(1, blk)], b)
    attend_own = jnp.stack(halves, 1).reshape(width, 3, group)
    vectors = first_all[:, share : share + small_rows].reshape(dp, -1, shard).astype(F32)
    names = [vectors[:, k].reshape(width) for k in range(8)]
    bias_query, bias_value, bias_mixer, gain_attn, shift_attn, bias_shrink = names[:6]
    gain_final, shift_final = names[6:]
    bias_expand = vectors[:, 8:].reshape(dp, parts, unit).transpose(1, 0, 2)
    bias_expand = jnp.stack(
        xor_order(list(bias_expand.reshape(parts, dp * unit)), b * uly + u), 0
    ).reshape(parts, 1, dp * unit)

    mixer_own = lax.dynamic_slice_in_dim(mixer_weight, b * share, share, 0)
    mixer_all = jnp.stack(
        xor_order([mixer_own] + [swap_with(mixer_own, "dp", j) for j in range(1, dp)], z), 0
    )
    mixer_all = jnp.stack(
        xor_order([mixer_all] + [swap_with(mixer_all, "blk", i) for i in range(1, blk)], b), 1
    ).reshape(width, width)

    part = b * uly + u
    expand_own = lax.dynamic_slice_in_dim(
        expand_weight.reshape(shard, dp, parts, unit), part, 1, 2
    ).reshape(-1, width)
    shrink_own = lax.dynamic_slice_in_dim(shrink_weight.reshape(parts, unit, width), part, 1, 0)
    expand_rows = expand_own.shape[0]
    feed_own = jnp.concatenate([expand_own, shrink_own.reshape(unit, width)], 0)
    feed_all = lax.all_gather(feed_own, "dp", axis=0, tiled=False)
    expand_part = feed_all[:, :expand_rows].reshape(width, dp * unit)
    shrink_part = feed_all[:, expand_rows:].reshape(dp * unit, width)
    expand_two = jnp.stack([expand_part, swap_with(expand_part, "uly", 1)])
    shrink_two = jnp.stack([shrink_part, swap_with(shrink_part, "uly", 2)])
    expand_far = swap_with(expand_two, "uly", 2)
    shrink_far = swap_with(shrink_two, "uly", 1)
    expand_here = jnp.concatenate([expand_two, expand_far], 0)
    shrink_here = jnp.stack([shrink_two[0], shrink_far[0], shrink_two[1], shrink_far[1]], 0)
    expand_full = jnp.concatenate(
        [expand_here] + [swap_with(expand_here, "blk", i) for i in range(1, blk)], 0
    )
    shrink_full = jnp.concatenate(
        [shrink_here] + [swap_with(shrink_here, "blk", i) for i in range(1, blk)], 0
    )

    lane_pad = ((0, 0), (0, wide - group))
    bias_row = jnp.pad(lax.dynamic_slice_in_dim(bias_query, u * group, group, 0), lane_pad[1:])
    ones_lane = (jnp.arange(wide) == group).astype(F32)
    q = dot_nn(x_rows, jnp.pad(attend_own[:, 0], lane_pad)) + bias_row
    q = (q * (0.125 * LOG2E) + ones_lane).astype(BF16)
    kv_weight = jnp.concatenate([jnp.pad(attend_own[:, 1], lane_pad), attend_own[:, 2]], 1)
    kv_bias = jnp.concatenate(
        [jnp.zeros((wide,), F32), lax.dynamic_slice_in_dim(bias_value, u * group, group, 0)]
    )
    kv_ones = jnp.pad(ones_lane, (0, group))
    row_index = jnp.arange(block_rows, dtype=jnp.int32)
    positions = b * block_rows + ((row_index // rows) ^ u) * rows + row_index % rows
    key_mask = jnp.where(positions < lengths[0], 0.0, MASKED)
    kv = (dot_nn(x_rows, kv_weight) + kv_bias + key_mask[:, None] * kv_ones).astype(BF16)
    kvs = [kv] + [swap_with(kv, "blk", i) for i in range(1, blk)]

    o_rows, lse = attend_forward(q, kvs, heads, min(256, block_rows))
    pieces = [o_rows[j * rows : (j + 1) * rows] for j in range(uly)]
    pieces = [pieces[0]] + [swap_with(pieces[j], "uly", j) for j in range(1, uly)]
    mixer_in = jnp.concatenate(xor_order(pieces, u), 1)

    first_sum = x.astype(F32) + (dot_nn(mixer_in, mixer_all) + bias_mixer)
    center = first_sum - jnp.mean(first_sum, -1, keepdims=True)
    first_inv = lax.rsqrt(jnp.mean(center * center, -1, keepdims=True) + EPSILON)
    first_normed = center * first_inv
    first_out = first_normed * gain_attn + shift_attn
    first_low = first_out.astype(BF16)

    mixed, first_grad, expand_grad, shrink_grad, expand_bias_grad, vec_grads = (
        feed_forward_backward(
            first_out,
            first_low,
            expand_full,
            shrink_full,
            bias_expand,
            bias_shrink[None],
            gain_final[None],
            shift_final[None],
            cotangent.reshape(rows, width),
        )
    )

    scaled = first_grad * gain_attn
    attn_grad = first_inv * (
        scaled
        - jnp.mean(scaled, -1, keepdims=True)
        - first_normed * jnp.mean(scaled * first_normed, -1, keepdims=True)
    )
    attn_low = attn_grad.astype(BF16)
    out_grad = dot_nt(attn_low, mixer_all).astype(BF16)
    sends = xor_order([out_grad[:, j * group : (j + 1) * group] for j in range(uly)], u)
    dout_rows = jnp.concatenate(
        [sends[0]] + [swap_with(sends[j], "uly", j) for j in range(1, uly)], 0
    )
    dq, dkvs = attend_backward(q, kvs, dout_rows, o_rows, lse, heads, min(256, block_rows))

    mixer_grad = dot_tn(mixer_in, attn_low).astype(BF16)
    attn_gain_grad = jnp.sum(first_grad * first_normed, 0)
    attn_shift_grad = jnp.sum(first_grad, 0)
    mixer_bias_grad = jnp.sum(attn_grad, 0)
    ebg = jnp.stack(xor_order(list(expand_bias_grad.reshape(parts, dp * unit)), part), 0)
    ebg = ebg.reshape(parts, dp, unit).transpose(1, 0, 2).reshape(dp, parts * unit)
    vec_all = jnp.concatenate(
        [
            v.reshape(dp, shard)
            for v in (
                mixer_bias_grad,
                attn_gain_grad,
                attn_shift_grad,
                vec_grads[2],
                vec_grads[0],
                vec_grads[1],
            )
        ]
        + [ebg],
        1,
    ).astype(BF16)

    mixer_cols = width // blk
    mixer_part_rows = shard // uly
    vec_len = vec_all.shape[1]
    vec_rows = -(-vec_len // mixer_cols)
    vec_rows = -(-vec_rows // 16) * 16
    vec_block = jnp.pad(vec_all, ((0, 0), (0, vec_rows * mixer_cols - vec_len))).reshape(
        dp, vec_rows, mixer_cols
    )
    mixer_view = mixer_grad.reshape(dp, uly, mixer_part_rows, blk, mixer_cols)
    by_blk = xor_order([mixer_view[:, :, :, i] for i in range(blk)], b)
    mixer_parts = []
    for i in range(blk):
        by_uly = xor_order([by_blk[i][:, j] for j in range(uly)], u)
        mixer_parts.append(
            jnp.stack([jnp.concatenate([piece, vec_block], 1) for piece in by_uly], 0)
        )
    mixer_sum = total(
        [mixer_parts[0]] + [swap_with(mixer_parts[i], "blk", i) for i in range(1, blk)]
    ).astype(BF16)
    mixer_sum = total(
        [mixer_sum[0]] + [swap_with(mixer_sum[j], "uly", j) for j in range(1, uly)]
    ).astype(BF16)

    def over_blk(grad):
        return total(
            [grad[:uly]]
            + [swap_with(grad[i * uly : (i + 1) * uly], "blk", i) for i in range(1, blk)]
        ).astype(BF16)

    shrink_sum = over_blk(shrink_grad)
    expand_sum = over_blk(expand_grad)
    shrink_sum = shrink_sum.reshape(2, 2, dp * unit, width)
    expand_sum = expand_sum.reshape(2, 2, width, dp * unit)
    shrink_sum = total([shrink_sum[0], swap_with(shrink_sum[1], "uly", 2)]).astype(BF16)
    expand_sum = total([expand_sum[:, 0], swap_with(expand_sum[:, 1], "uly", 1)]).astype(BF16)
    shrink_sum = total([shrink_sum[0], swap_with(shrink_sum[1], "uly", 1)]).astype(BF16)
    expand_sum = total([expand_sum[0], swap_with(expand_sum[1], "uly", 2)]).astype(BF16)

    mixer_rows = mixer_sum.shape[1] * mixer_cols // width
    packed = jnp.concatenate(
        [
            expand_sum.reshape(dp, expand_rows, width),
            shrink_sum.reshape(dp, unit, width),
            mixer_sum.reshape(dp, mixer_rows, width),
        ],
        1,
    )

    def over_dp(value):
        sends = [lax.dynamic_slice_in_dim(value, z ^ j, 1, 0)[0] for j in range(dp)]
        return total([sends[0]] + [swap_with(sends[j], "dp", j) for j in range(1, dp)])

    owned = over_dp(packed)
    vec_owned = owned[expand_rows + unit :].reshape(-1, mixer_cols)[mixer_part_rows:]
    vec_owned = vec_owned.reshape(-1)[:vec_len]

    def in_plane(value):
        value = value.astype(BF16)
        value = jnp.stack(
            xor_order([value] + [swap_with(value, "uly", j) for j in range(1, uly)], u), 0
        )
        return jnp.stack(
            xor_order([value] + [swap_with(value, "blk", i) for i in range(1, blk)], b), 0
        )

    gathered = in_plane(owned).reshape(parts, -1, width)
    expand_out = gathered[:, :expand_rows].reshape(parts, shard, dp, unit)
    expand_out = expand_out.transpose(1, 2, 0, 3).reshape(shard, hidden).astype(F32)
    shrink_out = gathered[:, expand_rows : expand_rows + unit]
    shrink_out = shrink_out.reshape(parts * unit, width).astype(F32)
    mixer_out = gathered[:, expand_rows + unit :].reshape(blk, uly, -1, mixer_cols)
    mixer_out = mixer_out[:, :, :mixer_part_rows].transpose(1, 2, 0, 3)
    mixer_out = mixer_out.reshape(shard, width).astype(F32)

    own_dkv = total([dkvs[0]] + [swap_with(dkvs[i], "blk", i) for i in range(1, blk)])
    own_dkv = own_dkv.astype(BF16)
    proj_grad = jnp.concatenate(
        [dq * jnp.asarray(0.125, BF16), own_dkv[:, :group], own_dkv[:, wide : wide + group]], 1
    )
    token_parts = dot_nt(proj_grad, attend_own.reshape(width, 3 * group))
    token_low = token_parts.astype(BF16)
    tokens_grad = attn_grad + total(
        [token_parts[:rows]]
        + [swap_with(token_low[j * rows : (j + 1) * rows], "uly", j) for j in range(1, uly)]
    )
    attend_grad = dot_tn(x_rows, proj_grad).astype(BF16)
    attend_grad = attend_grad.reshape(dp, blk, share, 3 * group)
    bias_sum = jnp.sum(proj_grad.astype(F32), 0)[None]
    bias_rows = pad_rows(bias_sum.astype(BF16), 16)
    attend_parts = [
        jnp.concatenate(
            [
                lax.dynamic_slice_in_dim(attend_grad, b ^ i, 1, 1).reshape(-1, 3 * group),
                bias_rows,
            ],
            0,
        )
        for i in range(blk)
    ]
    attend_sum = total(
        [attend_parts[0]] + [swap_with(attend_parts[i], "blk", i) for i in range(1, blk)]
    ).astype(BF16)
    bias_half = jnp.broadcast_to(attend_sum[dp * share :], (dp, 16, 3 * group))
    attend_sum = attend_sum[: dp * share].reshape(dp, share, 3 * group)
    attend_owned = over_dp(jnp.concatenate([attend_sum, bias_half], 1))
    attend_all = in_plane(attend_owned)
    attend_out = attend_all[:, :, :share].reshape(blk, uly, share, 3, group)
    attend_out = attend_out.transpose(0, 2, 3, 1, 4).reshape(shard, 3 * width).astype(F32)
    bias_out = attend_all[0, :, share].astype(F32).reshape(uly, 3, group)
    query_bias_grad = lax.dynamic_slice_in_dim(bias_out[:, 0].reshape(width), z * shard, shard, 0)
    value_bias_grad = lax.dynamic_slice_in_dim(bias_out[:, 2].reshape(width), z * shard, shard, 0)

    vecs = [vec_owned[k * shard : (k + 1) * shard] for k in range(6)]
    return (
        mixed.reshape(tokens.shape),
        tokens_grad.reshape(tokens.shape),
        attend_out,
        query_bias_grad,
        value_bias_grad,
        mixer_out,
        vecs[0],
        vecs[1],
        vecs[2],
        expand_out,
        vec_owned[6 * shard :],
        shrink_out,
        vecs[3],
        vecs[4],
        vecs[5],
    )


def call(
    kernel,
    name,
    scalars,
    args,
    in_specs,
    out_shape,
    out_specs,
    scratch,
    grid,
    flops,
    vmem,
    aliases={},
):
    return pl.pallas_call(
        kernel,
        grid_spec=pltpu.PrefetchScalarGridSpec(
            num_scalar_prefetch=1,
            grid=grid,
            in_specs=in_specs,
            out_specs=out_specs,
            scratch_shapes=scratch,
        ),
        out_shape=out_shape,
        compiler_params=pltpu.CompilerParams(vmem_limit_bytes=vmem * 2**20),
        input_output_aliases=aliases,
        cost_estimate=pl.CostEstimate(flops=flops, bytes_accessed=1, transcendentals=0),
        name=name,
    )(scalars, *args)


def whole(shape):
    return pl.BlockSpec(shape, lambda *_: (0,) * len(shape))


def after(value, *deps):
    return lax.optimization_barrier((value, *deps))[0]


def slot(offset):
    return (offset & 1) * 2 + (offset >> 1)


def one_hot(rows, cols, row_offset=0, col_offset=0):
    row = lax.broadcasted_iota(jnp.int32, (rows, cols), 0) + row_offset
    col = lax.broadcasted_iota(jnp.int32, (rows, cols), 1) + col_offset
    return jnp.where(row == col, 1.0, 0.0).astype(BF16)


def fetch_kernel(sizes, idx, attend_ref, expand_ref, shrink_ref, mixer_ref, *refs):
    uly, dp, group, unit = sizes
    vec_refs, (first_ref, feed_ref) = refs[:-2], refs[-2:]
    share = attend_ref.shape[1]
    shard, width = mixer_ref.shape
    u = idx[1]
    part = idx[0] * uly + u
    take = one_hot(width, group, 0, u * group)
    for c in range(3):
        cols = dot_nn(attend_ref[0, :, c * width : (c + 1) * width], take)
        first_ref[:share, c * group : (c + 1) * group] = cols.astype(BF16)
    first_ref[share:, :] = jnp.zeros_like(first_ref[share:, :])
    rows = share // dp
    mixer = dot_nn(one_hot(rows, shard, part * rows, 0), mixer_ref[...]).astype(BF16)
    for k in range(dp):
        here = slice(k * rows, (k + 1) * rows)
        first_ref[here, 3 * group :] = mixer[:, k * group : (k + 1) * group]
    line = share
    for ref in vec_refs:
        for k in range(ref.shape[0] // shard):
            first_ref[line : line + 1, :shard] = ref[k * shard : (k + 1) * shard].reshape(1, shard)
            line += 1
    take = one_hot(width, unit, 0, part * unit)
    half = shard // 2
    for k in range(dp):
        cols = dot_nn(expand_ref[:, k * width : (k + 1) * width], take).astype(BF16)
        feed_ref[:half, k * unit : (k + 1) * unit] = cols[:half]
        feed_ref[:half, (dp + k) * unit : (dp + k + 1) * unit] = cols[half:]
    feed_ref[half:, :] = shrink_ref[0]


def project_kernel(sizes, idx, *refs):
    uly, blk, dp, group, unit = sizes
    x_refs, refs = refs[:uly], refs[uly:]
    mine_refs, refs = refs[:dp], refs[dp:]
    other_refs, refs = refs[:dp], refs[dp:]
    w_ref, q_ref, kv_ref, vec_ref, eb_ref, mixer_ref = refs
    b, u, z, length = idx[0], idx[1], idx[2], idx[3]
    rows, width = x_refs[0].shape
    wide = q_ref.shape[1]
    pad = wide - group
    share = mine_refs[0].shape[0] - 16
    shard = 2 * share
    parts = uly * blk
    for c in range(3):
        w_ref[:, c * wide + group : (c + 1) * wide] = jnp.zeros((width, pad), BF16)
    own_vec = jnp.zeros((16, shard), F32)
    all_vec = jnp.zeros((16, width), F32)
    lines = share // dp
    for j in range(dp):
        for k in range(dp):
            mixer_ref[j * lines : (j + 1) * lines, k * group : (k + 1) * group] = mine_refs[j][
                k * lines : (k + 1) * lines, 3 * group :
            ]
        for ref, core in ((mine_refs[j], b), (other_refs[j], 1 - b)):
            start = pl.multiple_of((z ^ j) * shard + core * share, share)
            for c in range(3):
                w_ref[pl.ds(start, share), c * wide : c * wide + group] = ref[
                    :share, c * group : (c + 1) * group
                ]
        vec = mine_refs[j][share:, :shard]
        own_vec += jnp.where((z ^ j) == u, 1.0, 0.0) * vec.astype(F32)
        all_vec += dot_nn(vec, one_hot(shard, width, (z ^ j) * shard, 0))
    vec_ref[...] = all_vec

    low = all_vec.astype(BF16)
    part = b * uly + u
    eb = jnp.zeros((parts, dp * unit), F32)
    for parity in range(2):
        col = lax.broadcasted_iota(jnp.int32, (width, dp * unit), 1)
        row = lax.broadcasted_iota(jnp.int32, (width, dp * unit), 0)
        source = col + (col // unit) * (shard - unit) + parity * unit
        lanes = dot_nn(low, jnp.where(row == source, 1.0, 0.0).astype(BF16)).astype(BF16)
        owner = lax.broadcasted_iota(jnp.int32, (parts, 16), 0) ^ part
        line = lax.broadcasted_iota(jnp.int32, (parts, 16), 1)
        wanted = ((owner & 1) == parity) & (line == 8 + (owner >> 1))
        eb += dot_nn(jnp.where(wanted, 1.0, 0.0).astype(BF16), lanes)
    eb_ref[...] = eb

    lane = lax.broadcasted_iota(jnp.int32, (1, wide), 1)
    mark = jnp.where(lane == group, 1.0, 0.0)
    zeros = jnp.zeros((1, pad), F32)
    q_bias = jnp.concatenate([own_vec[0:1], zeros], 1)
    v_bias = jnp.concatenate([own_vec[1:2], zeros], 1)
    for j in range(uly):
        x = x_refs[j][...]
        here = slice(j * rows, (j + 1) * rows)
        q = dot_nn(x, w_ref[:, :wide]) + q_bias
        q_ref[here, :] = (q * (0.125 * LOG2E) + mark).astype(BF16)
        first = (b * uly + (u ^ j)) * rows
        position = lax.broadcasted_iota(jnp.int32, (rows, 1), 0) + first
        masked = jnp.where(position < length, 0.0, MASKED)
        k = dot_nn(x, w_ref[:, wide : 2 * wide]) + masked * mark
        kv_ref[here, :wide] = k.astype(BF16)
        kv_ref[here, wide:] = (dot_nn(x, w_ref[:, 2 * wide :]) + v_bias).astype(BF16)


def attend_kernel(heads, blocks, q_ref, *refs):
    kv_refs = refs[:blocks]
    o_refs = refs[blocks:-2]
    lse_ref, vt_ref = refs[-2:]
    group = heads * HD
    wide = q_ref.shape[1]
    rows = kv_refs[0].shape[0]

    @pl.when(pl.program_id(0) == 0)
    def _():
        for i in range(blocks):
            vt_ref[:, i * rows : (i + 1) * rows] = kv_refs[i][:, wide : wide + group].T

    q = q_ref[...]
    outs = []
    for head in range(heads):
        q_head = jnp.where(head_lanes(wide, head, group), q, jnp.zeros_like(q))
        scores = [dot_nt(kv_refs[i][:, :wide], q_head) for i in range(blocks)]
        top = jnp.max(scores[0], axis=0, keepdims=True)
        for i in range(1, blocks):
            top = jnp.maximum(top, jnp.max(scores[i], axis=0, keepdims=True))
        norm = jnp.zeros_like(top)
        acc = None
        for i in range(blocks):
            probs = jnp.exp2(scores[i] - top)
            norm = norm + jnp.sum(probs, axis=0, keepdims=True)
            part = dot_nn(
                vt_ref[head * HD : (head + 1) * HD, i * rows : (i + 1) * rows], probs.astype(BF16)
            )
            acc = part if acc is None else acc + part
        outs.append(acc / norm)
        lse_ref[head : head + 1, :] = top + jnp.log2(norm)
    out = jnp.concatenate(outs, axis=0).T.astype(BF16)
    for j, o_ref in enumerate(o_refs):

        @pl.when(pl.program_id(0) == j)
        def _(o_ref=o_ref):
            o_ref[...] = out


def attend(q, kvs, heads, pieces):
    rows, wide = q.shape
    tile = rows // pieces
    group = heads * HD
    blocks = len(kvs)
    keys = blocks * rows
    out = pl.pallas_call(
        functools.partial(attend_kernel, heads, blocks),
        grid=(pieces,),
        in_specs=[pl.BlockSpec((tile, wide), lambda t: (t, 0))] + [whole(kvs[0].shape)] * blocks,
        out_specs=[whole((tile, group))] * pieces + [pl.BlockSpec((8, tile), lambda t: (0, t))],
        out_shape=[jax.ShapeDtypeStruct((tile, group), BF16)] * pieces
        + [jax.ShapeDtypeStruct((8, rows), F32)],
        scratch_shapes=[pltpu.VMEM((group, keys), BF16)],
        compiler_params=pltpu.CompilerParams(vmem_limit_bytes=16 * 2**20),
        cost_estimate=pl.CostEstimate(
            flops=4 * heads * rows * keys * wide,
            transcendentals=heads * rows * keys,
            bytes_accessed=2 * rows * wide * 3 + 2 * keys * (wide + group),
        ),
        name="attend",
    )(q, *kvs)
    return out[:-1], out[-1]


def first_norm_kernel(uly, idx, x_ref, *refs):
    o_refs = refs[:uly]
    m_ref, vec_ref, x1_ref, x1b_ref, normed_ref, inverse_ref = refs[uly:]
    group = o_refs[0].shape[1]
    acc = vec_ref[2:3, :]
    for j in range(uly):
        start = pl.multiple_of((idx[1] ^ j) * group, group)
        acc = acc + dot_nn(o_refs[j][...], m_ref[pl.ds(start, group), :])
    hidden = x_ref[...].astype(F32) + acc
    center = hidden - jnp.mean(hidden, -1, keepdims=True)
    inverse = lax.rsqrt(jnp.mean(center * center, -1, keepdims=True) + EPSILON)
    normed = center * inverse
    out = normed * vec_ref[3:4, :] + vec_ref[4:5, :]
    x1_ref[...] = out
    x1b_ref[...] = out.astype(BF16)
    normed_ref[...] = normed
    inverse_ref[...] = inverse


def rest_kernel(sizes, idx, expand_ref, shrink_ref, out_ref):
    uly, dp, unit = sizes
    width = shrink_ref.shape[1]
    half = expand_ref.shape[0] // 2
    for j in range(1, uly):
        part = idx[0] * uly + (idx[1] ^ j)
        take = one_hot(width, unit, 0, part * unit)
        for k in range(dp):
            cols = dot_nn(expand_ref[:, k * width : (k + 1) * width], take).astype(BF16)
            out_ref[j - 1, :half, k * unit : (k + 1) * unit] = cols[:half]
            out_ref[j - 1, :half, (dp + k) * unit : (dp + k + 1) * unit] = cols[half:]
        start = pl.multiple_of(part * unit, unit)
        out_ref[j - 1, half:, :] = shrink_ref[pl.ds(start, unit), :]


def mixer_kernel(sizes, idx, *refs):
    uly, dp = sizes
    pieces, (m_ref, turn_ref) = refs[:-2], refs[-2:]
    lines = pieces[0].shape[0] // dp
    b, u, z = idx[0], idx[1], idx[2]
    shard = 2 * uly * lines
    for k in range(dp):
        for p, ref in enumerate(pieces):
            part = (b * uly + u) ^ p
            turn_ref[pl.ds(pl.multiple_of(part * lines, 8), lines), :] = ref[
                k * lines : (k + 1) * lines, :
            ].astype(F32)
        start = pl.multiple_of((z ^ k) * shard, shard)
        m_ref[pl.ds(start, shard), :] = turn_ref[...].astype(BF16)


def assemble_kernel(sizes, k, idx, *refs):
    uly, dp, unit = sizes
    e_ref, s_ref, sem = refs[-3:]
    block = dp * unit
    shard = e_ref.shape[0] // dp
    half = shard // 2
    owner = idx[2] ^ k
    copies = []
    for j in range(uly):
        if k == 0:
            piece = refs[0] if j == 0 else refs[1].at[j - 1]
        else:
            piece = refs[2 + j]
        for h in range(2):
            start = pl.multiple_of(owner * shard + h * half, half)
            copies.append(
                pltpu.make_async_copy(
                    piece.at[pl.ds(0, half), pl.ds(h * block, block)],
                    e_ref.at[pl.ds(start, half), pl.ds(j * block, block)],
                    sem.at[3 * j + h],
                )
            )
        start = pl.multiple_of(j * block + owner * unit, unit)
        copies.append(
            pltpu.make_async_copy(
                piece.at[pl.ds(half, unit), :], s_ref.at[pl.ds(start, unit), :], sem.at[3 * j + 2]
            )
        )
    for copy in copies:
        copy.start()
    for copy in copies:
        copy.wait()


def assemble(scalars, sizes, k, weights, pieces):
    uly, dp, unit = sizes
    width = pieces[0].shape[1]
    block = uly * dp * unit
    hbm = pl.BlockSpec(memory_space=pl.ANY)
    return call(
        functools.partial(assemble_kernel, sizes, k),
        "assemble",
        scalars,
        [*weights, *pieces],
        [hbm] * (len(weights) + len(pieces)),
        [jax.ShapeDtypeStruct((width, block), BF16), jax.ShapeDtypeStruct((block, width), BF16)],
        [hbm] * 2,
        [pltpu.SemaphoreType.DMA((3 * uly,))],
        (1,),
        10**6,
        16,
        {1: 0, 2: 1} if weights else {},
    )


def feed_forward_kernel(uly, idx, mine_ref, other_ref, eb_ref, e_ref, s_ref, *refs):
    act_ref, slope_ref, y_ref, send_ref, x_ref = refs
    rows = mine_ref.shape[0]
    block = e_ref.shape[1] // uly
    x_ref[:rows] = mine_ref[...]
    x_ref[rows:] = other_ref[...]
    for j in range(uly):
        lanes = slice(j * block, (j + 1) * block)
        pre = dot_nn(x_ref[...], e_ref[:, lanes]) + eb_ref[j : j + 1, :]
        cdf = 0.5 * (1.0 + lax.erf(pre * 0.7071067811865476))
        pdf = jnp.exp(-0.5 * pre * pre) * 0.3989422804014327
        act_ref[:, lanes] = (pre * cdf).astype(BF16)
        slope_ref[:, lanes] = (cdf + pre * pdf).astype(BF16)
    out = dot_nn(act_ref[...], s_ref[...])
    y_ref[...] = out[:rows]
    send_ref[...] = out[rows:].astype(BF16)


def feed_forward(scalars, uly, mine, other, eb, weights):
    rows, width = mine.shape
    block = weights[0].shape[1]
    args = [mine, other, eb, *weights]
    return call(
        functools.partial(feed_forward_kernel, uly),
        "feed_forward",
        scalars,
        args,
        [whole(arg.shape) for arg in args],
        [
            jax.ShapeDtypeStruct((2 * rows, block), BF16),
            jax.ShapeDtypeStruct((2 * rows, block), BF16),
            jax.ShapeDtypeStruct((rows, width), F32),
            jax.ShapeDtypeStruct((rows, width), BF16),
        ],
        [whole((2 * rows, block))] * 2 + [whole((rows, width))] * 2,
        [pltpu.VMEM((2 * rows, width), BF16)],
        (1,),
        8 * rows * width * block,
        24,
    )


def final_norm_kernel(idx, x1_ref, y_ref, got_ref, vec_ref, cot_ref, *refs):
    mixed_ref, dh_ref, low_ref, sums_ref = refs
    hidden = x1_ref[...] + (y_ref[...] + got_ref[...].astype(F32) + vec_ref[5:6, :])
    gain = vec_ref[6:7, :]
    center = hidden - jnp.mean(hidden, -1, keepdims=True)
    inverse = lax.rsqrt(jnp.mean(center * center, -1, keepdims=True) + EPSILON)
    normed = center * inverse
    mixed_ref[...] = (normed * gain + vec_ref[7:8, :]).astype(BF16)
    grad = cot_ref[...].astype(F32)
    scaled = grad * gain
    dhidden = inverse * (
        scaled
        - jnp.mean(scaled, -1, keepdims=True)
        - normed * jnp.mean(scaled * normed, -1, keepdims=True)
    )
    dh_ref[...] = dhidden
    low_ref[...] = dhidden.astype(BF16)
    sums_ref[...] = jnp.zeros_like(sums_ref)
    sums_ref[0:1, :] = jnp.sum(dhidden, 0, keepdims=True)
    sums_ref[1:2, :] = jnp.sum(grad * normed, 0, keepdims=True)
    sums_ref[2:3, :] = jnp.sum(grad, 0, keepdims=True)


def shrink_grad_kernel(sizes, idx, d_mine, d_other, act_ref, *refs):
    uly, dp, unit = sizes
    near_x, far_x, near_y, far_y = (refs[2 * i : 2 * i + 2] for i in range(4))
    d_ref, turn_ref = refs[8:]
    block = dp * unit
    rows = d_mine.shape[0]
    d_ref[:rows] = d_mine[...]
    d_ref[rows:] = d_other[...]
    for j in range(uly):
        turn_ref[...] = dot_tn(act_ref[:, j * block : (j + 1) * block], d_ref[...]).astype(BF16)
        for k in range(dp):
            if k % 2 == 0:
                ref, at = (far_x if j % 2 else near_x), j // 2
            else:
                ref, at = (near_y if j < uly // 2 else far_y), j % 2
            start = pl.multiple_of((idx[2] ^ k) * unit, unit)
            into = slice((k // 2) * unit, (k // 2 + 1) * unit)
            ref[at][into, :] = turn_ref[pl.ds(start, unit), :]


def shrink_grad(scalars, sizes, ds, act):
    uly, dp, unit = sizes
    rows, width = ds[0].shape
    block = dp * unit
    half = (block // 2, width)
    return call(
        functools.partial(shrink_grad_kernel, sizes),
        "shrink_grad",
        scalars,
        [*ds, act],
        [whole((rows, width))] * 2 + [whole(act.shape)],
        [jax.ShapeDtypeStruct(half, BF16)] * 8,
        [whole(half)] * 8,
        [pltpu.VMEM((2 * rows, width), BF16), pltpu.VMEM((block, width), BF16)],
        (1,),
        4 * rows * width * uly * block,
        16,
    )


def feed_backward_kernel(sizes, idx, x_mine, x_other, d_mine, d_other, slope_ref, *refs):
    uly, dp, unit = sizes
    e_ref, s_ref, *refs = refs
    near_x, far_x, near_y, far_y = (refs[2 * i : 2 * i + 2] for i in range(4))
    deb_ref, dx_ref, send_ref, xt_ref, d_ref, turn_ref, dpre_ref = refs[8:]
    rows, width = x_mine.shape
    shard = width // dp
    half = width // 2
    block = dp * unit
    turn_ref[:, :rows] = x_mine[...].T
    turn_ref[:, rows:] = x_other[...].T
    for k in range(dp):
        start = pl.multiple_of((idx[2] ^ k) * shard, shard)
        into = slice(slot(k) * shard, (slot(k) + 1) * shard)
        xt_ref[into, :] = turn_ref[pl.ds(start, shard), :]
    d_ref[:rows] = d_mine[...]
    d_ref[rows:] = d_other[...]
    for j in range(uly):
        lanes = slice(j * block, (j + 1) * block)
        dpre = dot_nt(d_ref[...], s_ref[lanes, :])
        dpre = (dpre * slope_ref[:, lanes].astype(F32)).astype(BF16)
        dpre_ref[:, lanes] = dpre
        deb_ref[j : j + 1, :] = jnp.sum(dpre.astype(F32), 0, keepdims=True)
        dexpand = dot_nn(xt_ref[...], dpre).astype(BF16)
        (far_x if j % 2 else near_x)[j // 2][...] = dexpand[:half]
        (near_y if j < uly // 2 else far_y)[j % 2][...] = dexpand[half:]
    grad = dot_nt(dpre_ref[...], e_ref[...])
    dx_ref[...] = grad[:rows]
    send_ref[...] = grad[rows:].astype(BF16)


def feed_backward(scalars, sizes, xs, ds, slope, weights):
    uly, dp, unit = sizes
    rows, width = xs[0].shape
    block = dp * unit
    half = (width // 2, block)
    args = [*xs, *ds, slope, *weights]
    return call(
        functools.partial(feed_backward_kernel, sizes),
        "feed_backward",
        scalars,
        args,
        [whole(arg.shape) for arg in args],
        [jax.ShapeDtypeStruct(half, BF16)] * 8
        + [
            jax.ShapeDtypeStruct((uly, block), F32),
            jax.ShapeDtypeStruct((rows, width), F32),
            jax.ShapeDtypeStruct((rows, width), BF16),
        ],
        [whole(half)] * 8 + [whole((uly, block)), whole((rows, width)), whole((rows, width))],
        [
            pltpu.VMEM((width, 2 * rows), BF16),
            pltpu.VMEM((2 * rows, width), BF16),
            pltpu.VMEM((width, 2 * rows), BF16),
            pltpu.VMEM((2 * rows, uly * block), BF16),
        ],
        (1,),
        12 * rows * width * uly * block,
        24,
    )


def norm_backward_kernel(sizes, idx, dh2_ref, dx_ref, got_ref, normed_ref, inverse_ref, *refs):
    uly, dp, unit = sizes
    m_ref, vec_ref, grads_ref, deb_ref, *refs = refs
    o_refs, refs = refs[:uly], refs[uly:]
    dh_ref, *refs = refs
    do_refs, refs = refs[:uly], refs[uly:]
    keep_ref, send_ref, turn_ref = refs
    b, u, z = idx[0], idx[1], idx[2]
    group = o_refs[0].shape[1]
    share = group // 2
    width = dx_ref.shape[1]
    parts = 2 * uly
    grad = dh2_ref[...] + dx_ref[...] + got_ref[...].astype(F32)
    normed = normed_ref[...]
    scaled = grad * vec_ref[3:4, :]
    dhidden = inverse_ref[...] * (
        scaled
        - jnp.mean(scaled, -1, keepdims=True)
        - normed * jnp.mean(scaled * normed, -1, keepdims=True)
    )
    dh_ref[...] = dhidden
    low = dhidden.astype(BF16)
    for j in range(uly):
        start = pl.multiple_of((u ^ j) * group, group)
        do_refs[j][...] = dot_nt(low, m_ref[pl.ds(start, group), :]).astype(BF16)
    line = lax.broadcasted_iota(jnp.int32, (8, width), 0)
    lines = jnp.zeros((8, width), F32)
    values = [
        jnp.sum(dhidden, 0, keepdims=True),
        jnp.sum(grad * normed, 0, keepdims=True),
        jnp.sum(grad, 0, keepdims=True),
        grads_ref[0:1, :],
        grads_ref[1:2, :],
        grads_ref[2:3, :],
    ]
    for k, value in enumerate(values):
        lines = jnp.where(line == k, value, lines)
    lines = lines.astype(BF16)
    owner = (lax.broadcasted_iota(jnp.int32, (parts, uly), 1) ^ u) + b * uly
    order = lax.broadcasted_iota(jnp.int32, (parts, uly), 0)
    order = jnp.where(order == owner, 1.0, 0.0).astype(BF16)
    ebs = dot_nn(order, deb_ref[...].astype(BF16)).astype(BF16)
    for j in range(uly):
        turn_ref[...] = dot_tn(o_refs[j][...], low).astype(BF16)
        place = slot(u ^ j ^ z)
        keep_ref[place, :share] = turn_ref[pl.ds(pl.multiple_of(b * share, share), share), :]
        send_ref[place, :share] = turn_ref[pl.ds(pl.multiple_of((1 - b) * share, share), share), :]
    for k in range(dp):
        shard = (z ^ k) * group
        own = dot_nn(lines, one_hot(width, group, 0, shard)).astype(BF16)
        ebk = dot_nn(ebs, one_hot(dp * unit, unit, 0, (z ^ k) * unit)).astype(BF16)
        for ref in (keep_ref, send_ref):
            ref[slot(k), share:, :] = jnp.zeros_like(ref[slot(k), share:, :])
            ref[slot(k), share : share + 8, :group] = own
            ref[slot(k), share + 8 : share + 16, :unit] = ebk


def attend_grad_kernel(heads, blocks, pieces, started, q_ref, lse_ref, *refs):
    do_refs, refs = refs[:pieces], refs[pieces:]
    o_refs, refs = refs[:pieces], refs[pieces:]
    kv_refs, refs = refs[:blocks], refs[blocks:]
    so_far, refs = refs[: blocks * started], refs[blocks * started :]
    dq_ref, *refs = refs
    dkv_refs, refs = refs[:blocks], refs[blocks:]
    kt_ref, dout_ref, prod_ref, *refs = refs
    dk_accs, dv_accs = refs[:blocks], refs[blocks:]
    group = heads * HD
    wide = q_ref.shape[1]
    rows = kv_refs[0].shape[0]

    @pl.when(pl.program_id(0) == 0)
    def _():
        for i in range(blocks):
            kt_ref[:, i * rows : (i + 1) * rows] = kv_refs[i][:, :group].T
            if started:
                dk_accs[i][...] = so_far[i][:, :wide].astype(F32) * LOG2E
                dv_accs[i][...] = so_far[i][:, wide : wide + group].astype(F32)
            else:
                dk_accs[i][...] = jnp.zeros_like(dk_accs[i])
                dv_accs[i][...] = jnp.zeros_like(dv_accs[i])

    for j in range(pieces):

        @pl.when(pl.program_id(0) == j)
        def _(j=j):
            dout_ref[...] = do_refs[j][...]
            prod_ref[...] = (do_refs[j][...].astype(F32) * o_refs[j][...].astype(F32)).T

    q = q_ref[...]
    dout = dout_ref[...]
    dqs = []
    for head in range(heads):
        q_head = jnp.where(head_lanes(wide, head, group), q, jnp.zeros_like(q))
        do_head = jnp.where(head_lanes(group, head), dout, jnp.zeros_like(dout))
        lse = lse_ref[head : head + 1, :]
        delta = jnp.sum(prod_ref[head * HD : (head + 1) * HD, :], axis=0, keepdims=True)
        acc = None
        for i in range(blocks):
            probs = jnp.exp2(dot_nt(kv_refs[i][:, :wide], q_head) - lse)
            dv_accs[i][...] += dot_nn(probs.astype(BF16), do_head)
            grads = dot_nt(kv_refs[i][:, wide : wide + group], do_head)
            grads = (probs * (grads - delta)).astype(BF16)
            dk_accs[i][...] += dot_nn(grads, q_head)
            part = dot_nn(
                kt_ref[head * HD : (head + 1) * HD, i * rows : (i + 1) * rows], grads
            )
            acc = part if acc is None else acc + part
        dqs.append(acc)
    dq_ref[...] = jnp.concatenate(dqs, axis=0).T.astype(BF16)

    @pl.when(pl.program_id(0) == pl.num_programs(0) - 1)
    def _():
        for i in range(blocks):
            dkv_refs[i][:, :group] = (dk_accs[i][:, :group] * LN2).astype(BF16)
            dkv_refs[i][:, group:wide] = jnp.zeros((rows, wide - group), BF16)
            dkv_refs[i][:, wide : wide + group] = dv_accs[i][...].astype(BF16)
            dkv_refs[i][:, wide + group :] = jnp.zeros((rows, wide - group), BF16)


def attend_grad(q, kvs, douts, outs, lse, heads, at, so_far):
    rows, wide = kvs[0].shape[0], q.shape[1]
    group = heads * HD
    blocks = len(kvs)
    pieces = len(douts)
    tile = douts[0].shape[0]
    keys = blocks * rows
    started = 1 if so_far else 0
    out = pl.pallas_call(
        functools.partial(attend_grad_kernel, heads, blocks, pieces, started),
        grid=(pieces,),
        in_specs=[
            pl.BlockSpec((tile, wide), lambda t: (t + at, 0)),
            pl.BlockSpec((8, tile), lambda t: (0, t + at)),
        ]
        + [whole((tile, group))] * (2 * pieces)
        + [whole(kvs[0].shape)] * (blocks + blocks * started),
        out_specs=[pl.BlockSpec((tile, group), lambda t: (t, 0))]
        + [whole(kvs[0].shape)] * blocks,
        out_shape=[jax.ShapeDtypeStruct((pieces * tile, group), BF16)]
        + [jax.ShapeDtypeStruct(kvs[0].shape, BF16)] * blocks,
        scratch_shapes=[
            pltpu.VMEM((group, keys), BF16),
            pltpu.VMEM((tile, group), BF16),
            pltpu.VMEM((group, tile), F32),
        ]
        + [pltpu.VMEM((rows, wide), F32)] * blocks
        + [pltpu.VMEM((rows, group), F32)] * blocks,
        compiler_params=pltpu.CompilerParams(vmem_limit_bytes=16 * 2**20),
        cost_estimate=pl.CostEstimate(
            flops=10 * heads * pieces * tile * keys * wide,
            transcendentals=heads * pieces * tile * keys,
            bytes_accessed=2 * rows * wide * 4 + 4 * keys * (wide + group),
        ),
        name="attend_grad",
    )(q, lse, *douts, *outs, *kvs, *so_far)
    return out[0], out[1:]


def project_grad_kernel(sizes, idx, *refs):
    uly, dp, group = sizes
    dq_refs, (own_ref, got_ref, *refs) = refs[:uly], refs[uly:]
    x_refs, refs = refs[:uly], refs[uly:]
    dproj_ref, keep_ref, send_ref = refs
    b, z = idx[0], idx[2]
    rows, width = x_refs[0].shape
    wide = own_ref.shape[1] // 2
    share = keep_ref.shape[1] - 16
    for k, ref in enumerate(dq_refs):
        here = slice(k * ref.shape[0], (k + 1) * ref.shape[0])
        dproj_ref[here, :group] = ref[...] * jnp.asarray(0.125, BF16)
    dproj_ref[:, group:wide] = jnp.zeros((uly * rows, wide - group), BF16)
    dproj_ref[:, wide:] = (own_ref[...].astype(F32) + got_ref[...].astype(F32)).astype(BF16)
    sums = jnp.sum(dproj_ref[...].astype(F32), 0, keepdims=True).astype(BF16)
    grad = None
    for j in range(uly):
        part = dot_tn(x_refs[j][...], dproj_ref[j * rows : (j + 1) * rows, :])
        grad = part if grad is None else grad + part
    grad = grad.astype(BF16)
    for ref, mine in ((keep_ref, True), (send_ref, False)):
        for c in range(3):
            lanes = slice(c * wide, c * wide + group)
            into = slice(c * group, (c + 1) * group)
            for s in range(dp):
                for core in range(2):
                    start = (s * 2 + core) * share

                    @pl.when((b == core) == mine)
                    def _(start=start, s=s, ref=ref, lanes=lanes, into=into):
                        ref[slot(s ^ z), :share, into] = grad[start : start + share, lanes]

                ref[s, share:, into] = jnp.broadcast_to(sums[:, lanes], (16, group))


def token_grad_kernel(uly, idx, dproj_ref, w_ref, dh_ref, *out_refs):
    rows = dh_ref.shape[0]
    for j in reversed(range(uly)):
        part = dot_nt(dproj_ref[j * rows : (j + 1) * rows, :], w_ref[...])
        if j == 0:
            part = part + dh_ref[...]
        out_refs[j][...] = part.astype(out_refs[j].dtype)


def pack_kernel(idx, sx_ref, sx1_ref, sx2_ref, sy_ref, sy1_ref, sy2_ref, keep_ref, got_ref, *refs):
    unit = sx2_ref.shape[0] // 2
    for out_refs, first, s_refs in (
        (refs[:2], 0, (sx_ref, sx1_ref, sx2_ref)),
        (refs[2:], 2, (sy_ref, sy1_ref, sy2_ref)),
    ):
        for k, out_ref in enumerate(out_refs):
            rows = slice(k * unit, (k + 1) * unit)
            value = s_refs[0][rows].astype(F32) + s_refs[1][rows].astype(F32)
            out_ref[:unit, :] = (value + s_refs[2][rows].astype(F32)).astype(BF16)
            value = keep_ref[first + k].astype(F32) + got_ref[first + k].astype(F32)
            out_ref[unit:, :] = value.astype(BF16)


def finish_shrink_kernel(sizes, idx, *refs):
    uly, unit = sizes
    pieces, (shrink_ref, mixer_ref, vec_ref) = refs[: 2 * uly], refs[2 * uly :]
    share = mixer_ref.shape[0] // 2
    for p, ref in enumerate(pieces):

        @pl.when(pl.program_id(0) == p)
        def _(ref=ref):
            shrink_ref[...] = ref[:unit, :].astype(F32)

    def plane_sum(refs, rows):
        values = [ref[rows, :].astype(F32) for ref in refs]
        return (values[0] + values[1]) + (values[2] + values[3])

    @pl.when(pl.program_id(0) == 0)
    def _():
        for group, core in ((pieces[:uly], idx[0]), (pieces[uly:], 1 - idx[0])):
            start = pl.multiple_of(core * share, share)
            mixer_ref[pl.ds(start, share), :] = plane_sum(group, slice(unit, unit + share))
        vec_ref[...] = plane_sum(pieces[:uly], slice(unit + share, unit + share + 16))


def finish_expand_kernel(sizes, idx, *refs):
    uly, dp, unit = sizes
    pieces, (out_ref, turn_ref) = refs[:-2], refs[-2:]
    width = turn_ref.shape[0]
    part = idx[0] * uly + idx[1]
    step = pl.program_id(0)

    @pl.when(step == 0)
    def _():
        col = lax.broadcasted_iota(jnp.int32, (width, width), 1)
        row = lax.broadcasted_iota(jnp.int32, (width, width), 0)
        source = col + ((col // unit) ^ part) * unit - (col // unit) * unit
        turn_ref[...] = jnp.where(row == source, 1.0, 0.0).astype(BF16)

    for k in range(dp):

        @pl.when(step == k)
        def _(k=k):
            line = jnp.concatenate([ref[:, k * unit : (k + 1) * unit] for ref in pieces], 1)
            out_ref[...] = dot_nn(line, turn_ref[...])


def finish_attend_kernel(uly, idx, *refs):
    mine, refs = refs[:uly], refs[uly:]
    other, refs = refs[:uly], refs[uly:]
    out_ref, bias_ref = refs
    b, u, z = idx[0], idx[1], idx[2]
    share = mine[0].shape[0] - 16
    group = mine[0].shape[1] // 3
    width = uly * group
    for group_refs, core in ((mine, b), (other, 1 - b)):
        start = pl.multiple_of(core * share, share)
        for c in range(3):
            acc = None
            for j in range(uly):
                put = one_hot(group, width, (u ^ j) * group, 0)
                value = dot_nn(group_refs[j][:share, c * group : (c + 1) * group], put)
                acc = value if acc is None else acc + value
            out_ref[pl.ds(start, share), c * width : (c + 1) * width] = acc
    bias = jnp.zeros((8, 3 * group), F32)
    for j in range(uly):
        lines = mine[j][share : share + 16, :].astype(F32)[:8]
        bias += jnp.where((u ^ j) == z, 1.0, 0.0) * lines
    bias_ref[...] = bias


def on_device(*args):
    (
        tokens,
        lengths,
        cotangent,
        attend_weight,
        query_bias,
        value_bias,
        mixer_weight,
        mixer_bias,
        attn_gain,
        attn_shift,
        expand_weight,
        expand_bias,
        shrink_weight,
        shrink_bias,
        final_gain,
        final_shift,
    ) = args
    uly = lax.axis_size("uly")
    blk = lax.axis_size("blk")
    dp = lax.axis_size("dp")
    width = tokens.shape[-1]
    rows = tokens.shape[0] * tokens.shape[1]
    heads = HEADS // uly
    group = heads * HD
    wide = -(-(group + 1) // 128) * 128
    shard = attend_weight.shape[0]
    hidden = expand_weight.shape[1]
    parts = blk * uly
    unit = hidden // (parts * dp)
    share = shard // blk
    if not (blk == 2 and uly == 4 and dp == 4 and shard == group and unit * 2 == shard and share % 16 == 0):
        return general_device(*args)
    u = lax.axis_index("uly")
    b = lax.axis_index("blk")
    z = lax.axis_index("dp")
    mixer_rows = share // dp
    feed_rows = shard // 2 + unit
    block_rows = uly * rows
    cols = 3 * wide

    x = tokens.reshape(rows, width)
    xs = [x, swap_with(x, "uly", 1), swap_with(x, "uly", 2)]
    xs.append(swap_with(after(x, *xs[1:]), "uly", 3))
    scalars = jnp.stack([b, u, z, lengths[0]]).astype(jnp.int32)
    vectors = [query_bias, value_bias, mixer_bias, attn_gain, attn_shift, shrink_bias]
    vectors += [final_gain, final_shift, expand_bias]
    first, feed = call(
        functools.partial(fetch_kernel, (uly, dp, group, unit)),
        "fetch",
        scalars,
        [
            attend_weight.reshape(blk, share, 3 * width),
            expand_weight,
            shrink_weight.reshape(parts, unit, width),
            mixer_weight,
            *vectors,
        ],
        [
            pl.BlockSpec((1, share, 3 * width), lambda t, s: (s[0], 0, 0)),
            whole(expand_weight.shape),
            pl.BlockSpec((1, unit, width), lambda t, s: (s[0] * uly + s[1], 0, 0)),
            whole(mixer_weight.shape),
            *[whole(vector.shape) for vector in vectors],
        ],
        [
            jax.ShapeDtypeStruct((share + 16, width), BF16),
            jax.ShapeDtypeStruct((feed_rows, width), BF16),
        ],
        [whole((share + 16, width)), whole((feed_rows, width))],
        [],
        (1,),
        10**9,
        58,
    )
    feeds = [None, swap_with(feed, "dp", 1)]
    mine = [first, None, swap_with(first, "dp", 2), swap_with(first, "dp", 3)]
    mine[1] = swap_with(after(first, *xs[1:3]), "dp", 1)
    feeds.append(swap_with(after(feed, *mine[1:]), "dp", 2))
    other = [swap_with(piece, "blk", 1) for piece in mine]
    rest = call(
        functools.partial(rest_kernel, (uly, dp, unit)),
        "fetch_rest",
        scalars,
        [expand_weight, shrink_weight],
        [whole(expand_weight.shape), whole(shrink_weight.shape)],
        jax.ShapeDtypeStruct((uly - 1, shard // 2 + unit, width), BF16),
        whole((uly - 1, shard // 2 + unit, width)),
        [],
        (1,),
        10**9,
        16,
    )

    w_own, q, kv, vec, eb, mixer_mine = call(
        functools.partial(project_kernel, (uly, blk, dp, group, unit)),
        "project",
        scalars,
        [*after(xs, feeds[1]), *mine, *other],
        [whole((rows, width))] * uly + [whole(first.shape)] * (2 * dp),
        [
            jax.ShapeDtypeStruct((width, cols), BF16),
            jax.ShapeDtypeStruct((block_rows, wide), BF16),
            jax.ShapeDtypeStruct((block_rows, 2 * wide), BF16),
            jax.ShapeDtypeStruct((16, width), F32),
            jax.ShapeDtypeStruct((parts, dp * unit), F32),
            jax.ShapeDtypeStruct((dp * mixer_rows, width), BF16),
        ],
        [
            whole((width, cols)),
            whole((block_rows, wide)),
            whole((block_rows, 2 * wide)),
            whole((16, width)),
            whole((parts, dp * unit)),
            whole((dp * mixer_rows, width)),
        ],
        [],
        (1,),
        2 * block_rows * width * cols,
        16,
    )
    kvs = [kv, swap_with(kv, "blk", 1)]

    mixer_plane = [swap_with(mixer_mine, "uly", j) for j in range(1, uly)]
    plane_one = [swap_with(feeds[1], "uly", j) for j in range(1, uly)]
    outs, lse = attend(after(q, rest, *mixer_plane), kvs, heads, uly)
    o_cols = after(outs, *plane_one)
    o_cols = [o_cols[0]] + [swap_with(o_cols[j], "uly", j) for j in range(1, uly)]
    feeds.append(swap_with(after(feed, feeds[2], *plane_one), "dp", 3))
    plane_two = [swap_with(after(feeds[2], *o_cols[1:]), "uly", j) for j in range(1, uly)]
    mixer_parts = [mixer_mine, *mixer_plane]
    mixer_parts += [swap_with(piece, "blk", 1) for piece in mixer_parts]
    mixer_all = call(
        functools.partial(mixer_kernel, (uly, dp)),
        "mixer_weight",
        scalars,
        mixer_parts,
        [whole(mixer_mine.shape)] * parts,
        jax.ShapeDtypeStruct((width, width), BF16),
        whole((width, width)),
        [pltpu.VMEM((shard, width), F32)],
        (1,),
        10**6,
        16,
    )

    square = (rows, width)
    x1, x1b, normed, inverse = call(
        functools.partial(first_norm_kernel, uly),
        "first_norm",
        scalars,
        [x, *o_cols, mixer_all, vec],
        [whole(square)] + [whole((rows, group))] * uly + [whole((width, width)), whole(vec.shape)],
        [
            jax.ShapeDtypeStruct(square, F32),
            jax.ShapeDtypeStruct(square, BF16),
            jax.ShapeDtypeStruct(square, F32),
            jax.ShapeDtypeStruct((rows, 1), F32),
        ],
        [whole(square), whole(square), whole(square), whole((rows, 1))],
        [],
        (1,),
        2 * rows * width * width,
        16,
    )
    sizes = (uly, dp, unit)
    plane_three = [swap_with(after(feeds[3], *plane_two), "uly", j) for j in range(1, uly)]
    weights = assemble(scalars, sizes, 0, [], [feed, rest])
    weights = assemble(scalars, sizes, 1, weights, [feeds[1], *plane_one])
    weights = assemble(scalars, sizes, 2, weights, [feeds[2], *plane_two])
    weights = assemble(scalars, sizes, 3, weights, [feeds[3], *plane_three])
    x1b_other = swap_with(x1b, "blk", 1)
    act, slope, y_own, y_send = feed_forward(scalars, uly, x1b, x1b_other, eb, weights)
    mixed, dh2, dh2b, sums2 = call(
        final_norm_kernel,
        "final_norm",
        scalars,
        [x1, y_own, swap_with(y_send, "blk", 1), vec, cotangent.reshape(square)],
        [whole(square)] * 3 + [whole(vec.shape), whole(square)],
        [
            jax.ShapeDtypeStruct(square, BF16),
            jax.ShapeDtypeStruct(square, F32),
            jax.ShapeDtypeStruct(square, BF16),
            jax.ShapeDtypeStruct((8, width), F32),
        ],
        [whole(square)] * 3 + [whole((8, width))],
        [],
        (1,),
        10**6,
        16,
    )
    dh2b_other = swap_with(dh2b, "blk", 1)
    ds = [dh2b, dh2b_other]
    s_grads = shrink_grad(scalars, sizes, ds, act)
    s_near_x, s_far_x, s_near_y, s_far_y = (s_grads[2 * i : 2 * i + 2] for i in range(4))
    s_x1 = swap_with(s_far_x[1], "uly", 1)
    s_y1 = swap_with(s_far_y[1], "uly", 2)
    ds = after(ds, s_far_x[0])
    grads = feed_backward(scalars, sizes, [x1b, x1b_other], ds, slope, weights)
    e_near_x, e_far_x, e_near_y, e_far_y = (grads[2 * i : 2 * i + 2] for i in range(4))
    deb, dx_own, dx_send = grads[8:]

    def add(*values):
        return total(values).astype(BF16)

    dx_send, s_far_x0, s_far_y0, s_x1, s_y1 = after(
        (dx_send, s_far_x[0], s_far_y[0], s_x1, s_y1)
    )
    dx_got = swap_with(dx_send, "blk", 1)
    s_x0 = swap_with(s_far_x0, "uly", 1)
    s_y0 = swap_with(s_far_y0, "uly", 2)
    block = (dp, share + 16, width)
    dh1, *rest_out = call(
        functools.partial(norm_backward_kernel, sizes),
        "norm_backward",
        scalars,
        [dh2, dx_own, dx_got, normed, inverse, mixer_all]
        + [vec, sums2]
        + [deb, *o_cols],
        [whole(square)] * 4
        + [whole((rows, 1)), whole((width, width)), whole(vec.shape), whole(sums2.shape)]
        + [whole((uly, dp * unit))]
        + [whole((rows, group))] * uly,
        [jax.ShapeDtypeStruct(square, F32)]
        + [jax.ShapeDtypeStruct((rows, group), BF16)] * uly
        + [jax.ShapeDtypeStruct(block, BF16)] * 2,
        [whole(square)] + [whole((rows, group))] * uly + [whole(block)] * 2,
        [pltpu.VMEM((group, width), BF16)],
        (1,),
        4 * rows * width * width,
        16,
    )
    douts = [rest_out[0]] + [swap_with(rest_out[j], "uly", j) for j in range(1, uly)]
    m_keep, m_send = rest_out[uly:]

    def quarter(j, so_far, *deps):
        dout = after(douts[j], *deps)
        return attend_grad(q, kvs, [dout], [outs[j]], lse, heads, j, so_far)

    dq_0, dkvs = quarter(0, [])
    dq_0, m_send, s_x0, s_y0, s_x1, s_y1, e_far_x, e_far_y, *douts[1:] = after(
        (dq_0, m_send, s_x0, s_y0, s_x1, s_y1, e_far_x, e_far_y, *douts[1:])
    )
    s_next_x = add(s_near_x[1], s_x1)
    s_next_y = add(s_near_y[1], s_y1)
    s_xy = swap_with(s_next_x, "uly", 2)
    s_yx = swap_with(s_next_y, "uly", 1)
    m_got = swap_with(m_send, "blk", 1)
    e_x1 = swap_with(e_far_x[1], "uly", 1)
    e_y1 = swap_with(e_far_y[1], "uly", 2)

    dq_1, dkvs = quarter(1, dkvs, s_next_x, s_next_y)
    dq_1, s_xy, s_yx, m_got, e_far_x, e_far_y = after((dq_1, s_xy, s_yx, m_got, e_far_x, e_far_y))
    packed = (unit + share + 16, width)
    p_near_0, p_near_1, p_far_0, p_far_1 = call(
        pack_kernel,
        "pack",
        scalars,
        [s_near_x[0], s_x0, s_xy, s_near_y[0], s_y0, s_yx, m_keep, m_got],
        [whole(s_xy.shape)] * 6 + [whole(m_keep.shape)] * 2,
        [jax.ShapeDtypeStruct(packed, BF16)] * 4,
        [whole(packed)] * 4,
        [],
        (1,),
        10**6,
        16,
    )
    p_one_1 = swap_with(p_far_1, "dp", 1)
    e_x0 = swap_with(e_far_x[0], "uly", 1)
    e_y0 = swap_with(e_far_y[0], "uly", 2)

    dq_2, dkvs = quarter(2, dkvs, p_far_1)
    dq_2, e_x0, e_y0, e_x1, e_y1, p_one_1, p_far_0 = after(
        (dq_2, e_x0, e_y0, e_x1, e_y1, p_one_1, p_far_0)
    )
    p_one_0 = swap_with(p_far_0, "dp", 1)
    p_next = add(p_near_1, p_one_1)
    p_two = swap_with(p_next, "dp", 2)
    e_next_x = add(e_near_x[1], e_x1)
    e_next_y = add(e_near_y[1], e_y1)
    e_xy = swap_with(e_next_x, "uly", 2)
    e_yx = swap_with(e_next_y, "uly", 1)

    dq_3, dkvs = quarter(3, dkvs, e_next_x, e_next_y, p_next)
    dq_3, e_xy, e_yx, p_one_0, *dkvs = after((dq_3, e_xy, e_yx, p_one_0, *dkvs))
    dkv_got = swap_with(dkvs[1], "blk", 1)
    pair = (2, shard, dp * unit)
    e_near = add(e_near_x[0], e_x0, e_xy).reshape(pair)
    e_far = add(e_near_y[0], e_y0, e_yx).reshape(pair)
    e_one = swap_with(e_far, "dp", 1)
    dkv_got = after(dkv_got, e_near, e_far)
    dqs = [dq_0, dq_1, dq_2, dq_3]
    dproj, a_keep, a_send = call(
        functools.partial(project_grad_kernel, (uly, dp, group)),
        "project_grad",
        scalars,
        [*dqs, dkvs[0], dkv_got, *xs],
        [whole(dq_0.shape)] * uly + [whole(kv.shape)] * 2 + [whole(square)] * uly,
        [
            jax.ShapeDtypeStruct((block_rows, cols), BF16),
            jax.ShapeDtypeStruct((dp, share + 16, 3 * group), BF16),
            jax.ShapeDtypeStruct((dp, share + 16, 3 * group), BF16),
        ],
        [whole((block_rows, cols))] + [whole((dp, share + 16, 3 * group))] * 2,
        [],
        (1,),
        2 * block_rows * width * cols,
        16,
    )
    a_got = swap_with(a_send, "blk", 1)
    token_parts = call(
        functools.partial(token_grad_kernel, uly),
        "token_grad",
        scalars,
        [dproj, w_own, dh1],
        [whole((block_rows, cols)), whole((width, cols)), whole(square)],
        [jax.ShapeDtypeStruct(square, F32)] + [jax.ShapeDtypeStruct(square, BF16)] * (uly - 1),
        [whole(square)] * uly,
        [],
        (1,),
        2 * block_rows * width * cols,
        16,
    )

    def in_plane(own, *deps):
        own = after(own, *deps)
        return [own] + [swap_with(own, "uly", j) for j in range(1, uly)]

    def both_cores(pieces, *deps):
        return pieces + [swap_with(after(piece, *deps), "blk", 1) for piece in pieces]

    a_got = after(a_got, token_parts[0])
    a_near, a_far = add(a_keep[:2], a_got[:2]), add(a_keep[2:], a_got[2:])
    token_parts = after(token_parts, a_near, a_far)
    token_got = [swap_with(token_parts[j], "uly", j) for j in range(1, uly)]
    e_next = add(e_near[1], e_one[1])
    e_two = swap_with(e_next, "dp", 2)
    a_one = swap_with(a_far, "dp", 1)
    tokens_grad = total([token_parts[0], *token_got])
    p_own = add(p_near_0, p_one_0, p_two)
    p_plane = in_plane(p_own, *token_got)
    a_next = add(a_near[1], a_one[1])
    a_two = swap_with(a_next, "dp", 2)
    p_plane = both_cores(p_plane)
    shrink_out, mixer_out, vecs = call(
        functools.partial(finish_shrink_kernel, (uly, unit)),
        "finish_shrink",
        scalars,
        p_plane,
        [whole(p_own.shape)] * parts,
        [
            jax.ShapeDtypeStruct((hidden // dp, width), F32),
            jax.ShapeDtypeStruct((shard, width), F32),
            jax.ShapeDtypeStruct((16, width), F32),
        ],
        [
            pl.BlockSpec((unit, width), lambda t, s: ((s[0] * uly + s[1]) ^ t, 0)),
            whole((shard, width)),
            whole((16, width)),
        ],
        [],
        (parts,),
        10**6,
        16,
    )
    e_own = add(e_near[0], e_one[0], e_two)
    e_plane = in_plane(e_own, *p_plane[1:uly])
    a_own = add(a_near[0], a_one[0], a_two)
    a_plane = in_plane(a_own, *p_plane[1:uly])
    e_plane = both_cores(e_plane, shrink_out)
    expand_out = call(
        functools.partial(finish_expand_kernel, sizes),
        "finish_expand",
        scalars,
        e_plane,
        [whole(e_own.shape)] * parts,
        jax.ShapeDtypeStruct((shard, hidden), F32),
        pl.BlockSpec((shard, width), lambda t, s: (0, t)),
        [pltpu.VMEM((width, width), BF16)],
        (dp,),
        10**9,
        16,
    )
    a_plane = both_cores(a_plane, expand_out)
    attend_out, biases = call(
        functools.partial(finish_attend_kernel, uly),
        "finish_attend",
        scalars,
        a_plane,
        [whole(a_own.shape)] * parts,
        [jax.ShapeDtypeStruct((shard, 3 * width), F32), jax.ShapeDtypeStruct((8, 3 * group), F32)],
        [whole((shard, 3 * width)), whole((8, 3 * group))],
        [],
        (1,),
        10**9,
        16,
    )
    eb_out = vecs[8 : 8 + parts, :unit].reshape(-1)
    vecs = [vecs[k, :shard] for k in range(6)]
    return (
        mixed.reshape(tokens.shape),
        tokens_grad.reshape(tokens.shape),
        attend_out,
        biases[0, :group],
        biases[0, 2 * group :],
        mixer_out,
        vecs[0],
        vecs[1],
        vecs[2],
        expand_out,
        eb_out,
        shrink_out,
        vecs[3],
        vecs[4],
        vecs[5],
    )


def solution(mesh):
    row_spec = P("dp", ("blk", "uly"), None)
    matrix = P("dp", None)
    vector = P("dp")
    return jax.shard_map(
        on_device,
        mesh=mesh,
        in_specs=(
            row_spec,
            vector,
            row_spec,
            matrix,
            vector,
            vector,
            matrix,
            vector,
            vector,
            vector,
            matrix,
            vector,
            matrix,
            vector,
            vector,
            vector,
        ),
        out_specs=(
            row_spec,
            row_spec,
            matrix,
            vector,
            vector,
            matrix,
            vector,
            vector,
            vector,
            matrix,
            vector,
            matrix,
            vector,
            vector,
            vector,
        ),
        check_vma=False,
    )
```

```python
import functools

import jax
import jax.numpy as jnp
from jax import lax
from jax.experimental import pallas as pl
from jax.experimental.pallas import tpu as pltpu
from jax.sharding import PartitionSpec as P

HEADS = 12
HD = 64

EPSILON = 1e-12
MASKED = -1000000000.0
LOG2E = 1.4426950408889634
LN2 = 0.6931471805599453
F32 = jnp.float32
BF16 = jnp.bfloat16


def dot_nn(left, right):
    return lax.dot_general(left, right, (((1,), (0,)), ((), ())), preferred_element_type=F32)


def dot_nt(left, right):
    return lax.dot_general(left, right, (((1,), (1,)), ((), ())), preferred_element_type=F32)


def dot_tn(left, right):
    return lax.dot_general(left, right, (((0,), (0,)), ((), ())), preferred_element_type=F32)


def swap_with(value, axis, offset):
    size = lax.axis_size(axis)
    return lax.ppermute(value, axis, [(i, i ^ offset) for i in range(size)])


def xor_order(pieces, index):
    bit = 1
    while bit < len(pieces):
        flag = (index & bit) != 0
        pieces = [jnp.where(flag, pieces[p ^ bit], pieces[p]) for p in range(len(pieces))]
        bit *= 2
    return pieces


def total(values):
    acc = values[0].astype(F32)
    for value in values[1:]:
        acc = acc + value.astype(F32)
    return acc


def pad_rows(value, rows):
    return jnp.pad(value, ((0, rows - value.shape[0]), (0, 0)))


def head_lanes(width, head, ones_lane=None):
    lane = lax.broadcasted_iota(jnp.int32, (1, width), 1)
    keep = (lane >= head * HD) & (lane < (head + 1) * HD)
    if ones_lane is not None:
        keep = keep | (lane == ones_lane)
    return keep


def attend_forward_kernel(heads, blocks, q_ref, *refs):
    kv_refs = refs[:blocks]
    o_ref, lse_ref, vt_ref = refs[blocks:]
    group = heads * HD
    wide = q_ref.shape[1]
    rows = kv_refs[0].shape[0]

    @pl.when(pl.program_id(0) == 0)
    def _():
        for i in range(blocks):
            vt_ref[:, i * rows : (i + 1) * rows] = kv_refs[i][:, wide : wide + group].T

    q = q_ref[...]
    outs = []
    stats = []
    for head in range(heads):
        q_head = jnp.where(head_lanes(wide, head, group), q, jnp.zeros_like(q))
        scores = [dot_nt(kv_refs[i][:, :wide], q_head) for i in range(blocks)]
        top = jnp.max(scores[0], axis=0, keepdims=True)
        for i in range(1, blocks):
            top = jnp.maximum(top, jnp.max(scores[i], axis=0, keepdims=True))
        norm = jnp.zeros_like(top)
        acc = None
        for i in range(blocks):
            probs = jnp.exp2(scores[i] - top)
            norm = norm + jnp.sum(probs, axis=0, keepdims=True)
            part = dot_nn(
                vt_ref[head * HD : (head + 1) * HD, i * rows : (i + 1) * rows], probs.astype(BF16)
            )
            acc = part if acc is None else acc + part
        outs.append(acc / norm)
        stats.append(top + jnp.log2(norm))
    o_ref[...] = jnp.concatenate(outs, axis=0).T.astype(BF16)
    for head in range(heads):
        lse_ref[head : head + 1, :] = stats[head]


def attend_forward(q, kvs, heads, tile):
    rows, wide = q.shape
    group = heads * HD
    blocks = len(kvs)
    keys = blocks * rows
    whole = pl.BlockSpec(kvs[0].shape, lambda t: (0, 0))
    return pl.pallas_call(
        functools.partial(attend_forward_kernel, heads, blocks),
        grid=(rows // tile,),
        in_specs=[pl.BlockSpec((tile, wide), lambda t: (t, 0))] + [whole] * blocks,
        out_specs=[
            pl.BlockSpec((tile, group), lambda t: (t, 0)),
            pl.BlockSpec((8, tile), lambda t: (0, t)),
        ],
        out_shape=[
            jax.ShapeDtypeStruct((rows, group), BF16),
            jax.ShapeDtypeStruct((8, rows), F32),
        ],
        scratch_shapes=[pltpu.VMEM((group, keys), BF16)],
        compiler_params=pltpu.CompilerParams(vmem_limit_bytes=56 * 2**20),
        cost_estimate=pl.CostEstimate(
            flops=4 * heads * rows * keys * wide,
            transcendentals=heads * rows * keys,
            bytes_accessed=2 * rows * wide * 3 + 2 * keys * (wide + group),
        ),
        name="attend_forward",
    )(q, *kvs)


def attend_backward_kernel(heads, blocks, q_ref, do_ref, o_ref, lse_ref, *refs):
    kv_refs = refs[:blocks]
    dq_ref = refs[blocks]
    dkv_refs = refs[blocks + 1 : 2 * blocks + 1]
    kt_ref = refs[2 * blocks + 1]
    dk_accs = refs[2 * blocks + 2 : 3 * blocks + 2]
    dv_accs = refs[3 * blocks + 2 :]
    group = heads * HD
    wide = q_ref.shape[1]
    rows = kv_refs[0].shape[0]

    @pl.when(pl.program_id(0) == 0)
    def _():
        for i in range(blocks):
            kt_ref[:, i * rows : (i + 1) * rows] = kv_refs[i][:, :group].T
            dk_accs[i][...] = jnp.zeros_like(dk_accs[i])
            dv_accs[i][...] = jnp.zeros_like(dv_accs[i])

    q = q_ref[...]
    dout = do_ref[...]
    products = (dout.astype(F32) * o_ref[...].astype(F32)).T
    dqs = []
    for head in range(heads):
        q_head = jnp.where(head_lanes(wide, head, group), q, jnp.zeros_like(q))
        do_head = jnp.where(head_lanes(group, head), dout, jnp.zeros_like(dout))
        lse = lse_ref[head : head + 1, :]
        delta = jnp.sum(products[head * HD : (head + 1) * HD], axis=0, keepdims=True)
        acc = None
        for i in range(blocks):
            probs = jnp.exp2(dot_nt(kv_refs[i][:, :wide], q_head) - lse)
            dv_accs[i][...] += dot_nn(probs.astype(BF16), do_head)
            grads = dot_nt(kv_refs[i][:, wide : wide + group], do_head)
            grads = (probs * (grads - delta)).astype(BF16)
            dk_accs[i][...] += dot_nn(grads, q_head)
            part = dot_nn(
                kt_ref[head * HD : (head + 1) * HD, i * rows : (i + 1) * rows], grads
            )
            acc = part if acc is None else acc + part
        dqs.append(acc)
    dq_ref[...] = jnp.concatenate(dqs, axis=0).T.astype(BF16)

    @pl.when(pl.program_id(0) == pl.num_programs(0) - 1)
    def _():
        for i in range(blocks):
            dkv_refs[i][:, :group] = (dk_accs[i][:, :group] * LN2).astype(BF16)
            dkv_refs[i][:, wide : wide + group] = dv_accs[i][...].astype(BF16)


def attend_backward(q, kvs, dout, o, lse, heads, tile):
    rows, wide = q.shape
    group = heads * HD
    blocks = len(kvs)
    keys = blocks * rows
    whole = pl.BlockSpec(kvs[0].shape, lambda t: (0, 0))
    out = pl.pallas_call(
        functools.partial(attend_backward_kernel, heads, blocks),
        grid=(rows // tile,),
        in_specs=[
            pl.BlockSpec((tile, wide), lambda t: (t, 0)),
            pl.BlockSpec((tile, group), lambda t: (t, 0)),
            pl.BlockSpec((tile, group), lambda t: (t, 0)),
            pl.BlockSpec((8, tile), lambda t: (0, t)),
        ]
        + [whole] * blocks,
        out_specs=[pl.BlockSpec((tile, group), lambda t: (t, 0))] + [whole] * blocks,
        out_shape=[jax.ShapeDtypeStruct((rows, group), BF16)]
        + [jax.ShapeDtypeStruct(kvs[0].shape, BF16)] * blocks,
        scratch_shapes=[pltpu.VMEM((group, keys), BF16)]
        + [pltpu.VMEM((rows, wide), F32)] * blocks
        + [pltpu.VMEM((rows, group), F32)] * blocks,
        compiler_params=pltpu.CompilerParams(vmem_limit_bytes=56 * 2**20),
        cost_estimate=pl.CostEstimate(
            flops=10 * heads * rows * keys * wide,
            transcendentals=heads * rows * keys,
            bytes_accessed=2 * rows * wide * 4 + 4 * keys * (wide + group),
        ),
        name="attend_backward",
    )(q, dout, o, lse, *kvs)
    return out[0], out[1:]


def feed_kernel(
    x1_ref,
    x1b_ref,
    expand_ref,
    shrink_ref,
    ebias_ref,
    sbias_ref,
    gain_ref,
    shift_ref,
    cot_ref,
    mixed_ref,
    dx1_ref,
    dexpand_ref,
    dshrink_ref,
    debias_ref,
    vec_ref,
    act_ref,
    slope_ref,
    acc_ref,
    d2b_ref,
    x1t_ref,
):
    phase = pl.program_id(0)
    step = pl.program_id(1)
    last = pl.num_programs(1) - 1
    width = x1_ref.shape[1]

    @pl.when(phase == 0)
    def _():
        pre = dot_nn(x1b_ref[...], expand_ref[0]) + ebias_ref[0]
        cdf = 0.5 * (1.0 + lax.erf(pre * 0.7071067811865476))
        pdf = jnp.exp(-0.5 * pre * pre) * 0.3989422804014327
        act = (pre * cdf).astype(BF16)
        act_ref[step] = act
        slope_ref[step] = (cdf + pre * pdf).astype(BF16)
        part = dot_nn(act, shrink_ref[0])

        @pl.when(step == 0)
        def _():
            acc_ref[...] = part
            x1t_ref[...] = x1b_ref[...].T

        @pl.when(step > 0)
        def _():
            acc_ref[...] += part

        @pl.when(step == last)
        def _():
            hidden = x1_ref[...] + (acc_ref[...] + sbias_ref[...])
            center = hidden - jnp.mean(hidden, -1, keepdims=True)
            inverse = lax.rsqrt(jnp.mean(center * center, -1, keepdims=True) + EPSILON)
            normed = center * inverse
            mixed_ref[...] = (normed * gain_ref[...] + shift_ref[...]).astype(BF16)
            grad = cot_ref[...].astype(F32)
            scaled = grad * gain_ref[...]
            dhidden = inverse * (
                scaled
                - jnp.mean(scaled, -1, keepdims=True)
                - normed * jnp.mean(scaled * normed, -1, keepdims=True)
            )
            acc_ref[...] = dhidden
            d2b_ref[...] = dhidden.astype(BF16)
            vec_ref[...] = jnp.zeros_like(vec_ref)
            vec_ref[0:1, :] = jnp.sum(grad * normed, 0, keepdims=True)
            vec_ref[1:2, :] = jnp.sum(grad, 0, keepdims=True)
            vec_ref[2:3, :] = jnp.sum(dhidden, 0, keepdims=True)

    @pl.when(phase == 1)
    def _():
        d2b = d2b_ref[...]
        dpre = (dot_nt(d2b, shrink_ref[0]) * slope_ref[step].astype(F32)).astype(BF16)
        debias_ref[0] = jnp.sum(dpre.astype(F32), 0, keepdims=True)
        dexpand_ref[0] = dot_nn(x1t_ref[...], dpre).astype(BF16)
        dshrink_ref[0] = dot_tn(act_ref[step], d2b).astype(BF16)
        acc_ref[...] += dot_nt(dpre, expand_ref[0])

        @pl.when(step == last)
        def _():
            dx1_ref[...] = acc_ref[...]


def feed_forward_backward(x1, x1b, expand, shrink, ebias, sbias, gain, shift, cot):
    rows, width = x1.shape
    parts, _, block = expand.shape
    full = pl.BlockSpec((rows, width), lambda p, k: (0, 0))
    line = pl.BlockSpec((1, width), lambda p, k: (0, 0))
    return pl.pallas_call(
        feed_kernel,
        grid=(2, parts),
        in_specs=[
            full,
            full,
            pl.BlockSpec((1, width, block), lambda p, k: (k, 0, 0)),
            pl.BlockSpec((1, block, width), lambda p, k: (k, 0, 0)),
            pl.BlockSpec((1, 1, block), lambda p, k: (k, 0, 0)),
            line,
            line,
            line,
            full,
        ],
        out_specs=[
            full,
            full,
            pl.BlockSpec((1, width, block), lambda p, k: (p * k, 0, 0)),
            pl.BlockSpec((1, block, width), lambda p, k: (p * k, 0, 0)),
            pl.BlockSpec((1, 1, block), lambda p, k: (p * k, 0, 0)),
            pl.BlockSpec((8, width), lambda p, k: (0, 0)),
        ],
        out_shape=[
            jax.ShapeDtypeStruct((rows, width), BF16),
            jax.ShapeDtypeStruct((rows, width), F32),
            jax.ShapeDtypeStruct((parts, width, block), BF16),
            jax.ShapeDtypeStruct((parts, block, width), BF16),
            jax.ShapeDtypeStruct((parts, 1, block), F32),
            jax.ShapeDtypeStruct((8, width), F32),
        ],
        scratch_shapes=[
            pltpu.VMEM((parts, rows, block), BF16),
            pltpu.VMEM((parts, rows, block), BF16),
            pltpu.VMEM((rows, width), F32),
            pltpu.VMEM((rows, width), BF16),
            pltpu.VMEM((width, rows), BF16),
        ],
        compiler_params=pltpu.CompilerParams(vmem_limit_bytes=48 * 2**20),
        cost_estimate=pl.CostEstimate(
            flops=12 * rows * width * parts * block,
            transcendentals=2 * rows * parts * block,
            bytes_accessed=12 * width * parts * block,
        ),
        name="feed_forward_backward",
    )(x1, x1b, expand, shrink, ebias, sbias, gain, shift, cot)


def general_device(
    tokens,
    lengths,
    cotangent,
    attend_weight,
    query_bias,
    value_bias,
    mixer_weight,
    mixer_bias,
    attn_gain,
    attn_shift,
    expand_weight,
    expand_bias,
    shrink_weight,
    shrink_bias,
    final_gain,
    final_shift,
):
    uly = lax.axis_size("uly")
    blk = lax.axis_size("blk")
    dp = lax.axis_size("dp")
    u = lax.axis_index("uly")
    b = lax.axis_index("blk")
    z = lax.axis_index("dp")
    width = tokens.shape[-1]
    rows = tokens.shape[0] * tokens.shape[1]
    block_rows = uly * rows
    heads = HEADS // uly
    group = heads * HD
    wide = -(-(group + 1) // 128) * 128
    shard = attend_weight.shape[0]
    hidden = expand_weight.shape[1]
    parts = blk * uly
    unit = hidden // (parts * dp)
    share = shard // blk

    x = tokens.reshape(rows, width)
    x_rows = jnp.concatenate([x] + [swap_with(x, "uly", j) for j in range(1, uly)], 0)

    small = jnp.concatenate(
        [query_bias, value_bias, mixer_bias, attn_gain, attn_shift, shrink_bias]
        + [final_gain, final_shift, expand_bias]
    )
    small_rows = small.shape[0] // (3 * group)
    own_heads = lax.dynamic_slice_in_dim(attend_weight.reshape(shard, 3, uly, group), u, 1, 2)
    own_heads = own_heads.reshape(shard, 3 * group)
    first_piece = jnp.concatenate(
        [
            lax.dynamic_slice_in_dim(own_heads, b * share, share, 0),
            pad_rows(small.reshape(small_rows, 3 * group), 16),
        ]
    )
    first_all = lax.all_gather(first_piece, "dp", axis=0, tiled=False)
    halves = first_all[:, :share]
    halves = xor_order([halves] + [swap_with(halves, "blk", i) for i in range(1, blk)], b)
    attend_own = jnp.stack(halves, 1).reshape(width, 3, group)
    vectors = first_all[:, share : share + small_rows].reshape(dp, -1, shard).astype(F32)
    names = [vectors[:, k].reshape(width) for k in range(8)]
    bias_query, bias_value, bias_mixer, gain_attn, shift_attn, bias_shrink = names[:6]
    gain_final, shift_final = names[6:]
    bias_expand = vectors[:, 8:].reshape(dp, parts, unit).transpose(1, 0, 2)
    bias_expand = jnp.stack(
        xor_order(list(bias_expand.reshape(parts, dp * unit)), b * uly + u), 0
    ).reshape(parts, 1, dp * unit)

    mixer_own = lax.dynamic_slice_in_dim(mixer_weight, b * share, share, 0)
    mixer_all = jnp.stack(
        xor_order([mixer_own] + [swap_with(mixer_own, "dp", j) for j in range(1, dp)], z), 0
    )
    mixer_all = jnp.stack(
        xor_order([mixer_all] + [swap_with(mixer_all, "blk", i) for i in range(1, blk)], b), 1
    ).reshape(width, width)

    part = b * uly + u
    expand_own = lax.dynamic_slice_in_dim(
        expand_weight.reshape(shard, dp, parts, unit), part, 1, 2
    ).reshape(-1, width)
    shrink_own = lax.dynamic_slice_in_dim(shrink_weight.reshape(parts, unit, width), part, 1, 0)
    expand_rows = expand_own.shape[0]
    feed_own = jnp.concatenate([expand_own, shrink_own.reshape(unit, width)], 0)
    feed_all = lax.all_gather(feed_own, "dp", axis=0, tiled=False)
    expand_part = feed_all[:, :expand_rows].reshape(width, dp * unit)
    shrink_part = feed_all[:, expand_rows:].reshape(dp * unit, width)
    expand_two = jnp.stack([expand_part, swap_with(expand_part, "uly", 1)])
    shrink_two = jnp.stack([shrink_part, swap_with(shrink_part, "uly", 2)])
    expand_far = swap_with(expand_two, "uly", 2)
    shrink_far = swap_with(shrink_two, "uly", 1)
    expand_here = jnp.concatenate([expand_two, expand_far], 0)
    shrink_here = jnp.stack([shrink_two[0], shrink_far[0], shrink_two[1], shrink_far[1]], 0)
    expand_full = jnp.concatenate(
        [expand_here] + [swap_with(expand_here, "blk", i) for i in range(1, blk)], 0
    )
    shrink_full = jnp.concatenate(
        [shrink_here] + [swap_with(shrink_here, "blk", i) for i in range(1, blk)], 0
    )

    lane_pad = ((0, 0), (0, wide - group))
    bias_row = jnp.pad(lax.dynamic_slice_in_dim(bias_query, u * group, group, 0), lane_pad[1:])
    ones_lane = (jnp.arange(wide) == group).astype(F32)
    q = dot_nn(x_rows, jnp.pad(attend_own[:, 0], lane_pad)) + bias_row
    q = (q * (0.125 * LOG2E) + ones_lane).astype(BF16)
    kv_weight = jnp.concatenate([jnp.pad(attend_own[:, 1], lane_pad), attend_own[:, 2]], 1)
    kv_bias = jnp.concatenate(
        [jnp.zeros((wide,), F32), lax.dynamic_slice_in_dim(bias_value, u * group, group, 0)]
    )
    kv_ones = jnp.pad(ones_lane, (0, group))
    row_index = jnp.arange(block_rows, dtype=jnp.int32)
    positions = b * block_rows + ((row_index // rows) ^ u) * rows + row_index % rows
    key_mask = jnp.where(positions < lengths[0], 0.0, MASKED)
    kv = (dot_nn(x_rows, kv_weight) + kv_bias + key_mask[:, None] * kv_ones).astype(BF16)
    kvs = [kv] + [swap_with(kv, "blk", i) for i in range(1, blk)]

    o_rows, lse = attend_forward(q, kvs, heads, min(256, block_rows))
    pieces = [o_rows[j * rows : (j + 1) * rows] for j in range(uly)]
    pieces = [pieces[0]] + [swap_with(pieces[j], "uly", j) for j in range(1, uly)]
    mixer_in = jnp.concatenate(xor_order(pieces, u), 1)

    first_sum = x.astype(F32) + (dot_nn(mixer_in, mixer_all) + bias_mixer)
    center = first_sum - jnp.mean(first_sum, -1, keepdims=True)
    first_inv = lax.rsqrt(jnp.mean(center * center, -1, keepdims=True) + EPSILON)
    first_normed = center * first_inv
    first_out = first_normed * gain_attn + shift_attn
    first_low = first_out.astype(BF16)

    mixed, first_grad, expand_grad, shrink_grad, expand_bias_grad, vec_grads = (
        feed_forward_backward(
            first_out,
            first_low,
            expand_full,
            shrink_full,
            bias_expand,
            bias_shrink[None],
            gain_final[None],
            shift_final[None],
            cotangent.reshape(rows, width),
        )
    )

    scaled = first_grad * gain_attn
    attn_grad = first_inv * (
        scaled
        - jnp.mean(scaled, -1, keepdims=True)
        - first_normed * jnp.mean(scaled * first_normed, -1, keepdims=True)
    )
    attn_low = attn_grad.astype(BF16)
    out_grad = dot_nt(attn_low, mixer_all).astype(BF16)
    sends = xor_order([out_grad[:, j * group : (j + 1) * group] for j in range(uly)], u)
    dout_rows = jnp.concatenate(
        [sends[0]] + [swap_with(sends[j], "uly", j) for j in range(1, uly)], 0
    )
    dq, dkvs = attend_backward(q, kvs, dout_rows, o_rows, lse, heads, min(256, block_rows))

    mixer_grad = dot_tn(mixer_in, attn_low).astype(BF16)
    attn_gain_grad = jnp.sum(first_grad * first_normed, 0)
    attn_shift_grad = jnp.sum(first_grad, 0)
    mixer_bias_grad = jnp.sum(attn_grad, 0)
    ebg = jnp.stack(xor_order(list(expand_bias_grad.reshape(parts, dp * unit)), part), 0)
    ebg = ebg.reshape(parts, dp, unit).transpose(1, 0, 2).reshape(dp, parts * unit)
    vec_all = jnp.concatenate(
        [
            v.reshape(dp, shard)
            for v in (
                mixer_bias_grad,
                attn_gain_grad,
                attn_shift_grad,
                vec_grads[2],
                vec_grads[0],
                vec_grads[1],
            )
        ]
        + [ebg],
        1,
    ).astype(BF16)

    mixer_cols = width // blk
    mixer_part_rows = shard // uly
    vec_len = vec_all.shape[1]
    vec_rows = -(-vec_len // mixer_cols)
    vec_rows = -(-vec_rows // 16) * 16
    vec_block = jnp.pad(vec_all, ((0, 0), (0, vec_rows * mixer_cols - vec_len))).reshape(
        dp, vec_rows, mixer_cols
    )
    mixer_view = mixer_grad.reshape(dp, uly, mixer_part_rows, blk, mixer_cols)
    by_blk = xor_order([mixer_view[:, :, :, i] for i in range(blk)], b)
    mixer_parts = []
    for i in range(blk):
        by_uly = xor_order([by_blk[i][:, j] for j in range(uly)], u)
        mixer_parts.append(
            jnp.stack([jnp.concatenate([piece, vec_block], 1) for piece in by_uly], 0)
        )
    mixer_sum = total(
        [mixer_parts[0]] + [swap_with(mixer_parts[i], "blk", i) for i in range(1, blk)]
    ).astype(BF16)
    mixer_sum = total(
        [mixer_sum[0]] + [swap_with(mixer_sum[j], "uly", j) for j in range(1, uly)]
    ).astype(BF16)

    def over_blk(grad):
        return total(
            [grad[:uly]]
            + [swap_with(grad[i * uly : (i + 1) * uly], "blk", i) for i in range(1, blk)]
        ).astype(BF16)

    shrink_sum = over_blk(shrink_grad)
    expand_sum = over_blk(expand_grad)
    shrink_sum = shrink_sum.reshape(2, 2, dp * unit, width)
    expand_sum = expand_sum.reshape(2, 2, width, dp * unit)
    shrink_sum = total([shrink_sum[0], swap_with(shrink_sum[1], "uly", 2)]).astype(BF16)
    expand_sum = total([expand_sum[:, 0], swap_with(expand_sum[:, 1], "uly", 1)]).astype(BF16)
    shrink_sum = total([shrink_sum[0], swap_with(shrink_sum[1], "uly", 1)]).astype(BF16)
    expand_sum = total([expand_sum[0], swap_with(expand_sum[1], "uly", 2)]).astype(BF16)

    mixer_rows = mixer_sum.shape[1] * mixer_cols // width
    packed = jnp.concatenate(
        [
            expand_sum.reshape(dp, expand_rows, width),
            shrink_sum.reshape(dp, unit, width),
            mixer_sum.reshape(dp, mixer_rows, width),
        ],
        1,
    )

    def over_dp(value):
        sends = [lax.dynamic_slice_in_dim(value, z ^ j, 1, 0)[0] for j in range(dp)]
        return total([sends[0]] + [swap_with(sends[j], "dp", j) for j in range(1, dp)])

    owned = over_dp(packed)
    vec_owned = owned[expand_rows + unit :].reshape(-1, mixer_cols)[mixer_part_rows:]
    vec_owned = vec_owned.reshape(-1)[:vec_len]

    def in_plane(value):
        value = value.astype(BF16)
        value = jnp.stack(
            xor_order([value] + [swap_with(value, "uly", j) for j in range(1, uly)], u), 0
        )
        return jnp.stack(
            xor_order([value] + [swap_with(value, "blk", i) for i in range(1, blk)], b), 0
        )

    gathered = in_plane(owned).reshape(parts, -1, width)
    expand_out = gathered[:, :expand_rows].reshape(parts, shard, dp, unit)
    expand_out = expand_out.transpose(1, 2, 0, 3).reshape(shard, hidden).astype(F32)
    shrink_out = gathered[:, expand_rows : expand_rows + unit]
    shrink_out = shrink_out.reshape(parts * unit, width).astype(F32)
    mixer_out = gathered[:, expand_rows + unit :].reshape(blk, uly, -1, mixer_cols)
    mixer_out = mixer_out[:, :, :mixer_part_rows].transpose(1, 2, 0, 3)
    mixer_out = mixer_out.reshape(shard, width).astype(F32)

    own_dkv = total([dkvs[0]] + [swap_with(dkvs[i], "blk", i) for i in range(1, blk)])
    own_dkv = own_dkv.astype(BF16)
    proj_grad = jnp.concatenate(
        [dq * jnp.asarray(0.125, BF16), own_dkv[:, :group], own_dkv[:, wide : wide + group]], 1
    )
    token_parts = dot_nt(proj_grad, attend_own.reshape(width, 3 * group))
    token_low = token_parts.astype(BF16)
    tokens_grad = attn_grad + total(
        [token_parts[:rows]]
        + [swap_with(token_low[j * rows : (j + 1) * rows], "uly", j) for j in range(1, uly)]
    )
    attend_grad = dot_tn(x_rows, proj_grad).astype(BF16)
    attend_grad = attend_grad.reshape(dp, blk, share, 3 * group)
    bias_sum = jnp.sum(proj_grad.astype(F32), 0)[None]
    bias_rows = pad_rows(bias_sum.astype(BF16), 16)
    attend_parts = [
        jnp.concatenate(
            [
                lax.dynamic_slice_in_dim(attend_grad, b ^ i, 1, 1).reshape(-1, 3 * group),
                bias_rows,
            ],
            0,
        )
        for i in range(blk)
    ]
    attend_sum = total(
        [attend_parts[0]] + [swap_with(attend_parts[i], "blk", i) for i in range(1, blk)]
    ).astype(BF16)
    bias_half = jnp.broadcast_to(attend_sum[dp * share :], (dp, 16, 3 * group))
    attend_sum = attend_sum[: dp * share].reshape(dp, share, 3 * group)
    attend_owned = over_dp(jnp.concatenate([attend_sum, bias_half], 1))
    attend_all = in_plane(attend_owned)
    attend_out = attend_all[:, :, :share].reshape(blk, uly, share, 3, group)
    attend_out = attend_out.transpose(0, 2, 3, 1, 4).reshape(shard, 3 * width).astype(F32)
    bias_out = attend_all[0, :, share].astype(F32).reshape(uly, 3, group)
    query_bias_grad = lax.dynamic_slice_in_dim(bias_out[:, 0].reshape(width), z * shard, shard, 0)
    value_bias_grad = lax.dynamic_slice_in_dim(bias_out[:, 2].reshape(width), z * shard, shard, 0)

    vecs = [vec_owned[k * shard : (k + 1) * shard] for k in range(6)]
    return (
        mixed.reshape(tokens.shape),
        tokens_grad.reshape(tokens.shape),
        attend_out,
        query_bias_grad,
        value_bias_grad,
        mixer_out,
        vecs[0],
        vecs[1],
        vecs[2],
        expand_out,
        vec_owned[6 * shard :],
        shrink_out,
        vecs[3],
        vecs[4],
        vecs[5],
    )


def call(
    kernel,
    name,
    scalars,
    args,
    in_specs,
    out_shape,
    out_specs,
    scratch,
    grid,
    flops,
    vmem,
    aliases={},
):
    return pl.pallas_call(
        kernel,
        grid_spec=pltpu.PrefetchScalarGridSpec(
            num_scalar_prefetch=1,
            grid=grid,
            in_specs=in_specs,
            out_specs=out_specs,
            scratch_shapes=scratch,
        ),
        out_shape=out_shape,
        compiler_params=pltpu.CompilerParams(vmem_limit_bytes=vmem * 2**20),
        input_output_aliases=aliases,
        cost_estimate=pl.CostEstimate(flops=flops, bytes_accessed=1, transcendentals=0),
        name=name,
    )(scalars, *args)


def whole(shape):
    return pl.BlockSpec(shape, lambda *_: (0,) * len(shape))


def after(value, *deps):
    return lax.optimization_barrier((value, *deps))[0]


def slot(offset):
    return (offset & 1) * 2 + (offset >> 1)


def one_hot(rows, cols, row_offset=0, col_offset=0):
    row = lax.broadcasted_iota(jnp.int32, (rows, cols), 0) + row_offset
    col = lax.broadcasted_iota(jnp.int32, (rows, cols), 1) + col_offset
    return jnp.where(row == col, 1.0, 0.0).astype(BF16)


def fetch_kernel(sizes, idx, attend_ref, expand_ref, shrink_ref, mixer_ref, *refs):
    uly, dp, group, unit = sizes
    vec_refs, (first_ref, feed_ref) = refs[:-2], refs[-2:]
    share = attend_ref.shape[1]
    shard, width = mixer_ref.shape
    u = idx[1]
    part = idx[0] * uly + u
    take = one_hot(width, group, 0, u * group)
    for c in range(3):
        cols = dot_nn(attend_ref[0, :, c * width : (c + 1) * width], take)
        first_ref[:share, c * group : (c + 1) * group] = cols.astype(BF16)
    first_ref[share:, :] = jnp.zeros_like(first_ref[share:, :])
    rows = share // dp
    mixer = dot_nn(one_hot(rows, shard, part * rows, 0), mixer_ref[...]).astype(BF16)
    for k in range(dp):
        here = slice(k * rows, (k + 1) * rows)
        first_ref[here, 3 * group :] = mixer[:, k * group : (k + 1) * group]
    line = share
    for ref in vec_refs:
        for k in range(ref.shape[0] // shard):
            first_ref[line : line + 1, :shard] = ref[k * shard : (k + 1) * shard].reshape(1, shard)
            line += 1
    take = one_hot(width, unit, 0, part * unit)
    half = shard // 2
    for k in range(dp):
        cols = dot_nn(expand_ref[:, k * width : (k + 1) * width], take).astype(BF16)
        feed_ref[:half, k * unit : (k + 1) * unit] = cols[:half]
        feed_ref[:half, (dp + k) * unit : (dp + k + 1) * unit] = cols[half:]
    feed_ref[half:, :] = shrink_ref[0]


def project_kernel(sizes, idx, *refs):
    uly, blk, dp, group, unit = sizes
    x_refs, refs = refs[:uly], refs[uly:]
    mine_refs, refs = refs[:dp], refs[dp:]
    other_refs, refs = refs[:dp], refs[dp:]
    w_ref, q_ref, kv_ref, vec_ref, eb_ref, mixer_ref = refs
    b, u, z, length = idx[0], idx[1], idx[2], idx[3]
    rows, width = x_refs[0].shape
    wide = q_ref.shape[1]
    pad = wide - group
    share = mine_refs[0].shape[0] - 16
    shard = 2 * share
    parts = uly * blk
    for c in range(3):
        w_ref[:, c * wide + group : (c + 1) * wide] = jnp.zeros((width, pad), BF16)
    own_vec = jnp.zeros((16, shard), F32)
    all_vec = jnp.zeros((16, width), F32)
    lines = share // dp
    for j in range(dp):
        for k in range(dp):
            mixer_ref[j * lines : (j + 1) * lines, k * group : (k + 1) * group] = mine_refs[j][
                k * lines : (k + 1) * lines, 3 * group :
            ]
        for ref, core in ((mine_refs[j], b), (other_refs[j], 1 - b)):
            start = pl.multiple_of((z ^ j) * shard + core * share, share)
            for c in range(3):
                w_ref[pl.ds(start, share), c * wide : c * wide + group] = ref[
                    :share, c * group : (c + 1) * group
                ]
        vec = mine_refs[j][share:, :shard]
        own_vec += jnp.where((z ^ j) == u, 1.0, 0.0) * vec.astype(F32)
        all_vec += dot_nn(vec, one_hot(shard, width, (z ^ j) * shard, 0))
    vec_ref[...] = all_vec

    low = all_vec.astype(BF16)
    part = b * uly + u
    eb = jnp.zeros((parts, dp * unit), F32)
    for parity in range(2):
        col = lax.broadcasted_iota(jnp.int32, (width, dp * unit), 1)
        row = lax.broadcasted_iota(jnp.int32, (width, dp * unit), 0)
        source = col + (col // unit) * (shard - unit) + parity * unit
        lanes = dot_nn(low, jnp.where(row == source, 1.0, 0.0).astype(BF16)).astype(BF16)
        owner = lax.broadcasted_iota(jnp.int32, (parts, 16), 0) ^ part
        line = lax.broadcasted_iota(jnp.int32, (parts, 16), 1)
        wanted = ((owner & 1) == parity) & (line == 8 + (owner >> 1))
        eb += dot_nn(jnp.where(wanted, 1.0, 0.0).astype(BF16), lanes)
    eb_ref[...] = eb

    lane = lax.broadcasted_iota(jnp.int32, (1, wide), 1)
    mark = jnp.where(lane == group, 1.0, 0.0)
    zeros = jnp.zeros((1, pad), F32)
    q_bias = jnp.concatenate([own_vec[0:1], zeros], 1)
    v_bias = jnp.concatenate([own_vec[1:2], zeros], 1)
    for j in range(uly):
        x = x_refs[j][...]
        here = slice(j * rows, (j + 1) * rows)
        q = dot_nn(x, w_ref[:, :wide]) + q_bias
        q_ref[here, :] = (q * (0.125 * LOG2E) + mark).astype(BF16)
        first = (b * uly + (u ^ j)) * rows
        position = lax.broadcasted_iota(jnp.int32, (rows, 1), 0) + first
        masked = jnp.where(position < length, 0.0, MASKED)
        k = dot_nn(x, w_ref[:, wide : 2 * wide]) + masked * mark
        kv_ref[here, :wide] = k.astype(BF16)
        kv_ref[here, wide:] = (dot_nn(x, w_ref[:, 2 * wide :]) + v_bias).astype(BF16)


def attend_kernel(heads, blocks, q_ref, *refs):
    kv_refs = refs[:blocks]
    o_refs = refs[blocks:-2]
    lse_ref, vt_ref = refs[-2:]
    group = heads * HD
    wide = q_ref.shape[1]
    rows = kv_refs[0].shape[0]

    @pl.when(pl.program_id(0) == 0)
    def _():
        for i in range(blocks):
            vt_ref[:, i * rows : (i + 1) * rows] = kv_refs[i][:, wide : wide + group].T

    q = q_ref[...]
    outs = []
    for head in range(heads):
        q_head = jnp.where(head_lanes(wide, head, group), q, jnp.zeros_like(q))
        scores = [dot_nt(kv_refs[i][:, :wide], q_head) for i in range(blocks)]
        top = jnp.max(scores[0], axis=0, keepdims=True)
        for i in range(1, blocks):
            top = jnp.maximum(top, jnp.max(scores[i], axis=0, keepdims=True))
        norm = jnp.zeros_like(top)
        acc = None
        for i in range(blocks):
            probs = jnp.exp2(scores[i] - top)
            norm = norm + jnp.sum(probs, axis=0, keepdims=True)
            part = dot_nn(
                vt_ref[head * HD : (head + 1) * HD, i * rows : (i + 1) * rows], probs.astype(BF16)
            )
            acc = part if acc is None else acc + part
        outs.append(acc / norm)
        lse_ref[head : head + 1, :] = top + jnp.log2(norm)
    out = jnp.concatenate(outs, axis=0).T.astype(BF16)
    for j, o_ref in enumerate(o_refs):

        @pl.when(pl.program_id(0) == j)
        def _(o_ref=o_ref):
            o_ref[...] = out


def attend(q, kvs, heads, pieces):
    rows, wide = q.shape
    tile = rows // pieces
    group = heads * HD
    blocks = len(kvs)
    keys = blocks * rows
    out = pl.pallas_call(
        functools.partial(attend_kernel, heads, blocks),
        grid=(pieces,),
        in_specs=[pl.BlockSpec((tile, wide), lambda t: (t, 0))] + [whole(kvs[0].shape)] * blocks,
        out_specs=[whole((tile, group))] * pieces + [pl.BlockSpec((8, tile), lambda t: (0, t))],
        out_shape=[jax.ShapeDtypeStruct((tile, group), BF16)] * pieces
        + [jax.ShapeDtypeStruct((8, rows), F32)],
        scratch_shapes=[pltpu.VMEM((group, keys), BF16)],
        compiler_params=pltpu.CompilerParams(vmem_limit_bytes=16 * 2**20),
        cost_estimate=pl.CostEstimate(
            flops=4 * heads * rows * keys * wide,
            transcendentals=heads * rows * keys,
            bytes_accessed=2 * rows * wide * 3 + 2 * keys * (wide + group),
        ),
        name="attend",
    )(q, *kvs)
    return out[:-1], out[-1]


def first_norm_kernel(uly, idx, x_ref, *refs):
    o_refs = refs[:uly]
    m_ref, vec_ref, x1_ref, x1b_ref, normed_ref, inverse_ref = refs[uly:]
    group = o_refs[0].shape[1]
    acc = vec_ref[2:3, :]
    for j in range(uly):
        start = pl.multiple_of((idx[1] ^ j) * group, group)
        acc = acc + dot_nn(o_refs[j][...], m_ref[pl.ds(start, group), :])
    hidden = x_ref[...].astype(F32) + acc
    center = hidden - jnp.mean(hidden, -1, keepdims=True)
    inverse = lax.rsqrt(jnp.mean(center * center, -1, keepdims=True) + EPSILON)
    normed = center * inverse
    out = normed * vec_ref[3:4, :] + vec_ref[4:5, :]
    x1_ref[...] = out
    x1b_ref[...] = out.astype(BF16)
    normed_ref[...] = normed
    inverse_ref[...] = inverse


def rest_kernel(sizes, idx, expand_ref, shrink_ref, out_ref):
    uly, dp, unit = sizes
    width = shrink_ref.shape[1]
    half = expand_ref.shape[0] // 2
    for j in range(1, uly):
        part = idx[0] * uly + (idx[1] ^ j)
        take = one_hot(width, unit, 0, part * unit)
        for k in range(dp):
            cols = dot_nn(expand_ref[:, k * width : (k + 1) * width], take).astype(BF16)
            out_ref[j - 1, :half, k * unit : (k + 1) * unit] = cols[:half]
            out_ref[j - 1, :half, (dp + k) * unit : (dp + k + 1) * unit] = cols[half:]
        start = pl.multiple_of(part * unit, unit)
        out_ref[j - 1, half:, :] = shrink_ref[pl.ds(start, unit), :]


def mixer_kernel(sizes, idx, *refs):
    uly, dp = sizes
    pieces, (m_ref, turn_ref) = refs[:-2], refs[-2:]
    lines = pieces[0].shape[0] // dp
    b, u, z = idx[0], idx[1], idx[2]
    shard = 2 * uly * lines
    for k in range(dp):
        for p, ref in enumerate(pieces):
            part = (b * uly + u) ^ p
            turn_ref[pl.ds(pl.multiple_of(part * lines, 8), lines), :] = ref[
                k * lines : (k + 1) * lines, :
            ].astype(F32)
        start = pl.multiple_of((z ^ k) * shard, shard)
        m_ref[pl.ds(start, shard), :] = turn_ref[...].astype(BF16)


def assemble_kernel(sizes, k, idx, *refs):
    uly, dp, unit = sizes
    e_ref, s_ref, sem = refs[-3:]
    block = dp * unit
    shard = e_ref.shape[0] // dp
    half = shard // 2
    owner = idx[2] ^ k
    copies = []
    for j in range(uly):
        if k == 0:
            piece = refs[0] if j == 0 else refs[1].at[j - 1]
        else:
            piece = refs[2 + j]
        for h in range(2):
            start = pl.multiple_of(owner * shard + h * half, half)
            copies.append(
                pltpu.make_async_copy(
                    piece.at[pl.ds(0, half), pl.ds(h * block, block)],
                    e_ref.at[pl.ds(start, half), pl.ds(j * block, block)],
                    sem.at[3 * j + h],
                )
            )
        start = pl.multiple_of(j * block + owner * unit, unit)
        copies.append(
            pltpu.make_async_copy(
                piece.at[pl.ds(half, unit), :], s_ref.at[pl.ds(start, unit), :], sem.at[3 * j + 2]
            )
        )
    for copy in copies:
        copy.start()
    for copy in copies:
        copy.wait()


def assemble(scalars, sizes, k, weights, pieces):
    uly, dp, unit = sizes
    width = pieces[0].shape[1]
    block = uly * dp * unit
    hbm = pl.BlockSpec(memory_space=pl.ANY)
    return call(
        functools.partial(assemble_kernel, sizes, k),
        "assemble",
        scalars,
        [*weights, *pieces],
        [hbm] * (len(weights) + len(pieces)),
        [jax.ShapeDtypeStruct((width, block), BF16), jax.ShapeDtypeStruct((block, width), BF16)],
        [hbm] * 2,
        [pltpu.SemaphoreType.DMA((3 * uly,))],
        (1,),
        10**6,
        16,
        {1: 0, 2: 1} if weights else {},
    )


def feed_forward_kernel(uly, idx, mine_ref, other_ref, eb_ref, e_ref, s_ref, *refs):
    act_ref, slope_ref, y_ref, send_ref, x_ref = refs
    rows = mine_ref.shape[0]
    block = e_ref.shape[1] // uly
    x_ref[:rows] = mine_ref[...]
    x_ref[rows:] = other_ref[...]
    for j in range(uly):
        lanes = slice(j * block, (j + 1) * block)
        pre = dot_nn(x_ref[...], e_ref[:, lanes]) + eb_ref[j : j + 1, :]
        cdf = 0.5 * (1.0 + lax.erf(pre * 0.7071067811865476))
        pdf = jnp.exp(-0.5 * pre * pre) * 0.3989422804014327
        act_ref[:, lanes] = (pre * cdf).astype(BF16)
        slope_ref[:, lanes] = (cdf + pre * pdf).astype(BF16)
    out = dot_nn(act_ref[...], s_ref[...])
    y_ref[...] = out[:rows]
    send_ref[...] = out[rows:].astype(BF16)


def feed_forward(scalars, uly, mine, other, eb, weights):
    rows, width = mine.shape
    block = weights[0].shape[1]
    args = [mine, other, eb, *weights]
    return call(
        functools.partial(feed_forward_kernel, uly),
        "feed_forward",
        scalars,
        args,
        [whole(arg.shape) for arg in args],
        [
            jax.ShapeDtypeStruct((2 * rows, block), BF16),
            jax.ShapeDtypeStruct((2 * rows, block), BF16),
            jax.ShapeDtypeStruct((rows, width), F32),
            jax.ShapeDtypeStruct((rows, width), BF16),
        ],
        [whole((2 * rows, block))] * 2 + [whole((rows, width))] * 2,
        [pltpu.VMEM((2 * rows, width), BF16)],
        (1,),
        8 * rows * width * block,
        24,
    )


def final_norm_kernel(idx, x1_ref, y_ref, got_ref, vec_ref, cot_ref, *refs):
    mixed_ref, dh_ref, low_ref, sums_ref = refs
    hidden = x1_ref[...] + (y_ref[...] + got_ref[...].astype(F32) + vec_ref[5:6, :])
    gain = vec_ref[6:7, :]
    center = hidden - jnp.mean(hidden, -1, keepdims=True)
    inverse = lax.rsqrt(jnp.mean(center * center, -1, keepdims=True) + EPSILON)
    normed = center * inverse
    mixed_ref[...] = (normed * gain + vec_ref[7:8, :]).astype(BF16)
    grad = cot_ref[...].astype(F32)
    scaled = grad * gain
    dhidden = inverse * (
        scaled
        - jnp.mean(scaled, -1, keepdims=True)
        - normed * jnp.mean(scaled * normed, -1, keepdims=True)
    )
    dh_ref[...] = dhidden
    low_ref[...] = dhidden.astype(BF16)
    sums_ref[...] = jnp.zeros_like(sums_ref)
    sums_ref[0:1, :] = jnp.sum(dhidden, 0, keepdims=True)
    sums_ref[1:2, :] = jnp.sum(grad * normed, 0, keepdims=True)
    sums_ref[2:3, :] = jnp.sum(grad, 0, keepdims=True)


def shrink_grad_kernel(sizes, idx, d_mine, d_other, act_ref, *refs):
    uly, dp, unit = sizes
    near_x, far_x, near_y, far_y = (refs[2 * i : 2 * i + 2] for i in range(4))
    d_ref, turn_ref = refs[8:]
    block = dp * unit
    rows = d_mine.shape[0]
    d_ref[:rows] = d_mine[...]
    d_ref[rows:] = d_other[...]
    for j in range(uly):
        turn_ref[...] = dot_tn(act_ref[:, j * block : (j + 1) * block], d_ref[...]).astype(BF16)
        for k in range(dp):
            if k % 2 == 0:
                ref, at = (far_x if j % 2 else near_x), j // 2
            else:
                ref, at = (near_y if j < uly // 2 else far_y), j % 2
            start = pl.multiple_of((idx[2] ^ k) * unit, unit)
            into = slice((k // 2) * unit, (k // 2 + 1) * unit)
            ref[at][into, :] = turn_ref[pl.ds(start, unit), :]


def shrink_grad(scalars, sizes, ds, act):
    uly, dp, unit = sizes
    rows, width = ds[0].shape
    block = dp * unit
    half = (block // 2, width)
    return call(
        functools.partial(shrink_grad_kernel, sizes),
        "shrink_grad",
        scalars,
        [*ds, act],
        [whole((rows, width))] * 2 + [whole(act.shape)],
        [jax.ShapeDtypeStruct(half, BF16)] * 8,
        [whole(half)] * 8,
        [pltpu.VMEM((2 * rows, width), BF16), pltpu.VMEM((block, width), BF16)],
        (1,),
        4 * rows * width * uly * block,
        16,
    )


def feed_backward_kernel(sizes, idx, x_mine, x_other, d_mine, d_other, slope_ref, *refs):
    uly, dp, unit = sizes
    e_ref, s_ref, *refs = refs
    near_x, far_x, near_y, far_y = (refs[2 * i : 2 * i + 2] for i in range(4))
    deb_ref, dx_ref, send_ref, xt_ref, d_ref, turn_ref, dpre_ref = refs[8:]
    rows, width = x_mine.shape
    shard = width // dp
    half = width // 2
    block = dp * unit
    turn_ref[:, :rows] = x_mine[...].T
    turn_ref[:, rows:] = x_other[...].T
    for k in range(dp):
        start = pl.multiple_of((idx[2] ^ k) * shard, shard)
        into = slice(slot(k) * shard, (slot(k) + 1) * shard)
        xt_ref[into, :] = turn_ref[pl.ds(start, shard), :]
    d_ref[:rows] = d_mine[...]
    d_ref[rows:] = d_other[...]
    for j in range(uly):
        lanes = slice(j * block, (j + 1) * block)
        dpre = dot_nt(d_ref[...], s_ref[lanes, :])
        dpre = (dpre * slope_ref[:, lanes].astype(F32)).astype(BF16)
        dpre_ref[:, lanes] = dpre
        deb_ref[j : j + 1, :] = jnp.sum(dpre.astype(F32), 0, keepdims=True)
        dexpand = dot_nn(xt_ref[...], dpre).astype(BF16)
        (far_x if j % 2 else near_x)[j // 2][...] = dexpand[:half]
        (near_y if j < uly // 2 else far_y)[j % 2][...] = dexpand[half:]
    grad = dot_nt(dpre_ref[...], e_ref[...])
    dx_ref[...] = grad[:rows]
    send_ref[...] = grad[rows:].astype(BF16)


def feed_backward(scalars, sizes, xs, ds, slope, weights):
    uly, dp, unit = sizes
    rows, width = xs[0].shape
    block = dp * unit
    half = (width // 2, block)
    args = [*xs, *ds, slope, *weights]
    return call(
        functools.partial(feed_backward_kernel, sizes),
        "feed_backward",
        scalars,
        args,
        [whole(arg.shape) for arg in args],
        [jax.ShapeDtypeStruct(half, BF16)] * 8
        + [
            jax.ShapeDtypeStruct((uly, block), F32),
            jax.ShapeDtypeStruct((rows, width), F32),
            jax.ShapeDtypeStruct((rows, width), BF16),
        ],
        [whole(half)] * 8 + [whole((uly, block)), whole((rows, width)), whole((rows, width))],
        [
            pltpu.VMEM((width, 2 * rows), BF16),
            pltpu.VMEM((2 * rows, width), BF16),
            pltpu.VMEM((width, 2 * rows), BF16),
            pltpu.VMEM((2 * rows, uly * block), BF16),
        ],
        (1,),
        12 * rows * width * uly * block,
        24,
    )


def norm_backward_kernel(sizes, idx, dh2_ref, dx_ref, got_ref, normed_ref, inverse_ref, *refs):
    uly, dp, unit = sizes
    m_ref, vec_ref, grads_ref, deb_ref, *refs = refs
    o_refs, refs = refs[:uly], refs[uly:]
    dh_ref, *refs = refs
    do_refs, refs = refs[:uly], refs[uly:]
    keep_ref, send_ref, turn_ref = refs
    b, u, z = idx[0], idx[1], idx[2]
    group = o_refs[0].shape[1]
    share = group // 2
    width = dx_ref.shape[1]
    parts = 2 * uly
    grad = dh2_ref[...] + dx_ref[...] + got_ref[...].astype(F32)
    normed = normed_ref[...]
    scaled = grad * vec_ref[3:4, :]
    dhidden = inverse_ref[...] * (
        scaled
        - jnp.mean(scaled, -1, keepdims=True)
        - normed * jnp.mean(scaled * normed, -1, keepdims=True)
    )
    dh_ref[...] = dhidden
    low = dhidden.astype(BF16)
    for j in range(uly):
        start = pl.multiple_of((u ^ j) * group, group)
        do_refs[j][...] = dot_nt(low, m_ref[pl.ds(start, group), :]).astype(BF16)
    line = lax.broadcasted_iota(jnp.int32, (8, width), 0)
    lines = jnp.zeros((8, width), F32)
    values = [
        jnp.sum(dhidden, 0, keepdims=True),
        jnp.sum(grad * normed, 0, keepdims=True),
        jnp.sum(grad, 0, keepdims=True),
        grads_ref[0:1, :],
        grads_ref[1:2, :],
        grads_ref[2:3, :],
    ]
    for k, value in enumerate(values):
        lines = jnp.where(line == k, value, lines)
    lines = lines.astype(BF16)
    owner = (lax.broadcasted_iota(jnp.int32, (parts, uly), 1) ^ u) + b * uly
    order = lax.broadcasted_iota(jnp.int32, (parts, uly), 0)
    order = jnp.where(order == owner, 1.0, 0.0).astype(BF16)
    ebs = dot_nn(order, deb_ref[...].astype(BF16)).astype(BF16)
    for j in range(uly):
        turn_ref[...] = dot_tn(o_refs[j][...], low).astype(BF16)
        place = slot(u ^ j ^ z)
        keep_ref[place, :share] = turn_ref[pl.ds(pl.multiple_of(b * share, share), share), :]
        send_ref[place, :share] = turn_ref[pl.ds(pl.multiple_of((1 - b) * share, share), share), :]
    for k in range(dp):
        shard = (z ^ k) * group
        own = dot_nn(lines, one_hot(width, group, 0, shard)).astype(BF16)
        ebk = dot_nn(ebs, one_hot(dp * unit, unit, 0, (z ^ k) * unit)).astype(BF16)
        for ref in (keep_ref, send_ref):
            ref[slot(k), share:, :] = jnp.zeros_like(ref[slot(k), share:, :])
            ref[slot(k), share : share + 8, :group] = own
            ref[slot(k), share + 8 : share + 16, :unit] = ebk


def attend_grad_kernel(heads, blocks, pieces, started, q_ref, lse_ref, *refs):
    do_refs, refs = refs[:pieces], refs[pieces:]
    o_refs, refs = refs[:pieces], refs[pieces:]
    kv_refs, refs = refs[:blocks], refs[blocks:]
    so_far, refs = refs[: blocks * started], refs[blocks * started :]
    dq_ref, *refs = refs
    dkv_refs, refs = refs[:blocks], refs[blocks:]
    kt_ref, dout_ref, prod_ref, *refs = refs
    dk_accs, dv_accs = refs[:blocks], refs[blocks:]
    group = heads * HD
    wide = q_ref.shape[1]
    rows = kv_refs[0].shape[0]

    @pl.when(pl.program_id(0) == 0)
    def _():
        for i in range(blocks):
            kt_ref[:, i * rows : (i + 1) * rows] = kv_refs[i][:, :group].T
            if started:
                dk_accs[i][...] = so_far[i][:, :wide].astype(F32) * LOG2E
                dv_accs[i][...] = so_far[i][:, wide : wide + group].astype(F32)
            else:
                dk_accs[i][...] = jnp.zeros_like(dk_accs[i])
                dv_accs[i][...] = jnp.zeros_like(dv_accs[i])

    for j in range(pieces):

        @pl.when(pl.program_id(0) == j)
        def _(j=j):
            dout_ref[...] = do_refs[j][...]
            prod_ref[...] = (do_refs[j][...].astype(F32) * o_refs[j][...].astype(F32)).T

    q = q_ref[...]
    dout = dout_ref[...]
    dqs = []
    for head in range(heads):
        q_head = jnp.where(head_lanes(wide, head, group), q, jnp.zeros_like(q))
        do_head = jnp.where(head_lanes(group, head), dout, jnp.zeros_like(dout))
        lse = lse_ref[head : head + 1, :]
        delta = jnp.sum(prod_ref[head * HD : (head + 1) * HD, :], axis=0, keepdims=True)
        acc = None
        for i in range(blocks):
            probs = jnp.exp2(dot_nt(kv_refs[i][:, :wide], q_head) - lse)
            dv_accs[i][...] += dot_nn(probs.astype(BF16), do_head)
            grads = dot_nt(kv_refs[i][:, wide : wide + group], do_head)
            grads = (probs * (grads - delta)).astype(BF16)
            dk_accs[i][...] += dot_nn(grads, q_head)
            part = dot_nn(
                kt_ref[head * HD : (head + 1) * HD, i * rows : (i + 1) * rows], grads
            )
            acc = part if acc is None else acc + part
        dqs.append(acc)
    dq_ref[...] = jnp.concatenate(dqs, axis=0).T.astype(BF16)

    @pl.when(pl.program_id(0) == pl.num_programs(0) - 1)
    def _():
        for i in range(blocks):
            dkv_refs[i][:, :group] = (dk_accs[i][:, :group] * LN2).astype(BF16)
            dkv_refs[i][:, group:wide] = jnp.zeros((rows, wide - group), BF16)
            dkv_refs[i][:, wide : wide + group] = dv_accs[i][...].astype(BF16)
            dkv_refs[i][:, wide + group :] = jnp.zeros((rows, wide - group), BF16)


def attend_grad(q, kvs, douts, outs, lse, heads, at, so_far):
    rows, wide = kvs[0].shape[0], q.shape[1]
    group = heads * HD
    blocks = len(kvs)
    pieces = len(douts)
    tile = douts[0].shape[0]
    keys = blocks * rows
    started = 1 if so_far else 0
    out = pl.pallas_call(
        functools.partial(attend_grad_kernel, heads, blocks, pieces, started),
        grid=(pieces,),
        in_specs=[
            pl.BlockSpec((tile, wide), lambda t: (t + at, 0)),
            pl.BlockSpec((8, tile), lambda t: (0, t + at)),
        ]
        + [whole((tile, group))] * (2 * pieces)
        + [whole(kvs[0].shape)] * (blocks + blocks * started),
        out_specs=[pl.BlockSpec((tile, group), lambda t: (t, 0))]
        + [whole(kvs[0].shape)] * blocks,
        out_shape=[jax.ShapeDtypeStruct((pieces * tile, group), BF16)]
        + [jax.ShapeDtypeStruct(kvs[0].shape, BF16)] * blocks,
        scratch_shapes=[
            pltpu.VMEM((group, keys), BF16),
            pltpu.VMEM((tile, group), BF16),
            pltpu.VMEM((group, tile), F32),
        ]
        + [pltpu.VMEM((rows, wide), F32)] * blocks
        + [pltpu.VMEM((rows, group), F32)] * blocks,
        compiler_params=pltpu.CompilerParams(vmem_limit_bytes=16 * 2**20),
        cost_estimate=pl.CostEstimate(
            flops=10 * heads * pieces * tile * keys * wide,
            transcendentals=heads * pieces * tile * keys,
            bytes_accessed=2 * rows * wide * 4 + 4 * keys * (wide + group),
        ),
        name="attend_grad",
    )(q, lse, *douts, *outs, *kvs, *so_far)
    return out[0], out[1:]


def project_grad_kernel(sizes, idx, *refs):
    uly, dp, group = sizes
    dq_refs, (own_ref, got_ref, *refs) = refs[:uly], refs[uly:]
    x_refs, refs = refs[:uly], refs[uly:]
    dproj_ref, keep_ref, send_ref = refs
    b, z = idx[0], idx[2]
    rows, width = x_refs[0].shape
    wide = own_ref.shape[1] // 2
    share = keep_ref.shape[1] - 16
    for k, ref in enumerate(dq_refs):
        here = slice(k * ref.shape[0], (k + 1) * ref.shape[0])
        dproj_ref[here, :group] = ref[...] * jnp.asarray(0.125, BF16)
    dproj_ref[:, group:wide] = jnp.zeros((uly * rows, wide - group), BF16)
    dproj_ref[:, wide:] = (own_ref[...].astype(F32) + got_ref[...].astype(F32)).astype(BF16)
    sums = jnp.sum(dproj_ref[...].astype(F32), 0, keepdims=True).astype(BF16)
    grad = None
    for j in range(uly):
        part = dot_tn(x_refs[j][...], dproj_ref[j * rows : (j + 1) * rows, :])
        grad = part if grad is None else grad + part
    grad = grad.astype(BF16)
    for ref, mine in ((keep_ref, True), (send_ref, False)):
        for c in range(3):
            lanes = slice(c * wide, c * wide + group)
            into = slice(c * group, (c + 1) * group)
            for s in range(dp):
                for core in range(2):
                    start = (s * 2 + core) * share

                    @pl.when((b == core) == mine)
                    def _(start=start, s=s, ref=ref, lanes=lanes, into=into):
                        ref[slot(s ^ z), :share, into] = grad[start : start + share, lanes]

                ref[s, share:, into] = jnp.broadcast_to(sums[:, lanes], (16, group))


def token_grad_kernel(uly, idx, dproj_ref, w_ref, dh_ref, *out_refs):
    rows = dh_ref.shape[0]
    for j in reversed(range(uly)):
        part = dot_nt(dproj_ref[j * rows : (j + 1) * rows, :], w_ref[...])
        if j == 0:
            part = part + dh_ref[...]
        out_refs[j][...] = part.astype(out_refs[j].dtype)


def pack_kernel(idx, sx_ref, sx1_ref, sx2_ref, sy_ref, sy1_ref, sy2_ref, keep_ref, got_ref, *refs):
    unit = sx2_ref.shape[0] // 2
    for out_refs, first, s_refs in (
        (refs[:2], 0, (sx_ref, sx1_ref, sx2_ref)),
        (refs[2:], 2, (sy_ref, sy1_ref, sy2_ref)),
    ):
        for k, out_ref in enumerate(out_refs):
            rows = slice(k * unit, (k + 1) * unit)
            value = s_refs[0][rows].astype(F32) + s_refs[1][rows].astype(F32)
            out_ref[:unit, :] = (value + s_refs[2][rows].astype(F32)).astype(BF16)
            value = keep_ref[first + k].astype(F32) + got_ref[first + k].astype(F32)
            out_ref[unit:, :] = value.astype(BF16)


def finish_shrink_kernel(sizes, idx, *refs):
    uly, unit = sizes
    pieces, (shrink_ref, mixer_ref, vec_ref, wide_ref, sum_ref, sem) = refs[: 2 * uly], refs[2 * uly :]
    share = mixer_ref.shape[0] // 2
    part = idx[0] * uly + idx[1]
    copies = []
    for p, ref in enumerate(pieces):
        wide_ref[p] = ref[:unit, :].astype(F32)
        start = pl.multiple_of((part ^ p) * unit, unit)
        copies.append(
            pltpu.make_async_copy(wide_ref.at[p], shrink_ref.at[pl.ds(start, unit), :], sem.at[p])
        )
        copies[-1].start()

    def plane_sum(refs, rows):
        values = [ref[rows, :].astype(F32) for ref in refs]
        return (values[0] + values[1]) + (values[2] + values[3])

    for i, core in enumerate((idx[0], 1 - idx[0])):
        group = pieces[i * uly : (i + 1) * uly]
        sum_ref[i] = plane_sum(group, slice(unit, unit + share))
        start = pl.multiple_of(core * share, share)
        copies.append(
            pltpu.make_async_copy(
                sum_ref.at[i], mixer_ref.at[pl.ds(start, share), :], sem.at[2 * uly + i]
            )
        )
        copies[-1].start()
    vec_ref[...] = plane_sum(pieces[:uly], slice(unit + share, unit + share + 16))
    for copy in copies:
        copy.wait()


def finish_expand_kernel(sizes, idx, *refs):
    uly, dp, unit = sizes
    pieces, (out_ref, turn_ref, wide_ref, sem) = refs[:-4], refs[-4:]
    width = turn_ref.shape[0]
    part = idx[0] * uly + idx[1]
    col = lax.broadcasted_iota(jnp.int32, (width, width), 1)
    row = lax.broadcasted_iota(jnp.int32, (width, width), 0)
    source = col + ((col // unit) ^ part) * unit - (col // unit) * unit
    turn_ref[...] = jnp.where(row == source, 1.0, 0.0).astype(BF16)
    copies = []
    for k in range(dp):
        line = jnp.concatenate([ref[:, k * unit : (k + 1) * unit] for ref in pieces], 1)
        wide_ref[k] = dot_nn(line, turn_ref[...])
        copies.append(
            pltpu.make_async_copy(
                wide_ref.at[k], out_ref.at[:, pl.ds(k * width, width)], sem.at[k]
            )
        )
        copies[-1].start()
    for copy in copies:
        copy.wait()


def finish_attend_kernel(uly, idx, *refs):
    mine, refs = refs[:uly], refs[uly:]
    other, refs = refs[:uly], refs[uly:]
    out_ref, bias_ref, wide_ref, sem = refs
    b, u, z = idx[0], idx[1], idx[2]
    share = mine[0].shape[0] - 16
    group = mine[0].shape[1] // 3
    width = uly * group
    copies = []
    for i, (group_refs, core) in enumerate(((mine, b), (other, 1 - b))):
        start = pl.multiple_of(core * share, share)
        for c in range(3):
            acc = None
            for j in range(uly):
                put = one_hot(group, width, (u ^ j) * group, 0)
                value = dot_nn(group_refs[j][:share, c * group : (c + 1) * group], put)
                acc = value if acc is None else acc + value
            wide_ref[3 * i + c] = acc
            copies.append(
                pltpu.make_async_copy(
                    wide_ref.at[3 * i + c],
                    out_ref.at[pl.ds(start, share), pl.ds(c * width, width)],
                    sem.at[3 * i + c],
                )
            )
            copies[-1].start()
    bias = jnp.zeros((8, 3 * group), F32)
    for j in range(uly):
        lines = mine[j][share : share + 16, :].astype(F32)[:8]
        bias += jnp.where((u ^ j) == z, 1.0, 0.0) * lines
    bias_ref[...] = bias
    for copy in copies:
        copy.wait()


def on_device(*args):
    (
        tokens,
        lengths,
        cotangent,
        attend_weight,
        query_bias,
        value_bias,
        mixer_weight,
        mixer_bias,
        attn_gain,
        attn_shift,
        expand_weight,
        expand_bias,
        shrink_weight,
        shrink_bias,
        final_gain,
        final_shift,
    ) = args
    uly = lax.axis_size("uly")
    blk = lax.axis_size("blk")
    dp = lax.axis_size("dp")
    width = tokens.shape[-1]
    rows = tokens.shape[0] * tokens.shape[1]
    heads = HEADS // uly
    group = heads * HD
    wide = -(-(group + 1) // 128) * 128
    shard = attend_weight.shape[0]
    hidden = expand_weight.shape[1]
    parts = blk * uly
    unit = hidden // (parts * dp)
    share = shard // blk
    if not (blk == 2 and uly == 4 and dp == 4 and shard == group and unit * 2 == shard and share % 16 == 0):
        return general_device(*args)
    u = lax.axis_index("uly")
    b = lax.axis_index("blk")
    z = lax.axis_index("dp")
    mixer_rows = share // dp
    feed_rows = shard // 2 + unit
    block_rows = uly * rows
    cols = 3 * wide

    x = tokens.reshape(rows, width)
    xs = [x, swap_with(x, "uly", 1), swap_with(x, "uly", 2)]
    xs.append(swap_with(after(x, *xs[1:]), "uly", 3))
    scalars = jnp.stack([b, u, z, lengths[0]]).astype(jnp.int32)
    vectors = [query_bias, value_bias, mixer_bias, attn_gain, attn_shift, shrink_bias]
    vectors += [final_gain, final_shift, expand_bias]
    first, feed = call(
        functools.partial(fetch_kernel, (uly, dp, group, unit)),
        "fetch",
        scalars,
        [
            attend_weight.reshape(blk, share, 3 * width),
            expand_weight,
            shrink_weight.reshape(parts, unit, width),
            mixer_weight,
            *vectors,
        ],
        [
            pl.BlockSpec((1, share, 3 * width), lambda t, s: (s[0], 0, 0)),
            whole(expand_weight.shape),
            pl.BlockSpec((1, unit, width), lambda t, s: (s[0] * uly + s[1], 0, 0)),
            whole(mixer_weight.shape),
            *[whole(vector.shape) for vector in vectors],
        ],
        [
            jax.ShapeDtypeStruct((share + 16, width), BF16),
            jax.ShapeDtypeStruct((feed_rows, width), BF16),
        ],
        [whole((share + 16, width)), whole((feed_rows, width))],
        [],
        (1,),
        10**9,
        58,
    )
    feeds = [None, swap_with(feed, "dp", 1)]
    mine = [first, None, swap_with(first, "dp", 2), swap_with(first, "dp", 3)]
    mine[1] = swap_with(after(first, *xs[1:3]), "dp", 1)
    feeds.append(swap_with(after(feed, *mine[1:]), "dp", 2))
    other = [swap_with(piece, "blk", 1) for piece in mine]
    rest = call(
        functools.partial(rest_kernel, (uly, dp, unit)),
        "fetch_rest",
        scalars,
        [expand_weight, shrink_weight],
        [whole(expand_weight.shape), whole(shrink_weight.shape)],
        jax.ShapeDtypeStruct((uly - 1, shard // 2 + unit, width), BF16),
        whole((uly - 1, shard // 2 + unit, width)),
        [],
        (1,),
        10**9,
        16,
    )

    w_own, q, kv, vec, eb, mixer_mine = call(
        functools.partial(project_kernel, (uly, blk, dp, group, unit)),
        "project",
        scalars,
        [*after(xs, feeds[1]), *mine, *other],
        [whole((rows, width))] * uly + [whole(first.shape)] * (2 * dp),
        [
            jax.ShapeDtypeStruct((width, cols), BF16),
            jax.ShapeDtypeStruct((block_rows, wide), BF16),
            jax.ShapeDtypeStruct((block_rows, 2 * wide), BF16),
            jax.ShapeDtypeStruct((16, width), F32),
            jax.ShapeDtypeStruct((parts, dp * unit), F32),
            jax.ShapeDtypeStruct((dp * mixer_rows, width), BF16),
        ],
        [
            whole((width, cols)),
            whole((block_rows, wide)),
            whole((block_rows, 2 * wide)),
            whole((16, width)),
            whole((parts, dp * unit)),
            whole((dp * mixer_rows, width)),
        ],
        [],
        (1,),
        2 * block_rows * width * cols,
        16,
    )
    kvs = [kv, swap_with(kv, "blk", 1)]

    mixer_plane = [swap_with(mixer_mine, "uly", j) for j in range(1, uly)]
    plane_one = [swap_with(feeds[1], "uly", j) for j in range(1, uly)]
    outs, lse = attend(after(q, rest, *mixer_plane), kvs, heads, uly)
    o_cols = after(outs, *plane_one)
    o_cols = [o_cols[0]] + [swap_with(o_cols[j], "uly", j) for j in range(1, uly)]
    feeds.append(swap_with(after(feed, feeds[2], *plane_one), "dp", 3))
    plane_two = [swap_with(after(feeds[2], *o_cols[1:]), "uly", j) for j in range(1, uly)]
    mixer_parts = after([mixer_mine, *mixer_plane], *o_cols[1:])
    mixer_parts += [swap_with(piece, "blk", 1) for piece in mixer_parts]
    mixer_all = call(
        functools.partial(mixer_kernel, (uly, dp)),
        "mixer_weight",
        scalars,
        mixer_parts,
        [whole(mixer_mine.shape)] * parts,
        jax.ShapeDtypeStruct((width, width), BF16),
        whole((width, width)),
        [pltpu.VMEM((shard, width), F32)],
        (1,),
        10**6,
        16,
    )

    square = (rows, width)
    x1, x1b, normed, inverse = call(
        functools.partial(first_norm_kernel, uly),
        "first_norm",
        scalars,
        [x, *o_cols, mixer_all, vec],
        [whole(square)] + [whole((rows, group))] * uly + [whole((width, width)), whole(vec.shape)],
        [
            jax.ShapeDtypeStruct(square, F32),
            jax.ShapeDtypeStruct(square, BF16),
            jax.ShapeDtypeStruct(square, F32),
            jax.ShapeDtypeStruct((rows, 1), F32),
        ],
        [whole(square), whole(square), whole(square), whole((rows, 1))],
        [],
        (1,),
        2 * rows * width * width,
        16,
    )
    sizes = (uly, dp, unit)
    plane_three = [swap_with(after(feeds[3], *plane_two), "uly", j) for j in range(1, uly)]
    weights = assemble(scalars, sizes, 0, [], [feed, rest])
    weights = assemble(scalars, sizes, 1, weights, [feeds[1], *plane_one])
    weights = assemble(scalars, sizes, 2, weights, [feeds[2], *plane_two])
    weights = assemble(scalars, sizes, 3, weights, [feeds[3], *plane_three])
    x1b_other = swap_with(x1b, "blk", 1)
    act, slope, y_own, y_send = feed_forward(scalars, uly, x1b, x1b_other, eb, weights)
    mixed, dh2, dh2b, sums2 = call(
        final_norm_kernel,
        "final_norm",
        scalars,
        [x1, y_own, swap_with(y_send, "blk", 1), vec, cotangent.reshape(square)],
        [whole(square)] * 3 + [whole(vec.shape), whole(square)],
        [
            jax.ShapeDtypeStruct(square, BF16),
            jax.ShapeDtypeStruct(square, F32),
            jax.ShapeDtypeStruct(square, BF16),
            jax.ShapeDtypeStruct((8, width), F32),
        ],
        [whole(square)] * 3 + [whole((8, width))],
        [],
        (1,),
        10**6,
        16,
    )
    dh2b_other = swap_with(dh2b, "blk", 1)
    ds = [dh2b, dh2b_other]
    s_grads = shrink_grad(scalars, sizes, ds, act)
    s_near_x, s_far_x, s_near_y, s_far_y = (s_grads[2 * i : 2 * i + 2] for i in range(4))
    s_x1 = swap_with(s_far_x[1], "uly", 1)
    s_y1 = swap_with(s_far_y[1], "uly", 2)
    ds = after(ds, s_far_x[0])
    grads = feed_backward(scalars, sizes, [x1b, x1b_other], ds, slope, weights)
    e_near_x, e_far_x, e_near_y, e_far_y = (grads[2 * i : 2 * i + 2] for i in range(4))
    deb, dx_own, dx_send = grads[8:]

    def add(*values):
        return total(values).astype(BF16)

    dx_send, s_far_x0, s_far_y0, s_x1, s_y1 = after(
        (dx_send, s_far_x[0], s_far_y[0], s_x1, s_y1)
    )
    dx_got = swap_with(dx_send, "blk", 1)
    s_x0 = swap_with(s_far_x0, "uly", 1)
    s_y0 = swap_with(s_far_y0, "uly", 2)
    block = (dp, share + 16, width)
    dh1, *rest_out = call(
        functools.partial(norm_backward_kernel, sizes),
        "norm_backward",
        scalars,
        [dh2, dx_own, dx_got, normed, inverse, mixer_all]
        + [vec, sums2]
        + [deb, *o_cols],
        [whole(square)] * 4
        + [whole((rows, 1)), whole((width, width)), whole(vec.shape), whole(sums2.shape)]
        + [whole((uly, dp * unit))]
        + [whole((rows, group))] * uly,
        [jax.ShapeDtypeStruct(square, F32)]
        + [jax.ShapeDtypeStruct((rows, group), BF16)] * uly
        + [jax.ShapeDtypeStruct(block, BF16)] * 2,
        [whole(square)] + [whole((rows, group))] * uly + [whole(block)] * 2,
        [pltpu.VMEM((group, width), BF16)],
        (1,),
        4 * rows * width * width,
        16,
    )
    douts = [rest_out[0]] + [swap_with(rest_out[j], "uly", j) for j in range(1, uly)]
    m_keep, m_send = rest_out[uly:]

    def quarter(j, so_far, *deps):
        dout = after(douts[j], *deps)
        return attend_grad(q, kvs, [dout], [outs[j]], lse, heads, j, so_far)

    dq_0, dkvs = quarter(0, [])
    dq_0, m_send, s_x0, s_y0, s_x1, s_y1, e_far_x, e_far_y, *douts[1:] = after(
        (dq_0, m_send, s_x0, s_y0, s_x1, s_y1, e_far_x, e_far_y, *douts[1:])
    )
    s_next_x = add(s_near_x[1], s_x1)
    s_next_y = add(s_near_y[1], s_y1)
    s_xy = swap_with(s_next_x, "uly", 2)
    s_yx = swap_with(s_next_y, "uly", 1)
    m_got = swap_with(m_send, "blk", 1)
    e_x1 = swap_with(e_far_x[1], "uly", 1)
    e_y1 = swap_with(e_far_y[1], "uly", 2)

    dq_1, dkvs = quarter(1, dkvs, s_next_x, s_next_y)
    dq_1, s_xy, s_yx, m_got, e_far_x, e_far_y = after((dq_1, s_xy, s_yx, m_got, e_far_x, e_far_y))
    packed = (unit + share + 16, width)
    p_near_0, p_near_1, p_far_0, p_far_1 = call(
        pack_kernel,
        "pack",
        scalars,
        [s_near_x[0], s_x0, s_xy, s_near_y[0], s_y0, s_yx, m_keep, m_got],
        [whole(s_xy.shape)] * 6 + [whole(m_keep.shape)] * 2,
        [jax.ShapeDtypeStruct(packed, BF16)] * 4,
        [whole(packed)] * 4,
        [],
        (1,),
        10**6,
        16,
    )
    p_one_1 = swap_with(p_far_1, "dp", 1)
    e_x0 = swap_with(e_far_x[0], "uly", 1)
    e_y0 = swap_with(e_far_y[0], "uly", 2)

    dq_2, dkvs = quarter(2, dkvs, p_far_1)
    dq_2, e_x0, e_y0, e_x1, e_y1, p_one_1, p_far_0 = after(
        (dq_2, e_x0, e_y0, e_x1, e_y1, p_one_1, p_far_0)
    )
    p_one_0 = swap_with(p_far_0, "dp", 1)
    p_next = add(p_near_1, p_one_1)
    p_two = swap_with(p_next, "dp", 2)
    e_next_x = add(e_near_x[1], e_x1)
    e_next_y = add(e_near_y[1], e_y1)
    e_xy = swap_with(e_next_x, "uly", 2)
    e_yx = swap_with(e_next_y, "uly", 1)

    dq_3, dkvs = quarter(3, dkvs, e_next_x, e_next_y, p_next)
    dq_3, e_xy, e_yx, p_one_0, *dkvs = after((dq_3, e_xy, e_yx, p_one_0, *dkvs))
    dkv_got = swap_with(dkvs[1], "blk", 1)
    pair = (2, shard, dp * unit)
    e_near = add(e_near_x[0], e_x0, e_xy).reshape(pair)
    e_far = add(e_near_y[0], e_y0, e_yx).reshape(pair)
    dkv_got = after(dkv_got, e_near, e_far)
    dqs = [dq_0, dq_1, dq_2, dq_3]
    dproj, a_keep, a_send = call(
        functools.partial(project_grad_kernel, (uly, dp, group)),
        "project_grad",
        scalars,
        [*dqs, dkvs[0], dkv_got, *xs],
        [whole(dq_0.shape)] * uly + [whole(kv.shape)] * 2 + [whole(square)] * uly,
        [
            jax.ShapeDtypeStruct((block_rows, cols), BF16),
            jax.ShapeDtypeStruct((dp, share + 16, 3 * group), BF16),
            jax.ShapeDtypeStruct((dp, share + 16, 3 * group), BF16),
        ],
        [whole((block_rows, cols))] + [whole((dp, share + 16, 3 * group))] * 2,
        [],
        (1,),
        2 * block_rows * width * cols,
        16,
    )
    a_got = swap_with(a_send, "blk", 1)
    token_parts = call(
        functools.partial(token_grad_kernel, uly),
        "token_grad",
        scalars,
        [dproj, w_own, dh1],
        [whole((block_rows, cols)), whole((width, cols)), whole(square)],
        [jax.ShapeDtypeStruct(square, F32)] + [jax.ShapeDtypeStruct(square, BF16)] * (uly - 1),
        [whole(square)] * uly,
        [],
        (1,),
        2 * block_rows * width * cols,
        16,
    )

    def in_plane(own, *deps):
        own = after(own, *deps)
        return [own] + [swap_with(own, "uly", j) for j in range(1, uly)]

    def both_cores(pieces, *deps):
        return pieces + [swap_with(after(piece, *deps), "blk", 1) for piece in pieces]

    a_got = after(a_got, token_parts[0])
    a_near, a_far = add(a_keep[:2], a_got[:2]), add(a_keep[2:], a_got[2:])
    token_parts = after(token_parts, a_near, a_far)
    token_got = [swap_with(token_parts[j], "uly", j) for j in range(1, uly)]
    a_one = swap_with(a_far, "dp", 1)
    a_next = add(a_near[1], a_one[1])
    a_two = swap_with(a_next, "dp", 2)
    e_one = swap_with(after(e_far, a_next), "dp", 1)
    e_next = add(e_near[1], e_one[1])
    e_two = swap_with(e_next, "dp", 2)
    tokens_grad = total([token_parts[0], *token_got])
    p_own = add(p_near_0, p_one_0, p_two)
    p_plane = in_plane(p_own, *token_got)
    p_plane = both_cores(p_plane, a_two)
    shrink_out, mixer_out, vecs = call(
        functools.partial(finish_shrink_kernel, (uly, unit)),
        "finish_shrink",
        scalars,
        p_plane,
        [whole(p_own.shape)] * parts,
        [
            jax.ShapeDtypeStruct((hidden // dp, width), F32),
            jax.ShapeDtypeStruct((shard, width), F32),
            jax.ShapeDtypeStruct((16, width), F32),
        ],
        [pl.BlockSpec(memory_space=pl.ANY)] * 2 + [whole((16, width))],
        [
            pltpu.VMEM((parts, unit, width), F32),
            pltpu.VMEM((2, share, width), F32),
            pltpu.SemaphoreType.DMA((parts + 2,)),
        ],
        (1,),
        10**6,
        16,
    )
    e_own = add(e_near[0], e_one[0], e_two)
    e_plane = in_plane(e_own, *p_plane[1:uly])
    a_own = add(a_near[0], a_one[0], a_two)
    a_plane = in_plane(a_own, *p_plane[1:uly])
    e_plane = both_cores(e_plane, shrink_out)
    expand_out = call(
        functools.partial(finish_expand_kernel, sizes),
        "finish_expand",
        scalars,
        e_plane,
        [whole(e_own.shape)] * parts,
        jax.ShapeDtypeStruct((shard, hidden), F32),
        pl.BlockSpec(memory_space=pl.ANY),
        [
            pltpu.VMEM((width, width), BF16),
            pltpu.VMEM((dp, shard, width), F32),
            pltpu.SemaphoreType.DMA((dp,)),
        ],
        (1,),
        10**9,
        16,
    )
    a_plane = both_cores(a_plane, expand_out)
    attend_out, biases = call(
        functools.partial(finish_attend_kernel, uly),
        "finish_attend",
        scalars,
        a_plane,
        [whole(a_own.shape)] * parts,
        [jax.ShapeDtypeStruct((shard, 3 * width), F32), jax.ShapeDtypeStruct((8, 3 * group), F32)],
        [pl.BlockSpec(memory_space=pl.ANY), whole((8, 3 * group))],
        [pltpu.VMEM((6, share, width), F32), pltpu.SemaphoreType.DMA((6,))],
        (1,),
        10**9,
        16,
    )
    eb_out = vecs[8 : 8 + parts, :unit].reshape(-1)
    vecs = [vecs[k, :shard] for k in range(6)]
    return (
        mixed.reshape(tokens.shape),
        tokens_grad.reshape(tokens.shape),
        attend_out,
        biases[0, :group],
        biases[0, 2 * group :],
        mixer_out,
        vecs[0],
        vecs[1],
        vecs[2],
        expand_out,
        eb_out,
        shrink_out,
        vecs[3],
        vecs[4],
        vecs[5],
    )


def solution(mesh):
    row_spec = P("dp", ("blk", "uly"), None)
    matrix = P("dp", None)
    vector = P("dp")
    return jax.shard_map(
        on_device,
        mesh=mesh,
        in_specs=(
            row_spec,
            vector,
            row_spec,
            matrix,
            vector,
            vector,
            matrix,
            vector,
            vector,
            vector,
            matrix,
            vector,
            matrix,
            vector,
            vector,
            vector,
        ),
        out_specs=(
            row_spec,
            row_spec,
            matrix,
            vector,
            vector,
            matrix,
            vector,
            vector,
            vector,
            matrix,
            vector,
            matrix,
            vector,
            vector,
            vector,
        ),
        check_vma=False,
    )
```

```python
import functools

import jax
import jax.numpy as jnp
from jax import lax
from jax.experimental import pallas as pl
from jax.experimental.pallas import tpu as pltpu
from jax.sharding import PartitionSpec as P

HEADS = 12
HD = 64

EPSILON = 1e-12
MASKED = -1000000000.0
LOG2E = 1.4426950408889634
LN2 = 0.6931471805599453
F32 = jnp.float32
BF16 = jnp.bfloat16


def dot_nn(left, right):
    return lax.dot_general(left, right, (((1,), (0,)), ((), ())), preferred_element_type=F32)


def dot_nt(left, right):
    return lax.dot_general(left, right, (((1,), (1,)), ((), ())), preferred_element_type=F32)


def dot_tn(left, right):
    return lax.dot_general(left, right, (((0,), (0,)), ((), ())), preferred_element_type=F32)


def swap_with(value, axis, offset):
    size = lax.axis_size(axis)
    return lax.ppermute(value, axis, [(i, i ^ offset) for i in range(size)])


def xor_order(pieces, index):
    bit = 1
    while bit < len(pieces):
        flag = (index & bit) != 0
        pieces = [jnp.where(flag, pieces[p ^ bit], pieces[p]) for p in range(len(pieces))]
        bit *= 2
    return pieces


def total(values):
    acc = values[0].astype(F32)
    for value in values[1:]:
        acc = acc + value.astype(F32)
    return acc


def pad_rows(value, rows):
    return jnp.pad(value, ((0, rows - value.shape[0]), (0, 0)))


def head_lanes(width, head, ones_lane=None):
    lane = lax.broadcasted_iota(jnp.int32, (1, width), 1)
    keep = (lane >= head * HD) & (lane < (head + 1) * HD)
    if ones_lane is not None:
        keep = keep | (lane == ones_lane)
    return keep


def attend_forward_kernel(heads, blocks, q_ref, *refs):
    kv_refs = refs[:blocks]
    o_ref, lse_ref, vt_ref = refs[blocks:]
    group = heads * HD
    wide = q_ref.shape[1]
    rows = kv_refs[0].shape[0]

    @pl.when(pl.program_id(0) == 0)
    def _():
        for i in range(blocks):
            vt_ref[:, i * rows : (i + 1) * rows] = kv_refs[i][:, wide : wide + group].T

    q = q_ref[...]
    outs = []
    stats = []
    for head in range(heads):
        q_head = jnp.where(head_lanes(wide, head, group), q, jnp.zeros_like(q))
        scores = [dot_nt(kv_refs[i][:, :wide], q_head) for i in range(blocks)]
        top = jnp.max(scores[0], axis=0, keepdims=True)
        for i in range(1, blocks):
            top = jnp.maximum(top, jnp.max(scores[i], axis=0, keepdims=True))
        norm = jnp.zeros_like(top)
        acc = None
        for i in range(blocks):
            probs = jnp.exp2(scores[i] - top)
            norm = norm + jnp.sum(probs, axis=0, keepdims=True)
            part = dot_nn(
                vt_ref[head * HD : (head + 1) * HD, i * rows : (i + 1) * rows], probs.astype(BF16)
            )
            acc = part if acc is None else acc + part
        outs.append(acc / norm)
        stats.append(top + jnp.log2(norm))
    o_ref[...] = jnp.concatenate(outs, axis=0).T.astype(BF16)
    for head in range(heads):
        lse_ref[head : head + 1, :] = stats[head]


def attend_forward(q, kvs, heads, tile):
    rows, wide = q.shape
    group = heads * HD
    blocks = len(kvs)
    keys = blocks * rows
    whole = pl.BlockSpec(kvs[0].shape, lambda t: (0, 0))
    return pl.pallas_call(
        functools.partial(attend_forward_kernel, heads, blocks),
        grid=(rows // tile,),
        in_specs=[pl.BlockSpec((tile, wide), lambda t: (t, 0))] + [whole] * blocks,
        out_specs=[
            pl.BlockSpec((tile, group), lambda t: (t, 0)),
            pl.BlockSpec((8, tile), lambda t: (0, t)),
        ],
        out_shape=[
            jax.ShapeDtypeStruct((rows, group), BF16),
            jax.ShapeDtypeStruct((8, rows), F32),
        ],
        scratch_shapes=[pltpu.VMEM((group, keys), BF16)],
        compiler_params=pltpu.CompilerParams(vmem_limit_bytes=56 * 2**20),
        cost_estimate=pl.CostEstimate(
            flops=4 * heads * rows * keys * wide,
            transcendentals=heads * rows * keys,
            bytes_accessed=2 * rows * wide * 3 + 2 * keys * (wide + group),
        ),
        name="attend_forward",
    )(q, *kvs)


def attend_backward_kernel(heads, blocks, q_ref, do_ref, o_ref, lse_ref, *refs):
    kv_refs = refs[:blocks]
    dq_ref = refs[blocks]
    dkv_refs = refs[blocks + 1 : 2 * blocks + 1]
    kt_ref = refs[2 * blocks + 1]
    dk_accs = refs[2 * blocks + 2 : 3 * blocks + 2]
    dv_accs = refs[3 * blocks + 2 :]
    group = heads * HD
    wide = q_ref.shape[1]
    rows = kv_refs[0].shape[0]

    @pl.when(pl.program_id(0) == 0)
    def _():
        for i in range(blocks):
            kt_ref[:, i * rows : (i + 1) * rows] = kv_refs[i][:, :group].T
            dk_accs[i][...] = jnp.zeros_like(dk_accs[i])
            dv_accs[i][...] = jnp.zeros_like(dv_accs[i])

    q = q_ref[...]
    dout = do_ref[...]
    products = (dout.astype(F32) * o_ref[...].astype(F32)).T
    dqs = []
    for head in range(heads):
        q_head = jnp.where(head_lanes(wide, head, group), q, jnp.zeros_like(q))
        do_head = jnp.where(head_lanes(group, head), dout, jnp.zeros_like(dout))
        lse = lse_ref[head : head + 1, :]
        delta = jnp.sum(products[head * HD : (head + 1) * HD], axis=0, keepdims=True)
        acc = None
        for i in range(blocks):
            probs = jnp.exp2(dot_nt(kv_refs[i][:, :wide], q_head) - lse)
            dv_accs[i][...] += dot_nn(probs.astype(BF16), do_head)
            grads = dot_nt(kv_refs[i][:, wide : wide + group], do_head)
            grads = (probs * (grads - delta)).astype(BF16)
            dk_accs[i][...] += dot_nn(grads, q_head)
            part = dot_nn(
                kt_ref[head * HD : (head + 1) * HD, i * rows : (i + 1) * rows], grads
            )
            acc = part if acc is None else acc + part
        dqs.append(acc)
    dq_ref[...] = jnp.concatenate(dqs, axis=0).T.astype(BF16)

    @pl.when(pl.program_id(0) == pl.num_programs(0) - 1)
    def _():
        for i in range(blocks):
            dkv_refs[i][:, :group] = (dk_accs[i][:, :group] * LN2).astype(BF16)
            dkv_refs[i][:, wide : wide + group] = dv_accs[i][...].astype(BF16)


def attend_backward(q, kvs, dout, o, lse, heads, tile):
    rows, wide = q.shape
    group = heads * HD
    blocks = len(kvs)
    keys = blocks * rows
    whole = pl.BlockSpec(kvs[0].shape, lambda t: (0, 0))
    out = pl.pallas_call(
        functools.partial(attend_backward_kernel, heads, blocks),
        grid=(rows // tile,),
        in_specs=[
            pl.BlockSpec((tile, wide), lambda t: (t, 0)),
            pl.BlockSpec((tile, group), lambda t: (t, 0)),
            pl.BlockSpec((tile, group), lambda t: (t, 0)),
            pl.BlockSpec((8, tile), lambda t: (0, t)),
        ]
        + [whole] * blocks,
        out_specs=[pl.BlockSpec((tile, group), lambda t: (t, 0))] + [whole] * blocks,
        out_shape=[jax.ShapeDtypeStruct((rows, group), BF16)]
        + [jax.ShapeDtypeStruct(kvs[0].shape, BF16)] * blocks,
        scratch_shapes=[pltpu.VMEM((group, keys), BF16)]
        + [pltpu.VMEM((rows, wide), F32)] * blocks
        + [pltpu.VMEM((rows, group), F32)] * blocks,
        compiler_params=pltpu.CompilerParams(vmem_limit_bytes=56 * 2**20),
        cost_estimate=pl.CostEstimate(
            flops=10 * heads * rows * keys * wide,
            transcendentals=heads * rows * keys,
            bytes_accessed=2 * rows * wide * 4 + 4 * keys * (wide + group),
        ),
        name="attend_backward",
    )(q, dout, o, lse, *kvs)
    return out[0], out[1:]


def feed_kernel(
    x1_ref,
    x1b_ref,
    expand_ref,
    shrink_ref,
    ebias_ref,
    sbias_ref,
    gain_ref,
    shift_ref,
    cot_ref,
    mixed_ref,
    dx1_ref,
    dexpand_ref,
    dshrink_ref,
    debias_ref,
    vec_ref,
    act_ref,
    slope_ref,
    acc_ref,
    d2b_ref,
    x1t_ref,
):
    phase = pl.program_id(0)
    step = pl.program_id(1)
    last = pl.num_programs(1) - 1
    width = x1_ref.shape[1]

    @pl.when(phase == 0)
    def _():
        pre = dot_nn(x1b_ref[...], expand_ref[0]) + ebias_ref[0]
        cdf = 0.5 * (1.0 + lax.erf(pre * 0.7071067811865476))
        pdf = jnp.exp(-0.5 * pre * pre) * 0.3989422804014327
        act = (pre * cdf).astype(BF16)
        act_ref[step] = act
        slope_ref[step] = (cdf + pre * pdf).astype(BF16)
        part = dot_nn(act, shrink_ref[0])

        @pl.when(step == 0)
        def _():
            acc_ref[...] = part
            x1t_ref[...] = x1b_ref[...].T

        @pl.when(step > 0)
        def _():
            acc_ref[...] += part

        @pl.when(step == last)
        def _():
            hidden = x1_ref[...] + (acc_ref[...] + sbias_ref[...])
            center = hidden - jnp.mean(hidden, -1, keepdims=True)
            inverse = lax.rsqrt(jnp.mean(center * center, -1, keepdims=True) + EPSILON)
            normed = center * inverse
            mixed_ref[...] = (normed * gain_ref[...] + shift_ref[...]).astype(BF16)
            grad = cot_ref[...].astype(F32)
            scaled = grad * gain_ref[...]
            dhidden = inverse * (
                scaled
                - jnp.mean(scaled, -1, keepdims=True)
                - normed * jnp.mean(scaled * normed, -1, keepdims=True)
            )
            acc_ref[...] = dhidden
            d2b_ref[...] = dhidden.astype(BF16)
            vec_ref[...] = jnp.zeros_like(vec_ref)
            vec_ref[0:1, :] = jnp.sum(grad * normed, 0, keepdims=True)
            vec_ref[1:2, :] = jnp.sum(grad, 0, keepdims=True)
            vec_ref[2:3, :] = jnp.sum(dhidden, 0, keepdims=True)

    @pl.when(phase == 1)
    def _():
        d2b = d2b_ref[...]
        dpre = (dot_nt(d2b, shrink_ref[0]) * slope_ref[step].astype(F32)).astype(BF16)
        debias_ref[0] = jnp.sum(dpre.astype(F32), 0, keepdims=True)
        dexpand_ref[0] = dot_nn(x1t_ref[...], dpre).astype(BF16)
        dshrink_ref[0] = dot_tn(act_ref[step], d2b).astype(BF16)
        acc_ref[...] += dot_nt(dpre, expand_ref[0])

        @pl.when(step == last)
        def _():
            dx1_ref[...] = acc_ref[...]


def feed_forward_backward(x1, x1b, expand, shrink, ebias, sbias, gain, shift, cot):
    rows, width = x1.shape
    parts, _, block = expand.shape
    full = pl.BlockSpec((rows, width), lambda p, k: (0, 0))
    line = pl.BlockSpec((1, width), lambda p, k: (0, 0))
    return pl.pallas_call(
        feed_kernel,
        grid=(2, parts),
        in_specs=[
            full,
            full,
            pl.BlockSpec((1, width, block), lambda p, k: (k, 0, 0)),
            pl.BlockSpec((1, block, width), lambda p, k: (k, 0, 0)),
            pl.BlockSpec((1, 1, block), lambda p, k: (k, 0, 0)),
            line,
            line,
            line,
            full,
        ],
        out_specs=[
            full,
            full,
            pl.BlockSpec((1, width, block), lambda p, k: (p * k, 0, 0)),
            pl.BlockSpec((1, block, width), lambda p, k: (p * k, 0, 0)),
            pl.BlockSpec((1, 1, block), lambda p, k: (p * k, 0, 0)),
            pl.BlockSpec((8, width), lambda p, k: (0, 0)),
        ],
        out_shape=[
            jax.ShapeDtypeStruct((rows, width), BF16),
            jax.ShapeDtypeStruct((rows, width), F32),
            jax.ShapeDtypeStruct((parts, width, block), BF16),
            jax.ShapeDtypeStruct((parts, block, width), BF16),
            jax.ShapeDtypeStruct((parts, 1, block), F32),
            jax.ShapeDtypeStruct((8, width), F32),
        ],
        scratch_shapes=[
            pltpu.VMEM((parts, rows, block), BF16),
            pltpu.VMEM((parts, rows, block), BF16),
            pltpu.VMEM((rows, width), F32),
            pltpu.VMEM((rows, width), BF16),
            pltpu.VMEM((width, rows), BF16),
        ],
        compiler_params=pltpu.CompilerParams(vmem_limit_bytes=48 * 2**20),
        cost_estimate=pl.CostEstimate(
            flops=12 * rows * width * parts * block,
            transcendentals=2 * rows * parts * block,
            bytes_accessed=12 * width * parts * block,
        ),
        name="feed_forward_backward",
    )(x1, x1b, expand, shrink, ebias, sbias, gain, shift, cot)


def general_device(
    tokens,
    lengths,
    cotangent,
    attend_weight,
    query_bias,
    value_bias,
    mixer_weight,
    mixer_bias,
    attn_gain,
    attn_shift,
    expand_weight,
    expand_bias,
    shrink_weight,
    shrink_bias,
    final_gain,
    final_shift,
):
    uly = lax.axis_size("uly")
    blk = lax.axis_size("blk")
    dp = lax.axis_size("dp")
    u = lax.axis_index("uly")
    b = lax.axis_index("blk")
    z = lax.axis_index("dp")
    width = tokens.shape[-1]
    rows = tokens.shape[0] * tokens.shape[1]
    block_rows = uly * rows
    heads = HEADS // uly
    group = heads * HD
    wide = -(-(group + 1) // 128) * 128
    shard = attend_weight.shape[0]
    hidden = expand_weight.shape[1]
    parts = blk * uly
    unit = hidden // (parts * dp)
    share = shard // blk

    x = tokens.reshape(rows, width)
    x_rows = jnp.concatenate([x] + [swap_with(x, "uly", j) for j in range(1, uly)], 0)

    small = jnp.concatenate(
        [query_bias, value_bias, mixer_bias, attn_gain, attn_shift, shrink_bias]
        + [final_gain, final_shift, expand_bias]
    )
    small_rows = small.shape[0] // (3 * group)
    own_heads = lax.dynamic_slice_in_dim(attend_weight.reshape(shard, 3, uly, group), u, 1, 2)
    own_heads = own_heads.reshape(shard, 3 * group)
    first_piece = jnp.concatenate(
        [
            lax.dynamic_slice_in_dim(own_heads, b * share, share, 0),
            pad_rows(small.reshape(small_rows, 3 * group), 16),
        ]
    )
    first_all = lax.all_gather(first_piece, "dp", axis=0, tiled=False)
    halves = first_all[:, :share]
    halves = xor_order([halves] + [swap_with(halves, "blk", i) for i in range(1, blk)], b)
    attend_own = jnp.stack(halves, 1).reshape(width, 3, group)
    vectors = first_all[:, share : share + small_rows].reshape(dp, -1, shard).astype(F32)
    names = [vectors[:, k].reshape(width) for k in range(8)]
    bias_query, bias_value, bias_mixer, gain_attn, shift_attn, bias_shrink = names[:6]
    gain_final, shift_final = names[6:]
    bias_expand = vectors[:, 8:].reshape(dp, parts, unit).transpose(1, 0, 2)
    bias_expand = jnp.stack(
        xor_order(list(bias_expand.reshape(parts, dp * unit)), b * uly + u), 0
    ).reshape(parts, 1, dp * unit)

    mixer_own = lax.dynamic_slice_in_dim(mixer_weight, b * share, share, 0)
    mixer_all = jnp.stack(
        xor_order([mixer_own] + [swap_with(mixer_own, "dp", j) for j in range(1, dp)], z), 0
    )
    mixer_all = jnp.stack(
        xor_order([mixer_all] + [swap_with(mixer_all, "blk", i) for i in range(1, blk)], b), 1
    ).reshape(width, width)

    part = b * uly + u
    expand_own = lax.dynamic_slice_in_dim(
        expand_weight.reshape(shard, dp, parts, unit), part, 1, 2
    ).reshape(-1, width)
    shrink_own = lax.dynamic_slice_in_dim(shrink_weight.reshape(parts, unit, width), part, 1, 0)
    expand_rows = expand_own.shape[0]
    feed_own = jnp.concatenate([expand_own, shrink_own.reshape(unit, width)], 0)
    feed_all = lax.all_gather(feed_own, "dp", axis=0, tiled=False)
    expand_part = feed_all[:, :expand_rows].reshape(width, dp * unit)
    shrink_part = feed_all[:, expand_rows:].reshape(dp * unit, width)
    expand_two = jnp.stack([expand_part, swap_with(expand_part, "uly", 1)])
    shrink_two = jnp.stack([shrink_part, swap_with(shrink_part, "uly", 2)])
    expand_far = swap_with(expand_two, "uly", 2)
    shrink_far = swap_with(shrink_two, "uly", 1)
    expand_here = jnp.concatenate([expand_two, expand_far], 0)
    shrink_here = jnp.stack([shrink_two[0], shrink_far[0], shrink_two[1], shrink_far[1]], 0)
    expand_full = jnp.concatenate(
        [expand_here] + [swap_with(expand_here, "blk", i) for i in range(1, blk)], 0
    )
    shrink_full = jnp.concatenate(
        [shrink_here] + [swap_with(shrink_here, "blk", i) for i in range(1, blk)], 0
    )

    lane_pad = ((0, 0), (0, wide - group))
    bias_row = jnp.pad(lax.dynamic_slice_in_dim(bias_query, u * group, group, 0), lane_pad[1:])
    ones_lane = (jnp.arange(wide) == group).astype(F32)
    q = dot_nn(x_rows, jnp.pad(attend_own[:, 0], lane_pad)) + bias_row
    q = (q * (0.125 * LOG2E) + ones_lane).astype(BF16)
    kv_weight = jnp.concatenate([jnp.pad(attend_own[:, 1], lane_pad), attend_own[:, 2]], 1)
    kv_bias = jnp.concatenate(
        [jnp.zeros((wide,), F32), lax.dynamic_slice_in_dim(bias_value, u * group, group, 0)]
    )
    kv_ones = jnp.pad(ones_lane, (0, group))
    row_index = jnp.arange(block_rows, dtype=jnp.int32)
    positions = b * block_rows + ((row_index // rows) ^ u) * rows + row_index % rows
    key_mask = jnp.where(positions < lengths[0], 0.0, MASKED)
    kv = (dot_nn(x_rows, kv_weight) + kv_bias + key_mask[:, None] * kv_ones).astype(BF16)
    kvs = [kv] + [swap_with(kv, "blk", i) for i in range(1, blk)]

    o_rows, lse = attend_forward(q, kvs, heads, min(256, block_rows))
    pieces = [o_rows[j * rows : (j + 1) * rows] for j in range(uly)]
    pieces = [pieces[0]] + [swap_with(pieces[j], "uly", j) for j in range(1, uly)]
    mixer_in = jnp.concatenate(xor_order(pieces, u), 1)

    first_sum = x.astype(F32) + (dot_nn(mixer_in, mixer_all) + bias_mixer)
    center = first_sum - jnp.mean(first_sum, -1, keepdims=True)
    first_inv = lax.rsqrt(jnp.mean(center * center, -1, keepdims=True) + EPSILON)
    first_normed = center * first_inv
    first_out = first_normed * gain_attn + shift_attn
    first_low = first_out.astype(BF16)

    mixed, first_grad, expand_grad, shrink_grad, expand_bias_grad, vec_grads = (
        feed_forward_backward(
            first_out,
            first_low,
            expand_full,
            shrink_full,
            bias_expand,
            bias_shrink[None],
            gain_final[None],
            shift_final[None],
            cotangent.reshape(rows, width),
        )
    )

    scaled = first_grad * gain_attn
    attn_grad = first_inv * (
        scaled
        - jnp.mean(scaled, -1, keepdims=True)
        - first_normed * jnp.mean(scaled * first_normed, -1, keepdims=True)
    )
    attn_low = attn_grad.astype(BF16)
    out_grad = dot_nt(attn_low, mixer_all).astype(BF16)
    sends = xor_order([out_grad[:, j * group : (j + 1) * group] for j in range(uly)], u)
    dout_rows = jnp.concatenate(
        [sends[0]] + [swap_with(sends[j], "uly", j) for j in range(1, uly)], 0
    )
    dq, dkvs = attend_backward(q, kvs, dout_rows, o_rows, lse, heads, min(256, block_rows))

    mixer_grad = dot_tn(mixer_in, attn_low).astype(BF16)
    attn_gain_grad = jnp.sum(first_grad * first_normed, 0)
    attn_shift_grad = jnp.sum(first_grad, 0)
    mixer_bias_grad = jnp.sum(attn_grad, 0)
    ebg = jnp.stack(xor_order(list(expand_bias_grad.reshape(parts, dp * unit)), part), 0)
    ebg = ebg.reshape(parts, dp, unit).transpose(1, 0, 2).reshape(dp, parts * unit)
    vec_all = jnp.concatenate(
        [
            v.reshape(dp, shard)
            for v in (
                mixer_bias_grad,
                attn_gain_grad,
                attn_shift_grad,
                vec_grads[2],
                vec_grads[0],
                vec_grads[1],
            )
        ]
        + [ebg],
        1,
    ).astype(BF16)

    mixer_cols = width // blk
    mixer_part_rows = shard // uly
    vec_len = vec_all.shape[1]
    vec_rows = -(-vec_len // mixer_cols)
    vec_rows = -(-vec_rows // 16) * 16
    vec_block = jnp.pad(vec_all, ((0, 0), (0, vec_rows * mixer_cols - vec_len))).reshape(
        dp, vec_rows, mixer_cols
    )
    mixer_view = mixer_grad.reshape(dp, uly, mixer_part_rows, blk, mixer_cols)
    by_blk = xor_order([mixer_view[:, :, :, i] for i in range(blk)], b)
    mixer_parts = []
    for i in range(blk):
        by_uly = xor_order([by_blk[i][:, j] for j in range(uly)], u)
        mixer_parts.append(
            jnp.stack([jnp.concatenate([piece, vec_block], 1) for piece in by_uly], 0)
        )
    mixer_sum = total(
        [mixer_parts[0]] + [swap_with(mixer_parts[i], "blk", i) for i in range(1, blk)]
    ).astype(BF16)
    mixer_sum = total(
        [mixer_sum[0]] + [swap_with(mixer_sum[j], "uly", j) for j in range(1, uly)]
    ).astype(BF16)

    def over_blk(grad):
        return total(
            [grad[:uly]]
            + [swap_with(grad[i * uly : (i + 1) * uly], "blk", i) for i in range(1, blk)]
        ).astype(BF16)

    shrink_sum = over_blk(shrink_grad)
    expand_sum = over_blk(expand_grad)
    shrink_sum = shrink_sum.reshape(2, 2, dp * unit, width)
    expand_sum = expand_sum.reshape(2, 2, width, dp * unit)
    shrink_sum = total([shrink_sum[0], swap_with(shrink_sum[1], "uly", 2)]).astype(BF16)
    expand_sum = total([expand_sum[:, 0], swap_with(expand_sum[:, 1], "uly", 1)]).astype(BF16)
    shrink_sum = total([shrink_sum[0], swap_with(shrink_sum[1], "uly", 1)]).astype(BF16)
    expand_sum = total([expand_sum[0], swap_with(expand_sum[1], "uly", 2)]).astype(BF16)

    mixer_rows = mixer_sum.shape[1] * mixer_cols // width
    packed = jnp.concatenate(
        [
            expand_sum.reshape(dp, expand_rows, width),
            shrink_sum.reshape(dp, unit, width),
            mixer_sum.reshape(dp, mixer_rows, width),
        ],
        1,
    )

    def over_dp(value):
        sends = [lax.dynamic_slice_in_dim(value, z ^ j, 1, 0)[0] for j in range(dp)]
        return total([sends[0]] + [swap_with(sends[j], "dp", j) for j in range(1, dp)])

    owned = over_dp(packed)
    vec_owned = owned[expand_rows + unit :].reshape(-1, mixer_cols)[mixer_part_rows:]
    vec_owned = vec_owned.reshape(-1)[:vec_len]

    def in_plane(value):
        value = value.astype(BF16)
        value = jnp.stack(
            xor_order([value] + [swap_with(value, "uly", j) for j in range(1, uly)], u), 0
        )
        return jnp.stack(
            xor_order([value] + [swap_with(value, "blk", i) for i in range(1, blk)], b), 0
        )

    gathered = in_plane(owned).reshape(parts, -1, width)
    expand_out = gathered[:, :expand_rows].reshape(parts, shard, dp, unit)
    expand_out = expand_out.transpose(1, 2, 0, 3).reshape(shard, hidden).astype(F32)
    shrink_out = gathered[:, expand_rows : expand_rows + unit]
    shrink_out = shrink_out.reshape(parts * unit, width).astype(F32)
    mixer_out = gathered[:, expand_rows + unit :].reshape(blk, uly, -1, mixer_cols)
    mixer_out = mixer_out[:, :, :mixer_part_rows].transpose(1, 2, 0, 3)
    mixer_out = mixer_out.reshape(shard, width).astype(F32)

    own_dkv = total([dkvs[0]] + [swap_with(dkvs[i], "blk", i) for i in range(1, blk)])
    own_dkv = own_dkv.astype(BF16)
    proj_grad = jnp.concatenate(
        [dq * jnp.asarray(0.125, BF16), own_dkv[:, :group], own_dkv[:, wide : wide + group]], 1
    )
    token_parts = dot_nt(proj_grad, attend_own.reshape(width, 3 * group))
    token_low = token_parts.astype(BF16)
    tokens_grad = attn_grad + total(
        [token_parts[:rows]]
        + [swap_with(token_low[j * rows : (j + 1) * rows], "uly", j) for j in range(1, uly)]
    )
    attend_grad = dot_tn(x_rows, proj_grad).astype(BF16)
    attend_grad = attend_grad.reshape(dp, blk, share, 3 * group)
    bias_sum = jnp.sum(proj_grad.astype(F32), 0)[None]
    bias_rows = pad_rows(bias_sum.astype(BF16), 16)
    attend_parts = [
        jnp.concatenate(
            [
                lax.dynamic_slice_in_dim(attend_grad, b ^ i, 1, 1).reshape(-1, 3 * group),
                bias_rows,
            ],
            0,
        )
        for i in range(blk)
    ]
    attend_sum = total(
        [attend_parts[0]] + [swap_with(attend_parts[i], "blk", i) for i in range(1, blk)]
    ).astype(BF16)
    bias_half = jnp.broadcast_to(attend_sum[dp * share :], (dp, 16, 3 * group))
    attend_sum = attend_sum[: dp * share].reshape(dp, share, 3 * group)
    attend_owned = over_dp(jnp.concatenate([attend_sum, bias_half], 1))
    attend_all = in_plane(attend_owned)
    attend_out = attend_all[:, :, :share].reshape(blk, uly, share, 3, group)
    attend_out = attend_out.transpose(0, 2, 3, 1, 4).reshape(shard, 3 * width).astype(F32)
    bias_out = attend_all[0, :, share].astype(F32).reshape(uly, 3, group)
    query_bias_grad = lax.dynamic_slice_in_dim(bias_out[:, 0].reshape(width), z * shard, shard, 0)
    value_bias_grad = lax.dynamic_slice_in_dim(bias_out[:, 2].reshape(width), z * shard, shard, 0)

    vecs = [vec_owned[k * shard : (k + 1) * shard] for k in range(6)]
    return (
        mixed.reshape(tokens.shape),
        tokens_grad.reshape(tokens.shape),
        attend_out,
        query_bias_grad,
        value_bias_grad,
        mixer_out,
        vecs[0],
        vecs[1],
        vecs[2],
        expand_out,
        vec_owned[6 * shard :],
        shrink_out,
        vecs[3],
        vecs[4],
        vecs[5],
    )


def call(
    kernel,
    name,
    scalars,
    args,
    in_specs,
    out_shape,
    out_specs,
    scratch,
    grid,
    flops,
    vmem,
    aliases={},
):
    return pl.pallas_call(
        kernel,
        grid_spec=pltpu.PrefetchScalarGridSpec(
            num_scalar_prefetch=1,
            grid=grid,
            in_specs=in_specs,
            out_specs=out_specs,
            scratch_shapes=scratch,
        ),
        out_shape=out_shape,
        compiler_params=pltpu.CompilerParams(vmem_limit_bytes=vmem * 2**20),
        input_output_aliases=aliases,
        cost_estimate=pl.CostEstimate(flops=flops, bytes_accessed=1, transcendentals=0),
        name=name,
    )(scalars, *args)


def whole(shape):
    return pl.BlockSpec(shape, lambda *_: (0,) * len(shape))


def after(value, *deps):
    return lax.optimization_barrier((value, *deps))[0]


def slot(offset):
    return (offset & 1) * 2 + (offset >> 1)


def one_hot(rows, cols, row_offset=0, col_offset=0):
    row = lax.broadcasted_iota(jnp.int32, (rows, cols), 0) + row_offset
    col = lax.broadcasted_iota(jnp.int32, (rows, cols), 1) + col_offset
    return jnp.where(row == col, 1.0, 0.0).astype(BF16)


def fetch_kernel(sizes, idx, attend_ref, expand_ref, shrink_ref, mixer_ref, *refs):
    uly, dp, group, unit = sizes
    vec_refs, (first_ref, feed_ref) = refs[:-2], refs[-2:]
    share = attend_ref.shape[1]
    shard, width = mixer_ref.shape
    u = idx[1]
    part = idx[0] * uly + u
    take = one_hot(width, group, 0, u * group)
    for c in range(3):
        cols = dot_nn(attend_ref[0, :, c * width : (c + 1) * width], take)
        first_ref[:share, c * group : (c + 1) * group] = cols.astype(BF16)
    first_ref[share:, :] = jnp.zeros_like(first_ref[share:, :])
    rows = share // dp
    mixer = dot_nn(one_hot(rows, shard, part * rows, 0), mixer_ref[...]).astype(BF16)
    for k in range(dp):
        here = slice(k * rows, (k + 1) * rows)
        first_ref[here, 3 * group :] = mixer[:, k * group : (k + 1) * group]
    line = share
    for ref in vec_refs:
        for k in range(ref.shape[0] // shard):
            first_ref[line : line + 1, :shard] = ref[k * shard : (k + 1) * shard].reshape(1, shard)
            line += 1
    take = one_hot(width, unit, 0, part * unit)
    half = shard // 2
    for k in range(dp):
        cols = dot_nn(expand_ref[:, k * width : (k + 1) * width], take).astype(BF16)
        feed_ref[:half, k * unit : (k + 1) * unit] = cols[:half]
        feed_ref[:half, (dp + k) * unit : (dp + k + 1) * unit] = cols[half:]
    feed_ref[half:, :] = shrink_ref[0]


def project_kernel(sizes, idx, *refs):
    uly, blk, dp, group, unit = sizes
    x_refs, refs = refs[:uly], refs[uly:]
    mine_refs, refs = refs[:dp], refs[dp:]
    other_refs, refs = refs[:dp], refs[dp:]
    w_ref, q_ref, kv_ref, vec_ref, eb_ref, mixer_ref = refs
    b, u, z, length = idx[0], idx[1], idx[2], idx[3]
    rows, width = x_refs[0].shape
    wide = q_ref.shape[1]
    pad = wide - group
    share = mine_refs[0].shape[0] - 16
    shard = 2 * share
    parts = uly * blk
    for c in range(3):
        w_ref[:, c * wide + group : (c + 1) * wide] = jnp.zeros((width, pad), BF16)
    own_vec = jnp.zeros((16, shard), F32)
    all_vec = jnp.zeros((16, width), F32)
    lines = share // dp
    for j in range(dp):
        for k in range(dp):
            mixer_ref[j * lines : (j + 1) * lines, k * group : (k + 1) * group] = mine_refs[j][
                k * lines : (k + 1) * lines, 3 * group :
            ]
        for ref, core in ((mine_refs[j], b), (other_refs[j], 1 - b)):
            start = pl.multiple_of((z ^ j) * shard + core * share, share)
            for c in range(3):
                w_ref[pl.ds(start, share), c * wide : c * wide + group] = ref[
                    :share, c * group : (c + 1) * group
                ]
        vec = mine_refs[j][share:, :shard]
        own_vec += jnp.where((z ^ j) == u, 1.0, 0.0) * vec.astype(F32)
        all_vec += dot_nn(vec, one_hot(shard, width, (z ^ j) * shard, 0))
    vec_ref[...] = all_vec

    low = all_vec.astype(BF16)
    part = b * uly + u
    eb = jnp.zeros((parts, dp * unit), F32)
    for parity in range(2):
        col = lax.broadcasted_iota(jnp.int32, (width, dp * unit), 1)
        row = lax.broadcasted_iota(jnp.int32, (width, dp * unit), 0)
        source = col + (col // unit) * (shard - unit) + parity * unit
        lanes = dot_nn(low, jnp.where(row == source, 1.0, 0.0).astype(BF16)).astype(BF16)
        owner = lax.broadcasted_iota(jnp.int32, (parts, 16), 0) ^ part
        line = lax.broadcasted_iota(jnp.int32, (parts, 16), 1)
        wanted = ((owner & 1) == parity) & (line == 8 + (owner >> 1))
        eb += dot_nn(jnp.where(wanted, 1.0, 0.0).astype(BF16), lanes)
    eb_ref[...] = eb

    lane = lax.broadcasted_iota(jnp.int32, (1, wide), 1)
    mark = jnp.where(lane == group, 1.0, 0.0)
    zeros = jnp.zeros((1, pad), F32)
    q_bias = jnp.concatenate([own_vec[0:1], zeros], 1)
    v_bias = jnp.concatenate([own_vec[1:2], zeros], 1)
    for j in range(uly):
        x = x_refs[j][...]
        here = slice(j * rows, (j + 1) * rows)
        q = dot_nn(x, w_ref[:, :wide]) + q_bias
        q_ref[here, :] = (q * (0.125 * LOG2E) + mark).astype(BF16)
        first = (b * uly + (u ^ j)) * rows
        position = lax.broadcasted_iota(jnp.int32, (rows, 1), 0) + first
        masked = jnp.where(position < length, 0.0, MASKED)
        k = dot_nn(x, w_ref[:, wide : 2 * wide]) + masked * mark
        kv_ref[here, :wide] = k.astype(BF16)
        kv_ref[here, wide:] = (dot_nn(x, w_ref[:, 2 * wide :]) + v_bias).astype(BF16)


def attend_kernel(heads, blocks, q_ref, *refs):
    kv_refs = refs[:blocks]
    o_refs = refs[blocks:-2]
    lse_ref, vt_ref = refs[-2:]
    group = heads * HD
    wide = q_ref.shape[1]
    rows = kv_refs[0].shape[0]

    @pl.when(pl.program_id(0) == 0)
    def _():
        for i in range(blocks):
            vt_ref[:, i * rows : (i + 1) * rows] = kv_refs[i][:, wide : wide + group].T

    q = q_ref[...]
    outs = []
    for head in range(heads):
        q_head = jnp.where(head_lanes(wide, head, group), q, jnp.zeros_like(q))
        scores = [dot_nt(kv_refs[i][:, :wide], q_head) for i in range(blocks)]
        top = jnp.max(scores[0], axis=0, keepdims=True)
        for i in range(1, blocks):
            top = jnp.maximum(top, jnp.max(scores[i], axis=0, keepdims=True))
        norm = jnp.zeros_like(top)
        acc = None
        for i in range(blocks):
            probs = jnp.exp2(scores[i] - top)
            norm = norm + jnp.sum(probs, axis=0, keepdims=True)
            part = dot_nn(
                vt_ref[head * HD : (head + 1) * HD, i * rows : (i + 1) * rows], probs.astype(BF16)
            )
            acc = part if acc is None else acc + part
        outs.append(acc / norm)
        lse_ref[head : head + 1, :] = top + jnp.log2(norm)
    out = jnp.concatenate(outs, axis=0).T.astype(BF16)
    for j, o_ref in enumerate(o_refs):

        @pl.when(pl.program_id(0) == j)
        def _(o_ref=o_ref):
            o_ref[...] = out


def attend(q, kvs, heads, pieces):
    rows, wide = q.shape
    tile = rows // pieces
    group = heads * HD
    blocks = len(kvs)
    keys = blocks * rows
    out = pl.pallas_call(
        functools.partial(attend_kernel, heads, blocks),
        grid=(pieces,),
        in_specs=[pl.BlockSpec((tile, wide), lambda t: (t, 0))] + [whole(kvs[0].shape)] * blocks,
        out_specs=[whole((tile, group))] * pieces + [pl.BlockSpec((8, tile), lambda t: (0, t))],
        out_shape=[jax.ShapeDtypeStruct((tile, group), BF16)] * pieces
        + [jax.ShapeDtypeStruct((8, rows), F32)],
        scratch_shapes=[pltpu.VMEM((group, keys), BF16)],
        compiler_params=pltpu.CompilerParams(vmem_limit_bytes=16 * 2**20),
        cost_estimate=pl.CostEstimate(
            flops=4 * heads * rows * keys * wide,
            transcendentals=heads * rows * keys,
            bytes_accessed=2 * rows * wide * 3 + 2 * keys * (wide + group),
        ),
        name="attend",
    )(q, *kvs)
    return out[:-1], out[-1]


def first_norm_kernel(uly, idx, x_ref, *refs):
    o_refs = refs[:uly]
    m_ref, vec_ref, x1_ref, x1b_ref, normed_ref, inverse_ref = refs[uly:]
    group = o_refs[0].shape[1]
    acc = vec_ref[2:3, :]
    for j in range(uly):
        start = pl.multiple_of((idx[1] ^ j) * group, group)
        acc = acc + dot_nn(o_refs[j][...], m_ref[pl.ds(start, group), :])
    hidden = x_ref[...].astype(F32) + acc
    center = hidden - jnp.mean(hidden, -1, keepdims=True)
    inverse = lax.rsqrt(jnp.mean(center * center, -1, keepdims=True) + EPSILON)
    normed = center * inverse
    out = normed * vec_ref[3:4, :] + vec_ref[4:5, :]
    x1_ref[...] = out
    x1b_ref[...] = out.astype(BF16)
    normed_ref[...] = normed
    inverse_ref[...] = inverse


def rest_kernel(sizes, idx, expand_ref, shrink_ref, out_ref):
    uly, dp, unit = sizes
    width = shrink_ref.shape[1]
    half = expand_ref.shape[0] // 2
    for j in range(1, uly):
        part = idx[0] * uly + (idx[1] ^ j)
        take = one_hot(width, unit, 0, part * unit)
        for k in range(dp):
            cols = dot_nn(expand_ref[:, k * width : (k + 1) * width], take).astype(BF16)
            out_ref[j - 1, :half, k * unit : (k + 1) * unit] = cols[:half]
            out_ref[j - 1, :half, (dp + k) * unit : (dp + k + 1) * unit] = cols[half:]
        start = pl.multiple_of(part * unit, unit)
        out_ref[j - 1, half:, :] = shrink_ref[pl.ds(start, unit), :]


def mixer_kernel(sizes, idx, *refs):
    uly, dp = sizes
    pieces, (m_ref, turn_ref) = refs[:-2], refs[-2:]
    lines = pieces[0].shape[0] // dp
    b, u, z = idx[0], idx[1], idx[2]
    shard = 2 * uly * lines
    for k in range(dp):
        for p, ref in enumerate(pieces):
            part = (b * uly + u) ^ p
            turn_ref[pl.ds(pl.multiple_of(part * lines, 8), lines), :] = ref[
                k * lines : (k + 1) * lines, :
            ].astype(F32)
        start = pl.multiple_of((z ^ k) * shard, shard)
        m_ref[pl.ds(start, shard), :] = turn_ref[...].astype(BF16)


def assemble_kernel(sizes, k, idx, *refs):
    uly, dp, unit = sizes
    e_ref, s_ref, sem = refs[-3:]
    block = dp * unit
    shard = e_ref.shape[0] // dp
    half = shard // 2
    owner = idx[2] ^ k
    copies = []
    for j in range(uly):
        if k == 0:
            piece = refs[0] if j == 0 else refs[1].at[j - 1]
        else:
            piece = refs[2 + j]
        for h in range(2):
            start = pl.multiple_of(owner * shard + h * half, half)
            copies.append(
                pltpu.make_async_copy(
                    piece.at[pl.ds(0, half), pl.ds(h * block, block)],
                    e_ref.at[pl.ds(start, half), pl.ds(j * block, block)],
                    sem.at[3 * j + h],
                )
            )
        start = pl.multiple_of(j * block + owner * unit, unit)
        copies.append(
            pltpu.make_async_copy(
                piece.at[pl.ds(half, unit), :], s_ref.at[pl.ds(start, unit), :], sem.at[3 * j + 2]
            )
        )
    for copy in copies:
        copy.start()
    for copy in copies:
        copy.wait()


def assemble(scalars, sizes, k, weights, pieces):
    uly, dp, unit = sizes
    width = pieces[0].shape[1]
    block = uly * dp * unit
    hbm = pl.BlockSpec(memory_space=pl.ANY)
    return call(
        functools.partial(assemble_kernel, sizes, k),
        "assemble",
        scalars,
        [*weights, *pieces],
        [hbm] * (len(weights) + len(pieces)),
        [jax.ShapeDtypeStruct((width, block), BF16), jax.ShapeDtypeStruct((block, width), BF16)],
        [hbm] * 2,
        [pltpu.SemaphoreType.DMA((3 * uly,))],
        (1,),
        10**6,
        16,
        {1: 0, 2: 1} if weights else {},
    )


def feed_forward_kernel(uly, idx, mine_ref, other_ref, eb_ref, e_ref, s_ref, *refs):
    act_ref, slope_ref, y_ref, send_ref, x_ref = refs
    rows = mine_ref.shape[0]
    block = e_ref.shape[1] // uly
    x_ref[:rows] = mine_ref[...]
    x_ref[rows:] = other_ref[...]
    for j in range(uly):
        lanes = slice(j * block, (j + 1) * block)
        pre = dot_nn(x_ref[...], e_ref[:, lanes]) + eb_ref[j : j + 1, :]
        cdf = 0.5 * (1.0 + lax.erf(pre * 0.7071067811865476))
        pdf = jnp.exp(-0.5 * pre * pre) * 0.3989422804014327
        act_ref[:, lanes] = (pre * cdf).astype(BF16)
        slope_ref[:, lanes] = (cdf + pre * pdf).astype(BF16)
    out = dot_nn(act_ref[...], s_ref[...])
    y_ref[...] = out[:rows]
    send_ref[...] = out[rows:].astype(BF16)


def feed_forward(scalars, uly, mine, other, eb, weights):
    rows, width = mine.shape
    block = weights[0].shape[1]
    args = [mine, other, eb, *weights]
    return call(
        functools.partial(feed_forward_kernel, uly),
        "feed_forward",
        scalars,
        args,
        [whole(arg.shape) for arg in args],
        [
            jax.ShapeDtypeStruct((2 * rows, block), BF16),
            jax.ShapeDtypeStruct((2 * rows, block), BF16),
            jax.ShapeDtypeStruct((rows, width), F32),
            jax.ShapeDtypeStruct((rows, width), BF16),
        ],
        [whole((2 * rows, block))] * 2 + [whole((rows, width))] * 2,
        [pltpu.VMEM((2 * rows, width), BF16)],
        (1,),
        8 * rows * width * block,
        24,
    )


def final_norm_kernel(idx, x1_ref, y_ref, got_ref, vec_ref, cot_ref, *refs):
    mixed_ref, dh_ref, low_ref, sums_ref = refs
    hidden = x1_ref[...] + (y_ref[...] + got_ref[...].astype(F32) + vec_ref[5:6, :])
    gain = vec_ref[6:7, :]
    center = hidden - jnp.mean(hidden, -1, keepdims=True)
    inverse = lax.rsqrt(jnp.mean(center * center, -1, keepdims=True) + EPSILON)
    normed = center * inverse
    mixed_ref[...] = (normed * gain + vec_ref[7:8, :]).astype(BF16)
    grad = cot_ref[...].astype(F32)
    scaled = grad * gain
    dhidden = inverse * (
        scaled
        - jnp.mean(scaled, -1, keepdims=True)
        - normed * jnp.mean(scaled * normed, -1, keepdims=True)
    )
    dh_ref[...] = dhidden
    low_ref[...] = dhidden.astype(BF16)
    sums_ref[...] = jnp.zeros_like(sums_ref)
    sums_ref[0:1, :] = jnp.sum(dhidden, 0, keepdims=True)
    sums_ref[1:2, :] = jnp.sum(grad * normed, 0, keepdims=True)
    sums_ref[2:3, :] = jnp.sum(grad, 0, keepdims=True)


def shrink_grad_kernel(sizes, idx, d_mine, d_other, act_ref, *refs):
    uly, dp, unit = sizes
    near_x, far_x, near_y, far_y = (refs[2 * i : 2 * i + 2] for i in range(4))
    d_ref, turn_ref = refs[8:]
    block = dp * unit
    rows = d_mine.shape[0]
    d_ref[:rows] = d_mine[...]
    d_ref[rows:] = d_other[...]
    for j in range(uly):
        turn_ref[...] = dot_tn(act_ref[:, j * block : (j + 1) * block], d_ref[...]).astype(BF16)
        for k in range(dp):
            if k % 2 == 0:
                ref, at = (far_x if j % 2 else near_x), j // 2
            else:
                ref, at = (near_y if j < uly // 2 else far_y), j % 2
            start = pl.multiple_of((idx[2] ^ k) * unit, unit)
            into = slice((k // 2) * unit, (k // 2 + 1) * unit)
            ref[at][into, :] = turn_ref[pl.ds(start, unit), :]


def shrink_grad(scalars, sizes, ds, act):
    uly, dp, unit = sizes
    rows, width = ds[0].shape
    block = dp * unit
    half = (block // 2, width)
    return call(
        functools.partial(shrink_grad_kernel, sizes),
        "shrink_grad",
        scalars,
        [*ds, act],
        [whole((rows, width))] * 2 + [whole(act.shape)],
        [jax.ShapeDtypeStruct(half, BF16)] * 8,
        [whole(half)] * 8,
        [pltpu.VMEM((2 * rows, width), BF16), pltpu.VMEM((block, width), BF16)],
        (1,),
        4 * rows * width * uly * block,
        16,
    )


def feed_backward_kernel(sizes, idx, x_mine, x_other, d_mine, d_other, slope_ref, *refs):
    uly, dp, unit = sizes
    e_ref, s_ref, *refs = refs
    near_x, far_x, near_y, far_y = (refs[2 * i : 2 * i + 2] for i in range(4))
    deb_ref, dx_ref, send_ref, xt_ref, d_ref, turn_ref, dpre_ref = refs[8:]
    rows, width = x_mine.shape
    shard = width // dp
    half = width // 2
    block = dp * unit
    turn_ref[:, :rows] = x_mine[...].T
    turn_ref[:, rows:] = x_other[...].T
    for k in range(dp):
        start = pl.multiple_of((idx[2] ^ k) * shard, shard)
        into = slice(slot(k) * shard, (slot(k) + 1) * shard)
        xt_ref[into, :] = turn_ref[pl.ds(start, shard), :]
    d_ref[:rows] = d_mine[...]
    d_ref[rows:] = d_other[...]
    for j in range(uly):
        lanes = slice(j * block, (j + 1) * block)
        dpre = dot_nt(d_ref[...], s_ref[lanes, :])
        dpre = (dpre * slope_ref[:, lanes].astype(F32)).astype(BF16)
        dpre_ref[:, lanes] = dpre
        deb_ref[j : j + 1, :] = jnp.sum(dpre.astype(F32), 0, keepdims=True)
        dexpand = dot_nn(xt_ref[...], dpre).astype(BF16)
        (far_x if j % 2 else near_x)[j // 2][...] = dexpand[:half]
        (near_y if j < uly // 2 else far_y)[j % 2][...] = dexpand[half:]
    grad = dot_nt(dpre_ref[...], e_ref[...])
    dx_ref[...] = grad[:rows]
    send_ref[...] = grad[rows:].astype(BF16)


def feed_backward(scalars, sizes, xs, ds, slope, weights):
    uly, dp, unit = sizes
    rows, width = xs[0].shape
    block = dp * unit
    half = (width // 2, block)
    args = [*xs, *ds, slope, *weights]
    return call(
        functools.partial(feed_backward_kernel, sizes),
        "feed_backward",
        scalars,
        args,
        [whole(arg.shape) for arg in args],
        [jax.ShapeDtypeStruct(half, BF16)] * 8
        + [
            jax.ShapeDtypeStruct((uly, block), F32),
            jax.ShapeDtypeStruct((rows, width), F32),
            jax.ShapeDtypeStruct((rows, width), BF16),
        ],
        [whole(half)] * 8 + [whole((uly, block)), whole((rows, width)), whole((rows, width))],
        [
            pltpu.VMEM((width, 2 * rows), BF16),
            pltpu.VMEM((2 * rows, width), BF16),
            pltpu.VMEM((width, 2 * rows), BF16),
            pltpu.VMEM((2 * rows, uly * block), BF16),
        ],
        (1,),
        12 * rows * width * uly * block,
        24,
    )


def norm_backward_kernel(sizes, idx, dh2_ref, dx_ref, got_ref, normed_ref, inverse_ref, *refs):
    uly, dp, unit = sizes
    m_ref, vec_ref, grads_ref, deb_ref, *refs = refs
    o_refs, refs = refs[:uly], refs[uly:]
    dh_ref, *refs = refs
    do_refs, refs = refs[:uly], refs[uly:]
    keep_ref, send_ref, turn_ref = refs
    b, u, z = idx[0], idx[1], idx[2]
    group = o_refs[0].shape[1]
    share = group // 2
    width = dx_ref.shape[1]
    parts = 2 * uly
    grad = dh2_ref[...] + dx_ref[...] + got_ref[...].astype(F32)
    normed = normed_ref[...]
    scaled = grad * vec_ref[3:4, :]
    dhidden = inverse_ref[...] * (
        scaled
        - jnp.mean(scaled, -1, keepdims=True)
        - normed * jnp.mean(scaled * normed, -1, keepdims=True)
    )
    dh_ref[...] = dhidden
    low = dhidden.astype(BF16)
    for j in range(uly):
        start = pl.multiple_of((u ^ j) * group, group)
        do_refs[j][...] = dot_nt(low, m_ref[pl.ds(start, group), :]).astype(BF16)
    line = lax.broadcasted_iota(jnp.int32, (8, width), 0)
    lines = jnp.zeros((8, width), F32)
    values = [
        jnp.sum(dhidden, 0, keepdims=True),
        jnp.sum(grad * normed, 0, keepdims=True),
        jnp.sum(grad, 0, keepdims=True),
        grads_ref[0:1, :],
        grads_ref[1:2, :],
        grads_ref[2:3, :],
    ]
    for k, value in enumerate(values):
        lines = jnp.where(line == k, value, lines)
    lines = lines.astype(BF16)
    owner = (lax.broadcasted_iota(jnp.int32, (parts, uly), 1) ^ u) + b * uly
    order = lax.broadcasted_iota(jnp.int32, (parts, uly), 0)
    order = jnp.where(order == owner, 1.0, 0.0).astype(BF16)
    ebs = dot_nn(order, deb_ref[...].astype(BF16)).astype(BF16)
    for j in range(uly):
        turn_ref[...] = dot_tn(o_refs[j][...], low).astype(BF16)
        place = slot(u ^ j ^ z)
        keep_ref[place, :share] = turn_ref[pl.ds(pl.multiple_of(b * share, share), share), :]
        send_ref[place, :share] = turn_ref[pl.ds(pl.multiple_of((1 - b) * share, share), share), :]
    for k in range(dp):
        shard = (z ^ k) * group
        own = dot_nn(lines, one_hot(width, group, 0, shard)).astype(BF16)
        ebk = dot_nn(ebs, one_hot(dp * unit, unit, 0, (z ^ k) * unit)).astype(BF16)
        for ref in (keep_ref, send_ref):
            ref[slot(k), share:, :] = jnp.zeros_like(ref[slot(k), share:, :])
            ref[slot(k), share : share + 8, :group] = own
            ref[slot(k), share + 8 : share + 16, :unit] = ebk


def attend_grad_kernel(heads, blocks, pieces, started, q_ref, lse_ref, *refs):
    do_refs, refs = refs[:pieces], refs[pieces:]
    o_refs, refs = refs[:pieces], refs[pieces:]
    kv_refs, refs = refs[:blocks], refs[blocks:]
    so_far, refs = refs[: blocks * started], refs[blocks * started :]
    dq_ref, *refs = refs
    dkv_refs, refs = refs[:blocks], refs[blocks:]
    kt_ref, dout_ref, prod_ref, *refs = refs
    dk_accs, dv_accs = refs[:blocks], refs[blocks:]
    group = heads * HD
    wide = q_ref.shape[1]
    rows = kv_refs[0].shape[0]

    @pl.when(pl.program_id(0) == 0)
    def _():
        for i in range(blocks):
            kt_ref[:, i * rows : (i + 1) * rows] = kv_refs[i][:, :group].T
            if started:
                dk_accs[i][...] = so_far[i][:, :wide].astype(F32) * LOG2E
                dv_accs[i][...] = so_far[i][:, wide : wide + group].astype(F32)
            else:
                dk_accs[i][...] = jnp.zeros_like(dk_accs[i])
                dv_accs[i][...] = jnp.zeros_like(dv_accs[i])

    for j in range(pieces):

        @pl.when(pl.program_id(0) == j)
        def _(j=j):
            dout_ref[...] = do_refs[j][...]
            prod_ref[...] = (do_refs[j][...].astype(F32) * o_refs[j][...].astype(F32)).T

    q = q_ref[...]
    dout = dout_ref[...]
    dqs = []
    for head in range(heads):
        q_head = jnp.where(head_lanes(wide, head, group), q, jnp.zeros_like(q))
        do_head = jnp.where(head_lanes(group, head), dout, jnp.zeros_like(dout))
        lse = lse_ref[head : head + 1, :]
        delta = jnp.sum(prod_ref[head * HD : (head + 1) * HD, :], axis=0, keepdims=True)
        acc = None
        for i in range(blocks):
            probs = jnp.exp2(dot_nt(kv_refs[i][:, :wide], q_head) - lse)
            dv_accs[i][...] += dot_nn(probs.astype(BF16), do_head)
            grads = dot_nt(kv_refs[i][:, wide : wide + group], do_head)
            grads = (probs * (grads - delta)).astype(BF16)
            dk_accs[i][...] += dot_nn(grads, q_head)
            part = dot_nn(
                kt_ref[head * HD : (head + 1) * HD, i * rows : (i + 1) * rows], grads
            )
            acc = part if acc is None else acc + part
        dqs.append(acc)
    dq_ref[...] = jnp.concatenate(dqs, axis=0).T.astype(BF16)

    @pl.when(pl.program_id(0) == pl.num_programs(0) - 1)
    def _():
        for i in range(blocks):
            dkv_refs[i][:, :group] = (dk_accs[i][:, :group] * LN2).astype(BF16)
            dkv_refs[i][:, group:wide] = jnp.zeros((rows, wide - group), BF16)
            dkv_refs[i][:, wide : wide + group] = dv_accs[i][...].astype(BF16)
            dkv_refs[i][:, wide + group :] = jnp.zeros((rows, wide - group), BF16)


def attend_grad(q, kvs, douts, outs, lse, heads, at, so_far):
    rows, wide = kvs[0].shape[0], q.shape[1]
    group = heads * HD
    blocks = len(kvs)
    pieces = len(douts)
    tile = douts[0].shape[0]
    keys = blocks * rows
    started = 1 if so_far else 0
    out = pl.pallas_call(
        functools.partial(attend_grad_kernel, heads, blocks, pieces, started),
        grid=(pieces,),
        in_specs=[
            pl.BlockSpec((tile, wide), lambda t: (t + at, 0)),
            pl.BlockSpec((8, tile), lambda t: (0, t + at)),
        ]
        + [whole((tile, group))] * (2 * pieces)
        + [whole(kvs[0].shape)] * (blocks + blocks * started),
        out_specs=[pl.BlockSpec((tile, group), lambda t: (t, 0))]
        + [whole(kvs[0].shape)] * blocks,
        out_shape=[jax.ShapeDtypeStruct((pieces * tile, group), BF16)]
        + [jax.ShapeDtypeStruct(kvs[0].shape, BF16)] * blocks,
        scratch_shapes=[
            pltpu.VMEM((group, keys), BF16),
            pltpu.VMEM((tile, group), BF16),
            pltpu.VMEM((group, tile), F32),
        ]
        + [pltpu.VMEM((rows, wide), F32)] * blocks
        + [pltpu.VMEM((rows, group), F32)] * blocks,
        compiler_params=pltpu.CompilerParams(vmem_limit_bytes=16 * 2**20),
        cost_estimate=pl.CostEstimate(
            flops=10 * heads * pieces * tile * keys * wide,
            transcendentals=heads * pieces * tile * keys,
            bytes_accessed=2 * rows * wide * 4 + 4 * keys * (wide + group),
        ),
        name="attend_grad",
    )(q, lse, *douts, *outs, *kvs, *so_far)
    return out[0], out[1:]


def project_grad_kernel(sizes, idx, *refs):
    uly, dp, group = sizes
    dq_refs, (own_ref, got_ref, *refs) = refs[:uly], refs[uly:]
    x_refs, refs = refs[:uly], refs[uly:]
    dproj_ref, keep_ref, send_ref = refs
    b, z = idx[0], idx[2]
    rows, width = x_refs[0].shape
    wide = own_ref.shape[1] // 2
    share = keep_ref.shape[1] - 16
    for k, ref in enumerate(dq_refs):
        here = slice(k * ref.shape[0], (k + 1) * ref.shape[0])
        dproj_ref[here, :group] = ref[...] * jnp.asarray(0.125, BF16)
    dproj_ref[:, group:wide] = jnp.zeros((uly * rows, wide - group), BF16)
    dproj_ref[:, wide:] = (own_ref[...].astype(F32) + got_ref[...].astype(F32)).astype(BF16)
    sums = jnp.sum(dproj_ref[...].astype(F32), 0, keepdims=True).astype(BF16)
    grad = None
    for j in range(uly):
        part = dot_tn(x_refs[j][...], dproj_ref[j * rows : (j + 1) * rows, :])
        grad = part if grad is None else grad + part
    grad = grad.astype(BF16)
    for ref, mine in ((keep_ref, True), (send_ref, False)):
        for c in range(3):
            lanes = slice(c * wide, c * wide + group)
            into = slice(c * group, (c + 1) * group)
            for s in range(dp):
                for core in range(2):
                    start = (s * 2 + core) * share

                    @pl.when((b == core) == mine)
                    def _(start=start, s=s, ref=ref, lanes=lanes, into=into):
                        ref[slot(s ^ z), :share, into] = grad[start : start + share, lanes]

                ref[s, share:, into] = jnp.broadcast_to(sums[:, lanes], (16, group))


def token_grad_kernel(uly, idx, dproj_ref, w_ref, dh_ref, *out_refs):
    rows = dh_ref.shape[0]
    for j in reversed(range(uly)):
        part = dot_nt(dproj_ref[j * rows : (j + 1) * rows, :], w_ref[...])
        if j == 0:
            part = part + dh_ref[...]
        out_refs[j][...] = part.astype(out_refs[j].dtype)


def pack_kernel(idx, sx_ref, sx1_ref, sx2_ref, sy_ref, sy1_ref, sy2_ref, keep_ref, got_ref, *refs):
    unit = sx2_ref.shape[0] // 2
    for out_refs, first, s_refs in (
        (refs[:2], 0, (sx_ref, sx1_ref, sx2_ref)),
        (refs[2:], 2, (sy_ref, sy1_ref, sy2_ref)),
    ):
        for k, out_ref in enumerate(out_refs):
            rows = slice(k * unit, (k + 1) * unit)
            value = s_refs[0][rows].astype(F32) + s_refs[1][rows].astype(F32)
            out_ref[:unit, :] = (value + s_refs[2][rows].astype(F32)).astype(BF16)
            value = keep_ref[first + k].astype(F32) + got_ref[first + k].astype(F32)
            out_ref[unit:, :] = value.astype(BF16)


def finish_shrink_kernel(sizes, idx, *refs):
    uly, unit = sizes
    pieces, (shrink_ref, mixer_ref, vec_ref, wide_ref, sum_ref, sem) = refs[: 2 * uly], refs[2 * uly :]
    share = mixer_ref.shape[0] // 2
    part = idx[0] * uly + idx[1]
    copies = []
    for p, ref in enumerate(pieces):
        wide_ref[p] = ref[:unit, :].astype(F32)
        start = pl.multiple_of((part ^ p) * unit, unit)
        copies.append(
            pltpu.make_async_copy(wide_ref.at[p], shrink_ref.at[pl.ds(start, unit), :], sem.at[p])
        )
        copies[-1].start()

    def plane_sum(refs, rows):
        values = [ref[rows, :].astype(F32) for ref in refs]
        return (values[0] + values[1]) + (values[2] + values[3])

    for i, core in enumerate((idx[0], 1 - idx[0])):
        group = pieces[i * uly : (i + 1) * uly]
        sum_ref[i] = plane_sum(group, slice(unit, unit + share))
        start = pl.multiple_of(core * share, share)
        copies.append(
            pltpu.make_async_copy(
                sum_ref.at[i], mixer_ref.at[pl.ds(start, share), :], sem.at[2 * uly + i]
            )
        )
        copies[-1].start()
    vec_ref[...] = plane_sum(pieces[:uly], slice(unit + share, unit + share + 16))
    for copy in copies:
        copy.wait()


def finish_expand_kernel(sizes, idx, *refs):
    uly, dp, unit = sizes
    pieces, (out_ref, turn_ref, wide_ref, sem) = refs[:-4], refs[-4:]
    width = turn_ref.shape[0]
    part = idx[0] * uly + idx[1]
    col = lax.broadcasted_iota(jnp.int32, (width, width), 1)
    row = lax.broadcasted_iota(jnp.int32, (width, width), 0)
    source = col + ((col // unit) ^ part) * unit - (col // unit) * unit
    turn_ref[...] = jnp.where(row == source, 1.0, 0.0).astype(BF16)
    copies = []
    for k in range(dp):
        line = jnp.concatenate([ref[:, k * unit : (k + 1) * unit] for ref in pieces], 1)
        wide_ref[k] = dot_nn(line, turn_ref[...])
        copies.append(
            pltpu.make_async_copy(
                wide_ref.at[k], out_ref.at[:, pl.ds(k * width, width)], sem.at[k]
            )
        )
        copies[-1].start()
    for copy in copies:
        copy.wait()


def finish_attend_kernel(uly, idx, *refs):
    mine, refs = refs[:uly], refs[uly:]
    other, refs = refs[:uly], refs[uly:]
    out_ref, bias_ref, wide_ref, sem = refs
    b, u, z = idx[0], idx[1], idx[2]
    share = mine[0].shape[0] - 16
    group = mine[0].shape[1] // 3
    width = uly * group
    copies = []
    for i, (group_refs, core) in enumerate(((mine, b), (other, 1 - b))):
        start = pl.multiple_of(core * share, share)
        for c in range(3):
            acc = None
            for j in range(uly):
                put = one_hot(group, width, (u ^ j) * group, 0)
                value = dot_nn(group_refs[j][:share, c * group : (c + 1) * group], put)
                acc = value if acc is None else acc + value
            wide_ref[3 * i + c] = acc
            copies.append(
                pltpu.make_async_copy(
                    wide_ref.at[3 * i + c],
                    out_ref.at[pl.ds(start, share), pl.ds(c * width, width)],
                    sem.at[3 * i + c],
                )
            )
            copies[-1].start()
    bias = jnp.zeros((8, 3 * group), F32)
    for j in range(uly):
        lines = mine[j][share : share + 16, :].astype(F32)[:8]
        bias += jnp.where((u ^ j) == z, 1.0, 0.0) * lines
    bias_ref[...] = bias
    for copy in copies:
        copy.wait()


def on_device(*args):
    (
        tokens,
        lengths,
        cotangent,
        attend_weight,
        query_bias,
        value_bias,
        mixer_weight,
        mixer_bias,
        attn_gain,
        attn_shift,
        expand_weight,
        expand_bias,
        shrink_weight,
        shrink_bias,
        final_gain,
        final_shift,
    ) = args
    uly = lax.axis_size("uly")
    blk = lax.axis_size("blk")
    dp = lax.axis_size("dp")
    width = tokens.shape[-1]
    rows = tokens.shape[0] * tokens.shape[1]
    heads = HEADS // uly
    group = heads * HD
    wide = -(-(group + 1) // 128) * 128
    shard = attend_weight.shape[0]
    hidden = expand_weight.shape[1]
    parts = blk * uly
    unit = hidden // (parts * dp)
    share = shard // blk
    if not (blk == 2 and uly == 4 and dp == 4 and shard == group and unit * 2 == shard and share % 16 == 0):
        return general_device(*args)
    u = lax.axis_index("uly")
    b = lax.axis_index("blk")
    z = lax.axis_index("dp")
    mixer_rows = share // dp
    feed_rows = shard // 2 + unit
    block_rows = uly * rows
    cols = 3 * wide

    x = tokens.reshape(rows, width)
    xs = [x, swap_with(x, "uly", 1), swap_with(x, "uly", 2)]
    xs.append(swap_with(after(x, *xs[1:]), "uly", 3))
    scalars = jnp.stack([b, u, z, lengths[0]]).astype(jnp.int32)
    vectors = [query_bias, value_bias, mixer_bias, attn_gain, attn_shift, shrink_bias]
    vectors += [final_gain, final_shift, expand_bias]
    first, feed = call(
        functools.partial(fetch_kernel, (uly, dp, group, unit)),
        "fetch",
        scalars,
        [
            attend_weight.reshape(blk, share, 3 * width),
            expand_weight,
            shrink_weight.reshape(parts, unit, width),
            mixer_weight,
            *vectors,
        ],
        [
            pl.BlockSpec((1, share, 3 * width), lambda t, s: (s[0], 0, 0)),
            whole(expand_weight.shape),
            pl.BlockSpec((1, unit, width), lambda t, s: (s[0] * uly + s[1], 0, 0)),
            whole(mixer_weight.shape),
            *[whole(vector.shape) for vector in vectors],
        ],
        [
            jax.ShapeDtypeStruct((share + 16, width), BF16),
            jax.ShapeDtypeStruct((feed_rows, width), BF16),
        ],
        [whole((share + 16, width)), whole((feed_rows, width))],
        [],
        (1,),
        10**9,
        58,
    )
    feeds = [None, swap_with(feed, "dp", 1)]
    mine = [first, None, swap_with(first, "dp", 2), swap_with(first, "dp", 3)]
    mine[1] = swap_with(after(first, *xs[1:3]), "dp", 1)
    feeds.append(swap_with(after(feed, *mine[1:]), "dp", 2))
    plane_one = [swap_with(feeds[1], "uly", j) for j in range(1, uly)]
    other = [swap_with(after(piece, *plane_one), "blk", 1) for piece in mine]
    rest = call(
        functools.partial(rest_kernel, (uly, dp, unit)),
        "fetch_rest",
        scalars,
        [expand_weight, shrink_weight],
        [whole(expand_weight.shape), whole(shrink_weight.shape)],
        jax.ShapeDtypeStruct((uly - 1, shard // 2 + unit, width), BF16),
        whole((uly - 1, shard // 2 + unit, width)),
        [],
        (1,),
        10**9,
        16,
    )

    w_own, q, kv, vec, eb, mixer_mine = call(
        functools.partial(project_kernel, (uly, blk, dp, group, unit)),
        "project",
        scalars,
        [*after(xs, feeds[1]), *mine, *other],
        [whole((rows, width))] * uly + [whole(first.shape)] * (2 * dp),
        [
            jax.ShapeDtypeStruct((width, cols), BF16),
            jax.ShapeDtypeStruct((block_rows, wide), BF16),
            jax.ShapeDtypeStruct((block_rows, 2 * wide), BF16),
            jax.ShapeDtypeStruct((16, width), F32),
            jax.ShapeDtypeStruct((parts, dp * unit), F32),
            jax.ShapeDtypeStruct((dp * mixer_rows, width), BF16),
        ],
        [
            whole((width, cols)),
            whole((block_rows, wide)),
            whole((block_rows, 2 * wide)),
            whole((16, width)),
            whole((parts, dp * unit)),
            whole((dp * mixer_rows, width)),
        ],
        [],
        (1,),
        2 * block_rows * width * cols,
        16,
    )
    kv_send, mixer_mine = after((kv, mixer_mine), feeds[2])
    kvs = [kv, swap_with(kv_send, "blk", 1)]

    mixer_plane = [swap_with(mixer_mine, "uly", j) for j in range(1, uly)]

    plane_two = [swap_with(feeds[2], "uly", j) for j in range(1, uly)]
    feed_three = swap_with(after(feed, feeds[2]), "dp", 3)
    outs, lse = attend(after(q, rest, feeds[2]), kvs, heads, uly)
    outs, mixer_plane, plane_two, feed_three = after((outs, mixer_plane, plane_two, feed_three))
    feeds.append(feed_three)
    plane_three = [swap_with(feed_three, "uly", j) for j in range(1, uly)]
    mixer_parts = [mixer_mine, *mixer_plane]
    mixer_parts += [swap_with(piece, "blk", 1) for piece in mixer_parts]
    mixer_all = call(
        functools.partial(mixer_kernel, (uly, dp)),
        "mixer_weight",
        scalars,
        mixer_parts,
        [whole(mixer_mine.shape)] * parts,
        jax.ShapeDtypeStruct((width, width), BF16),
        whole((width, width)),
        [pltpu.VMEM((shard, width), F32)],
        (1,),
        10**6,
        16,
    )

    sizes = (uly, dp, unit)
    weights = assemble(scalars, sizes, 0, [], [feed, rest])
    weights = assemble(scalars, sizes, 1, weights, [feeds[1], *plane_one])
    weights = assemble(scalars, sizes, 2, weights, [feeds[2], *plane_two])
    o_cols = after(outs, *plane_three, *weights, mixer_all)
    o_cols = [o_cols[0]] + [swap_with(o_cols[j], "uly", j) for j in range(1, uly)]
    square = (rows, width)
    weights = assemble(scalars, sizes, 3, weights, [feeds[3], *plane_three])
    x1, x1b, normed, inverse = call(
        functools.partial(first_norm_kernel, uly),
        "first_norm",
        scalars,
        [x, *o_cols, after(mixer_all, *weights), vec],
        [whole(square)] + [whole((rows, group))] * uly + [whole((width, width)), whole(vec.shape)],
        [
            jax.ShapeDtypeStruct(square, F32),
            jax.ShapeDtypeStruct(square, BF16),
            jax.ShapeDtypeStruct(square, F32),
            jax.ShapeDtypeStruct((rows, 1), F32),
        ],
        [whole(square), whole(square), whole(square), whole((rows, 1))],
        [],
        (1,),
        2 * rows * width * width,
        16,
    )
    x1b_other = swap_with(x1b, "blk", 1)
    act, slope, y_own, y_send = feed_forward(scalars, uly, x1b, x1b_other, eb, weights)
    mixed, dh2, dh2b, sums2 = call(
        final_norm_kernel,
        "final_norm",
        scalars,
        [x1, y_own, swap_with(y_send, "blk", 1), vec, cotangent.reshape(square)],
        [whole(square)] * 3 + [whole(vec.shape), whole(square)],
        [
            jax.ShapeDtypeStruct(square, BF16),
            jax.ShapeDtypeStruct(square, F32),
            jax.ShapeDtypeStruct(square, BF16),
            jax.ShapeDtypeStruct((8, width), F32),
        ],
        [whole(square)] * 3 + [whole((8, width))],
        [],
        (1,),
        10**6,
        16,
    )
    dh2b_other = swap_with(dh2b, "blk", 1)
    ds = [dh2b, dh2b_other]
    s_grads = shrink_grad(scalars, sizes, ds, act)
    s_near_x, s_far_x, s_near_y, s_far_y = (s_grads[2 * i : 2 * i + 2] for i in range(4))
    s_x1 = swap_with(s_far_x[1], "uly", 1)
    s_y1 = swap_with(s_far_y[1], "uly", 2)
    ds = after(ds, s_far_x[0])
    grads = feed_backward(scalars, sizes, [x1b, x1b_other], ds, slope, weights)
    e_near_x, e_far_x, e_near_y, e_far_y = (grads[2 * i : 2 * i + 2] for i in range(4))
    deb, dx_own, dx_send = grads[8:]

    def add(*values):
        return total(values).astype(BF16)

    dx_send, s_far_x0, s_far_y0, s_x1, s_y1 = after(
        (dx_send, s_far_x[0], s_far_y[0], s_x1, s_y1)
    )
    dx_got = swap_with(dx_send, "blk", 1)
    s_x0 = swap_with(s_far_x0, "uly", 1)
    s_y0 = swap_with(s_far_y0, "uly", 2)
    block = (dp, share + 16, width)
    dh1, *rest_out = call(
        functools.partial(norm_backward_kernel, sizes),
        "norm_backward",
        scalars,
        [dh2, dx_own, dx_got, normed, inverse, mixer_all]
        + [vec, sums2]
        + [deb, *o_cols],
        [whole(square)] * 4
        + [whole((rows, 1)), whole((width, width)), whole(vec.shape), whole(sums2.shape)]
        + [whole((uly, dp * unit))]
        + [whole((rows, group))] * uly,
        [jax.ShapeDtypeStruct(square, F32)]
        + [jax.ShapeDtypeStruct((rows, group), BF16)] * uly
        + [jax.ShapeDtypeStruct(block, BF16)] * 2,
        [whole(square)] + [whole((rows, group))] * uly + [whole(block)] * 2,
        [pltpu.VMEM((group, width), BF16)],
        (1,),
        4 * rows * width * width,
        16,
    )
    douts = [rest_out[0]] + [swap_with(rest_out[j], "uly", j) for j in range(1, uly)]
    m_keep, m_send = rest_out[uly:]

    def quarter(j, so_far, *deps):
        dout = after(douts[j], *deps)
        return attend_grad(q, kvs, [dout], [outs[j]], lse, heads, j, so_far)

    dq_0, dkvs = quarter(0, [])
    dq_0, m_send, s_x0, s_y0, s_x1, s_y1, e_far_x, e_far_y, *douts[1:] = after(
        (dq_0, m_send, s_x0, s_y0, s_x1, s_y1, e_far_x, e_far_y, *douts[1:])
    )
    s_next_x = add(s_near_x[1], s_x1)
    s_next_y = add(s_near_y[1], s_y1)
    s_xy = swap_with(s_next_x, "uly", 2)
    s_yx = swap_with(s_next_y, "uly", 1)
    m_got = swap_with(m_send, "blk", 1)
    e_x1 = swap_with(e_far_x[1], "uly", 1)
    e_y1 = swap_with(e_far_y[1], "uly", 2)

    dq_1, dkvs = quarter(1, dkvs, s_next_x, s_next_y)
    dq_1, s_xy, s_yx, m_got, e_far_x, e_far_y = after((dq_1, s_xy, s_yx, m_got, e_far_x, e_far_y))
    packed = (unit + share + 16, width)
    p_near_0, p_near_1, p_far_0, p_far_1 = call(
        pack_kernel,
        "pack",
        scalars,
        [s_near_x[0], s_x0, s_xy, s_near_y[0], s_y0, s_yx, m_keep, m_got],
        [whole(s_xy.shape)] * 6 + [whole(m_keep.shape)] * 2,
        [jax.ShapeDtypeStruct(packed, BF16)] * 4,
        [whole(packed)] * 4,
        [],
        (1,),
        10**6,
        16,
    )
    p_one_1 = swap_with(p_far_1, "dp", 1)
    e_x0 = swap_with(e_far_x[0], "uly", 1)
    e_y0 = swap_with(e_far_y[0], "uly", 2)

    dq_2, dkvs = quarter(2, dkvs, p_far_1)
    dq_2, e_x0, e_y0, e_x1, e_y1, p_one_1, p_far_0 = after(
        (dq_2, e_x0, e_y0, e_x1, e_y1, p_one_1, p_far_0)
    )
    p_one_0 = swap_with(p_far_0, "dp", 1)
    p_next = add(p_near_1, p_one_1)
    p_two = swap_with(p_next, "dp", 2)
    e_next_x = add(e_near_x[1], e_x1)
    e_next_y = add(e_near_y[1], e_y1)
    e_xy = swap_with(e_next_x, "uly", 2)
    e_yx = swap_with(e_next_y, "uly", 1)

    dq_3, dkvs = quarter(3, dkvs, e_next_x, e_next_y, p_next)
    dq_3, e_xy, e_yx, p_one_0, *dkvs = after((dq_3, e_xy, e_yx, p_one_0, *dkvs))
    dkv_got = swap_with(dkvs[1], "blk", 1)
    pair = (2, shard, dp * unit)
    e_near = add(e_near_x[0], e_x0, e_xy).reshape(pair)
    e_far = add(e_near_y[0], e_y0, e_yx).reshape(pair)
    dkv_got = after(dkv_got, e_near, e_far)
    dqs = [dq_0, dq_1, dq_2, dq_3]
    dproj, a_keep, a_send = call(
        functools.partial(project_grad_kernel, (uly, dp, group)),
        "project_grad",
        scalars,
        [*dqs, dkvs[0], dkv_got, *xs],
        [whole(dq_0.shape)] * uly + [whole(kv.shape)] * 2 + [whole(square)] * uly,
        [
            jax.ShapeDtypeStruct((block_rows, cols), BF16),
            jax.ShapeDtypeStruct((dp, share + 16, 3 * group), BF16),
            jax.ShapeDtypeStruct((dp, share + 16, 3 * group), BF16),
        ],
        [whole((block_rows, cols))] + [whole((dp, share + 16, 3 * group))] * 2,
        [],
        (1,),
        2 * block_rows * width * cols,
        16,
    )
    a_got = swap_with(a_send, "blk", 1)
    token_parts = call(
        functools.partial(token_grad_kernel, uly),
        "token_grad",
        scalars,
        [dproj, w_own, dh1],
        [whole((block_rows, cols)), whole((width, cols)), whole(square)],
        [jax.ShapeDtypeStruct(square, F32)] + [jax.ShapeDtypeStruct(square, BF16)] * (uly - 1),
        [whole(square)] * uly,
        [],
        (1,),
        2 * block_rows * width * cols,
        16,
    )

    def in_plane(own, *deps):
        own = after(own, *deps)
        return [own] + [swap_with(own, "uly", j) for j in range(1, uly)]

    def both_cores(pieces, *deps):
        return pieces + [swap_with(after(piece, *deps), "blk", 1) for piece in pieces]

    a_got = after(a_got, token_parts[0])
    a_near, a_far = add(a_keep[:2], a_got[:2]), add(a_keep[2:], a_got[2:])
    token_parts = after(token_parts, a_near, a_far)
    token_got = [swap_with(token_parts[j], "uly", j) for j in range(1, uly)]
    a_one = swap_with(a_far, "dp", 1)
    a_next = add(a_near[1], a_one[1])
    a_two = swap_with(a_next, "dp", 2)
    e_one = swap_with(after(e_far, a_next), "dp", 1)
    e_next = add(e_near[1], e_one[1])
    e_two = swap_with(e_next, "dp", 2)
    tokens_grad = total([token_parts[0], *token_got])
    p_own = add(p_near_0, p_one_0, p_two)
    p_plane = in_plane(p_own, *token_got)
    p_plane = both_cores(p_plane, a_two)
    shrink_out, mixer_out, vecs = call(
        functools.partial(finish_shrink_kernel, (uly, unit)),
        "finish_shrink",
        scalars,
        p_plane,
        [whole(p_own.shape)] * parts,
        [
            jax.ShapeDtypeStruct((hidden // dp, width), F32),
            jax.ShapeDtypeStruct((shard, width), F32),
            jax.ShapeDtypeStruct((16, width), F32),
        ],
        [pl.BlockSpec(memory_space=pl.ANY)] * 2 + [whole((16, width))],
        [
            pltpu.VMEM((parts, unit, width), F32),
            pltpu.VMEM((2, share, width), F32),
            pltpu.SemaphoreType.DMA((parts + 2,)),
        ],
        (1,),
        10**6,
        16,
    )
    e_own = add(e_near[0], e_one[0], e_two)
    e_plane = in_plane(e_own, *p_plane[1:uly])
    a_own = add(a_near[0], a_one[0], a_two)
    a_plane = in_plane(a_own, *p_plane[1:uly])
    e_plane = both_cores(e_plane, shrink_out)
    expand_out = call(
        functools.partial(finish_expand_kernel, sizes),
        "finish_expand",
        scalars,
        e_plane,
        [whole(e_own.shape)] * parts,
        jax.ShapeDtypeStruct((shard, hidden), F32),
        pl.BlockSpec(memory_space=pl.ANY),
        [
            pltpu.VMEM((width, width), BF16),
            pltpu.VMEM((dp, shard, width), F32),
            pltpu.SemaphoreType.DMA((dp,)),
        ],
        (1,),
        10**9,
        16,
    )
    a_plane = both_cores(a_plane, expand_out)
    attend_out, biases = call(
        functools.partial(finish_attend_kernel, uly),
        "finish_attend",
        scalars,
        a_plane,
        [whole(a_own.shape)] * parts,
        [jax.ShapeDtypeStruct((shard, 3 * width), F32), jax.ShapeDtypeStruct((8, 3 * group), F32)],
        [pl.BlockSpec(memory_space=pl.ANY), whole((8, 3 * group))],
        [pltpu.VMEM((6, share, width), F32), pltpu.SemaphoreType.DMA((6,))],
        (1,),
        10**9,
        16,
    )
    eb_out = vecs[8 : 8 + parts, :unit].reshape(-1)
    vecs = [vecs[k, :shard] for k in range(6)]
    return (
        mixed.reshape(tokens.shape),
        tokens_grad.reshape(tokens.shape),
        attend_out,
        biases[0, :group],
        biases[0, 2 * group :],
        mixer_out,
        vecs[0],
        vecs[1],
        vecs[2],
        expand_out,
        eb_out,
        shrink_out,
        vecs[3],
        vecs[4],
        vecs[5],
    )


def solution(mesh):
    row_spec = P("dp", ("blk", "uly"), None)
    matrix = P("dp", None)
    vector = P("dp")
    return jax.shard_map(
        on_device,
        mesh=mesh,
        in_specs=(
            row_spec,
            vector,
            row_spec,
            matrix,
            vector,
            vector,
            matrix,
            vector,
            vector,
            vector,
            matrix,
            vector,
            matrix,
            vector,
            vector,
            vector,
        ),
        out_specs=(
            row_spec,
            row_spec,
            matrix,
            vector,
            vector,
            matrix,
            vector,
            vector,
            vector,
            matrix,
            vector,
            matrix,
            vector,
            vector,
            vector,
        ),
        check_vma=False,
    )
```

```python
import functools

import jax
import jax.numpy as jnp
from jax import lax
from jax.experimental import pallas as pl
from jax.experimental.pallas import tpu as pltpu
from jax.sharding import PartitionSpec as P

HEADS = 12
HD = 64

EPSILON = 1e-12
MASKED = -1000000000.0
LOG2E = 1.4426950408889634
LN2 = 0.6931471805599453
F32 = jnp.float32
BF16 = jnp.bfloat16


def dot_nn(left, right):
    return lax.dot_general(left, right, (((1,), (0,)), ((), ())), preferred_element_type=F32)


def dot_nt(left, right):
    return lax.dot_general(left, right, (((1,), (1,)), ((), ())), preferred_element_type=F32)


def dot_tn(left, right):
    return lax.dot_general(left, right, (((0,), (0,)), ((), ())), preferred_element_type=F32)


def swap_with(value, axis, offset):
    size = lax.axis_size(axis)
    return lax.ppermute(value, axis, [(i, i ^ offset) for i in range(size)])


def xor_order(pieces, index):
    bit = 1
    while bit < len(pieces):
        flag = (index & bit) != 0
        pieces = [jnp.where(flag, pieces[p ^ bit], pieces[p]) for p in range(len(pieces))]
        bit *= 2
    return pieces


def total(values):
    acc = values[0].astype(F32)
    for value in values[1:]:
        acc = acc + value.astype(F32)
    return acc


def pad_rows(value, rows):
    return jnp.pad(value, ((0, rows - value.shape[0]), (0, 0)))


def head_lanes(width, head, ones_lane=None):
    lane = lax.broadcasted_iota(jnp.int32, (1, width), 1)
    keep = (lane >= head * HD) & (lane < (head + 1) * HD)
    if ones_lane is not None:
        keep = keep | (lane == ones_lane)
    return keep


def attend_forward_kernel(heads, blocks, q_ref, *refs):
    kv_refs = refs[:blocks]
    o_ref, lse_ref, vt_ref = refs[blocks:]
    group = heads * HD
    wide = q_ref.shape[1]
    rows = kv_refs[0].shape[0]

    @pl.when(pl.program_id(0) == 0)
    def _():
        for i in range(blocks):
            vt_ref[:, i * rows : (i + 1) * rows] = kv_refs[i][:, wide : wide + group].T

    q = q_ref[...]
    outs = []
    stats = []
    for head in range(heads):
        q_head = jnp.where(head_lanes(wide, head, group), q, jnp.zeros_like(q))
        scores = [dot_nt(kv_refs[i][:, :wide], q_head) for i in range(blocks)]
        top = jnp.max(scores[0], axis=0, keepdims=True)
        for i in range(1, blocks):
            top = jnp.maximum(top, jnp.max(scores[i], axis=0, keepdims=True))
        norm = jnp.zeros_like(top)
        acc = None
        for i in range(blocks):
            probs = jnp.exp2(scores[i] - top)
            norm = norm + jnp.sum(probs, axis=0, keepdims=True)
            part = dot_nn(
                vt_ref[head * HD : (head + 1) * HD, i * rows : (i + 1) * rows], probs.astype(BF16)
            )
            acc = part if acc is None else acc + part
        outs.append(acc / norm)
        stats.append(top + jnp.log2(norm))
    o_ref[...] = jnp.concatenate(outs, axis=0).T.astype(BF16)
    for head in range(heads):
        lse_ref[head : head + 1, :] = stats[head]


def attend_forward(q, kvs, heads, tile):
    rows, wide = q.shape
    group = heads * HD
    blocks = len(kvs)
    keys = blocks * rows
    whole = pl.BlockSpec(kvs[0].shape, lambda t: (0, 0))
    return pl.pallas_call(
        functools.partial(attend_forward_kernel, heads, blocks),
        grid=(rows // tile,),
        in_specs=[pl.BlockSpec((tile, wide), lambda t: (t, 0))] + [whole] * blocks,
        out_specs=[
            pl.BlockSpec((tile, group), lambda t: (t, 0)),
            pl.BlockSpec((8, tile), lambda t: (0, t)),
        ],
        out_shape=[
            jax.ShapeDtypeStruct((rows, group), BF16),
            jax.ShapeDtypeStruct((8, rows), F32),
        ],
        scratch_shapes=[pltpu.VMEM((group, keys), BF16)],
        compiler_params=pltpu.CompilerParams(vmem_limit_bytes=56 * 2**20),
        cost_estimate=pl.CostEstimate(
            flops=4 * heads * rows * keys * wide,
            transcendentals=heads * rows * keys,
            bytes_accessed=2 * rows * wide * 3 + 2 * keys * (wide + group),
        ),
        name="attend_forward",
    )(q, *kvs)


def attend_backward_kernel(heads, blocks, q_ref, do_ref, o_ref, lse_ref, *refs):
    kv_refs = refs[:blocks]
    dq_ref = refs[blocks]
    dkv_refs = refs[blocks + 1 : 2 * blocks + 1]
    kt_ref = refs[2 * blocks + 1]
    dk_accs = refs[2 * blocks + 2 : 3 * blocks + 2]
    dv_accs = refs[3 * blocks + 2 :]
    group = heads * HD
    wide = q_ref.shape[1]
    rows = kv_refs[0].shape[0]

    @pl.when(pl.program_id(0) == 0)
    def _():
        for i in range(blocks):
            kt_ref[:, i * rows : (i + 1) * rows] = kv_refs[i][:, :group].T
            dk_accs[i][...] = jnp.zeros_like(dk_accs[i])
            dv_accs[i][...] = jnp.zeros_like(dv_accs[i])

    q = q_ref[...]
    dout = do_ref[...]
    products = (dout.astype(F32) * o_ref[...].astype(F32)).T
    dqs = []
    for head in range(heads):
        q_head = jnp.where(head_lanes(wide, head, group), q, jnp.zeros_like(q))
        do_head = jnp.where(head_lanes(group, head), dout, jnp.zeros_like(dout))
        lse = lse_ref[head : head + 1, :]
        delta = jnp.sum(products[head * HD : (head + 1) * HD], axis=0, keepdims=True)
        acc = None
        for i in range(blocks):
            probs = jnp.exp2(dot_nt(kv_refs[i][:, :wide], q_head) - lse)
            dv_accs[i][...] += dot_nn(probs.astype(BF16), do_head)
            grads = dot_nt(kv_refs[i][:, wide : wide + group], do_head)
            grads = (probs * (grads - delta)).astype(BF16)
            dk_accs[i][...] += dot_nn(grads, q_head)
            part = dot_nn(
                kt_ref[head * HD : (head + 1) * HD, i * rows : (i + 1) * rows], grads
            )
            acc = part if acc is None else acc + part
        dqs.append(acc)
    dq_ref[...] = jnp.concatenate(dqs, axis=0).T.astype(BF16)

    @pl.when(pl.program_id(0) == pl.num_programs(0) - 1)
    def _():
        for i in range(blocks):
            dkv_refs[i][:, :group] = (dk_accs[i][:, :group] * LN2).astype(BF16)
            dkv_refs[i][:, wide : wide + group] = dv_accs[i][...].astype(BF16)


def attend_backward(q, kvs, dout, o, lse, heads, tile):
    rows, wide = q.shape
    group = heads * HD
    blocks = len(kvs)
    keys = blocks * rows
    whole = pl.BlockSpec(kvs[0].shape, lambda t: (0, 0))
    out = pl.pallas_call(
        functools.partial(attend_backward_kernel, heads, blocks),
        grid=(rows // tile,),
        in_specs=[
            pl.BlockSpec((tile, wide), lambda t: (t, 0)),
            pl.BlockSpec((tile, group), lambda t: (t, 0)),
            pl.BlockSpec((tile, group), lambda t: (t, 0)),
            pl.BlockSpec((8, tile), lambda t: (0, t)),
        ]
        + [whole] * blocks,
        out_specs=[pl.BlockSpec((tile, group), lambda t: (t, 0))] + [whole] * blocks,
        out_shape=[jax.ShapeDtypeStruct((rows, group), BF16)]
        + [jax.ShapeDtypeStruct(kvs[0].shape, BF16)] * blocks,
        scratch_shapes=[pltpu.VMEM((group, keys), BF16)]
        + [pltpu.VMEM((rows, wide), F32)] * blocks
        + [pltpu.VMEM((rows, group), F32)] * blocks,
        compiler_params=pltpu.CompilerParams(vmem_limit_bytes=56 * 2**20),
        cost_estimate=pl.CostEstimate(
            flops=10 * heads * rows * keys * wide,
            transcendentals=heads * rows * keys,
            bytes_accessed=2 * rows * wide * 4 + 4 * keys * (wide + group),
        ),
        name="attend_backward",
    )(q, dout, o, lse, *kvs)
    return out[0], out[1:]


def feed_kernel(
    x1_ref,
    x1b_ref,
    expand_ref,
    shrink_ref,
    ebias_ref,
    sbias_ref,
    gain_ref,
    shift_ref,
    cot_ref,
    mixed_ref,
    dx1_ref,
    dexpand_ref,
    dshrink_ref,
    debias_ref,
    vec_ref,
    act_ref,
    slope_ref,
    acc_ref,
    d2b_ref,
    x1t_ref,
):
    phase = pl.program_id(0)
    step = pl.program_id(1)
    last = pl.num_programs(1) - 1
    width = x1_ref.shape[1]

    @pl.when(phase == 0)
    def _():
        pre = dot_nn(x1b_ref[...], expand_ref[0]) + ebias_ref[0]
        cdf = 0.5 * (1.0 + lax.erf(pre * 0.7071067811865476))
        pdf = jnp.exp(-0.5 * pre * pre) * 0.3989422804014327
        act = (pre * cdf).astype(BF16)
        act_ref[step] = act
        slope_ref[step] = (cdf + pre * pdf).astype(BF16)
        part = dot_nn(act, shrink_ref[0])

        @pl.when(step == 0)
        def _():
            acc_ref[...] = part
            x1t_ref[...] = x1b_ref[...].T

        @pl.when(step > 0)
        def _():
            acc_ref[...] += part

        @pl.when(step == last)
        def _():
            hidden = x1_ref[...] + (acc_ref[...] + sbias_ref[...])
            center = hidden - jnp.mean(hidden, -1, keepdims=True)
            inverse = lax.rsqrt(jnp.mean(center * center, -1, keepdims=True) + EPSILON)
            normed = center * inverse
            mixed_ref[...] = (normed * gain_ref[...] + shift_ref[...]).astype(BF16)
            grad = cot_ref[...].astype(F32)
            scaled = grad * gain_ref[...]
            dhidden = inverse * (
                scaled
                - jnp.mean(scaled, -1, keepdims=True)
                - normed * jnp.mean(scaled * normed, -1, keepdims=True)
            )
            acc_ref[...] = dhidden
            d2b_ref[...] = dhidden.astype(BF16)
            vec_ref[...] = jnp.zeros_like(vec_ref)
            vec_ref[0:1, :] = jnp.sum(grad * normed, 0, keepdims=True)
            vec_ref[1:2, :] = jnp.sum(grad, 0, keepdims=True)
            vec_ref[2:3, :] = jnp.sum(dhidden, 0, keepdims=True)

    @pl.when(phase == 1)
    def _():
        d2b = d2b_ref[...]
        dpre = (dot_nt(d2b, shrink_ref[0]) * slope_ref[step].astype(F32)).astype(BF16)
        debias_ref[0] = jnp.sum(dpre.astype(F32), 0, keepdims=True)
        dexpand_ref[0] = dot_nn(x1t_ref[...], dpre).astype(BF16)
        dshrink_ref[0] = dot_tn(act_ref[step], d2b).astype(BF16)
        acc_ref[...] += dot_nt(dpre, expand_ref[0])

        @pl.when(step == last)
        def _():
            dx1_ref[...] = acc_ref[...]


def feed_forward_backward(x1, x1b, expand, shrink, ebias, sbias, gain, shift, cot):
    rows, width = x1.shape
    parts, _, block = expand.shape
    full = pl.BlockSpec((rows, width), lambda p, k: (0, 0))
    line = pl.BlockSpec((1, width), lambda p, k: (0, 0))
    return pl.pallas_call(
        feed_kernel,
        grid=(2, parts),
        in_specs=[
            full,
            full,
            pl.BlockSpec((1, width, block), lambda p, k: (k, 0, 0)),
            pl.BlockSpec((1, block, width), lambda p, k: (k, 0, 0)),
            pl.BlockSpec((1, 1, block), lambda p, k: (k, 0, 0)),
            line,
            line,
            line,
            full,
        ],
        out_specs=[
            full,
            full,
            pl.BlockSpec((1, width, block), lambda p, k: (p * k, 0, 0)),
            pl.BlockSpec((1, block, width), lambda p, k: (p * k, 0, 0)),
            pl.BlockSpec((1, 1, block), lambda p, k: (p * k, 0, 0)),
            pl.BlockSpec((8, width), lambda p, k: (0, 0)),
        ],
        out_shape=[
            jax.ShapeDtypeStruct((rows, width), BF16),
            jax.ShapeDtypeStruct((rows, width), F32),
            jax.ShapeDtypeStruct((parts, width, block), BF16),
            jax.ShapeDtypeStruct((parts, block, width), BF16),
            jax.ShapeDtypeStruct((parts, 1, block), F32),
            jax.ShapeDtypeStruct((8, width), F32),
        ],
        scratch_shapes=[
            pltpu.VMEM((parts, rows, block), BF16),
            pltpu.VMEM((parts, rows, block), BF16),
            pltpu.VMEM((rows, width), F32),
            pltpu.VMEM((rows, width), BF16),
            pltpu.VMEM((width, rows), BF16),
        ],
        compiler_params=pltpu.CompilerParams(vmem_limit_bytes=48 * 2**20),
        cost_estimate=pl.CostEstimate(
            flops=12 * rows * width * parts * block,
            transcendentals=2 * rows * parts * block,
            bytes_accessed=12 * width * parts * block,
        ),
        name="feed_forward_backward",
    )(x1, x1b, expand, shrink, ebias, sbias, gain, shift, cot)


def general_device(
    tokens,
    lengths,
    cotangent,
    attend_weight,
    query_bias,
    value_bias,
    mixer_weight,
    mixer_bias,
    attn_gain,
    attn_shift,
    expand_weight,
    expand_bias,
    shrink_weight,
    shrink_bias,
    final_gain,
    final_shift,
):
    uly = lax.axis_size("uly")
    blk = lax.axis_size("blk")
    dp = lax.axis_size("dp")
    u = lax.axis_index("uly")
    b = lax.axis_index("blk")
    z = lax.axis_index("dp")
    width = tokens.shape[-1]
    rows = tokens.shape[0] * tokens.shape[1]
    block_rows = uly * rows
    heads = HEADS // uly
    group = heads * HD
    wide = -(-(group + 1) // 128) * 128
    shard = attend_weight.shape[0]
    hidden = expand_weight.shape[1]
    parts = blk * uly
    unit = hidden // (parts * dp)
    share = shard // blk

    x = tokens.reshape(rows, width)
    x_rows = jnp.concatenate([x] + [swap_with(x, "uly", j) for j in range(1, uly)], 0)

    small = jnp.concatenate(
        [query_bias, value_bias, mixer_bias, attn_gain, attn_shift, shrink_bias]
        + [final_gain, final_shift, expand_bias]
    )
    small_rows = small.shape[0] // (3 * group)
    own_heads = lax.dynamic_slice_in_dim(attend_weight.reshape(shard, 3, uly, group), u, 1, 2)
    own_heads = own_heads.reshape(shard, 3 * group)
    first_piece = jnp.concatenate(
        [
            lax.dynamic_slice_in_dim(own_heads, b * share, share, 0),
            pad_rows(small.reshape(small_rows, 3 * group), 16),
        ]
    )
    first_all = lax.all_gather(first_piece, "dp", axis=0, tiled=False)
    halves = first_all[:, :share]
    halves = xor_order([halves] + [swap_with(halves, "blk", i) for i in range(1, blk)], b)
    attend_own = jnp.stack(halves, 1).reshape(width, 3, group)
    vectors = first_all[:, share : share + small_rows].reshape(dp, -1, shard).astype(F32)
    names = [vectors[:, k].reshape(width) for k in range(8)]
    bias_query, bias_value, bias_mixer, gain_attn, shift_attn, bias_shrink = names[:6]
    gain_final, shift_final = names[6:]
    bias_expand = vectors[:, 8:].reshape(dp, parts, unit).transpose(1, 0, 2)
    bias_expand = jnp.stack(
        xor_order(list(bias_expand.reshape(parts, dp * unit)), b * uly + u), 0
    ).reshape(parts, 1, dp * unit)

    mixer_own = lax.dynamic_slice_in_dim(mixer_weight, b * share, share, 0)
    mixer_all = jnp.stack(
        xor_order([mixer_own] + [swap_with(mixer_own, "dp", j) for j in range(1, dp)], z), 0
    )
    mixer_all = jnp.stack(
        xor_order([mixer_all] + [swap_with(mixer_all, "blk", i) for i in range(1, blk)], b), 1
    ).reshape(width, width)

    part = b * uly + u
    expand_own = lax.dynamic_slice_in_dim(
        expand_weight.reshape(shard, dp, parts, unit), part, 1, 2
    ).reshape(-1, width)
    shrink_own = lax.dynamic_slice_in_dim(shrink_weight.reshape(parts, unit, width), part, 1, 0)
    expand_rows = expand_own.shape[0]
    feed_own = jnp.concatenate([expand_own, shrink_own.reshape(unit, width)], 0)
    feed_all = lax.all_gather(feed_own, "dp", axis=0, tiled=False)
    expand_part = feed_all[:, :expand_rows].reshape(width, dp * unit)
    shrink_part = feed_all[:, expand_rows:].reshape(dp * unit, width)
    expand_two = jnp.stack([expand_part, swap_with(expand_part, "uly", 1)])
    shrink_two = jnp.stack([shrink_part, swap_with(shrink_part, "uly", 2)])
    expand_far = swap_with(expand_two, "uly", 2)
    shrink_far = swap_with(shrink_two, "uly", 1)
    expand_here = jnp.concatenate([expand_two, expand_far], 0)
    shrink_here = jnp.stack([shrink_two[0], shrink_far[0], shrink_two[1], shrink_far[1]], 0)
    expand_full = jnp.concatenate(
        [expand_here] + [swap_with(expand_here, "blk", i) for i in range(1, blk)], 0
    )
    shrink_full = jnp.concatenate(
        [shrink_here] + [swap_with(shrink_here, "blk", i) for i in range(1, blk)], 0
    )

    lane_pad = ((0, 0), (0, wide - group))
    bias_row = jnp.pad(lax.dynamic_slice_in_dim(bias_query, u * group, group, 0), lane_pad[1:])
    ones_lane = (jnp.arange(wide) == group).astype(F32)
    q = dot_nn(x_rows, jnp.pad(attend_own[:, 0], lane_pad)) + bias_row
    q = (q * (0.125 * LOG2E) + ones_lane).astype(BF16)
    kv_weight = jnp.concatenate([jnp.pad(attend_own[:, 1], lane_pad), attend_own[:, 2]], 1)
    kv_bias = jnp.concatenate(
        [jnp.zeros((wide,), F32), lax.dynamic_slice_in_dim(bias_value, u * group, group, 0)]
    )
    kv_ones = jnp.pad(ones_lane, (0, group))
    row_index = jnp.arange(block_rows, dtype=jnp.int32)
    positions = b * block_rows + ((row_index // rows) ^ u) * rows + row_index % rows
    key_mask = jnp.where(positions < lengths[0], 0.0, MASKED)
    kv = (dot_nn(x_rows, kv_weight) + kv_bias + key_mask[:, None] * kv_ones).astype(BF16)
    kvs = [kv] + [swap_with(kv, "blk", i) for i in range(1, blk)]

    o_rows, lse = attend_forward(q, kvs, heads, min(256, block_rows))
    pieces = [o_rows[j * rows : (j + 1) * rows] for j in range(uly)]
    pieces = [pieces[0]] + [swap_with(pieces[j], "uly", j) for j in range(1, uly)]
    mixer_in = jnp.concatenate(xor_order(pieces, u), 1)

    first_sum = x.astype(F32) + (dot_nn(mixer_in, mixer_all) + bias_mixer)
    center = first_sum - jnp.mean(first_sum, -1, keepdims=True)
    first_inv = lax.rsqrt(jnp.mean(center * center, -1, keepdims=True) + EPSILON)
    first_normed = center * first_inv
    first_out = first_normed * gain_attn + shift_attn
    first_low = first_out.astype(BF16)

    mixed, first_grad, expand_grad, shrink_grad, expand_bias_grad, vec_grads = (
        feed_forward_backward(
            first_out,
            first_low,
            expand_full,
            shrink_full,
            bias_expand,
            bias_shrink[None],
            gain_final[None],
            shift_final[None],
            cotangent.reshape(rows, width),
        )
    )

    scaled = first_grad * gain_attn
    attn_grad = first_inv * (
        scaled
        - jnp.mean(scaled, -1, keepdims=True)
        - first_normed * jnp.mean(scaled * first_normed, -1, keepdims=True)
    )
    attn_low = attn_grad.astype(BF16)
    out_grad = dot_nt(attn_low, mixer_all).astype(BF16)
    sends = xor_order([out_grad[:, j * group : (j + 1) * group] for j in range(uly)], u)
    dout_rows = jnp.concatenate(
        [sends[0]] + [swap_with(sends[j], "uly", j) for j in range(1, uly)], 0
    )
    dq, dkvs = attend_backward(q, kvs, dout_rows, o_rows, lse, heads, min(256, block_rows))

    mixer_grad = dot_tn(mixer_in, attn_low).astype(BF16)
    attn_gain_grad = jnp.sum(first_grad * first_normed, 0)
    attn_shift_grad = jnp.sum(first_grad, 0)
    mixer_bias_grad = jnp.sum(attn_grad, 0)
    ebg = jnp.stack(xor_order(list(expand_bias_grad.reshape(parts, dp * unit)), part), 0)
    ebg = ebg.reshape(parts, dp, unit).transpose(1, 0, 2).reshape(dp, parts * unit)
    vec_all = jnp.concatenate(
        [
            v.reshape(dp, shard)
            for v in (
                mixer_bias_grad,
                attn_gain_grad,
                attn_shift_grad,
                vec_grads[2],
                vec_grads[0],
                vec_grads[1],
            )
        ]
        + [ebg],
        1,
    ).astype(BF16)

    mixer_cols = width // blk
    mixer_part_rows = shard // uly
    vec_len = vec_all.shape[1]
    vec_rows = -(-vec_len // mixer_cols)
    vec_rows = -(-vec_rows // 16) * 16
    vec_block = jnp.pad(vec_all, ((0, 0), (0, vec_rows * mixer_cols - vec_len))).reshape(
        dp, vec_rows, mixer_cols
    )
    mixer_view = mixer_grad.reshape(dp, uly, mixer_part_rows, blk, mixer_cols)
    by_blk = xor_order([mixer_view[:, :, :, i] for i in range(blk)], b)
    mixer_parts = []
    for i in range(blk):
        by_uly = xor_order([by_blk[i][:, j] for j in range(uly)], u)
        mixer_parts.append(
            jnp.stack([jnp.concatenate([piece, vec_block], 1) for piece in by_uly], 0)
        )
    mixer_sum = total(
        [mixer_parts[0]] + [swap_with(mixer_parts[i], "blk", i) for i in range(1, blk)]
    ).astype(BF16)
    mixer_sum = total(
        [mixer_sum[0]] + [swap_with(mixer_sum[j], "uly", j) for j in range(1, uly)]
    ).astype(BF16)

    def over_blk(grad):
        return total(
            [grad[:uly]]
            + [swap_with(grad[i * uly : (i + 1) * uly], "blk", i) for i in range(1, blk)]
        ).astype(BF16)

    shrink_sum = over_blk(shrink_grad)
    expand_sum = over_blk(expand_grad)
    shrink_sum = shrink_sum.reshape(2, 2, dp * unit, width)
    expand_sum = expand_sum.reshape(2, 2, width, dp * unit)
    shrink_sum = total([shrink_sum[0], swap_with(shrink_sum[1], "uly", 2)]).astype(BF16)
    expand_sum = total([expand_sum[:, 0], swap_with(expand_sum[:, 1], "uly", 1)]).astype(BF16)
    shrink_sum = total([shrink_sum[0], swap_with(shrink_sum[1], "uly", 1)]).astype(BF16)
    expand_sum = total([expand_sum[0], swap_with(expand_sum[1], "uly", 2)]).astype(BF16)

    mixer_rows = mixer_sum.shape[1] * mixer_cols // width
    packed = jnp.concatenate(
        [
            expand_sum.reshape(dp, expand_rows, width),
            shrink_sum.reshape(dp, unit, width),
            mixer_sum.reshape(dp, mixer_rows, width),
        ],
        1,
    )

    def over_dp(value):
        sends = [lax.dynamic_slice_in_dim(value, z ^ j, 1, 0)[0] for j in range(dp)]
        return total([sends[0]] + [swap_with(sends[j], "dp", j) for j in range(1, dp)])

    owned = over_dp(packed)
    vec_owned = owned[expand_rows + unit :].reshape(-1, mixer_cols)[mixer_part_rows:]
    vec_owned = vec_owned.reshape(-1)[:vec_len]

    def in_plane(value):
        value = value.astype(BF16)
        value = jnp.stack(
            xor_order([value] + [swap_with(value, "uly", j) for j in range(1, uly)], u), 0
        )
        return jnp.stack(
            xor_order([value] + [swap_with(value, "blk", i) for i in range(1, blk)], b), 0
        )

    gathered = in_plane(owned).reshape(parts, -1, width)
    expand_out = gathered[:, :expand_rows].reshape(parts, shard, dp, unit)
    expand_out = expand_out.transpose(1, 2, 0, 3).reshape(shard, hidden).astype(F32)
    shrink_out = gathered[:, expand_rows : expand_rows + unit]
    shrink_out = shrink_out.reshape(parts * unit, width).astype(F32)
    mixer_out = gathered[:, expand_rows + unit :].reshape(blk, uly, -1, mixer_cols)
    mixer_out = mixer_out[:, :, :mixer_part_rows].transpose(1, 2, 0, 3)
    mixer_out = mixer_out.reshape(shard, width).astype(F32)

    own_dkv = total([dkvs[0]] + [swap_with(dkvs[i], "blk", i) for i in range(1, blk)])
    own_dkv = own_dkv.astype(BF16)
    proj_grad = jnp.concatenate(
        [dq * jnp.asarray(0.125, BF16), own_dkv[:, :group], own_dkv[:, wide : wide + group]], 1
    )
    token_parts = dot_nt(proj_grad, attend_own.reshape(width, 3 * group))
    token_low = token_parts.astype(BF16)
    tokens_grad = attn_grad + total(
        [token_parts[:rows]]
        + [swap_with(token_low[j * rows : (j + 1) * rows], "uly", j) for j in range(1, uly)]
    )
    attend_grad = dot_tn(x_rows, proj_grad).astype(BF16)
    attend_grad = attend_grad.reshape(dp, blk, share, 3 * group)
    bias_sum = jnp.sum(proj_grad.astype(F32), 0)[None]
    bias_rows = pad_rows(bias_sum.astype(BF16), 16)
    attend_parts = [
        jnp.concatenate(
            [
                lax.dynamic_slice_in_dim(attend_grad, b ^ i, 1, 1).reshape(-1, 3 * group),
                bias_rows,
            ],
            0,
        )
        for i in range(blk)
    ]
    attend_sum = total(
        [attend_parts[0]] + [swap_with(attend_parts[i], "blk", i) for i in range(1, blk)]
    ).astype(BF16)
    bias_half = jnp.broadcast_to(attend_sum[dp * share :], (dp, 16, 3 * group))
    attend_sum = attend_sum[: dp * share].reshape(dp, share, 3 * group)
    attend_owned = over_dp(jnp.concatenate([attend_sum, bias_half], 1))
    attend_all = in_plane(attend_owned)
    attend_out = attend_all[:, :, :share].reshape(blk, uly, share, 3, group)
    attend_out = attend_out.transpose(0, 2, 3, 1, 4).reshape(shard, 3 * width).astype(F32)
    bias_out = attend_all[0, :, share].astype(F32).reshape(uly, 3, group)
    query_bias_grad = lax.dynamic_slice_in_dim(bias_out[:, 0].reshape(width), z * shard, shard, 0)
    value_bias_grad = lax.dynamic_slice_in_dim(bias_out[:, 2].reshape(width), z * shard, shard, 0)

    vecs = [vec_owned[k * shard : (k + 1) * shard] for k in range(6)]
    return (
        mixed.reshape(tokens.shape),
        tokens_grad.reshape(tokens.shape),
        attend_out,
        query_bias_grad,
        value_bias_grad,
        mixer_out,
        vecs[0],
        vecs[1],
        vecs[2],
        expand_out,
        vec_owned[6 * shard :],
        shrink_out,
        vecs[3],
        vecs[4],
        vecs[5],
    )


def call(
    kernel,
    name,
    scalars,
    args,
    in_specs,
    out_shape,
    out_specs,
    scratch,
    grid,
    flops,
    vmem,
    aliases={},
):
    return pl.pallas_call(
        kernel,
        grid_spec=pltpu.PrefetchScalarGridSpec(
            num_scalar_prefetch=1,
            grid=grid,
            in_specs=in_specs,
            out_specs=out_specs,
            scratch_shapes=scratch,
        ),
        out_shape=out_shape,
        compiler_params=pltpu.CompilerParams(vmem_limit_bytes=vmem * 2**20),
        input_output_aliases=aliases,
        cost_estimate=pl.CostEstimate(flops=flops, bytes_accessed=1, transcendentals=0),
        name=name,
    )(scalars, *args)


def whole(shape):
    return pl.BlockSpec(shape, lambda *_: (0,) * len(shape))


def after(value, *deps):
    return lax.optimization_barrier((value, *deps))[0]


def slot(offset):
    return (offset & 1) * 2 + (offset >> 1)


def one_hot(rows, cols, row_offset=0, col_offset=0):
    row = lax.broadcasted_iota(jnp.int32, (rows, cols), 0) + row_offset
    col = lax.broadcasted_iota(jnp.int32, (rows, cols), 1) + col_offset
    return jnp.where(row == col, 1.0, 0.0).astype(BF16)


def fetch_kernel(sizes, idx, attend_ref, expand_ref, shrink_ref, mixer_ref, *refs):
    uly, dp, group, unit = sizes
    vec_refs, (first_ref, feed_ref) = refs[:-2], refs[-2:]
    share = attend_ref.shape[1]
    shard, width = mixer_ref.shape
    u = idx[1]
    part = idx[0] * uly + u
    take = one_hot(width, group, 0, u * group)
    for c in range(3):
        cols = dot_nn(attend_ref[0, :, c * width : (c + 1) * width], take)
        first_ref[:share, c * group : (c + 1) * group] = cols.astype(BF16)
    first_ref[share:, :] = jnp.zeros_like(first_ref[share:, :])
    rows = share // dp
    mixer = dot_nn(one_hot(rows, shard, part * rows, 0), mixer_ref[...]).astype(BF16)
    for k in range(dp):
        here = slice(k * rows, (k + 1) * rows)
        first_ref[here, 3 * group :] = mixer[:, k * group : (k + 1) * group]
    line = share
    for ref in vec_refs:
        for k in range(ref.shape[0] // shard):
            first_ref[line : line + 1, :shard] = ref[k * shard : (k + 1) * shard].reshape(1, shard)
            line += 1
    take = one_hot(width, unit, 0, part * unit)
    half = shard // 2
    for k in range(dp):
        cols = dot_nn(expand_ref[:, k * width : (k + 1) * width], take).astype(BF16)
        feed_ref[:half, k * unit : (k + 1) * unit] = cols[:half]
        feed_ref[:half, (dp + k) * unit : (dp + k + 1) * unit] = cols[half:]
    feed_ref[half:, :] = shrink_ref[0]


def project_kernel(sizes, idx, *refs):
    uly, blk, dp, group, unit = sizes
    x_refs, refs = refs[:uly], refs[uly:]
    mine_refs, refs = refs[:dp], refs[dp:]
    other_refs, refs = refs[:dp], refs[dp:]
    w_ref, q_ref, kv_ref, vec_ref, eb_ref, mixer_ref = refs
    b, u, z, length = idx[0], idx[1], idx[2], idx[3]
    rows, width = x_refs[0].shape
    wide = q_ref.shape[1]
    pad = wide - group
    share = mine_refs[0].shape[0] - 16
    shard = 2 * share
    parts = uly * blk
    for c in range(3):
        w_ref[:, c * wide + group : (c + 1) * wide] = jnp.zeros((width, pad), BF16)
    own_vec = jnp.zeros((16, shard), F32)
    all_vec = jnp.zeros((16, width), F32)
    lines = share // dp
    for j in range(dp):
        for k in range(dp):
            mixer_ref[j * lines : (j + 1) * lines, k * group : (k + 1) * group] = mine_refs[j][
                k * lines : (k + 1) * lines, 3 * group :
            ]
        for ref, core in ((mine_refs[j], b), (other_refs[j], 1 - b)):
            start = pl.multiple_of((z ^ j) * shard + core * share, share)
            for c in range(3):
                w_ref[pl.ds(start, share), c * wide : c * wide + group] = ref[
                    :share, c * group : (c + 1) * group
                ]
        vec = mine_refs[j][share:, :shard]
        own_vec += jnp.where((z ^ j) == u, 1.0, 0.0) * vec.astype(F32)
        all_vec += dot_nn(vec, one_hot(shard, width, (z ^ j) * shard, 0))
    vec_ref[...] = all_vec

    low = all_vec.astype(BF16)
    part = b * uly + u
    eb = jnp.zeros((parts, dp * unit), F32)
    for parity in range(2):
        col = lax.broadcasted_iota(jnp.int32, (width, dp * unit), 1)
        row = lax.broadcasted_iota(jnp.int32, (width, dp * unit), 0)
        source = col + (col // unit) * (shard - unit) + parity * unit
        lanes = dot_nn(low, jnp.where(row == source, 1.0, 0.0).astype(BF16)).astype(BF16)
        owner = lax.broadcasted_iota(jnp.int32, (parts, 16), 0) ^ part
        line = lax.broadcasted_iota(jnp.int32, (parts, 16), 1)
        wanted = ((owner & 1) == parity) & (line == 8 + (owner >> 1))
        eb += dot_nn(jnp.where(wanted, 1.0, 0.0).astype(BF16), lanes)
    eb_ref[...] = eb

    lane = lax.broadcasted_iota(jnp.int32, (1, wide), 1)
    mark = jnp.where(lane == group, 1.0, 0.0)
    zeros = jnp.zeros((1, pad), F32)
    q_bias = jnp.concatenate([own_vec[0:1], zeros], 1)
    v_bias = jnp.concatenate([own_vec[1:2], zeros], 1)
    for j in range(uly):
        x = x_refs[j][...]
        here = slice(j * rows, (j + 1) * rows)
        q = dot_nn(x, w_ref[:, :wide]) + q_bias
        q_ref[here, :] = (q * (0.125 * LOG2E) + mark).astype(BF16)
        first = (b * uly + (u ^ j)) * rows
        position = lax.broadcasted_iota(jnp.int32, (rows, 1), 0) + first
        masked = jnp.where(position < length, 0.0, MASKED)
        k = dot_nn(x, w_ref[:, wide : 2 * wide]) + masked * mark
        kv_ref[here, :wide] = k.astype(BF16)
        kv_ref[here, wide:] = (dot_nn(x, w_ref[:, 2 * wide :]) + v_bias).astype(BF16)


def attend_kernel(heads, blocks, q_ref, *refs):
    kv_refs = refs[:blocks]
    o_refs = refs[blocks:-2]
    lse_ref, vt_ref = refs[-2:]
    group = heads * HD
    wide = q_ref.shape[1]
    rows = kv_refs[0].shape[0]

    @pl.when(pl.program_id(0) == 0)
    def _():
        for i in range(blocks):
            vt_ref[:, i * rows : (i + 1) * rows] = kv_refs[i][:, wide : wide + group].T

    q = q_ref[...]
    outs = []
    for head in range(heads):
        q_head = jnp.where(head_lanes(wide, head, group), q, jnp.zeros_like(q))
        scores = [dot_nt(kv_refs[i][:, :wide], q_head) for i in range(blocks)]
        top = jnp.max(scores[0], axis=0, keepdims=True)
        for i in range(1, blocks):
            top = jnp.maximum(top, jnp.max(scores[i], axis=0, keepdims=True))
        norm = jnp.zeros_like(top)
        acc = None
        for i in range(blocks):
            probs = jnp.exp2(scores[i] - top)
            norm = norm + jnp.sum(probs, axis=0, keepdims=True)
            part = dot_nn(
                vt_ref[head * HD : (head + 1) * HD, i * rows : (i + 1) * rows], probs.astype(BF16)
            )
            acc = part if acc is None else acc + part
        outs.append(acc / norm)
        lse_ref[head : head + 1, :] = top + jnp.log2(norm)
    out = jnp.concatenate(outs, axis=0).T.astype(BF16)
    for j, o_ref in enumerate(o_refs):

        @pl.when(pl.program_id(0) == j)
        def _(o_ref=o_ref):
            o_ref[...] = out


def attend(q, kvs, heads, pieces):
    rows, wide = q.shape
    tile = rows // pieces
    group = heads * HD
    blocks = len(kvs)
    keys = blocks * rows
    out = pl.pallas_call(
        functools.partial(attend_kernel, heads, blocks),
        grid=(pieces,),
        in_specs=[pl.BlockSpec((tile, wide), lambda t: (t, 0))] + [whole(kvs[0].shape)] * blocks,
        out_specs=[whole((tile, group))] * pieces + [pl.BlockSpec((8, tile), lambda t: (0, t))],
        out_shape=[jax.ShapeDtypeStruct((tile, group), BF16)] * pieces
        + [jax.ShapeDtypeStruct((8, rows), F32)],
        scratch_shapes=[pltpu.VMEM((group, keys), BF16)],
        compiler_params=pltpu.CompilerParams(vmem_limit_bytes=16 * 2**20),
        cost_estimate=pl.CostEstimate(
            flops=4 * heads * rows * keys * wide,
            transcendentals=heads * rows * keys,
            bytes_accessed=2 * rows * wide * 3 + 2 * keys * (wide + group),
        ),
        name="attend",
    )(q, *kvs)
    return out[:-1], out[-1]


def first_norm_kernel(uly, idx, x_ref, *refs):
    o_refs = refs[:uly]
    m_ref, vec_ref, x1_ref, x1b_ref, normed_ref, inverse_ref = refs[uly:]
    group = o_refs[0].shape[1]
    acc = vec_ref[2:3, :]
    for j in range(uly):
        start = pl.multiple_of((idx[1] ^ j) * group, group)
        acc = acc + dot_nn(o_refs[j][...], m_ref[pl.ds(start, group), :])
    hidden = x_ref[...].astype(F32) + acc
    center = hidden - jnp.mean(hidden, -1, keepdims=True)
    inverse = lax.rsqrt(jnp.mean(center * center, -1, keepdims=True) + EPSILON)
    normed = center * inverse
    out = normed * vec_ref[3:4, :] + vec_ref[4:5, :]
    x1_ref[...] = out
    x1b_ref[...] = out.astype(BF16)
    normed_ref[...] = normed
    inverse_ref[...] = inverse


def rest_kernel(sizes, idx, expand_ref, shrink_ref, out_ref):
    uly, dp, unit = sizes
    width = shrink_ref.shape[1]
    half = expand_ref.shape[0] // 2
    for j in range(1, uly):
        part = idx[0] * uly + (idx[1] ^ j)
        take = one_hot(width, unit, 0, part * unit)
        for k in range(dp):
            cols = dot_nn(expand_ref[:, k * width : (k + 1) * width], take).astype(BF16)
            out_ref[j - 1, :half, k * unit : (k + 1) * unit] = cols[:half]
            out_ref[j - 1, :half, (dp + k) * unit : (dp + k + 1) * unit] = cols[half:]
        start = pl.multiple_of(part * unit, unit)
        out_ref[j - 1, half:, :] = shrink_ref[pl.ds(start, unit), :]


def mixer_kernel(sizes, idx, *refs):
    uly, dp = sizes
    pieces, (m_ref, turn_ref) = refs[:-2], refs[-2:]
    lines = pieces[0].shape[0] // dp
    b, u, z = idx[0], idx[1], idx[2]
    shard = 2 * uly * lines
    for k in range(dp):
        for p, ref in enumerate(pieces):
            part = (b * uly + u) ^ p
            turn_ref[pl.ds(pl.multiple_of(part * lines, 8), lines), :] = ref[
                k * lines : (k + 1) * lines, :
            ].astype(F32)
        start = pl.multiple_of((z ^ k) * shard, shard)
        m_ref[pl.ds(start, shard), :] = turn_ref[...].astype(BF16)


def assemble_kernel(sizes, k, idx, *refs):
    uly, dp, unit = sizes
    e_ref, s_ref, sem = refs[-3:]
    block = dp * unit
    shard = e_ref.shape[0] // dp
    half = shard // 2
    owner = idx[2] ^ k
    copies = []
    for j in range(uly):
        if k == 0:
            piece = refs[0] if j == 0 else refs[1].at[j - 1]
        else:
            piece = refs[2 + j]
        for h in range(2):
            start = pl.multiple_of(owner * shard + h * half, half)
            copies.append(
                pltpu.make_async_copy(
                    piece.at[pl.ds(0, half), pl.ds(h * block, block)],
                    e_ref.at[pl.ds(start, half), pl.ds(j * block, block)],
                    sem.at[3 * j + h],
                )
            )
        start = pl.multiple_of(j * block + owner * unit, unit)
        copies.append(
            pltpu.make_async_copy(
                piece.at[pl.ds(half, unit), :], s_ref.at[pl.ds(start, unit), :], sem.at[3 * j + 2]
            )
        )
    for copy in copies:
        copy.start()
    for copy in copies:
        copy.wait()


def assemble(scalars, sizes, k, weights, pieces):
    uly, dp, unit = sizes
    width = pieces[0].shape[1]
    block = uly * dp * unit
    hbm = pl.BlockSpec(memory_space=pl.ANY)
    return call(
        functools.partial(assemble_kernel, sizes, k),
        "assemble",
        scalars,
        [*weights, *pieces],
        [hbm] * (len(weights) + len(pieces)),
        [jax.ShapeDtypeStruct((width, block), BF16), jax.ShapeDtypeStruct((block, width), BF16)],
        [hbm] * 2,
        [pltpu.SemaphoreType.DMA((3 * uly,))],
        (1,),
        10**6,
        16,
        {1: 0, 2: 1} if weights else {},
    )


def feed_forward_kernel(uly, idx, mine_ref, other_ref, eb_ref, e_ref, s_ref, *refs):
    act_ref, slope_ref, y_ref, send_ref, x_ref = refs
    rows = mine_ref.shape[0]
    block = e_ref.shape[1] // uly
    x_ref[:rows] = mine_ref[...]
    x_ref[rows:] = other_ref[...]
    for j in range(uly):
        lanes = slice(j * block, (j + 1) * block)
        pre = dot_nn(x_ref[...], e_ref[:, lanes]) + eb_ref[j : j + 1, :]
        cdf = 0.5 * (1.0 + lax.erf(pre * 0.7071067811865476))
        pdf = jnp.exp(-0.5 * pre * pre) * 0.3989422804014327
        act_ref[:, lanes] = (pre * cdf).astype(BF16)
        slope_ref[:, lanes] = (cdf + pre * pdf).astype(BF16)
    out = dot_nn(act_ref[...], s_ref[...])
    y_ref[...] = out[:rows]
    send_ref[...] = out[rows:].astype(BF16)


def feed_forward(scalars, uly, mine, other, eb, weights):
    rows, width = mine.shape
    block = weights[0].shape[1]
    args = [mine, other, eb, *weights]
    return call(
        functools.partial(feed_forward_kernel, uly),
        "feed_forward",
        scalars,
        args,
        [whole(arg.shape) for arg in args],
        [
            jax.ShapeDtypeStruct((2 * rows, block), BF16),
            jax.ShapeDtypeStruct((2 * rows, block), BF16),
            jax.ShapeDtypeStruct((rows, width), F32),
            jax.ShapeDtypeStruct((rows, width), BF16),
        ],
        [whole((2 * rows, block))] * 2 + [whole((rows, width))] * 2,
        [pltpu.VMEM((2 * rows, width), BF16)],
        (1,),
        8 * rows * width * block,
        24,
    )


def final_norm_kernel(idx, x1_ref, y_ref, got_ref, vec_ref, cot_ref, *refs):
    mixed_ref, dh_ref, low_ref, sums_ref = refs
    hidden = x1_ref[...] + (y_ref[...] + got_ref[...].astype(F32) + vec_ref[5:6, :])
    gain = vec_ref[6:7, :]
    center = hidden - jnp.mean(hidden, -1, keepdims=True)
    inverse = lax.rsqrt(jnp.mean(center * center, -1, keepdims=True) + EPSILON)
    normed = center * inverse
    mixed_ref[...] = (normed * gain + vec_ref[7:8, :]).astype(BF16)
    grad = cot_ref[...].astype(F32)
    scaled = grad * gain
    dhidden = inverse * (
        scaled
        - jnp.mean(scaled, -1, keepdims=True)
        - normed * jnp.mean(scaled * normed, -1, keepdims=True)
    )
    dh_ref[...] = dhidden
    low_ref[...] = dhidden.astype(BF16)
    sums_ref[...] = jnp.zeros_like(sums_ref)
    sums_ref[0:1, :] = jnp.sum(dhidden, 0, keepdims=True)
    sums_ref[1:2, :] = jnp.sum(grad * normed, 0, keepdims=True)
    sums_ref[2:3, :] = jnp.sum(grad, 0, keepdims=True)


def shrink_grad_kernel(sizes, idx, d_mine, d_other, act_ref, *refs):
    uly, dp, unit = sizes
    near_x, far_x, near_y, far_y = (refs[2 * i : 2 * i + 2] for i in range(4))
    d_ref, turn_ref = refs[8:]
    block = dp * unit
    rows = d_mine.shape[0]
    d_ref[:rows] = d_mine[...]
    d_ref[rows:] = d_other[...]
    for j in range(uly):
        turn_ref[...] = dot_tn(act_ref[:, j * block : (j + 1) * block], d_ref[...]).astype(BF16)
        for k in range(dp):
            if k % 2 == 0:
                ref, at = (far_x if j % 2 else near_x), j // 2
            else:
                ref, at = (near_y if j < uly // 2 else far_y), j % 2
            start = pl.multiple_of((idx[2] ^ k) * unit, unit)
            into = slice((k // 2) * unit, (k // 2 + 1) * unit)
            ref[at][into, :] = turn_ref[pl.ds(start, unit), :]


def shrink_grad(scalars, sizes, ds, act):
    uly, dp, unit = sizes
    rows, width = ds[0].shape
    block = dp * unit
    half = (block // 2, width)
    return call(
        functools.partial(shrink_grad_kernel, sizes),
        "shrink_grad",
        scalars,
        [*ds, act],
        [whole((rows, width))] * 2 + [whole(act.shape)],
        [jax.ShapeDtypeStruct(half, BF16)] * 8,
        [whole(half)] * 8,
        [pltpu.VMEM((2 * rows, width), BF16), pltpu.VMEM((block, width), BF16)],
        (1,),
        4 * rows * width * uly * block,
        16,
    )


def feed_backward_kernel(sizes, idx, x_mine, x_other, d_mine, d_other, slope_ref, *refs):
    uly, dp, unit = sizes
    e_ref, s_ref, *refs = refs
    near_x, far_x, near_y, far_y = (refs[2 * i : 2 * i + 2] for i in range(4))
    deb_ref, dx_ref, send_ref, xt_ref, d_ref, turn_ref, dpre_ref = refs[8:]
    rows, width = x_mine.shape
    shard = width // dp
    half = width // 2
    block = dp * unit
    turn_ref[:, :rows] = x_mine[...].T
    turn_ref[:, rows:] = x_other[...].T
    for k in range(dp):
        start = pl.multiple_of((idx[2] ^ k) * shard, shard)
        into = slice(slot(k) * shard, (slot(k) + 1) * shard)
        xt_ref[into, :] = turn_ref[pl.ds(start, shard), :]
    d_ref[:rows] = d_mine[...]
    d_ref[rows:] = d_other[...]
    for j in range(uly):
        lanes = slice(j * block, (j + 1) * block)
        dpre = dot_nt(d_ref[...], s_ref[lanes, :])
        dpre = (dpre * slope_ref[:, lanes].astype(F32)).astype(BF16)
        dpre_ref[:, lanes] = dpre
        deb_ref[j : j + 1, :] = jnp.sum(dpre.astype(F32), 0, keepdims=True)
        dexpand = dot_nn(xt_ref[...], dpre).astype(BF16)
        (far_x if j % 2 else near_x)[j // 2][...] = dexpand[:half]
        (near_y if j < uly // 2 else far_y)[j % 2][...] = dexpand[half:]
    grad = dot_nt(dpre_ref[...], e_ref[...])
    dx_ref[...] = grad[:rows]
    send_ref[...] = grad[rows:].astype(BF16)


def feed_backward(scalars, sizes, xs, ds, slope, weights):
    uly, dp, unit = sizes
    rows, width = xs[0].shape
    block = dp * unit
    half = (width // 2, block)
    args = [*xs, *ds, slope, *weights]
    return call(
        functools.partial(feed_backward_kernel, sizes),
        "feed_backward",
        scalars,
        args,
        [whole(arg.shape) for arg in args],
        [jax.ShapeDtypeStruct(half, BF16)] * 8
        + [
            jax.ShapeDtypeStruct((uly, block), F32),
            jax.ShapeDtypeStruct((rows, width), F32),
            jax.ShapeDtypeStruct((rows, width), BF16),
        ],
        [whole(half)] * 8 + [whole((uly, block)), whole((rows, width)), whole((rows, width))],
        [
            pltpu.VMEM((width, 2 * rows), BF16),
            pltpu.VMEM((2 * rows, width), BF16),
            pltpu.VMEM((width, 2 * rows), BF16),
            pltpu.VMEM((2 * rows, uly * block), BF16),
        ],
        (1,),
        12 * rows * width * uly * block,
        24,
    )


def norm_backward_kernel(sizes, idx, dh2_ref, dx_ref, got_ref, normed_ref, inverse_ref, *refs):
    uly, dp, unit = sizes
    m_ref, vec_ref, grads_ref, deb_ref, *refs = refs
    o_refs, refs = refs[:uly], refs[uly:]
    dh_ref, *refs = refs
    do_refs, refs = refs[:uly], refs[uly:]
    keep_ref, send_ref, turn_ref = refs
    b, u, z = idx[0], idx[1], idx[2]
    group = o_refs[0].shape[1]
    share = group // 2
    width = dx_ref.shape[1]
    parts = 2 * uly
    grad = dh2_ref[...] + dx_ref[...] + got_ref[...].astype(F32)
    normed = normed_ref[...]
    scaled = grad * vec_ref[3:4, :]
    dhidden = inverse_ref[...] * (
        scaled
        - jnp.mean(scaled, -1, keepdims=True)
        - normed * jnp.mean(scaled * normed, -1, keepdims=True)
    )
    dh_ref[...] = dhidden
    low = dhidden.astype(BF16)
    for j in range(uly):
        start = pl.multiple_of((u ^ j) * group, group)
        do_refs[j][...] = dot_nt(low, m_ref[pl.ds(start, group), :]).astype(BF16)
    line = lax.broadcasted_iota(jnp.int32, (8, width), 0)
    lines = jnp.zeros((8, width), F32)
    values = [
        jnp.sum(dhidden, 0, keepdims=True),
        jnp.sum(grad * normed, 0, keepdims=True),
        jnp.sum(grad, 0, keepdims=True),
        grads_ref[0:1, :],
        grads_ref[1:2, :],
        grads_ref[2:3, :],
    ]
    for k, value in enumerate(values):
        lines = jnp.where(line == k, value, lines)
    lines = lines.astype(BF16)
    owner = (lax.broadcasted_iota(jnp.int32, (parts, uly), 1) ^ u) + b * uly
    order = lax.broadcasted_iota(jnp.int32, (parts, uly), 0)
    order = jnp.where(order == owner, 1.0, 0.0).astype(BF16)
    ebs = dot_nn(order, deb_ref[...].astype(BF16)).astype(BF16)
    for j in range(uly):
        turn_ref[...] = dot_tn(o_refs[j][...], low).astype(BF16)
        place = slot(u ^ j ^ z)
        keep_ref[place, :share] = turn_ref[pl.ds(pl.multiple_of(b * share, share), share), :]
        send_ref[place, :share] = turn_ref[pl.ds(pl.multiple_of((1 - b) * share, share), share), :]
    for k in range(dp):
        shard = (z ^ k) * group
        own = dot_nn(lines, one_hot(width, group, 0, shard)).astype(BF16)
        ebk = dot_nn(ebs, one_hot(dp * unit, unit, 0, (z ^ k) * unit)).astype(BF16)
        for ref in (keep_ref, send_ref):
            ref[slot(k), share:, :] = jnp.zeros_like(ref[slot(k), share:, :])
            ref[slot(k), share : share + 8, :group] = own
            ref[slot(k), share + 8 : share + 16, :unit] = ebk


def attend_grad_kernel(heads, blocks, pieces, started, q_ref, lse_ref, *refs):
    do_refs, refs = refs[:pieces], refs[pieces:]
    o_refs, refs = refs[:pieces], refs[pieces:]
    kv_refs, refs = refs[:blocks], refs[blocks:]
    so_far, refs = refs[: blocks * started], refs[blocks * started :]
    dq_ref, *refs = refs
    dkv_refs, refs = refs[:blocks], refs[blocks:]
    kt_ref, dout_ref, prod_ref, *refs = refs
    dk_accs, dv_accs = refs[:blocks], refs[blocks:]
    group = heads * HD
    wide = q_ref.shape[1]
    rows = kv_refs[0].shape[0]

    @pl.when(pl.program_id(0) == 0)
    def _():
        for i in range(blocks):
            kt_ref[:, i * rows : (i + 1) * rows] = kv_refs[i][:, :group].T
            if started:
                dk_accs[i][...] = so_far[i][:, :wide].astype(F32) * LOG2E
                dv_accs[i][...] = so_far[i][:, wide : wide + group].astype(F32)
            else:
                dk_accs[i][...] = jnp.zeros_like(dk_accs[i])
                dv_accs[i][...] = jnp.zeros_like(dv_accs[i])

    for j in range(pieces):

        @pl.when(pl.program_id(0) == j)
        def _(j=j):
            dout_ref[...] = do_refs[j][...]
            prod_ref[...] = (do_refs[j][...].astype(F32) * o_refs[j][...].astype(F32)).T

    q = q_ref[...]
    dout = dout_ref[...]
    dqs = []
    for head in range(heads):
        q_head = jnp.where(head_lanes(wide, head, group), q, jnp.zeros_like(q))
        do_head = jnp.where(head_lanes(group, head), dout, jnp.zeros_like(dout))
        lse = lse_ref[head : head + 1, :]
        delta = jnp.sum(prod_ref[head * HD : (head + 1) * HD, :], axis=0, keepdims=True)
        acc = None
        for i in range(blocks):
            probs = jnp.exp2(dot_nt(kv_refs[i][:, :wide], q_head) - lse)
            dv_accs[i][...] += dot_nn(probs.astype(BF16), do_head)
            grads = dot_nt(kv_refs[i][:, wide : wide + group], do_head)
            grads = (probs * (grads - delta)).astype(BF16)
            dk_accs[i][...] += dot_nn(grads, q_head)
            part = dot_nn(
                kt_ref[head * HD : (head + 1) * HD, i * rows : (i + 1) * rows], grads
            )
            acc = part if acc is None else acc + part
        dqs.append(acc)
    dq_ref[...] = jnp.concatenate(dqs, axis=0).T.astype(BF16)

    @pl.when(pl.program_id(0) == pl.num_programs(0) - 1)
    def _():
        for i in range(blocks):
            dkv_refs[i][:, :group] = (dk_accs[i][:, :group] * LN2).astype(BF16)
            dkv_refs[i][:, group:wide] = jnp.zeros((rows, wide - group), BF16)
            dkv_refs[i][:, wide : wide + group] = dv_accs[i][...].astype(BF16)
            dkv_refs[i][:, wide + group :] = jnp.zeros((rows, wide - group), BF16)


def attend_grad(q, kvs, douts, outs, lse, heads, at, so_far):
    rows, wide = kvs[0].shape[0], q.shape[1]
    group = heads * HD
    blocks = len(kvs)
    pieces = len(douts)
    tile = douts[0].shape[0]
    keys = blocks * rows
    started = 1 if so_far else 0
    out = pl.pallas_call(
        functools.partial(attend_grad_kernel, heads, blocks, pieces, started),
        grid=(pieces,),
        in_specs=[
            pl.BlockSpec((tile, wide), lambda t: (t + at, 0)),
            pl.BlockSpec((8, tile), lambda t: (0, t + at)),
        ]
        + [whole((tile, group))] * (2 * pieces)
        + [whole(kvs[0].shape)] * (blocks + blocks * started),
        out_specs=[pl.BlockSpec((tile, group), lambda t: (t, 0))]
        + [whole(kvs[0].shape)] * blocks,
        out_shape=[jax.ShapeDtypeStruct((pieces * tile, group), BF16)]
        + [jax.ShapeDtypeStruct(kvs[0].shape, BF16)] * blocks,
        scratch_shapes=[
            pltpu.VMEM((group, keys), BF16),
            pltpu.VMEM((tile, group), BF16),
            pltpu.VMEM((group, tile), F32),
        ]
        + [pltpu.VMEM((rows, wide), F32)] * blocks
        + [pltpu.VMEM((rows, group), F32)] * blocks,
        compiler_params=pltpu.CompilerParams(vmem_limit_bytes=16 * 2**20),
        cost_estimate=pl.CostEstimate(
            flops=10 * heads * pieces * tile * keys * wide,
            transcendentals=heads * pieces * tile * keys,
            bytes_accessed=2 * rows * wide * 4 + 4 * keys * (wide + group),
        ),
        name="attend_grad",
    )(q, lse, *douts, *outs, *kvs, *so_far)
    return out[0], out[1:]


def project_grad_kernel(sizes, idx, *refs):
    uly, dp, group = sizes
    dq_refs, (own_ref, got_ref, *refs) = refs[:uly], refs[uly:]
    x_refs, refs = refs[:uly], refs[uly:]
    dproj_ref, keep_ref, send_ref = refs
    b, z = idx[0], idx[2]
    rows, width = x_refs[0].shape
    wide = own_ref.shape[1] // 2
    share = keep_ref.shape[1] - 16
    for k, ref in enumerate(dq_refs):
        here = slice(k * ref.shape[0], (k + 1) * ref.shape[0])
        dproj_ref[here, :group] = ref[...] * jnp.asarray(0.125, BF16)
    dproj_ref[:, group:wide] = jnp.zeros((uly * rows, wide - group), BF16)
    dproj_ref[:, wide:] = (own_ref[...].astype(F32) + got_ref[...].astype(F32)).astype(BF16)
    sums = jnp.sum(dproj_ref[...].astype(F32), 0, keepdims=True).astype(BF16)
    grad = None
    for j in range(uly):
        part = dot_tn(x_refs[j][...], dproj_ref[j * rows : (j + 1) * rows, :])
        grad = part if grad is None else grad + part
    grad = grad.astype(BF16)
    for ref, mine in ((keep_ref, True), (send_ref, False)):
        for c in range(3):
            lanes = slice(c * wide, c * wide + group)
            into = slice(c * group, (c + 1) * group)
            for s in range(dp):
                for core in range(2):
                    start = (s * 2 + core) * share

                    @pl.when((b == core) == mine)
                    def _(start=start, s=s, ref=ref, lanes=lanes, into=into):
                        ref[slot(s ^ z), :share, into] = grad[start : start + share, lanes]

                ref[s, share:, into] = jnp.broadcast_to(sums[:, lanes], (16, group))


def token_grad_kernel(uly, idx, dproj_ref, w_ref, dh_ref, *out_refs):
    rows = dh_ref.shape[0]
    for j in reversed(range(uly)):
        part = dot_nt(dproj_ref[j * rows : (j + 1) * rows, :], w_ref[...])
        if j == 0:
            part = part + dh_ref[...]
        out_refs[j][...] = part.astype(out_refs[j].dtype)


def pack_kernel(idx, sx_ref, sx1_ref, sx2_ref, sy_ref, sy1_ref, sy2_ref, keep_ref, got_ref, *refs):
    unit = sx2_ref.shape[0] // 2
    for out_refs, first, s_refs in (
        (refs[:2], 0, (sx_ref, sx1_ref, sx2_ref)),
        (refs[2:], 2, (sy_ref, sy1_ref, sy2_ref)),
    ):
        for k, out_ref in enumerate(out_refs):
            rows = slice(k * unit, (k + 1) * unit)
            value = s_refs[0][rows].astype(F32) + s_refs[1][rows].astype(F32)
            out_ref[:unit, :] = (value + s_refs[2][rows].astype(F32)).astype(BF16)
            value = keep_ref[first + k].astype(F32) + got_ref[first + k].astype(F32)
            out_ref[unit:, :] = value.astype(BF16)


def finish_shrink_kernel(sizes, idx, *refs):
    uly, unit = sizes
    pieces, (shrink_ref, mixer_ref, vec_ref, wide_ref, sum_ref, sem) = refs[: 2 * uly], refs[2 * uly :]
    share = mixer_ref.shape[0] // 2
    part = idx[0] * uly + idx[1]
    copies = []
    for p, ref in enumerate(pieces):
        wide_ref[p] = ref[:unit, :].astype(F32)
        start = pl.multiple_of((part ^ p) * unit, unit)
        copies.append(
            pltpu.make_async_copy(wide_ref.at[p], shrink_ref.at[pl.ds(start, unit), :], sem.at[p])
        )
        copies[-1].start()

    def plane_sum(refs, rows):
        values = [ref[rows, :].astype(F32) for ref in refs]
        return (values[0] + values[1]) + (values[2] + values[3])

    for i, core in enumerate((idx[0], 1 - idx[0])):
        group = pieces[i * uly : (i + 1) * uly]
        sum_ref[i] = plane_sum(group, slice(unit, unit + share))
        start = pl.multiple_of(core * share, share)
        copies.append(
            pltpu.make_async_copy(
                sum_ref.at[i], mixer_ref.at[pl.ds(start, share), :], sem.at[2 * uly + i]
            )
        )
        copies[-1].start()
    vec_ref[...] = plane_sum(pieces[:uly], slice(unit + share, unit + share + 16))
    for copy in copies:
        copy.wait()


def finish_expand_kernel(sizes, idx, *refs):
    uly, dp, unit = sizes
    pieces, (out_ref, turn_ref, wide_ref, sem) = refs[:-4], refs[-4:]
    width = turn_ref.shape[0]
    part = idx[0] * uly + idx[1]
    col = lax.broadcasted_iota(jnp.int32, (width, width), 1)
    row = lax.broadcasted_iota(jnp.int32, (width, width), 0)
    source = col + ((col // unit) ^ part) * unit - (col // unit) * unit
    turn_ref[...] = jnp.where(row == source, 1.0, 0.0).astype(BF16)
    copies = []
    for k in range(dp):
        line = jnp.concatenate([ref[:, k * unit : (k + 1) * unit] for ref in pieces], 1)
        wide_ref[k] = dot_nn(line, turn_ref[...])
        copies.append(
            pltpu.make_async_copy(
                wide_ref.at[k], out_ref.at[:, pl.ds(k * width, width)], sem.at[k]
            )
        )
        copies[-1].start()
    for copy in copies:
        copy.wait()


def finish_attend_kernel(uly, idx, *refs):
    mine, refs = refs[:uly], refs[uly:]
    other, refs = refs[:uly], refs[uly:]
    out_ref, bias_ref, wide_ref, sem = refs
    b, u, z = idx[0], idx[1], idx[2]
    share = mine[0].shape[0] - 16
    group = mine[0].shape[1] // 3
    width = uly * group
    copies = []
    for i, (group_refs, core) in enumerate(((mine, b), (other, 1 - b))):
        start = pl.multiple_of(core * share, share)
        for c in range(3):
            acc = None
            for j in range(uly):
                put = one_hot(group, width, (u ^ j) * group, 0)
                value = dot_nn(group_refs[j][:share, c * group : (c + 1) * group], put)
                acc = value if acc is None else acc + value
            wide_ref[3 * i + c] = acc
            copies.append(
                pltpu.make_async_copy(
                    wide_ref.at[3 * i + c],
                    out_ref.at[pl.ds(start, share), pl.ds(c * width, width)],
                    sem.at[3 * i + c],
                )
            )
            copies[-1].start()
    bias = jnp.zeros((8, 3 * group), F32)
    for j in range(uly):
        lines = mine[j][share : share + 16, :].astype(F32)[:8]
        bias += jnp.where((u ^ j) == z, 1.0, 0.0) * lines
    bias_ref[...] = bias
    for copy in copies:
        copy.wait()


def on_device(*args):
    (
        tokens,
        lengths,
        cotangent,
        attend_weight,
        query_bias,
        value_bias,
        mixer_weight,
        mixer_bias,
        attn_gain,
        attn_shift,
        expand_weight,
        expand_bias,
        shrink_weight,
        shrink_bias,
        final_gain,
        final_shift,
    ) = args
    uly = lax.axis_size("uly")
    blk = lax.axis_size("blk")
    dp = lax.axis_size("dp")
    width = tokens.shape[-1]
    rows = tokens.shape[0] * tokens.shape[1]
    heads = HEADS // uly
    group = heads * HD
    wide = -(-(group + 1) // 128) * 128
    shard = attend_weight.shape[0]
    hidden = expand_weight.shape[1]
    parts = blk * uly
    unit = hidden // (parts * dp)
    share = shard // blk
    if not (blk == 2 and uly == 4 and dp == 4 and shard == group and unit * 2 == shard and share % 16 == 0):
        return general_device(*args)
    u = lax.axis_index("uly")
    b = lax.axis_index("blk")
    z = lax.axis_index("dp")
    mixer_rows = share // dp
    feed_rows = shard // 2 + unit
    block_rows = uly * rows
    cols = 3 * wide

    x = tokens.reshape(rows, width)
    xs = [x, swap_with(x, "uly", 1), swap_with(x, "uly", 2)]
    xs.append(swap_with(after(x, *xs[1:]), "uly", 3))
    scalars = jnp.stack([b, u, z, lengths[0]]).astype(jnp.int32)
    vectors = [query_bias, value_bias, mixer_bias, attn_gain, attn_shift, shrink_bias]
    vectors += [final_gain, final_shift, expand_bias]
    first, feed = call(
        functools.partial(fetch_kernel, (uly, dp, group, unit)),
        "fetch",
        scalars,
        [
            attend_weight.reshape(blk, share, 3 * width),
            expand_weight,
            shrink_weight.reshape(parts, unit, width),
            mixer_weight,
            *vectors,
        ],
        [
            pl.BlockSpec((1, share, 3 * width), lambda t, s: (s[0], 0, 0)),
            whole(expand_weight.shape),
            pl.BlockSpec((1, unit, width), lambda t, s: (s[0] * uly + s[1], 0, 0)),
            whole(mixer_weight.shape),
            *[whole(vector.shape) for vector in vectors],
        ],
        [
            jax.ShapeDtypeStruct((share + 16, width), BF16),
            jax.ShapeDtypeStruct((feed_rows, width), BF16),
        ],
        [whole((share + 16, width)), whole((feed_rows, width))],
        [],
        (1,),
        10**9,
        58,
    )
    feeds = [None, swap_with(feed, "dp", 1)]
    mine = [first, None, swap_with(first, "dp", 2), swap_with(first, "dp", 3)]
    mine[1] = swap_with(after(first, *xs[1:3]), "dp", 1)
    feeds.append(swap_with(after(feed, *mine[1:]), "dp", 2))
    plane_one = [swap_with(feeds[1], "uly", j) for j in range(1, uly)]
    other = [swap_with(after(piece, *plane_one), "blk", 1) for piece in mine]
    rest = call(
        functools.partial(rest_kernel, (uly, dp, unit)),
        "fetch_rest",
        scalars,
        [expand_weight, shrink_weight],
        [whole(expand_weight.shape), whole(shrink_weight.shape)],
        jax.ShapeDtypeStruct((uly - 1, shard // 2 + unit, width), BF16),
        whole((uly - 1, shard // 2 + unit, width)),
        [],
        (1,),
        10**9,
        16,
    )

    w_own, q, kv, vec, eb, mixer_mine = call(
        functools.partial(project_kernel, (uly, blk, dp, group, unit)),
        "project",
        scalars,
        [*after(xs, feeds[1], rest), *mine, *other],
        [whole((rows, width))] * uly + [whole(first.shape)] * (2 * dp),
        [
            jax.ShapeDtypeStruct((width, cols), BF16),
            jax.ShapeDtypeStruct((block_rows, wide), BF16),
            jax.ShapeDtypeStruct((block_rows, 2 * wide), BF16),
            jax.ShapeDtypeStruct((16, width), F32),
            jax.ShapeDtypeStruct((parts, dp * unit), F32),
            jax.ShapeDtypeStruct((dp * mixer_rows, width), BF16),
        ],
        [
            whole((width, cols)),
            whole((block_rows, wide)),
            whole((block_rows, 2 * wide)),
            whole((16, width)),
            whole((parts, dp * unit)),
            whole((dp * mixer_rows, width)),
        ],
        [],
        (1,),
        2 * block_rows * width * cols,
        16,
    )
    kv_send, mixer_mine = after((kv, mixer_mine), feeds[2])
    kvs = [kv, swap_with(kv_send, "blk", 1)]

    mixer_plane = [swap_with(mixer_mine, "uly", j) for j in range(1, uly)]

    plane_two = [swap_with(feeds[2], "uly", j) for j in range(1, uly)]
    feed_three = swap_with(after(feed, feeds[2]), "dp", 3)
    outs, lse = attend(after(q, feeds[2]), kvs, heads, uly)
    outs, mixer_plane, plane_two, feed_three = after((outs, mixer_plane, plane_two, feed_three))
    feeds.append(feed_three)
    plane_three = [swap_with(feed_three, "uly", j) for j in range(1, uly)]
    mixer_parts = [mixer_mine, *mixer_plane]
    mixer_parts += [swap_with(piece, "blk", 1) for piece in mixer_parts]
    mixer_all = call(
        functools.partial(mixer_kernel, (uly, dp)),
        "mixer_weight",
        scalars,
        mixer_parts,
        [whole(mixer_mine.shape)] * parts,
        jax.ShapeDtypeStruct((width, width), BF16),
        whole((width, width)),
        [pltpu.VMEM((shard, width), F32)],
        (1,),
        10**6,
        16,
    )

    sizes = (uly, dp, unit)
    weights = assemble(scalars, sizes, 0, [], [feed, rest])
    weights = assemble(scalars, sizes, 1, weights, [feeds[1], *plane_one])
    weights = assemble(scalars, sizes, 2, weights, [feeds[2], *plane_two])
    o_cols = after(outs, *plane_three, *weights, mixer_all)
    o_cols = [o_cols[0]] + [swap_with(o_cols[j], "uly", j) for j in range(1, uly)]
    square = (rows, width)
    weights = assemble(scalars, sizes, 3, weights, [feeds[3], *plane_three])
    x1, x1b, normed, inverse = call(
        functools.partial(first_norm_kernel, uly),
        "first_norm",
        scalars,
        [x, *o_cols, after(mixer_all, *weights), vec],
        [whole(square)] + [whole((rows, group))] * uly + [whole((width, width)), whole(vec.shape)],
        [
            jax.ShapeDtypeStruct(square, F32),
            jax.ShapeDtypeStruct(square, BF16),
            jax.ShapeDtypeStruct(square, F32),
            jax.ShapeDtypeStruct((rows, 1), F32),
        ],
        [whole(square), whole(square), whole(square), whole((rows, 1))],
        [],
        (1,),
        2 * rows * width * width,
        16,
    )
    x1b_other = swap_with(x1b, "blk", 1)
    act, slope, y_own, y_send = feed_forward(scalars, uly, x1b, x1b_other, eb, weights)
    mixed, dh2, dh2b, sums2 = call(
        final_norm_kernel,
        "final_norm",
        scalars,
        [x1, y_own, swap_with(y_send, "blk", 1), vec, cotangent.reshape(square)],
        [whole(square)] * 3 + [whole(vec.shape), whole(square)],
        [
            jax.ShapeDtypeStruct(square, BF16),
            jax.ShapeDtypeStruct(square, F32),
            jax.ShapeDtypeStruct(square, BF16),
            jax.ShapeDtypeStruct((8, width), F32),
        ],
        [whole(square)] * 3 + [whole((8, width))],
        [],
        (1,),
        10**6,
        16,
    )
    dh2b_other = swap_with(dh2b, "blk", 1)
    ds = [dh2b, dh2b_other]
    s_grads = shrink_grad(scalars, sizes, ds, act)
    s_near_x, s_far_x, s_near_y, s_far_y = (s_grads[2 * i : 2 * i + 2] for i in range(4))
    s_x1 = swap_with(s_far_x[1], "uly", 1)
    s_y1 = swap_with(s_far_y[1], "uly", 2)
    ds = after(ds, s_far_x[0])
    grads = feed_backward(scalars, sizes, [x1b, x1b_other], ds, slope, weights)
    e_near_x, e_far_x, e_near_y, e_far_y = (grads[2 * i : 2 * i + 2] for i in range(4))
    deb, dx_own, dx_send = grads[8:]

    def add(*values):
        return total(values).astype(BF16)

    dx_send, s_far_x0, s_far_y0, s_x1, s_y1 = after(
        (dx_send, s_far_x[0], s_far_y[0], s_x1, s_y1)
    )
    dx_got = swap_with(dx_send, "blk", 1)
    s_x0 = swap_with(s_far_x0, "uly", 1)
    s_y0 = swap_with(s_far_y0, "uly", 2)
    block = (dp, share + 16, width)
    dh1, *rest_out = call(
        functools.partial(norm_backward_kernel, sizes),
        "norm_backward",
        scalars,
        [dh2, dx_own, dx_got, normed, inverse, mixer_all]
        + [vec, sums2]
        + [deb, *o_cols],
        [whole(square)] * 4
        + [whole((rows, 1)), whole((width, width)), whole(vec.shape), whole(sums2.shape)]
        + [whole((uly, dp * unit))]
        + [whole((rows, group))] * uly,
        [jax.ShapeDtypeStruct(square, F32)]
        + [jax.ShapeDtypeStruct((rows, group), BF16)] * uly
        + [jax.ShapeDtypeStruct(block, BF16)] * 2,
        [whole(square)] + [whole((rows, group))] * uly + [whole(block)] * 2,
        [pltpu.VMEM((group, width), BF16)],
        (1,),
        4 * rows * width * width,
        16,
    )
    douts = [rest_out[0]] + [swap_with(rest_out[j], "uly", j) for j in range(1, uly)]
    m_keep, m_send = rest_out[uly:]

    def quarter(j, so_far, *deps):
        dout = after(douts[j], *deps)
        return attend_grad(q, kvs, [dout], [outs[j]], lse, heads, j, so_far)

    dq_0, dkvs = quarter(0, [])
    dq_0, m_send, s_x0, s_y0, s_x1, s_y1, e_far_x, e_far_y, *douts[1:] = after(
        (dq_0, m_send, s_x0, s_y0, s_x1, s_y1, e_far_x, e_far_y, *douts[1:])
    )
    s_next_x = add(s_near_x[1], s_x1)
    s_next_y = add(s_near_y[1], s_y1)
    s_xy = swap_with(s_next_x, "uly", 2)
    s_yx = swap_with(s_next_y, "uly", 1)
    m_got = swap_with(m_send, "blk", 1)
    e_x1 = swap_with(e_far_x[1], "uly", 1)
    e_y1 = swap_with(e_far_y[1], "uly", 2)

    dq_1, dkvs = quarter(1, dkvs, s_next_x, s_next_y)
    dq_1, s_xy, s_yx, m_got, e_far_x, e_far_y = after((dq_1, s_xy, s_yx, m_got, e_far_x, e_far_y))
    packed = (unit + share + 16, width)
    p_near_0, p_near_1, p_far_0, p_far_1 = call(
        pack_kernel,
        "pack",
        scalars,
        [s_near_x[0], s_x0, s_xy, s_near_y[0], s_y0, s_yx, m_keep, m_got],
        [whole(s_xy.shape)] * 6 + [whole(m_keep.shape)] * 2,
        [jax.ShapeDtypeStruct(packed, BF16)] * 4,
        [whole(packed)] * 4,
        [],
        (1,),
        10**6,
        16,
    )
    p_one_1 = swap_with(p_far_1, "dp", 1)
    e_x0 = swap_with(e_far_x[0], "uly", 1)
    e_y0 = swap_with(e_far_y[0], "uly", 2)

    dq_2, dkvs = quarter(2, dkvs, p_far_1)
    dq_2, e_x0, e_y0, e_x1, e_y1, p_one_1, p_far_0 = after(
        (dq_2, e_x0, e_y0, e_x1, e_y1, p_one_1, p_far_0)
    )
    p_one_0 = swap_with(p_far_0, "dp", 1)
    p_next = add(p_near_1, p_one_1)
    p_two = swap_with(p_next, "dp", 2)
    e_next_x = add(e_near_x[1], e_x1)
    e_next_y = add(e_near_y[1], e_y1)
    e_xy = swap_with(e_next_x, "uly", 2)
    e_yx = swap_with(e_next_y, "uly", 1)

    dq_3, dkvs = quarter(3, dkvs, e_next_x, e_next_y, p_next)
    dq_3, e_xy, e_yx, p_one_0, *dkvs = after((dq_3, e_xy, e_yx, p_one_0, *dkvs))
    dkv_got = swap_with(dkvs[1], "blk", 1)
    pair = (2, shard, dp * unit)
    e_near = add(e_near_x[0], e_x0, e_xy).reshape(pair)
    e_far = add(e_near_y[0], e_y0, e_yx).reshape(pair)
    dkv_got = after(dkv_got, e_near, e_far)
    dqs = [dq_0, dq_1, dq_2, dq_3]
    dproj, a_keep, a_send = call(
        functools.partial(project_grad_kernel, (uly, dp, group)),
        "project_grad",
        scalars,
        [*dqs, dkvs[0], dkv_got, *xs],
        [whole(dq_0.shape)] * uly + [whole(kv.shape)] * 2 + [whole(square)] * uly,
        [
            jax.ShapeDtypeStruct((block_rows, cols), BF16),
            jax.ShapeDtypeStruct((dp, share + 16, 3 * group), BF16),
            jax.ShapeDtypeStruct((dp, share + 16, 3 * group), BF16),
        ],
        [whole((block_rows, cols))] + [whole((dp, share + 16, 3 * group))] * 2,
        [],
        (1,),
        2 * block_rows * width * cols,
        16,
    )
    a_got = swap_with(a_send, "blk", 1)
    token_parts = call(
        functools.partial(token_grad_kernel, uly),
        "token_grad",
        scalars,
        [dproj, w_own, dh1],
        [whole((block_rows, cols)), whole((width, cols)), whole(square)],
        [jax.ShapeDtypeStruct(square, F32)] + [jax.ShapeDtypeStruct(square, BF16)] * (uly - 1),
        [whole(square)] * uly,
        [],
        (1,),
        2 * block_rows * width * cols,
        16,
    )

    def in_plane(own, *deps):
        own = after(own, *deps)
        return [own] + [swap_with(own, "uly", j) for j in range(1, uly)]

    def both_cores(pieces, *deps):
        return pieces + [swap_with(after(piece, *deps), "blk", 1) for piece in pieces]

    a_got = after(a_got, token_parts[0])
    a_near, a_far = add(a_keep[:2], a_got[:2]), add(a_keep[2:], a_got[2:])
    token_parts = after(token_parts, a_near, a_far)
    token_got = [swap_with(token_parts[j], "uly", j) for j in range(1, uly)]
    a_one = swap_with(a_far, "dp", 1)
    a_next = add(a_near[1], a_one[1])
    a_two = swap_with(a_next, "dp", 2)
    e_one = swap_with(after(e_far, a_next), "dp", 1)
    e_next = add(e_near[1], e_one[1])
    e_two = swap_with(e_next, "dp", 2)
    tokens_grad = total([token_parts[0], *token_got])
    p_own = add(p_near_0, p_one_0, p_two)
    p_plane = in_plane(p_own, *token_got)
    p_plane = both_cores(p_plane, a_two)
    shrink_out, mixer_out, vecs = call(
        functools.partial(finish_shrink_kernel, (uly, unit)),
        "finish_shrink",
        scalars,
        p_plane,
        [whole(p_own.shape)] * parts,
        [
            jax.ShapeDtypeStruct((hidden // dp, width), F32),
            jax.ShapeDtypeStruct((shard, width), F32),
            jax.ShapeDtypeStruct((16, width), F32),
        ],
        [pl.BlockSpec(memory_space=pl.ANY)] * 2 + [whole((16, width))],
        [
            pltpu.VMEM((parts, unit, width), F32),
            pltpu.VMEM((2, share, width), F32),
            pltpu.SemaphoreType.DMA((parts + 2,)),
        ],
        (1,),
        10**6,
        16,
    )
    e_own = add(e_near[0], e_one[0], e_two)
    e_plane = in_plane(e_own, *p_plane[1:uly])
    a_own = add(a_near[0], a_one[0], a_two)
    a_plane = in_plane(a_own, *p_plane[1:uly])
    e_plane = both_cores(e_plane, shrink_out, *a_plane[1:3])
    expand_out = call(
        functools.partial(finish_expand_kernel, sizes),
        "finish_expand",
        scalars,
        e_plane,
        [whole(e_own.shape)] * parts,
        jax.ShapeDtypeStruct((shard, hidden), F32),
        pl.BlockSpec(memory_space=pl.ANY),
        [
            pltpu.VMEM((width, width), BF16),
            pltpu.VMEM((dp, shard, width), F32),
            pltpu.SemaphoreType.DMA((dp,)),
        ],
        (1,),
        10**9,
        16,
    )
    a_plane = both_cores(a_plane, expand_out)
    attend_out, biases = call(
        functools.partial(finish_attend_kernel, uly),
        "finish_attend",
        scalars,
        a_plane,
        [whole(a_own.shape)] * parts,
        [jax.ShapeDtypeStruct((shard, 3 * width), F32), jax.ShapeDtypeStruct((8, 3 * group), F32)],
        [pl.BlockSpec(memory_space=pl.ANY), whole((8, 3 * group))],
        [pltpu.VMEM((6, share, width), F32), pltpu.SemaphoreType.DMA((6,))],
        (1,),
        10**9,
        16,
    )
    eb_out = vecs[8 : 8 + parts, :unit].reshape(-1)
    vecs = [vecs[k, :shard] for k in range(6)]
    return (
        mixed.reshape(tokens.shape),
        tokens_grad.reshape(tokens.shape),
        attend_out,
        biases[0, :group],
        biases[0, 2 * group :],
        mixer_out,
        vecs[0],
        vecs[1],
        vecs[2],
        expand_out,
        eb_out,
        shrink_out,
        vecs[3],
        vecs[4],
        vecs[5],
    )


def solution(mesh):
    row_spec = P("dp", ("blk", "uly"), None)
    matrix = P("dp", None)
    vector = P("dp")
    return jax.shard_map(
        on_device,
        mesh=mesh,
        in_specs=(
            row_spec,
            vector,
            row_spec,
            matrix,
            vector,
            vector,
            matrix,
            vector,
            vector,
            vector,
            matrix,
            vector,
            matrix,
            vector,
            vector,
            vector,
        ),
        out_specs=(
            row_spec,
            row_spec,
            matrix,
            vector,
            vector,
            matrix,
            vector,
            vector,
            vector,
            matrix,
            vector,
            matrix,
            vector,
            vector,
            vector,
        ),
        check_vma=False,
    )
```

```python
import functools

import jax
import jax.numpy as jnp
from jax import lax
from jax.experimental import pallas as pl
from jax.experimental.pallas import tpu as pltpu
from jax.sharding import PartitionSpec as P

HEADS = 12
HD = 64

EPSILON = 1e-12
MASKED = -1000000000.0
LOG2E = 1.4426950408889634
LN2 = 0.6931471805599453
F32 = jnp.float32
BF16 = jnp.bfloat16


def dot_nn(left, right):
    return lax.dot_general(left, right, (((1,), (0,)), ((), ())), preferred_element_type=F32)


def dot_nt(left, right):
    return lax.dot_general(left, right, (((1,), (1,)), ((), ())), preferred_element_type=F32)


def dot_tn(left, right):
    return lax.dot_general(left, right, (((0,), (0,)), ((), ())), preferred_element_type=F32)


def swap_with(value, axis, offset):
    size = lax.axis_size(axis)
    return lax.ppermute(value, axis, [(i, i ^ offset) for i in range(size)])


def xor_order(pieces, index):
    bit = 1
    while bit < len(pieces):
        flag = (index & bit) != 0
        pieces = [jnp.where(flag, pieces[p ^ bit], pieces[p]) for p in range(len(pieces))]
        bit *= 2
    return pieces


def total(values):
    acc = values[0].astype(F32)
    for value in values[1:]:
        acc = acc + value.astype(F32)
    return acc


def pad_rows(value, rows):
    return jnp.pad(value, ((0, rows - value.shape[0]), (0, 0)))


def head_lanes(width, head, ones_lane=None):
    lane = lax.broadcasted_iota(jnp.int32, (1, width), 1)
    keep = (lane >= head * HD) & (lane < (head + 1) * HD)
    if ones_lane is not None:
        keep = keep | (lane == ones_lane)
    return keep


def attend_forward_kernel(heads, blocks, q_ref, *refs):
    kv_refs = refs[:blocks]
    o_ref, lse_ref, vt_ref = refs[blocks:]
    group = heads * HD
    wide = q_ref.shape[1]
    rows = kv_refs[0].shape[0]

    @pl.when(pl.program_id(0) == 0)
    def _():
        for i in range(blocks):
            vt_ref[:, i * rows : (i + 1) * rows] = kv_refs[i][:, wide : wide + group].T

    q = q_ref[...]
    outs = []
    stats = []
    for head in range(heads):
        q_head = jnp.where(head_lanes(wide, head, group), q, jnp.zeros_like(q))
        scores = [dot_nt(kv_refs[i][:, :wide], q_head) for i in range(blocks)]
        top = jnp.max(scores[0], axis=0, keepdims=True)
        for i in range(1, blocks):
            top = jnp.maximum(top, jnp.max(scores[i], axis=0, keepdims=True))
        norm = jnp.zeros_like(top)
        acc = None
        for i in range(blocks):
            probs = jnp.exp2(scores[i] - top)
            norm = norm + jnp.sum(probs, axis=0, keepdims=True)
            part = dot_nn(
                vt_ref[head * HD : (head + 1) * HD, i * rows : (i + 1) * rows], probs.astype(BF16)
            )
            acc = part if acc is None else acc + part
        outs.append(acc / norm)
        stats.append(top + jnp.log2(norm))
    o_ref[...] = jnp.concatenate(outs, axis=0).T.astype(BF16)
    for head in range(heads):
        lse_ref[head : head + 1, :] = stats[head]


def attend_forward(q, kvs, heads, tile):
    rows, wide = q.shape
    group = heads * HD
    blocks = len(kvs)
    keys = blocks * rows
    whole = pl.BlockSpec(kvs[0].shape, lambda t: (0, 0))
    return pl.pallas_call(
        functools.partial(attend_forward_kernel, heads, blocks),
        grid=(rows // tile,),
        in_specs=[pl.BlockSpec((tile, wide), lambda t: (t, 0))] + [whole] * blocks,
        out_specs=[
            pl.BlockSpec((tile, group), lambda t: (t, 0)),
            pl.BlockSpec((8, tile), lambda t: (0, t)),
        ],
        out_shape=[
            jax.ShapeDtypeStruct((rows, group), BF16),
            jax.ShapeDtypeStruct((8, rows), F32),
        ],
        scratch_shapes=[pltpu.VMEM((group, keys), BF16)],
        compiler_params=pltpu.CompilerParams(vmem_limit_bytes=56 * 2**20),
        cost_estimate=pl.CostEstimate(
            flops=4 * heads * rows * keys * wide,
            transcendentals=heads * rows * keys,
            bytes_accessed=2 * rows * wide * 3 + 2 * keys * (wide + group),
        ),
        name="attend_forward",
    )(q, *kvs)


def attend_backward_kernel(heads, blocks, q_ref, do_ref, o_ref, lse_ref, *refs):
    kv_refs = refs[:blocks]
    dq_ref = refs[blocks]
    dkv_refs = refs[blocks + 1 : 2 * blocks + 1]
    kt_ref = refs[2 * blocks + 1]
    dk_accs = refs[2 * blocks + 2 : 3 * blocks + 2]
    dv_accs = refs[3 * blocks + 2 :]
    group = heads * HD
    wide = q_ref.shape[1]
    rows = kv_refs[0].shape[0]

    @pl.when(pl.program_id(0) == 0)
    def _():
        for i in range(blocks):
            kt_ref[:, i * rows : (i + 1) * rows] = kv_refs[i][:, :group].T
            dk_accs[i][...] = jnp.zeros_like(dk_accs[i])
            dv_accs[i][...] = jnp.zeros_like(dv_accs[i])

    q = q_ref[...]
    dout = do_ref[...]
    products = (dout.astype(F32) * o_ref[...].astype(F32)).T
    dqs = []
    for head in range(heads):
        q_head = jnp.where(head_lanes(wide, head, group), q, jnp.zeros_like(q))
        do_head = jnp.where(head_lanes(group, head), dout, jnp.zeros_like(dout))
        lse = lse_ref[head : head + 1, :]
        delta = jnp.sum(products[head * HD : (head + 1) * HD], axis=0, keepdims=True)
        acc = None
        for i in range(blocks):
            probs = jnp.exp2(dot_nt(kv_refs[i][:, :wide], q_head) - lse)
            dv_accs[i][...] += dot_nn(probs.astype(BF16), do_head)
            grads = dot_nt(kv_refs[i][:, wide : wide + group], do_head)
            grads = (probs * (grads - delta)).astype(BF16)
            dk_accs[i][...] += dot_nn(grads, q_head)
            part = dot_nn(
                kt_ref[head * HD : (head + 1) * HD, i * rows : (i + 1) * rows], grads
            )
            acc = part if acc is None else acc + part
        dqs.append(acc)
    dq_ref[...] = jnp.concatenate(dqs, axis=0).T.astype(BF16)

    @pl.when(pl.program_id(0) == pl.num_programs(0) - 1)
    def _():
        for i in range(blocks):
            dkv_refs[i][:, :group] = (dk_accs[i][:, :group] * LN2).astype(BF16)
            dkv_refs[i][:, wide : wide + group] = dv_accs[i][...].astype(BF16)


def attend_backward(q, kvs, dout, o, lse, heads, tile):
    rows, wide = q.shape
    group = heads * HD
    blocks = len(kvs)
    keys = blocks * rows
    whole = pl.BlockSpec(kvs[0].shape, lambda t: (0, 0))
    out = pl.pallas_call(
        functools.partial(attend_backward_kernel, heads, blocks),
        grid=(rows // tile,),
        in_specs=[
            pl.BlockSpec((tile, wide), lambda t: (t, 0)),
            pl.BlockSpec((tile, group), lambda t: (t, 0)),
            pl.BlockSpec((tile, group), lambda t: (t, 0)),
            pl.BlockSpec((8, tile), lambda t: (0, t)),
        ]
        + [whole] * blocks,
        out_specs=[pl.BlockSpec((tile, group), lambda t: (t, 0))] + [whole] * blocks,
        out_shape=[jax.ShapeDtypeStruct((rows, group), BF16)]
        + [jax.ShapeDtypeStruct(kvs[0].shape, BF16)] * blocks,
        scratch_shapes=[pltpu.VMEM((group, keys), BF16)]
        + [pltpu.VMEM((rows, wide), F32)] * blocks
        + [pltpu.VMEM((rows, group), F32)] * blocks,
        compiler_params=pltpu.CompilerParams(vmem_limit_bytes=56 * 2**20),
        cost_estimate=pl.CostEstimate(
            flops=10 * heads * rows * keys * wide,
            transcendentals=heads * rows * keys,
            bytes_accessed=2 * rows * wide * 4 + 4 * keys * (wide + group),
        ),
        name="attend_backward",
    )(q, dout, o, lse, *kvs)
    return out[0], out[1:]


def feed_kernel(
    x1_ref,
    x1b_ref,
    expand_ref,
    shrink_ref,
    ebias_ref,
    sbias_ref,
    gain_ref,
    shift_ref,
    cot_ref,
    mixed_ref,
    dx1_ref,
    dexpand_ref,
    dshrink_ref,
    debias_ref,
    vec_ref,
    act_ref,
    slope_ref,
    acc_ref,
    d2b_ref,
    x1t_ref,
):
    phase = pl.program_id(0)
    step = pl.program_id(1)
    last = pl.num_programs(1) - 1
    width = x1_ref.shape[1]

    @pl.when(phase == 0)
    def _():
        pre = dot_nn(x1b_ref[...], expand_ref[0]) + ebias_ref[0]
        cdf = 0.5 * (1.0 + lax.erf(pre * 0.7071067811865476))
        pdf = jnp.exp(-0.5 * pre * pre) * 0.3989422804014327
        act = (pre * cdf).astype(BF16)
        act_ref[step] = act
        slope_ref[step] = (cdf + pre * pdf).astype(BF16)
        part = dot_nn(act, shrink_ref[0])

        @pl.when(step == 0)
        def _():
            acc_ref[...] = part
            x1t_ref[...] = x1b_ref[...].T

        @pl.when(step > 0)
        def _():
            acc_ref[...] += part

        @pl.when(step == last)
        def _():
            hidden = x1_ref[...] + (acc_ref[...] + sbias_ref[...])
            center = hidden - jnp.mean(hidden, -1, keepdims=True)
            inverse = lax.rsqrt(jnp.mean(center * center, -1, keepdims=True) + EPSILON)
            normed = center * inverse
            mixed_ref[...] = (normed * gain_ref[...] + shift_ref[...]).astype(BF16)
            grad = cot_ref[...].astype(F32)
            scaled = grad * gain_ref[...]
            dhidden = inverse * (
                scaled
                - jnp.mean(scaled, -1, keepdims=True)
                - normed * jnp.mean(scaled * normed, -1, keepdims=True)
            )
            acc_ref[...] = dhidden
            d2b_ref[...] = dhidden.astype(BF16)
            vec_ref[...] = jnp.zeros_like(vec_ref)
            vec_ref[0:1, :] = jnp.sum(grad * normed, 0, keepdims=True)
            vec_ref[1:2, :] = jnp.sum(grad, 0, keepdims=True)
            vec_ref[2:3, :] = jnp.sum(dhidden, 0, keepdims=True)

    @pl.when(phase == 1)
    def _():
        d2b = d2b_ref[...]
        dpre = (dot_nt(d2b, shrink_ref[0]) * slope_ref[step].astype(F32)).astype(BF16)
        debias_ref[0] = jnp.sum(dpre.astype(F32), 0, keepdims=True)
        dexpand_ref[0] = dot_nn(x1t_ref[...], dpre).astype(BF16)
        dshrink_ref[0] = dot_tn(act_ref[step], d2b).astype(BF16)
        acc_ref[...] += dot_nt(dpre, expand_ref[0])

        @pl.when(step == last)
        def _():
            dx1_ref[...] = acc_ref[...]


def feed_forward_backward(x1, x1b, expand, shrink, ebias, sbias, gain, shift, cot):
    rows, width = x1.shape
    parts, _, block = expand.shape
    full = pl.BlockSpec((rows, width), lambda p, k: (0, 0))
    line = pl.BlockSpec((1, width), lambda p, k: (0, 0))
    return pl.pallas_call(
        feed_kernel,
        grid=(2, parts),
        in_specs=[
            full,
            full,
            pl.BlockSpec((1, width, block), lambda p, k: (k, 0, 0)),
            pl.BlockSpec((1, block, width), lambda p, k: (k, 0, 0)),
            pl.BlockSpec((1, 1, block), lambda p, k: (k, 0, 0)),
            line,
            line,
            line,
            full,
        ],
        out_specs=[
            full,
            full,
            pl.BlockSpec((1, width, block), lambda p, k: (p * k, 0, 0)),
            pl.BlockSpec((1, block, width), lambda p, k: (p * k, 0, 0)),
            pl.BlockSpec((1, 1, block), lambda p, k: (p * k, 0, 0)),
            pl.BlockSpec((8, width), lambda p, k: (0, 0)),
        ],
        out_shape=[
            jax.ShapeDtypeStruct((rows, width), BF16),
            jax.ShapeDtypeStruct((rows, width), F32),
            jax.ShapeDtypeStruct((parts, width, block), BF16),
            jax.ShapeDtypeStruct((parts, block, width), BF16),
            jax.ShapeDtypeStruct((parts, 1, block), F32),
            jax.ShapeDtypeStruct((8, width), F32),
        ],
        scratch_shapes=[
            pltpu.VMEM((parts, rows, block), BF16),
            pltpu.VMEM((parts, rows, block), BF16),
            pltpu.VMEM((rows, width), F32),
            pltpu.VMEM((rows, width), BF16),
            pltpu.VMEM((width, rows), BF16),
        ],
        compiler_params=pltpu.CompilerParams(vmem_limit_bytes=48 * 2**20),
        cost_estimate=pl.CostEstimate(
            flops=12 * rows * width * parts * block,
            transcendentals=2 * rows * parts * block,
            bytes_accessed=12 * width * parts * block,
        ),
        name="feed_forward_backward",
    )(x1, x1b, expand, shrink, ebias, sbias, gain, shift, cot)


def general_device(
    tokens,
    lengths,
    cotangent,
    attend_weight,
    query_bias,
    value_bias,
    mixer_weight,
    mixer_bias,
    attn_gain,
    attn_shift,
    expand_weight,
    expand_bias,
    shrink_weight,
    shrink_bias,
    final_gain,
    final_shift,
):
    uly = lax.axis_size("uly")
    blk = lax.axis_size("blk")
    dp = lax.axis_size("dp")
    u = lax.axis_index("uly")
    b = lax.axis_index("blk")
    z = lax.axis_index("dp")
    width = tokens.shape[-1]
    rows = tokens.shape[0] * tokens.shape[1]
    block_rows = uly * rows
    heads = HEADS // uly
    group = heads * HD
    wide = -(-(group + 1) // 128) * 128
    shard = attend_weight.shape[0]
    hidden = expand_weight.shape[1]
    parts = blk * uly
    unit = hidden // (parts * dp)
    share = shard // blk

    x = tokens.reshape(rows, width)
    x_rows = jnp.concatenate([x] + [swap_with(x, "uly", j) for j in range(1, uly)], 0)

    small = jnp.concatenate(
        [query_bias, value_bias, mixer_bias, attn_gain, attn_shift, shrink_bias]
        + [final_gain, final_shift, expand_bias]
    )
    small_rows = small.shape[0] // (3 * group)
    own_heads = lax.dynamic_slice_in_dim(attend_weight.reshape(shard, 3, uly, group), u, 1, 2)
    own_heads = own_heads.reshape(shard, 3 * group)
    first_piece = jnp.concatenate(
        [
            lax.dynamic_slice_in_dim(own_heads, b * share, share, 0),
            pad_rows(small.reshape(small_rows, 3 * group), 16),
        ]
    )
    first_all = lax.all_gather(first_piece, "dp", axis=0, tiled=False)
    halves = first_all[:, :share]
    halves = xor_order([halves] + [swap_with(halves, "blk", i) for i in range(1, blk)], b)
    attend_own = jnp.stack(halves, 1).reshape(width, 3, group)
    vectors = first_all[:, share : share + small_rows].reshape(dp, -1, shard).astype(F32)
    names = [vectors[:, k].reshape(width) for k in range(8)]
    bias_query, bias_value, bias_mixer, gain_attn, shift_attn, bias_shrink = names[:6]
    gain_final, shift_final = names[6:]
    bias_expand = vectors[:, 8:].reshape(dp, parts, unit).transpose(1, 0, 2)
    bias_expand = jnp.stack(
        xor_order(list(bias_expand.reshape(parts, dp * unit)), b * uly + u), 0
    ).reshape(parts, 1, dp * unit)

    mixer_own = lax.dynamic_slice_in_dim(mixer_weight, b * share, share, 0)
    mixer_all = jnp.stack(
        xor_order([mixer_own] + [swap_with(mixer_own, "dp", j) for j in range(1, dp)], z), 0
    )
    mixer_all = jnp.stack(
        xor_order([mixer_all] + [swap_with(mixer_all, "blk", i) for i in range(1, blk)], b), 1
    ).reshape(width, width)

    part = b * uly + u
    expand_own = lax.dynamic_slice_in_dim(
        expand_weight.reshape(shard, dp, parts, unit), part, 1, 2
    ).reshape(-1, width)
    shrink_own = lax.dynamic_slice_in_dim(shrink_weight.reshape(parts, unit, width), part, 1, 0)
    expand_rows = expand_own.shape[0]
    feed_own = jnp.concatenate([expand_own, shrink_own.reshape(unit, width)], 0)
    feed_all = lax.all_gather(feed_own, "dp", axis=0, tiled=False)
    expand_part = feed_all[:, :expand_rows].reshape(width, dp * unit)
    shrink_part = feed_all[:, expand_rows:].reshape(dp * unit, width)
    expand_two = jnp.stack([expand_part, swap_with(expand_part, "uly", 1)])
    shrink_two = jnp.stack([shrink_part, swap_with(shrink_part, "uly", 2)])
    expand_far = swap_with(expand_two, "uly", 2)
    shrink_far = swap_with(shrink_two, "uly", 1)
    expand_here = jnp.concatenate([expand_two, expand_far], 0)
    shrink_here = jnp.stack([shrink_two[0], shrink_far[0], shrink_two[1], shrink_far[1]], 0)
    expand_full = jnp.concatenate(
        [expand_here] + [swap_with(expand_here, "blk", i) for i in range(1, blk)], 0
    )
    shrink_full = jnp.concatenate(
        [shrink_here] + [swap_with(shrink_here, "blk", i) for i in range(1, blk)], 0
    )

    lane_pad = ((0, 0), (0, wide - group))
    bias_row = jnp.pad(lax.dynamic_slice_in_dim(bias_query, u * group, group, 0), lane_pad[1:])
    ones_lane = (jnp.arange(wide) == group).astype(F32)
    q = dot_nn(x_rows, jnp.pad(attend_own[:, 0], lane_pad)) + bias_row
    q = (q * (0.125 * LOG2E) + ones_lane).astype(BF16)
    kv_weight = jnp.concatenate([jnp.pad(attend_own[:, 1], lane_pad), attend_own[:, 2]], 1)
    kv_bias = jnp.concatenate(
        [jnp.zeros((wide,), F32), lax.dynamic_slice_in_dim(bias_value, u * group, group, 0)]
    )
    kv_ones = jnp.pad(ones_lane, (0, group))
    row_index = jnp.arange(block_rows, dtype=jnp.int32)
    positions = b * block_rows + ((row_index // rows) ^ u) * rows + row_index % rows
    key_mask = jnp.where(positions < lengths[0], 0.0, MASKED)
    kv = (dot_nn(x_rows, kv_weight) + kv_bias + key_mask[:, None] * kv_ones).astype(BF16)
    kvs = [kv] + [swap_with(kv, "blk", i) for i in range(1, blk)]

    o_rows, lse = attend_forward(q, kvs, heads, min(256, block_rows))
    pieces = [o_rows[j * rows : (j + 1) * rows] for j in range(uly)]
    pieces = [pieces[0]] + [swap_with(pieces[j], "uly", j) for j in range(1, uly)]
    mixer_in = jnp.concatenate(xor_order(pieces, u), 1)

    first_sum = x.astype(F32) + (dot_nn(mixer_in, mixer_all) + bias_mixer)
    center = first_sum - jnp.mean(first_sum, -1, keepdims=True)
    first_inv = lax.rsqrt(jnp.mean(center * center, -1, keepdims=True) + EPSILON)
    first_normed = center * first_inv
    first_out = first_normed * gain_attn + shift_attn
    first_low = first_out.astype(BF16)

    mixed, first_grad, expand_grad, shrink_grad, expand_bias_grad, vec_grads = (
        feed_forward_backward(
            first_out,
            first_low,
            expand_full,
            shrink_full,
            bias_expand,
            bias_shrink[None],
            gain_final[None],
            shift_final[None],
            cotangent.reshape(rows, width),
        )
    )

    scaled = first_grad * gain_attn
    attn_grad = first_inv * (
        scaled
        - jnp.mean(scaled, -1, keepdims=True)
        - first_normed * jnp.mean(scaled * first_normed, -1, keepdims=True)
    )
    attn_low = attn_grad.astype(BF16)
    out_grad = dot_nt(attn_low, mixer_all).astype(BF16)
    sends = xor_order([out_grad[:, j * group : (j + 1) * group] for j in range(uly)], u)
    dout_rows = jnp.concatenate(
        [sends[0]] + [swap_with(sends[j], "uly", j) for j in range(1, uly)], 0
    )
    dq, dkvs = attend_backward(q, kvs, dout_rows, o_rows, lse, heads, min(256, block_rows))

    mixer_grad = dot_tn(mixer_in, attn_low).astype(BF16)
    attn_gain_grad = jnp.sum(first_grad * first_normed, 0)
    attn_shift_grad = jnp.sum(first_grad, 0)
    mixer_bias_grad = jnp.sum(attn_grad, 0)
    ebg = jnp.stack(xor_order(list(expand_bias_grad.reshape(parts, dp * unit)), part), 0)
    ebg = ebg.reshape(parts, dp, unit).transpose(1, 0, 2).reshape(dp, parts * unit)
    vec_all = jnp.concatenate(
        [
            v.reshape(dp, shard)
            for v in (
                mixer_bias_grad,
                attn_gain_grad,
                attn_shift_grad,
                vec_grads[2],
                vec_grads[0],
                vec_grads[1],
            )
        ]
        + [ebg],
        1,
    ).astype(BF16)

    mixer_cols = width // blk
    mixer_part_rows = shard // uly
    vec_len = vec_all.shape[1]
    vec_rows = -(-vec_len // mixer_cols)
    vec_rows = -(-vec_rows // 16) * 16
    vec_block = jnp.pad(vec_all, ((0, 0), (0, vec_rows * mixer_cols - vec_len))).reshape(
        dp, vec_rows, mixer_cols
    )
    mixer_view = mixer_grad.reshape(dp, uly, mixer_part_rows, blk, mixer_cols)
    by_blk = xor_order([mixer_view[:, :, :, i] for i in range(blk)], b)
    mixer_parts = []
    for i in range(blk):
        by_uly = xor_order([by_blk[i][:, j] for j in range(uly)], u)
        mixer_parts.append(
            jnp.stack([jnp.concatenate([piece, vec_block], 1) for piece in by_uly], 0)
        )
    mixer_sum = total(
        [mixer_parts[0]] + [swap_with(mixer_parts[i], "blk", i) for i in range(1, blk)]
    ).astype(BF16)
    mixer_sum = total(
        [mixer_sum[0]] + [swap_with(mixer_sum[j], "uly", j) for j in range(1, uly)]
    ).astype(BF16)

    def over_blk(grad):
        return total(
            [grad[:uly]]
            + [swap_with(grad[i * uly : (i + 1) * uly], "blk", i) for i in range(1, blk)]
        ).astype(BF16)

    shrink_sum = over_blk(shrink_grad)
    expand_sum = over_blk(expand_grad)
    shrink_sum = shrink_sum.reshape(2, 2, dp * unit, width)
    expand_sum = expand_sum.reshape(2, 2, width, dp * unit)
    shrink_sum = total([shrink_sum[0], swap_with(shrink_sum[1], "uly", 2)]).astype(BF16)
    expand_sum = total([expand_sum[:, 0], swap_with(expand_sum[:, 1], "uly", 1)]).astype(BF16)
    shrink_sum = total([shrink_sum[0], swap_with(shrink_sum[1], "uly", 1)]).astype(BF16)
    expand_sum = total([expand_sum[0], swap_with(expand_sum[1], "uly", 2)]).astype(BF16)

    mixer_rows = mixer_sum.shape[1] * mixer_cols // width
    packed = jnp.concatenate(
        [
            expand_sum.reshape(dp, expand_rows, width),
            shrink_sum.reshape(dp, unit, width),
            mixer_sum.reshape(dp, mixer_rows, width),
        ],
        1,
    )

    def over_dp(value):
        sends = [lax.dynamic_slice_in_dim(value, z ^ j, 1, 0)[0] for j in range(dp)]
        return total([sends[0]] + [swap_with(sends[j], "dp", j) for j in range(1, dp)])

    owned = over_dp(packed)
    vec_owned = owned[expand_rows + unit :].reshape(-1, mixer_cols)[mixer_part_rows:]
    vec_owned = vec_owned.reshape(-1)[:vec_len]

    def in_plane(value):
        value = value.astype(BF16)
        value = jnp.stack(
            xor_order([value] + [swap_with(value, "uly", j) for j in range(1, uly)], u), 0
        )
        return jnp.stack(
            xor_order([value] + [swap_with(value, "blk", i) for i in range(1, blk)], b), 0
        )

    gathered = in_plane(owned).reshape(parts, -1, width)
    expand_out = gathered[:, :expand_rows].reshape(parts, shard, dp, unit)
    expand_out = expand_out.transpose(1, 2, 0, 3).reshape(shard, hidden).astype(F32)
    shrink_out = gathered[:, expand_rows : expand_rows + unit]
    shrink_out = shrink_out.reshape(parts * unit, width).astype(F32)
    mixer_out = gathered[:, expand_rows + unit :].reshape(blk, uly, -1, mixer_cols)
    mixer_out = mixer_out[:, :, :mixer_part_rows].transpose(1, 2, 0, 3)
    mixer_out = mixer_out.reshape(shard, width).astype(F32)

    own_dkv = total([dkvs[0]] + [swap_with(dkvs[i], "blk", i) for i in range(1, blk)])
    own_dkv = own_dkv.astype(BF16)
    proj_grad = jnp.concatenate(
        [dq * jnp.asarray(0.125, BF16), own_dkv[:, :group], own_dkv[:, wide : wide + group]], 1
    )
    token_parts = dot_nt(proj_grad, attend_own.reshape(width, 3 * group))
    token_low = token_parts.astype(BF16)
    tokens_grad = attn_grad + total(
        [token_parts[:rows]]
        + [swap_with(token_low[j * rows : (j + 1) * rows], "uly", j) for j in range(1, uly)]
    )
    attend_grad = dot_tn(x_rows, proj_grad).astype(BF16)
    attend_grad = attend_grad.reshape(dp, blk, share, 3 * group)
    bias_sum = jnp.sum(proj_grad.astype(F32), 0)[None]
    bias_rows = pad_rows(bias_sum.astype(BF16), 16)
    attend_parts = [
        jnp.concatenate(
            [
                lax.dynamic_slice_in_dim(attend_grad, b ^ i, 1, 1).reshape(-1, 3 * group),
                bias_rows,
            ],
            0,
        )
        for i in range(blk)
    ]
    attend_sum = total(
        [attend_parts[0]] + [swap_with(attend_parts[i], "blk", i) for i in range(1, blk)]
    ).astype(BF16)
    bias_half = jnp.broadcast_to(attend_sum[dp * share :], (dp, 16, 3 * group))
    attend_sum = attend_sum[: dp * share].reshape(dp, share, 3 * group)
    attend_owned = over_dp(jnp.concatenate([attend_sum, bias_half], 1))
    attend_all = in_plane(attend_owned)
    attend_out = attend_all[:, :, :share].reshape(blk, uly, share, 3, group)
    attend_out = attend_out.transpose(0, 2, 3, 1, 4).reshape(shard, 3 * width).astype(F32)
    bias_out = attend_all[0, :, share].astype(F32).reshape(uly, 3, group)
    query_bias_grad = lax.dynamic_slice_in_dim(bias_out[:, 0].reshape(width), z * shard, shard, 0)
    value_bias_grad = lax.dynamic_slice_in_dim(bias_out[:, 2].reshape(width), z * shard, shard, 0)

    vecs = [vec_owned[k * shard : (k + 1) * shard] for k in range(6)]
    return (
        mixed.reshape(tokens.shape),
        tokens_grad.reshape(tokens.shape),
        attend_out,
        query_bias_grad,
        value_bias_grad,
        mixer_out,
        vecs[0],
        vecs[1],
        vecs[2],
        expand_out,
        vec_owned[6 * shard :],
        shrink_out,
        vecs[3],
        vecs[4],
        vecs[5],
    )


def call(
    kernel,
    name,
    scalars,
    args,
    in_specs,
    out_shape,
    out_specs,
    scratch,
    grid,
    flops,
    vmem,
    aliases={},
):
    return pl.pallas_call(
        kernel,
        grid_spec=pltpu.PrefetchScalarGridSpec(
            num_scalar_prefetch=1,
            grid=grid,
            in_specs=in_specs,
            out_specs=out_specs,
            scratch_shapes=scratch,
        ),
        out_shape=out_shape,
        compiler_params=pltpu.CompilerParams(vmem_limit_bytes=vmem * 2**20),
        input_output_aliases=aliases,
        cost_estimate=pl.CostEstimate(flops=flops, bytes_accessed=1, transcendentals=0),
        name=name,
    )(scalars, *args)


def whole(shape):
    return pl.BlockSpec(shape, lambda *_: (0,) * len(shape))


def after(value, *deps):
    return lax.optimization_barrier((value, *deps))[0]


def slot(offset):
    return (offset & 1) * 2 + (offset >> 1)


def one_hot(rows, cols, row_offset=0, col_offset=0):
    row = lax.broadcasted_iota(jnp.int32, (rows, cols), 0) + row_offset
    col = lax.broadcasted_iota(jnp.int32, (rows, cols), 1) + col_offset
    return jnp.where(row == col, 1.0, 0.0).astype(BF16)


def fetch_kernel(sizes, idx, attend_ref, expand_ref, shrink_ref, mixer_ref, *refs):
    uly, dp, group, unit = sizes
    vec_refs, (first_ref, feed_ref) = refs[:-2], refs[-2:]
    share = attend_ref.shape[1]
    shard, width = mixer_ref.shape
    u = idx[1]
    part = idx[0] * uly + u
    take = one_hot(width, group, 0, u * group)
    for c in range(3):
        cols = dot_nn(attend_ref[0, :, c * width : (c + 1) * width], take)
        first_ref[:share, c * group : (c + 1) * group] = cols.astype(BF16)
    first_ref[share:, :] = jnp.zeros_like(first_ref[share:, :])
    rows = share // dp
    mixer = dot_nn(one_hot(rows, shard, part * rows, 0), mixer_ref[...]).astype(BF16)
    for k in range(dp):
        here = slice(k * rows, (k + 1) * rows)
        first_ref[here, 3 * group :] = mixer[:, k * group : (k + 1) * group]
    line = share
    for ref in vec_refs:
        for k in range(ref.shape[0] // shard):
            first_ref[line : line + 1, :shard] = ref[k * shard : (k + 1) * shard].reshape(1, shard)
            line += 1
    take = one_hot(width, unit, 0, part * unit)
    half = shard // 2
    for k in range(dp):
        cols = dot_nn(expand_ref[:, k * width : (k + 1) * width], take).astype(BF16)
        feed_ref[:half, k * unit : (k + 1) * unit] = cols[:half]
        feed_ref[:half, (dp + k) * unit : (dp + k + 1) * unit] = cols[half:]
    feed_ref[half:, :] = shrink_ref[0]


def project_kernel(sizes, idx, *refs):
    uly, blk, dp, group, unit = sizes
    x_refs, refs = refs[:uly], refs[uly:]
    mine_refs, refs = refs[:dp], refs[dp:]
    other_refs, refs = refs[:dp], refs[dp:]
    w_ref, q_ref, kv_ref, vec_ref, eb_ref, mixer_ref = refs
    b, u, z, length = idx[0], idx[1], idx[2], idx[3]
    rows, width = x_refs[0].shape
    wide = q_ref.shape[1]
    pad = wide - group
    share = mine_refs[0].shape[0] - 16
    shard = 2 * share
    parts = uly * blk
    for c in range(3):
        w_ref[:, c * wide + group : (c + 1) * wide] = jnp.zeros((width, pad), BF16)
    own_vec = jnp.zeros((16, shard), F32)
    all_vec = jnp.zeros((16, width), F32)
    lines = share // dp
    for j in range(dp):
        for k in range(dp):
            mixer_ref[j * lines : (j + 1) * lines, k * group : (k + 1) * group] = mine_refs[j][
                k * lines : (k + 1) * lines, 3 * group :
            ]
        for ref, core in ((mine_refs[j], b), (other_refs[j], 1 - b)):
            start = pl.multiple_of((z ^ j) * shard + core * share, share)
            for c in range(3):
                w_ref[pl.ds(start, share), c * wide : c * wide + group] = ref[
                    :share, c * group : (c + 1) * group
                ]
        vec = mine_refs[j][share:, :shard]
        own_vec += jnp.where((z ^ j) == u, 1.0, 0.0) * vec.astype(F32)
        all_vec += dot_nn(vec, one_hot(shard, width, (z ^ j) * shard, 0))
    vec_ref[...] = all_vec

    low = all_vec.astype(BF16)
    part = b * uly + u
    eb = jnp.zeros((parts, dp * unit), F32)
    for parity in range(2):
        col = lax.broadcasted_iota(jnp.int32, (width, dp * unit), 1)
        row = lax.broadcasted_iota(jnp.int32, (width, dp * unit), 0)
        source = col + (col // unit) * (shard - unit) + parity * unit
        lanes = dot_nn(low, jnp.where(row == source, 1.0, 0.0).astype(BF16)).astype(BF16)
        owner = lax.broadcasted_iota(jnp.int32, (parts, 16), 0) ^ part
        line = lax.broadcasted_iota(jnp.int32, (parts, 16), 1)
        wanted = ((owner & 1) == parity) & (line == 8 + (owner >> 1))
        eb += dot_nn(jnp.where(wanted, 1.0, 0.0).astype(BF16), lanes)
    eb_ref[...] = eb

    lane = lax.broadcasted_iota(jnp.int32, (1, wide), 1)
    mark = jnp.where(lane == group, 1.0, 0.0)
    zeros = jnp.zeros((1, pad), F32)
    q_bias = jnp.concatenate([own_vec[0:1], zeros], 1)
    v_bias = jnp.concatenate([own_vec[1:2], zeros], 1)
    for j in range(uly):
        x = x_refs[j][...]
        here = slice(j * rows, (j + 1) * rows)
        q = dot_nn(x, w_ref[:, :wide]) + q_bias
        q_ref[here, :] = (q * (0.125 * LOG2E) + mark).astype(BF16)
        first = (b * uly + (u ^ j)) * rows
        position = lax.broadcasted_iota(jnp.int32, (rows, 1), 0) + first
        masked = jnp.where(position < length, 0.0, MASKED)
        k = dot_nn(x, w_ref[:, wide : 2 * wide]) + masked * mark
        kv_ref[here, :wide] = k.astype(BF16)
        kv_ref[here, wide:] = (dot_nn(x, w_ref[:, 2 * wide :]) + v_bias).astype(BF16)


def attend_kernel(heads, blocks, q_ref, *refs):
    kv_refs = refs[:blocks]
    o_refs = refs[blocks:-2]
    lse_ref, vt_ref = refs[-2:]
    group = heads * HD
    wide = q_ref.shape[1]
    rows = kv_refs[0].shape[0]

    @pl.when(pl.program_id(0) == 0)
    def _():
        for i in range(blocks):
            vt_ref[:, i * rows : (i + 1) * rows] = kv_refs[i][:, wide : wide + group].T

    q = q_ref[...]
    outs = []
    for head in range(heads):
        q_head = jnp.where(head_lanes(wide, head, group), q, jnp.zeros_like(q))
        scores = [dot_nt(kv_refs[i][:, :wide], q_head) for i in range(blocks)]
        top = jnp.max(scores[0], axis=0, keepdims=True)
        for i in range(1, blocks):
            top = jnp.maximum(top, jnp.max(scores[i], axis=0, keepdims=True))
        norm = jnp.zeros_like(top)
        acc = None
        for i in range(blocks):
            probs = jnp.exp2(scores[i] - top)
            norm = norm + jnp.sum(probs, axis=0, keepdims=True)
            part = dot_nn(
                vt_ref[head * HD : (head + 1) * HD, i * rows : (i + 1) * rows], probs.astype(BF16)
            )
            acc = part if acc is None else acc + part
        outs.append(acc / norm)
        lse_ref[head : head + 1, :] = top + jnp.log2(norm)
    out = jnp.concatenate(outs, axis=0).T.astype(BF16)
    for j, o_ref in enumerate(o_refs):

        @pl.when(pl.program_id(0) == j)
        def _(o_ref=o_ref):
            o_ref[...] = out


def attend(q, kvs, heads, pieces):
    rows, wide = q.shape
    tile = rows // pieces
    group = heads * HD
    blocks = len(kvs)
    keys = blocks * rows
    out = pl.pallas_call(
        functools.partial(attend_kernel, heads, blocks),
        grid=(pieces,),
        in_specs=[pl.BlockSpec((tile, wide), lambda t: (t, 0))] + [whole(kvs[0].shape)] * blocks,
        out_specs=[whole((tile, group))] * pieces + [pl.BlockSpec((8, tile), lambda t: (0, t))],
        out_shape=[jax.ShapeDtypeStruct((tile, group), BF16)] * pieces
        + [jax.ShapeDtypeStruct((8, rows), F32)],
        scratch_shapes=[pltpu.VMEM((group, keys), BF16)],
        compiler_params=pltpu.CompilerParams(vmem_limit_bytes=16 * 2**20),
        cost_estimate=pl.CostEstimate(
            flops=4 * heads * rows * keys * wide,
            transcendentals=heads * rows * keys,
            bytes_accessed=2 * rows * wide * 3 + 2 * keys * (wide + group),
        ),
        name="attend",
    )(q, *kvs)
    return out[:-1], out[-1]


def first_norm_kernel(uly, idx, x_ref, *refs):
    o_refs = refs[:uly]
    m_ref, vec_ref, x1_ref, x1b_ref, normed_ref, inverse_ref = refs[uly:]
    group = o_refs[0].shape[1]
    acc = vec_ref[2:3, :]
    for j in range(uly):
        start = pl.multiple_of((idx[1] ^ j) * group, group)
        acc = acc + dot_nn(o_refs[j][...], m_ref[pl.ds(start, group), :])
    hidden = x_ref[...].astype(F32) + acc
    center = hidden - jnp.mean(hidden, -1, keepdims=True)
    inverse = lax.rsqrt(jnp.mean(center * center, -1, keepdims=True) + EPSILON)
    normed = center * inverse
    out = normed * vec_ref[3:4, :] + vec_ref[4:5, :]
    x1_ref[...] = out
    x1b_ref[...] = out.astype(BF16)
    normed_ref[...] = normed
    inverse_ref[...] = inverse


def rest_kernel(sizes, idx, expand_ref, shrink_ref, out_ref):
    uly, dp, unit = sizes
    width = shrink_ref.shape[1]
    half = expand_ref.shape[0] // 2
    for j in range(1, uly):
        part = idx[0] * uly + (idx[1] ^ j)
        take = one_hot(width, unit, 0, part * unit)
        for k in range(dp):
            cols = dot_nn(expand_ref[:, k * width : (k + 1) * width], take).astype(BF16)
            out_ref[j - 1, :half, k * unit : (k + 1) * unit] = cols[:half]
            out_ref[j - 1, :half, (dp + k) * unit : (dp + k + 1) * unit] = cols[half:]
        start = pl.multiple_of(part * unit, unit)
        out_ref[j - 1, half:, :] = shrink_ref[pl.ds(start, unit), :]


def mixer_kernel(sizes, idx, *refs):
    uly, dp = sizes
    pieces, (m_ref, turn_ref) = refs[:-2], refs[-2:]
    lines = pieces[0].shape[0] // dp
    b, u, z = idx[0], idx[1], idx[2]
    shard = 2 * uly * lines
    for k in range(dp):
        for p, ref in enumerate(pieces):
            part = (b * uly + u) ^ p
            turn_ref[pl.ds(pl.multiple_of(part * lines, 8), lines), :] = ref[
                k * lines : (k + 1) * lines, :
            ].astype(F32)
        start = pl.multiple_of((z ^ k) * shard, shard)
        m_ref[pl.ds(start, shard), :] = turn_ref[...].astype(BF16)


def assemble_kernel(sizes, k, idx, *refs):
    uly, dp, unit = sizes
    e_ref, s_ref, sem = refs[-3:]
    block = dp * unit
    shard = e_ref.shape[0] // dp
    half = shard // 2
    owner = idx[2] ^ k
    copies = []
    for j in range(uly):
        if k == 0:
            piece = refs[0] if j == 0 else refs[1].at[j - 1]
        else:
            piece = refs[2 + j]
        for h in range(2):
            start = pl.multiple_of(owner * shard + h * half, half)
            copies.append(
                pltpu.make_async_copy(
                    piece.at[pl.ds(0, half), pl.ds(h * block, block)],
                    e_ref.at[pl.ds(start, half), pl.ds(j * block, block)],
                    sem.at[3 * j + h],
                )
            )
        start = pl.multiple_of(j * block + owner * unit, unit)
        copies.append(
            pltpu.make_async_copy(
                piece.at[pl.ds(half, unit), :], s_ref.at[pl.ds(start, unit), :], sem.at[3 * j + 2]
            )
        )
    for copy in copies:
        copy.start()
    for copy in copies:
        copy.wait()


def assemble(scalars, sizes, k, weights, pieces):
    uly, dp, unit = sizes
    width = pieces[0].shape[1]
    block = uly * dp * unit
    hbm = pl.BlockSpec(memory_space=pl.ANY)
    return call(
        functools.partial(assemble_kernel, sizes, k),
        "assemble",
        scalars,
        [*weights, *pieces],
        [hbm] * (len(weights) + len(pieces)),
        [jax.ShapeDtypeStruct((width, block), BF16), jax.ShapeDtypeStruct((block, width), BF16)],
        [hbm] * 2,
        [pltpu.SemaphoreType.DMA((3 * uly,))],
        (1,),
        10**6,
        16,
        {1: 0, 2: 1} if weights else {},
    )


def feed_forward_kernel(uly, idx, mine_ref, other_ref, eb_ref, e_ref, s_ref, *refs):
    act_ref, slope_ref, y_ref, send_ref, x_ref = refs
    rows = mine_ref.shape[0]
    block = e_ref.shape[1] // uly
    x_ref[:rows] = mine_ref[...]
    x_ref[rows:] = other_ref[...]
    for j in range(uly):
        lanes = slice(j * block, (j + 1) * block)
        pre = dot_nn(x_ref[...], e_ref[:, lanes]) + eb_ref[j : j + 1, :]
        cdf = 0.5 * (1.0 + lax.erf(pre * 0.7071067811865476))
        pdf = jnp.exp(-0.5 * pre * pre) * 0.3989422804014327
        act_ref[:, lanes] = (pre * cdf).astype(BF16)
        slope_ref[:, lanes] = (cdf + pre * pdf).astype(BF16)
    out = dot_nn(act_ref[...], s_ref[...])
    y_ref[...] = out[:rows]
    send_ref[...] = out[rows:].astype(BF16)


def feed_forward(scalars, uly, mine, other, eb, weights):
    rows, width = mine.shape
    block = weights[0].shape[1]
    args = [mine, other, eb, *weights]
    return call(
        functools.partial(feed_forward_kernel, uly),
        "feed_forward",
        scalars,
        args,
        [whole(arg.shape) for arg in args],
        [
            jax.ShapeDtypeStruct((2 * rows, block), BF16),
            jax.ShapeDtypeStruct((2 * rows, block), BF16),
            jax.ShapeDtypeStruct((rows, width), F32),
            jax.ShapeDtypeStruct((rows, width), BF16),
        ],
        [whole((2 * rows, block))] * 2 + [whole((rows, width))] * 2,
        [pltpu.VMEM((2 * rows, width), BF16)],
        (1,),
        8 * rows * width * block,
        24,
    )


def final_norm_kernel(idx, x1_ref, y_ref, got_ref, vec_ref, cot_ref, *refs):
    mixed_ref, dh_ref, low_ref, sums_ref = refs
    hidden = x1_ref[...] + (y_ref[...] + got_ref[...].astype(F32) + vec_ref[5:6, :])
    gain = vec_ref[6:7, :]
    center = hidden - jnp.mean(hidden, -1, keepdims=True)
    inverse = lax.rsqrt(jnp.mean(center * center, -1, keepdims=True) + EPSILON)
    normed = center * inverse
    mixed_ref[...] = (normed * gain + vec_ref[7:8, :]).astype(BF16)
    grad = cot_ref[...].astype(F32)
    scaled = grad * gain
    dhidden = inverse * (
        scaled
        - jnp.mean(scaled, -1, keepdims=True)
        - normed * jnp.mean(scaled * normed, -1, keepdims=True)
    )
    dh_ref[...] = dhidden
    low_ref[...] = dhidden.astype(BF16)
    sums_ref[...] = jnp.zeros_like(sums_ref)
    sums_ref[0:1, :] = jnp.sum(dhidden, 0, keepdims=True)
    sums_ref[1:2, :] = jnp.sum(grad * normed, 0, keepdims=True)
    sums_ref[2:3, :] = jnp.sum(grad, 0, keepdims=True)


def shrink_grad_kernel(sizes, idx, d_mine, d_other, act_ref, *refs):
    uly, dp, unit = sizes
    near_x, far_x, near_y, far_y = (refs[2 * i : 2 * i + 2] for i in range(4))
    d_ref, turn_ref = refs[8:]
    block = dp * unit
    rows = d_mine.shape[0]
    d_ref[:rows] = d_mine[...]
    d_ref[rows:] = d_other[...]
    for j in range(uly):
        turn_ref[...] = dot_tn(act_ref[:, j * block : (j + 1) * block], d_ref[...]).astype(BF16)
        for k in range(dp):
            if k % 2 == 0:
                ref, at = (far_x if j % 2 else near_x), j // 2
            else:
                ref, at = (near_y if j < uly // 2 else far_y), j % 2
            start = pl.multiple_of((idx[2] ^ k) * unit, unit)
            into = slice((k // 2) * unit, (k // 2 + 1) * unit)
            ref[at][into, :] = turn_ref[pl.ds(start, unit), :]


def shrink_grad(scalars, sizes, ds, act):
    uly, dp, unit = sizes
    rows, width = ds[0].shape
    block = dp * unit
    half = (block // 2, width)
    return call(
        functools.partial(shrink_grad_kernel, sizes),
        "shrink_grad",
        scalars,
        [*ds, act],
        [whole((rows, width))] * 2 + [whole(act.shape)],
        [jax.ShapeDtypeStruct(half, BF16)] * 8,
        [whole(half)] * 8,
        [pltpu.VMEM((2 * rows, width), BF16), pltpu.VMEM((block, width), BF16)],
        (1,),
        4 * rows * width * uly * block,
        16,
    )


def feed_backward_kernel(sizes, idx, x_mine, x_other, d_mine, d_other, slope_ref, *refs):
    uly, dp, unit = sizes
    e_ref, s_ref, *refs = refs
    near_x, far_x, near_y, far_y = (refs[2 * i : 2 * i + 2] for i in range(4))
    deb_ref, dx_ref, send_ref, xt_ref, d_ref, turn_ref, dpre_ref = refs[8:]
    rows, width = x_mine.shape
    shard = width // dp
    half = width // 2
    block = dp * unit
    turn_ref[:, :rows] = x_mine[...].T
    turn_ref[:, rows:] = x_other[...].T
    for k in range(dp):
        start = pl.multiple_of((idx[2] ^ k) * shard, shard)
        into = slice(slot(k) * shard, (slot(k) + 1) * shard)
        xt_ref[into, :] = turn_ref[pl.ds(start, shard), :]
    d_ref[:rows] = d_mine[...]
    d_ref[rows:] = d_other[...]
    for j in range(uly):
        lanes = slice(j * block, (j + 1) * block)
        dpre = dot_nt(d_ref[...], s_ref[lanes, :])
        dpre = (dpre * slope_ref[:, lanes].astype(F32)).astype(BF16)
        dpre_ref[:, lanes] = dpre
        deb_ref[j : j + 1, :] = jnp.sum(dpre.astype(F32), 0, keepdims=True)
        dexpand = dot_nn(xt_ref[...], dpre).astype(BF16)
        (far_x if j % 2 else near_x)[j // 2][...] = dexpand[:half]
        (near_y if j < uly // 2 else far_y)[j % 2][...] = dexpand[half:]
    grad = dot_nt(dpre_ref[...], e_ref[...])
    dx_ref[...] = grad[:rows]
    send_ref[...] = grad[rows:].astype(BF16)


def feed_backward(scalars, sizes, xs, ds, slope, weights):
    uly, dp, unit = sizes
    rows, width = xs[0].shape
    block = dp * unit
    half = (width // 2, block)
    args = [*xs, *ds, slope, *weights]
    return call(
        functools.partial(feed_backward_kernel, sizes),
        "feed_backward",
        scalars,
        args,
        [whole(arg.shape) for arg in args],
        [jax.ShapeDtypeStruct(half, BF16)] * 8
        + [
            jax.ShapeDtypeStruct((uly, block), F32),
            jax.ShapeDtypeStruct((rows, width), F32),
            jax.ShapeDtypeStruct((rows, width), BF16),
        ],
        [whole(half)] * 8 + [whole((uly, block)), whole((rows, width)), whole((rows, width))],
        [
            pltpu.VMEM((width, 2 * rows), BF16),
            pltpu.VMEM((2 * rows, width), BF16),
            pltpu.VMEM((width, 2 * rows), BF16),
            pltpu.VMEM((2 * rows, uly * block), BF16),
        ],
        (1,),
        12 * rows * width * uly * block,
        24,
    )


def norm_backward_kernel(sizes, idx, dh2_ref, dx_ref, got_ref, normed_ref, inverse_ref, *refs):
    uly, dp, unit = sizes
    m_ref, vec_ref, grads_ref, deb_ref, *refs = refs
    o_refs, refs = refs[:uly], refs[uly:]
    dh_ref, *refs = refs
    do_refs, refs = refs[:uly], refs[uly:]
    keep_ref, send_ref, turn_ref = refs
    b, u, z = idx[0], idx[1], idx[2]
    group = o_refs[0].shape[1]
    share = group // 2
    width = dx_ref.shape[1]
    parts = 2 * uly
    grad = dh2_ref[...] + dx_ref[...] + got_ref[...].astype(F32)
    normed = normed_ref[...]
    scaled = grad * vec_ref[3:4, :]
    dhidden = inverse_ref[...] * (
        scaled
        - jnp.mean(scaled, -1, keepdims=True)
        - normed * jnp.mean(scaled * normed, -1, keepdims=True)
    )
    dh_ref[...] = dhidden
    low = dhidden.astype(BF16)
    for j in range(uly):
        start = pl.multiple_of((u ^ j) * group, group)
        do_refs[j][...] = dot_nt(low, m_ref[pl.ds(start, group), :]).astype(BF16)
    line = lax.broadcasted_iota(jnp.int32, (8, width), 0)
    lines = jnp.zeros((8, width), F32)
    values = [
        jnp.sum(dhidden, 0, keepdims=True),
        jnp.sum(grad * normed, 0, keepdims=True),
        jnp.sum(grad, 0, keepdims=True),
        grads_ref[0:1, :],
        grads_ref[1:2, :],
        grads_ref[2:3, :],
    ]
    for k, value in enumerate(values):
        lines = jnp.where(line == k, value, lines)
    lines = lines.astype(BF16)
    owner = (lax.broadcasted_iota(jnp.int32, (parts, uly), 1) ^ u) + b * uly
    order = lax.broadcasted_iota(jnp.int32, (parts, uly), 0)
    order = jnp.where(order == owner, 1.0, 0.0).astype(BF16)
    ebs = dot_nn(order, deb_ref[...].astype(BF16)).astype(BF16)
    for j in range(uly):
        turn_ref[...] = dot_tn(o_refs[j][...], low).astype(BF16)
        place = slot(u ^ j ^ z)
        keep_ref[place, :share] = turn_ref[pl.ds(pl.multiple_of(b * share, share), share), :]
        send_ref[place, :share] = turn_ref[pl.ds(pl.multiple_of((1 - b) * share, share), share), :]
    for k in range(dp):
        shard = (z ^ k) * group
        own = dot_nn(lines, one_hot(width, group, 0, shard)).astype(BF16)
        ebk = dot_nn(ebs, one_hot(dp * unit, unit, 0, (z ^ k) * unit)).astype(BF16)
        for ref in (keep_ref, send_ref):
            ref[slot(k), share:, :] = jnp.zeros_like(ref[slot(k), share:, :])
            ref[slot(k), share : share + 8, :group] = own
            ref[slot(k), share + 8 : share + 16, :unit] = ebk


def attend_grad_kernel(heads, blocks, pieces, started, q_ref, lse_ref, *refs):
    do_refs, refs = refs[:pieces], refs[pieces:]
    o_refs, refs = refs[:pieces], refs[pieces:]
    kv_refs, refs = refs[:blocks], refs[blocks:]
    so_far, refs = refs[: blocks * started], refs[blocks * started :]
    dq_ref, *refs = refs
    dkv_refs, refs = refs[:blocks], refs[blocks:]
    kt_ref, dout_ref, prod_ref, *refs = refs
    dk_accs, dv_accs = refs[:blocks], refs[blocks:]
    group = heads * HD
    wide = q_ref.shape[1]
    rows = kv_refs[0].shape[0]

    @pl.when(pl.program_id(0) == 0)
    def _():
        for i in range(blocks):
            kt_ref[:, i * rows : (i + 1) * rows] = kv_refs[i][:, :group].T
            if started:
                dk_accs[i][...] = so_far[i][:, :wide].astype(F32) * LOG2E
                dv_accs[i][...] = so_far[i][:, wide : wide + group].astype(F32)
            else:
                dk_accs[i][...] = jnp.zeros_like(dk_accs[i])
                dv_accs[i][...] = jnp.zeros_like(dv_accs[i])

    for j in range(pieces):

        @pl.when(pl.program_id(0) == j)
        def _(j=j):
            dout_ref[...] = do_refs[j][...]
            prod_ref[...] = (do_refs[j][...].astype(F32) * o_refs[j][...].astype(F32)).T

    q = q_ref[...]
    dout = dout_ref[...]
    dqs = []
    for head in range(heads):
        q_head = jnp.where(head_lanes(wide, head, group), q, jnp.zeros_like(q))
        do_head = jnp.where(head_lanes(group, head), dout, jnp.zeros_like(dout))
        lse = lse_ref[head : head + 1, :]
        delta = jnp.sum(prod_ref[head * HD : (head + 1) * HD, :], axis=0, keepdims=True)
        acc = None
        for i in range(blocks):
            probs = jnp.exp2(dot_nt(kv_refs[i][:, :wide], q_head) - lse)
            dv_accs[i][...] += dot_nn(probs.astype(BF16), do_head)
            grads = dot_nt(kv_refs[i][:, wide : wide + group], do_head)
            grads = (probs * (grads - delta)).astype(BF16)
            dk_accs[i][...] += dot_nn(grads, q_head)
            part = dot_nn(
                kt_ref[head * HD : (head + 1) * HD, i * rows : (i + 1) * rows], grads
            )
            acc = part if acc is None else acc + part
        dqs.append(acc)
    dq_ref[...] = jnp.concatenate(dqs, axis=0).T.astype(BF16)

    @pl.when(pl.program_id(0) == pl.num_programs(0) - 1)
    def _():
        for i in range(blocks):
            dkv_refs[i][:, :group] = (dk_accs[i][:, :group] * LN2).astype(BF16)
            dkv_refs[i][:, group:wide] = jnp.zeros((rows, wide - group), BF16)
            dkv_refs[i][:, wide : wide + group] = dv_accs[i][...].astype(BF16)
            dkv_refs[i][:, wide + group :] = jnp.zeros((rows, wide - group), BF16)


def attend_grad(q, kvs, douts, outs, lse, heads, at, so_far):
    rows, wide = kvs[0].shape[0], q.shape[1]
    group = heads * HD
    blocks = len(kvs)
    pieces = len(douts)
    tile = douts[0].shape[0]
    keys = blocks * rows
    started = 1 if so_far else 0
    out = pl.pallas_call(
        functools.partial(attend_grad_kernel, heads, blocks, pieces, started),
        grid=(pieces,),
        in_specs=[
            pl.BlockSpec((tile, wide), lambda t: (t + at, 0)),
            pl.BlockSpec((8, tile), lambda t: (0, t + at)),
        ]
        + [whole((tile, group))] * (2 * pieces)
        + [whole(kvs[0].shape)] * (blocks + blocks * started),
        out_specs=[pl.BlockSpec((tile, group), lambda t: (t, 0))]
        + [whole(kvs[0].shape)] * blocks,
        out_shape=[jax.ShapeDtypeStruct((pieces * tile, group), BF16)]
        + [jax.ShapeDtypeStruct(kvs[0].shape, BF16)] * blocks,
        scratch_shapes=[
            pltpu.VMEM((group, keys), BF16),
            pltpu.VMEM((tile, group), BF16),
            pltpu.VMEM((group, tile), F32),
        ]
        + [pltpu.VMEM((rows, wide), F32)] * blocks
        + [pltpu.VMEM((rows, group), F32)] * blocks,
        compiler_params=pltpu.CompilerParams(vmem_limit_bytes=16 * 2**20),
        cost_estimate=pl.CostEstimate(
            flops=10 * heads * pieces * tile * keys * wide,
            transcendentals=heads * pieces * tile * keys,
            bytes_accessed=2 * rows * wide * 4 + 4 * keys * (wide + group),
        ),
        name="attend_grad",
    )(q, lse, *douts, *outs, *kvs, *so_far)
    return out[0], out[1:]


def project_grad_kernel(sizes, idx, *refs):
    uly, dp, group = sizes
    dq_refs, (own_ref, got_ref, *refs) = refs[:uly], refs[uly:]
    x_refs, refs = refs[:uly], refs[uly:]
    dproj_ref, keep_ref, send_ref = refs
    b, z = idx[0], idx[2]
    rows, width = x_refs[0].shape
    wide = own_ref.shape[1] // 2
    share = keep_ref.shape[1] - 16
    for k, ref in enumerate(dq_refs):
        here = slice(k * ref.shape[0], (k + 1) * ref.shape[0])
        dproj_ref[here, :group] = ref[...] * jnp.asarray(0.125, BF16)
    dproj_ref[:, group:wide] = jnp.zeros((uly * rows, wide - group), BF16)
    dproj_ref[:, wide:] = (own_ref[...].astype(F32) + got_ref[...].astype(F32)).astype(BF16)
    sums = jnp.sum(dproj_ref[...].astype(F32), 0, keepdims=True).astype(BF16)
    grad = None
    for j in range(uly):
        part = dot_tn(x_refs[j][...], dproj_ref[j * rows : (j + 1) * rows, :])
        grad = part if grad is None else grad + part
    grad = grad.astype(BF16)
    for ref, mine in ((keep_ref, True), (send_ref, False)):
        for c in range(3):
            lanes = slice(c * wide, c * wide + group)
            into = slice(c * group, (c + 1) * group)
            for s in range(dp):
                for core in range(2):
                    start = (s * 2 + core) * share

                    @pl.when((b == core) == mine)
                    def _(start=start, s=s, ref=ref, lanes=lanes, into=into):
                        ref[slot(s ^ z), :share, into] = grad[start : start + share, lanes]

                ref[s, share:, into] = jnp.broadcast_to(sums[:, lanes], (16, group))


def token_grad_kernel(uly, idx, dproj_ref, w_ref, dh_ref, *out_refs):
    rows = dh_ref.shape[0]
    for j in reversed(range(uly)):
        part = dot_nt(dproj_ref[j * rows : (j + 1) * rows, :], w_ref[...])
        if j == 0:
            part = part + dh_ref[...]
        out_refs[j][...] = part.astype(out_refs[j].dtype)


def pack_kernel(idx, sx_ref, sx1_ref, sx2_ref, sy_ref, sy1_ref, sy2_ref, keep_ref, got_ref, *refs):
    unit = sx2_ref.shape[0] // 2
    for out_refs, first, s_refs in (
        (refs[:2], 0, (sx_ref, sx1_ref, sx2_ref)),
        (refs[2:], 2, (sy_ref, sy1_ref, sy2_ref)),
    ):
        for k, out_ref in enumerate(out_refs):
            rows = slice(k * unit, (k + 1) * unit)
            value = s_refs[0][rows].astype(F32) + s_refs[1][rows].astype(F32)
            out_ref[:unit, :] = (value + s_refs[2][rows].astype(F32)).astype(BF16)
            value = keep_ref[first + k].astype(F32) + got_ref[first + k].astype(F32)
            out_ref[unit:, :] = value.astype(BF16)


def finish_shrink_kernel(sizes, idx, *refs):
    uly, unit = sizes
    pieces, (shrink_ref, mixer_ref, vec_ref, wide_ref, sum_ref, sem) = refs[: 2 * uly], refs[2 * uly :]
    share = mixer_ref.shape[0] // 2
    part = idx[0] * uly + idx[1]
    copies = []
    for p, ref in enumerate(pieces):
        wide_ref[p] = ref[:unit, :].astype(F32)
        start = pl.multiple_of((part ^ p) * unit, unit)
        copies.append(
            pltpu.make_async_copy(wide_ref.at[p], shrink_ref.at[pl.ds(start, unit), :], sem.at[p])
        )
        copies[-1].start()

    def plane_sum(refs, rows):
        values = [ref[rows, :].astype(F32) for ref in refs]
        return (values[0] + values[1]) + (values[2] + values[3])

    for i, core in enumerate((idx[0], 1 - idx[0])):
        group = pieces[i * uly : (i + 1) * uly]
        sum_ref[i] = plane_sum(group, slice(unit, unit + share))
        start = pl.multiple_of(core * share, share)
        copies.append(
            pltpu.make_async_copy(
                sum_ref.at[i], mixer_ref.at[pl.ds(start, share), :], sem.at[2 * uly + i]
            )
        )
        copies[-1].start()
    vec_ref[...] = plane_sum(pieces[:uly], slice(unit + share, unit + share + 16))
    for copy in copies:
        copy.wait()


def finish_expand_kernel(sizes, idx, *refs):
    uly, dp, unit = sizes
    pieces, (out_ref, turn_ref, wide_ref, sem) = refs[:-4], refs[-4:]
    width = turn_ref.shape[0]
    part = idx[0] * uly + idx[1]
    col = lax.broadcasted_iota(jnp.int32, (width, width), 1)
    row = lax.broadcasted_iota(jnp.int32, (width, width), 0)
    source = col + ((col // unit) ^ part) * unit - (col // unit) * unit
    turn_ref[...] = jnp.where(row == source, 1.0, 0.0).astype(BF16)
    copies = []
    for k in range(dp):
        line = jnp.concatenate([ref[:, k * unit : (k + 1) * unit] for ref in pieces], 1)
        wide_ref[k] = dot_nn(line, turn_ref[...])
        copies.append(
            pltpu.make_async_copy(
                wide_ref.at[k], out_ref.at[:, pl.ds(k * width, width)], sem.at[k]
            )
        )
        copies[-1].start()
    for copy in copies:
        copy.wait()


def finish_attend_kernel(uly, idx, *refs):
    mine, refs = refs[:uly], refs[uly:]
    other, refs = refs[:uly], refs[uly:]
    out_ref, query_ref, value_ref, wide_ref, sem = refs
    b, u, z = idx[0], idx[1], idx[2]
    share = mine[0].shape[0] - 16
    group = mine[0].shape[1] // 3
    width = uly * group
    copies = []
    for i, (group_refs, core) in enumerate(((mine, b), (other, 1 - b))):
        start = pl.multiple_of(core * share, share)
        for c in range(3):
            acc = None
            for j in range(uly):
                put = one_hot(group, width, (u ^ j) * group, 0)
                value = dot_nn(group_refs[j][:share, c * group : (c + 1) * group], put)
                acc = value if acc is None else acc + value
            wide_ref[3 * i + c] = acc
            copies.append(
                pltpu.make_async_copy(
                    wide_ref.at[3 * i + c],
                    out_ref.at[pl.ds(start, share), pl.ds(c * width, width)],
                    sem.at[3 * i + c],
                )
            )
            copies[-1].start()
    bias = jnp.zeros((8, 3 * group), F32)
    for j in range(uly):
        lines = mine[j][share : share + 16, :].astype(F32)[:8]
        bias += jnp.where((u ^ j) == z, 1.0, 0.0) * lines
    query_ref[...] = bias[0, :group]
    value_ref[...] = bias[0, 2 * group :]
    for copy in copies:
        copy.wait()


def on_device(*args):
    (
        tokens,
        lengths,
        cotangent,
        attend_weight,
        query_bias,
        value_bias,
        mixer_weight,
        mixer_bias,
        attn_gain,
        attn_shift,
        expand_weight,
        expand_bias,
        shrink_weight,
        shrink_bias,
        final_gain,
        final_shift,
    ) = args
    uly = lax.axis_size("uly")
    blk = lax.axis_size("blk")
    dp = lax.axis_size("dp")
    width = tokens.shape[-1]
    rows = tokens.shape[0] * tokens.shape[1]
    heads = HEADS // uly
    group = heads * HD
    wide = -(-(group + 1) // 128) * 128
    shard = attend_weight.shape[0]
    hidden = expand_weight.shape[1]
    parts = blk * uly
    unit = hidden // (parts * dp)
    share = shard // blk
    if not (blk == 2 and uly == 4 and dp == 4 and shard == group and unit * 2 == shard and share % 16 == 0):
        return general_device(*args)
    u = lax.axis_index("uly")
    b = lax.axis_index("blk")
    z = lax.axis_index("dp")
    mixer_rows = share // dp
    feed_rows = shard // 2 + unit
    block_rows = uly * rows
    cols = 3 * wide

    x = tokens.reshape(rows, width)
    xs = [x, swap_with(x, "uly", 1), swap_with(x, "uly", 2)]
    xs.append(swap_with(after(x, *xs[1:]), "uly", 3))
    scalars = jnp.stack([b, u, z, lengths[0]]).astype(jnp.int32)
    vectors = [query_bias, value_bias, mixer_bias, attn_gain, attn_shift, shrink_bias]
    vectors += [final_gain, final_shift, expand_bias]
    first, feed = call(
        functools.partial(fetch_kernel, (uly, dp, group, unit)),
        "fetch",
        scalars,
        [
            attend_weight.reshape(blk, share, 3 * width),
            expand_weight,
            shrink_weight.reshape(parts, unit, width),
            mixer_weight,
            *vectors,
        ],
        [
            pl.BlockSpec((1, share, 3 * width), lambda t, s: (s[0], 0, 0)),
            whole(expand_weight.shape),
            pl.BlockSpec((1, unit, width), lambda t, s: (s[0] * uly + s[1], 0, 0)),
            whole(mixer_weight.shape),
            *[whole(vector.shape) for vector in vectors],
        ],
        [
            jax.ShapeDtypeStruct((share + 16, width), BF16),
            jax.ShapeDtypeStruct((feed_rows, width), BF16),
        ],
        [whole((share + 16, width)), whole((feed_rows, width))],
        [],
        (1,),
        10**9,
        58,
    )
    feeds = [None, swap_with(feed, "dp", 1)]
    mine = [first, None, swap_with(first, "dp", 2), swap_with(first, "dp", 3)]
    mine[1] = swap_with(after(first, *xs[1:3]), "dp", 1)
    feeds.append(swap_with(after(feed, *mine[1:]), "dp", 2))
    plane_one = [swap_with(feeds[1], "uly", j) for j in range(1, uly)]
    other = [swap_with(after(piece, *plane_one), "blk", 1) for piece in mine]
    rest = call(
        functools.partial(rest_kernel, (uly, dp, unit)),
        "fetch_rest",
        scalars,
        [expand_weight, shrink_weight],
        [whole(expand_weight.shape), whole(shrink_weight.shape)],
        jax.ShapeDtypeStruct((uly - 1, shard // 2 + unit, width), BF16),
        whole((uly - 1, shard // 2 + unit, width)),
        [],
        (1,),
        10**9,
        16,
    )

    w_own, q, kv, vec, eb, mixer_mine = call(
        functools.partial(project_kernel, (uly, blk, dp, group, unit)),
        "project",
        scalars,
        [*after(xs, feeds[1], rest), *mine, *other],
        [whole((rows, width))] * uly + [whole(first.shape)] * (2 * dp),
        [
            jax.ShapeDtypeStruct((width, cols), BF16),
            jax.ShapeDtypeStruct((block_rows, wide), BF16),
            jax.ShapeDtypeStruct((block_rows, 2 * wide), BF16),
            jax.ShapeDtypeStruct((16, width), F32),
            jax.ShapeDtypeStruct((parts, dp * unit), F32),
            jax.ShapeDtypeStruct((dp * mixer_rows, width), BF16),
        ],
        [
            whole((width, cols)),
            whole((block_rows, wide)),
            whole((block_rows, 2 * wide)),
            whole((16, width)),
            whole((parts, dp * unit)),
            whole((dp * mixer_rows, width)),
        ],
        [],
        (1,),
        2 * block_rows * width * cols,
        16,
    )
    kv_send, mixer_mine = after((kv, mixer_mine), feeds[2])
    kvs = [kv, swap_with(kv_send, "blk", 1)]

    mixer_plane = [swap_with(mixer_mine, "uly", j) for j in range(1, uly)]

    plane_two = [swap_with(feeds[2], "uly", j) for j in range(1, uly)]
    feed_three = swap_with(after(feed, feeds[2]), "dp", 3)
    outs, lse = attend(after(q, feeds[2]), kvs, heads, uly)
    outs, mixer_plane, plane_two, feed_three = after((outs, mixer_plane, plane_two, feed_three))
    feeds.append(feed_three)
    plane_three = [swap_with(feed_three, "uly", j) for j in range(1, uly)]
    mixer_parts = [mixer_mine, *mixer_plane]
    mixer_parts += [swap_with(piece, "blk", 1) for piece in mixer_parts]
    mixer_all = call(
        functools.partial(mixer_kernel, (uly, dp)),
        "mixer_weight",
        scalars,
        mixer_parts,
        [whole(mixer_mine.shape)] * parts,
        jax.ShapeDtypeStruct((width, width), BF16),
        whole((width, width)),
        [pltpu.VMEM((shard, width), F32)],
        (1,),
        10**6,
        16,
    )

    sizes = (uly, dp, unit)
    weights = assemble(scalars, sizes, 0, [], [feed, rest])
    weights = assemble(scalars, sizes, 1, weights, [feeds[1], *plane_one])
    weights = assemble(scalars, sizes, 2, weights, [feeds[2], *plane_two])
    o_cols = after(outs, *plane_three, *weights, mixer_all)
    o_cols = [o_cols[0]] + [swap_with(o_cols[j], "uly", j) for j in range(1, uly)]
    square = (rows, width)
    weights = assemble(scalars, sizes, 3, weights, [feeds[3], *plane_three])
    x1, x1b, normed, inverse = call(
        functools.partial(first_norm_kernel, uly),
        "first_norm",
        scalars,
        [x, *o_cols, after(mixer_all, *weights), vec],
        [whole(square)] + [whole((rows, group))] * uly + [whole((width, width)), whole(vec.shape)],
        [
            jax.ShapeDtypeStruct(square, F32),
            jax.ShapeDtypeStruct(square, BF16),
            jax.ShapeDtypeStruct(square, F32),
            jax.ShapeDtypeStruct((rows, 1), F32),
        ],
        [whole(square), whole(square), whole(square), whole((rows, 1))],
        [],
        (1,),
        2 * rows * width * width,
        16,
    )
    x1b_other = swap_with(x1b, "blk", 1)
    act, slope, y_own, y_send = feed_forward(scalars, uly, x1b, x1b_other, eb, weights)
    mixed, dh2, dh2b, sums2 = call(
        final_norm_kernel,
        "final_norm",
        scalars,
        [x1, y_own, swap_with(y_send, "blk", 1), vec, cotangent.reshape(square)],
        [whole(square)] * 3 + [whole(vec.shape), whole(square)],
        [
            jax.ShapeDtypeStruct(square, BF16),
            jax.ShapeDtypeStruct(square, F32),
            jax.ShapeDtypeStruct(square, BF16),
            jax.ShapeDtypeStruct((8, width), F32),
        ],
        [whole(square)] * 3 + [whole((8, width))],
        [],
        (1,),
        10**6,
        16,
    )
    dh2b_other = swap_with(dh2b, "blk", 1)
    ds = [dh2b, dh2b_other]
    s_grads = shrink_grad(scalars, sizes, ds, act)
    s_near_x, s_far_x, s_near_y, s_far_y = (s_grads[2 * i : 2 * i + 2] for i in range(4))
    s_x1 = swap_with(s_far_x[1], "uly", 1)
    s_y1 = swap_with(s_far_y[1], "uly", 2)
    ds = after(ds, s_far_x[0])
    grads = feed_backward(scalars, sizes, [x1b, x1b_other], ds, slope, weights)
    e_near_x, e_far_x, e_near_y, e_far_y = (grads[2 * i : 2 * i + 2] for i in range(4))
    deb, dx_own, dx_send = grads[8:]

    def add(*values):
        return total(values).astype(BF16)

    dx_send, s_far_x0, s_far_y0, s_x1, s_y1 = after(
        (dx_send, s_far_x[0], s_far_y[0], s_x1, s_y1)
    )
    dx_got = swap_with(dx_send, "blk", 1)
    s_x0 = swap_with(s_far_x0, "uly", 1)
    s_y0 = swap_with(s_far_y0, "uly", 2)
    block = (dp, share + 16, width)
    dh1, *rest_out = call(
        functools.partial(norm_backward_kernel, sizes),
        "norm_backward",
        scalars,
        [dh2, dx_own, dx_got, normed, inverse, mixer_all]
        + [vec, sums2]
        + [deb, *o_cols],
        [whole(square)] * 4
        + [whole((rows, 1)), whole((width, width)), whole(vec.shape), whole(sums2.shape)]
        + [whole((uly, dp * unit))]
        + [whole((rows, group))] * uly,
        [jax.ShapeDtypeStruct(square, F32)]
        + [jax.ShapeDtypeStruct((rows, group), BF16)] * uly
        + [jax.ShapeDtypeStruct(block, BF16)] * 2,
        [whole(square)] + [whole((rows, group))] * uly + [whole(block)] * 2,
        [pltpu.VMEM((group, width), BF16)],
        (1,),
        4 * rows * width * width,
        16,
    )
    douts = [rest_out[0]] + [swap_with(rest_out[j], "uly", j) for j in range(1, uly)]
    m_keep, m_send = rest_out[uly:]

    def quarter(j, so_far, *deps):
        dout = after(douts[j], *deps)
        return attend_grad(q, kvs, [dout], [outs[j]], lse, heads, j, so_far)

    dq_0, dkvs = quarter(0, [])
    dq_0, m_send, s_x0, s_y0, s_x1, s_y1, e_far_x, e_far_y, *douts[1:] = after(
        (dq_0, m_send, s_x0, s_y0, s_x1, s_y1, e_far_x, e_far_y, *douts[1:])
    )
    s_next_x = add(s_near_x[1], s_x1)
    s_next_y = add(s_near_y[1], s_y1)
    s_xy = swap_with(s_next_x, "uly", 2)
    s_yx = swap_with(s_next_y, "uly", 1)
    m_got = swap_with(m_send, "blk", 1)
    e_x1 = swap_with(e_far_x[1], "uly", 1)
    e_y1 = swap_with(e_far_y[1], "uly", 2)

    dq_1, dkvs = quarter(1, dkvs, s_next_x, s_next_y)
    dq_1, s_xy, s_yx, m_got, e_far_x, e_far_y = after((dq_1, s_xy, s_yx, m_got, e_far_x, e_far_y))
    packed = (unit + share + 16, width)
    p_near_0, p_near_1, p_far_0, p_far_1 = call(
        pack_kernel,
        "pack",
        scalars,
        [s_near_x[0], s_x0, s_xy, s_near_y[0], s_y0, s_yx, m_keep, m_got],
        [whole(s_xy.shape)] * 6 + [whole(m_keep.shape)] * 2,
        [jax.ShapeDtypeStruct(packed, BF16)] * 4,
        [whole(packed)] * 4,
        [],
        (1,),
        10**6,
        16,
    )
    p_one_1 = swap_with(p_far_1, "dp", 1)
    e_x0 = swap_with(e_far_x[0], "uly", 1)
    e_y0 = swap_with(e_far_y[0], "uly", 2)

    dq_2, dkvs = quarter(2, dkvs, p_far_1)
    dq_2, e_x0, e_y0, e_x1, e_y1, p_one_1, p_far_0 = after(
        (dq_2, e_x0, e_y0, e_x1, e_y1, p_one_1, p_far_0)
    )
    p_one_0 = swap_with(p_far_0, "dp", 1)
    p_next = add(p_near_1, p_one_1)
    p_two = swap_with(p_next, "dp", 2)
    e_next_x = add(e_near_x[1], e_x1)
    e_next_y = add(e_near_y[1], e_y1)
    e_xy = swap_with(e_next_x, "uly", 2)
    e_yx = swap_with(e_next_y, "uly", 1)

    dq_3, dkvs = quarter(3, dkvs, e_next_x, e_next_y, p_next)
    dq_3, e_xy, e_yx, p_one_0, *dkvs = after((dq_3, e_xy, e_yx, p_one_0, *dkvs))
    dkv_got = swap_with(dkvs[1], "blk", 1)
    pair = (2, shard, dp * unit)
    e_near = add(e_near_x[0], e_x0, e_xy).reshape(pair)
    e_far = add(e_near_y[0], e_y0, e_yx).reshape(pair)
    dkv_got = after(dkv_got, e_near, e_far)
    dqs = [dq_0, dq_1, dq_2, dq_3]
    dproj, a_keep, a_send = call(
        functools.partial(project_grad_kernel, (uly, dp, group)),
        "project_grad",
        scalars,
        [*dqs, dkvs[0], dkv_got, *xs],
        [whole(dq_0.shape)] * uly + [whole(kv.shape)] * 2 + [whole(square)] * uly,
        [
            jax.ShapeDtypeStruct((block_rows, cols), BF16),
            jax.ShapeDtypeStruct((dp, share + 16, 3 * group), BF16),
            jax.ShapeDtypeStruct((dp, share + 16, 3 * group), BF16),
        ],
        [whole((block_rows, cols))] + [whole((dp, share + 16, 3 * group))] * 2,
        [],
        (1,),
        2 * block_rows * width * cols,
        16,
    )
    a_got = swap_with(a_send, "blk", 1)
    token_parts = call(
        functools.partial(token_grad_kernel, uly),
        "token_grad",
        scalars,
        [dproj, w_own, dh1],
        [whole((block_rows, cols)), whole((width, cols)), whole(square)],
        [jax.ShapeDtypeStruct(square, F32)] + [jax.ShapeDtypeStruct(square, BF16)] * (uly - 1),
        [whole(square)] * uly,
        [],
        (1,),
        2 * block_rows * width * cols,
        16,
    )

    def in_plane(own, *deps):
        own = after(own, *deps)
        return [own] + [swap_with(own, "uly", j) for j in range(1, uly)]

    def both_cores(pieces, *deps):
        return pieces + [swap_with(after(piece, *deps), "blk", 1) for piece in pieces]

    a_got = after(a_got, token_parts[0])
    a_near, a_far = add(a_keep[:2], a_got[:2]), add(a_keep[2:], a_got[2:])
    token_parts = after(token_parts, a_near, a_far)
    token_got = [swap_with(token_parts[j], "uly", j) for j in range(1, uly)]
    a_one = swap_with(a_far, "dp", 1)
    a_next = add(a_near[1], a_one[1])
    a_two = swap_with(a_next, "dp", 2)
    e_one = swap_with(after(e_far, a_next), "dp", 1)
    e_next = add(e_near[1], e_one[1])
    e_two = swap_with(e_next, "dp", 2)
    tokens_grad = total([token_parts[0], *token_got])
    p_own = add(p_near_0, p_one_0, p_two)
    p_plane = in_plane(p_own, *token_got)
    p_plane = both_cores(p_plane, a_two)
    shrink_out, mixer_out, vecs = call(
        functools.partial(finish_shrink_kernel, (uly, unit)),
        "finish_shrink",
        scalars,
        p_plane,
        [whole(p_own.shape)] * parts,
        [
            jax.ShapeDtypeStruct((hidden // dp, width), F32),
            jax.ShapeDtypeStruct((shard, width), F32),
            jax.ShapeDtypeStruct((16, width), F32),
        ],
        [pl.BlockSpec(memory_space=pl.ANY)] * 2 + [whole((16, width))],
        [
            pltpu.VMEM((parts, unit, width), F32),
            pltpu.VMEM((2, share, width), F32),
            pltpu.SemaphoreType.DMA((parts + 2,)),
        ],
        (1,),
        10**6,
        16,
    )
    e_own = add(e_near[0], e_one[0], e_two)
    e_plane = in_plane(e_own, *p_plane[1:uly])
    a_own = add(a_near[0], a_one[0], a_two)
    a_plane = in_plane(a_own, *p_plane[1:uly])
    e_plane = both_cores(e_plane, shrink_out, *a_plane[1:3])
    expand_out = call(
        functools.partial(finish_expand_kernel, sizes),
        "finish_expand",
        scalars,
        e_plane,
        [whole(e_own.shape)] * parts,
        jax.ShapeDtypeStruct((shard, hidden), F32),
        pl.BlockSpec(memory_space=pl.ANY),
        [
            pltpu.VMEM((width, width), BF16),
            pltpu.VMEM((dp, shard, width), F32),
            pltpu.SemaphoreType.DMA((dp,)),
        ],
        (1,),
        10**9,
        16,
    )
    a_plane = both_cores(a_plane, expand_out)
    attend_out, query_out, value_out = call(
        functools.partial(finish_attend_kernel, uly),
        "finish_attend",
        scalars,
        a_plane,
        [whole(a_own.shape)] * parts,
        [jax.ShapeDtypeStruct((shard, 3 * width), F32)]
        + [jax.ShapeDtypeStruct((group,), F32)] * 2,
        [pl.BlockSpec(memory_space=pl.ANY)] + [whole((group,))] * 2,
        [pltpu.VMEM((6, share, width), F32), pltpu.SemaphoreType.DMA((6,))],
        (1,),
        10**9,
        16,
    )
    eb_out = vecs[8 : 8 + parts, :unit].reshape(-1)
    vecs = [vecs[k, :shard] for k in range(6)]
    return (
        mixed.reshape(tokens.shape),
        tokens_grad.reshape(tokens.shape),
        attend_out,
        query_out,
        value_out,
        mixer_out,
        vecs[0],
        vecs[1],
        vecs[2],
        expand_out,
        eb_out,
        shrink_out,
        vecs[3],
        vecs[4],
        vecs[5],
    )


def solution(mesh):
    row_spec = P("dp", ("blk", "uly"), None)
    matrix = P("dp", None)
    vector = P("dp")
    return jax.shard_map(
        on_device,
        mesh=mesh,
        in_specs=(
            row_spec,
            vector,
            row_spec,
            matrix,
            vector,
            vector,
            matrix,
            vector,
            vector,
            vector,
            matrix,
            vector,
            matrix,
            vector,
            vector,
            vector,
        ),
        out_specs=(
            row_spec,
            row_spec,
            matrix,
            vector,
            vector,
            matrix,
            vector,
            vector,
            vector,
            matrix,
            vector,
            matrix,
            vector,
            vector,
            vector,
        ),
        check_vma=False,
    )
```
